32 devices in a mesh: dp: 4 (over x, core), fsdp: 2 (over y), tensor: 4 (over z).
Axes of the slice: x: 2, y: 2, z: 4, core: 2. Of those that a mesh axis runs over, the one named last changes fastest.
Arguments:
- layer_input: bfloat16 [4096, 2048], P(('dp', 'fsdp', 'tensor')), may hold values from -6 to 6
- first_gain: bfloat16 [2048], P('fsdp'), may hold values from 0.5 to 1.5
- w_query: bfloat16 [2048, 2048], P('fsdp', 'tensor'), may hold values from -0.125 to 0.125
- w_key: bfloat16 [2048, 2048], P('fsdp', 'tensor'), may hold values from -0.125 to 0.125
- w_value: bfloat16 [2048, 2048], P('fsdp', 'tensor'), may hold values from -0.125 to 0.125
- w_gating: bfloat16 [2048, 2048], P('fsdp', 'tensor'), may hold values from -0.125 to 0.125
- w_beta: bfloat16 [2048, 16], P('fsdp', 'tensor'), may hold values from -0.125 to 0.125
- conv_query: bfloat16 [4, 2048], P(None, 'tensor'), may hold values from -3 to 3
- conv_key: bfloat16 [4, 2048], P(None, 'tensor'), may hold values from -3 to 3
- conv_value: bfloat16 [4, 2048], P(None, 'tensor'), may hold values from -3 to 3
- head_gain: bfloat16 [128], replicated, may hold values from 0.5 to 1.5
- w_project: bfloat16 [2048, 2048], P('tensor', 'fsdp'), may hold values from -0.1875 to 0.1875
- second_gain: bfloat16 [2048], P('fsdp'), may hold values from 0.5 to 1.5
- w_gate: bfloat16 [2048, 5632], P('fsdp', 'tensor'), may hold values from -0.125 to 0.125
- w_up: bfloat16 [2048, 5632], P('fsdp', 'tensor'), may hold values from -0.125 to 0.125
- w_down: bfloat16 [5632, 2048], P('tensor', 'fsdp'), may hold values from -0.109375 to 0.109375
- doc_starts: int32 [8, 4], P(('dp', 'fsdp')), may hold values from 1 to 508, as said below
- seq_lengths: int32 [8], P(('dp', 'fsdp')), may hold values from 256 to 512, as said below
- output_grad: bfloat16 [4096, 2048], P(('dp', 'fsdp', 'tensor')), may hold values from -6 to 6
Outputs:
- result: bfloat16 [4096, 2048], P(('dp', 'fsdp', 'tensor'))
- input_grad: float32 [4096, 2048], P(('dp', 'fsdp', 'tensor'))
- grad_first: float32 [2048], P(('dp', 'fsdp'))
- grad_query: float32 [2048, 2048], P(('dp', 'fsdp'), 'tensor')
- grad_key: float32 [2048, 2048], P(('dp', 'fsdp'), 'tensor')
- grad_value: float32 [2048, 2048], P(('dp', 'fsdp'), 'tensor')
- grad_gating: float32 [2048, 2048], P(('dp', 'fsdp'), 'tensor')
- grad_beta: float32 [2048, 16], P(('dp', 'fsdp'), 'tensor')
- convgrad_query: float32 [4, 2048], P(None, 'tensor')
- convgrad_key: float32 [4, 2048], P(None, 'tensor')
- convgrad_value: float32 [4, 2048], P(None, 'tensor')
- grad_head: float32 [128], replicated
- grad_project: float32 [2048, 2048], P('tensor', ('dp', 'fsdp'))
- grad_second: float32 [2048], P(('dp', 'fsdp'))
- grad_gate: float32 [2048, 5632], P(('dp', 'fsdp'), 'tensor')
- grad_up: float32 [2048, 5632], P(('dp', 'fsdp'), 'tensor')
- grad_down: float32 [5632, 2048], P('tensor', ('dp', 'fsdp'))
The draws below stay inside these ranges and needn't reach their ends.
Inputs may be any that keep to these rules, and one draw needn't show every extreme that they name: `doc_starts`: each row rises strictly; position 0 begins the first document of a sequence and each entry begins the next. `seq_lengths`: rows at positions at or past a sequence's length are padding.
All inputs are finite; a program needn't handle non-finite values.
Results may differ from the reference program's by a relative error of at most 0.015.
Values may be sent and summed in bfloat16 or wider, within the bound.
A program may use at most 256 MiB of HBM per device.

```python
import jax
import jax.numpy as jnp
from jax import lax

D = 2048
HEADS = 16
HEAD = 128
FF = 5632
KERNEL = 4
BLOCK = 64
DOCS = 4
LENGTH = 512
SEQS = 8
TOKENS = 4096


def draw_doc_starts(key, part):
    region = (LENGTH - 1) // DOCS
    offsets = jax.random.randint(key, (SEQS, DOCS), 0, region)
    anchor = 1 + jnp.arange(DOCS, dtype=jnp.int32) * region
    starts = anchor[None, :] + offsets
    starts = starts.at[0, 0].set(1)
    starts = starts.at[0, DOCS - 1].set(DOCS * region)
    return starts.astype(jnp.int32)


def draw_seq_lengths(key, part):
    lengths = jax.random.randint(key, (SEQS,), LENGTH // 2, LENGTH + 1)
    lengths = lengths.at[0].set(LENGTH)
    lengths = lengths.at[1].set(LENGTH // 2)
    return lengths.astype(jnp.int32)


def block_levels(key, dims, split, smallest, high):
    loudness = 1.0
    for position, blocks in split:
        heights = jax.random.uniform(jax.random.fold_in(jax.random.fold_in(key, 6), position), (blocks,), jnp.float32, smallest / len(split), high / len(split))
        loudness = loudness * jnp.repeat(jnp.exp(heights), dims[position] // blocks).reshape((-1,) + (1,) * (len(dims) - 1 - position))
    return loudness


def noise(rng, extent, spread, reach, pieces=(), kind=jnp.bfloat16):
    level = block_levels(rng, extent, pieces, -0.22, 0.18) if pieces else 1.0
    drawn = jax.random.normal(rng, extent, jnp.float32) * spread * level
    return jnp.minimum(jnp.maximum(drawn, -reach), reach).astype(kind)


def setup_inputs(seed: int = 0) -> dict:
    seeds = jax.random.split(jax.random.key(seed), 20)
    return {
        "layer_input": noise(seeds[0], (TOKENS, D), 1.0, 6.0, ((0, 32),)),
        "first_gain": jnp.clip(1.0 + 0.1 * jax.random.normal(seeds[1], (D,), jnp.float32), 0.5, 1.5).astype(jnp.bfloat16),
        "w_query": noise(seeds[2], (D, D), D ** -0.5, 0.125, ((0, 2), (1, 4))),
        "w_key": noise(seeds[3], (D, D), D ** -0.5, 0.125, ((0, 2), (1, 4))),
        "w_value": noise(seeds[4], (D, D), D ** -0.5, 0.125, ((0, 2), (1, 4))),
        "w_gating": noise(seeds[5], (D, D), D ** -0.5, 0.125, ((0, 2), (1, 4))),
        "w_beta": noise(seeds[6], (D, HEADS), D ** -0.5, 0.125, ((0, 2), (1, 4))),
        "conv_query": noise(seeds[7], (KERNEL, D), KERNEL ** -0.5, 3.0, ((1, 4),)),
        "conv_key": noise(seeds[8], (KERNEL, D), KERNEL ** -0.5, 3.0, ((1, 4),)),
        "conv_value": noise(seeds[9], (KERNEL, D), KERNEL ** -0.5, 3.0, ((1, 4),)),
        "head_gain": jnp.clip(1.0 + 0.1 * jax.random.normal(seeds[10], (HEAD,), jnp.float32), 0.5, 1.5).astype(jnp.bfloat16),
        "w_project": noise(seeds[11], (D, D), (D // 2) ** -0.5, 0.1875, ((0, 4), (1, 2))),
        "second_gain": jnp.clip(1.0 + 0.1 * jax.random.normal(seeds[12], (D,), jnp.float32), 0.5, 1.5).astype(jnp.bfloat16),
        "w_gate": noise(seeds[13], (D, FF), D ** -0.5, 0.125, ((0, 2), (1, 4))),
        "w_up": noise(seeds[14], (D, FF), D ** -0.5, 0.125, ((0, 2), (1, 4))),
        "w_down": noise(seeds[15], (FF, D), (FF // 2) ** -0.5, 0.109375, ((0, 4), (1, 2))),
        "doc_starts": draw_doc_starts(jax.random.fold_in(seeds[19], 71), 0),
        "seq_lengths": draw_seq_lengths(jax.random.fold_in(seeds[19], 71), 0),
        "output_grad": noise(seeds[18], (TOKENS, D), 1.0, 6.0, ((0, 32),)),
    }


@jax.custom_vjp
def low(v):
    return lax.optimization_barrier(v.astype(jnp.bfloat16)).astype(jnp.float32)

@jax.custom_vjp
def low_back(v):
    return v

def low_keep(v):
    return (low(v), None)

def low_pass(kept, grad):
    return (grad,)

def back_keep(v):
    return (v, None)

def back_low(kept, grad):
    return (low(grad),)
low.defvjp(low_keep, low_pass)
low_back.defvjp(back_keep, back_low)

def rms_scale(values):
    return lax.rsqrt(lax.optimization_barrier(jnp.mean(values * values, axis=-1, keepdims=True)) + 1e-05)

def short_conv(raw_rows, weights, doc_ids):
    row_count = raw_rows.shape[0]
    total = jnp.zeros_like(raw_rows)
    for tap_index in range(KERNEL):
        delay_rows = KERNEL - 1 - tap_index
        moved = jnp.pad(raw_rows, ((delay_rows, 0), (0, 0)))[:row_count]
        moved_doc = jnp.pad(doc_ids, (delay_rows, 0), constant_values=-1)[:row_count]
        keep_mask = (moved_doc == doc_ids).astype(raw_rows.dtype)
        total = total + weights[tap_index] * moved * keep_mask[:, None]
    return total

def delta_rule(query, keyed, valued, rate, doc_ids):
    row_count, head_count, head_width = query.shape
    blocks = row_count // BLOCK
    float_type = query.dtype

    def to_blocks(array):
        return array.reshape(blocks, BLOCK, head_count, head_width).transpose(0, 2, 1, 3)
    query_blk = to_blocks(query)
    key_blk = to_blocks(keyed)
    value_blk = to_blocks(valued)
    rate_blk = rate.reshape(blocks, BLOCK, head_count).transpose(0, 2, 1)
    doc_blk = doc_ids.reshape(blocks, BLOCK)
    prior_doc = jnp.concatenate([jnp.full((1,), -1, jnp.int32), doc_blk[:-1, -1].astype(jnp.int32)])
    carry_in = (doc_blk == prior_doc[:, None]).astype(float_type)
    same_doc = doc_blk[:, :, None] == doc_blk[:, None, :]
    positions = jnp.arange(BLOCK)
    strict = positions[:, None] > positions[None, :]
    inclusive = positions[:, None] >= positions[None, :]
    key_key = jnp.einsum('nhtd,nhsd->nhts', key_blk, key_blk, precision=lax.Precision.HIGHEST)
    mixing = key_key * rate_blk[..., None] * (same_doc & strict)[:, None].astype(float_type)
    system = mixing + jnp.eye(BLOCK, dtype=float_type)
    scaled_values = value_blk * rate_blk[..., None]
    scaled_keys = key_blk * (rate_blk * carry_in[:, None, :])[..., None]
    solved_values = jax.scipy.linalg.solve_triangular(system, scaled_values, lower=True, unit_diagonal=True)
    solved_keys = jax.scipy.linalg.solve_triangular(system, scaled_keys, lower=True, unit_diagonal=True)
    scores = jnp.einsum('nhtd,nhsd->nhts', query_blk, key_blk, precision=lax.Precision.HIGHEST)
    scores = scores * (same_doc & inclusive)[:, None].astype(float_type)
    last_same = (doc_blk == doc_blk[:, -1:]).astype(float_type)
    carry_end = carry_in[:, -1]

    def advance(memory, inputs):
        solved_v, solved_k, score_n, query_n, key_n, carry_n, last_n, end_n = inputs
        update = solved_v - jnp.einsum('htk,hvk->htv', solved_k, memory, precision=lax.Precision.HIGHEST)
        output = carry_n[None, :, None] * jnp.einsum('hvk,htk->htv', memory, query_n, precision=lax.Precision.HIGHEST)
        output = output + jnp.einsum('hts,hsv->htv', score_n, update, precision=lax.Precision.HIGHEST)
        memory = end_n * memory + jnp.einsum('htv,htk->hvk', update * last_n[None, :, None], key_n, precision=lax.Precision.HIGHEST)
        return (memory, output)
    initial = jnp.zeros((head_count, head_width, head_width), float_type)
    _, outputs = lax.scan(jax.checkpoint(advance), initial, (solved_values, solved_keys, scores, query_blk, key_blk, carry_in, last_same, carry_end))
    return outputs.transpose(0, 2, 1, 3).reshape(row_count, head_count, head_width)

def mixer(query_raw, key_raw, value_raw, gating_raw, beta_raw, conv_q, conv_k, conv_v, gain_head, doc_ids, live):
    head_width = gain_head.shape[0]
    row_count = query_raw.shape[0]
    query_unit = jax.nn.silu(short_conv(query_raw, conv_q, doc_ids)).reshape(row_count, -1, head_width)
    query_unit = query_unit * lax.rsqrt(lax.optimization_barrier(jnp.sum(query_unit * query_unit, axis=-1, keepdims=True)) + 1e-06)
    key_unit = jax.nn.silu(short_conv(key_raw, conv_k, doc_ids)).reshape(row_count, -1, head_width)
    key_unit = key_unit * lax.rsqrt(lax.optimization_barrier(jnp.sum(key_unit * key_unit, axis=-1, keepdims=True)) + 1e-06)
    value_rows = jax.nn.silu(short_conv(value_raw, conv_v, doc_ids)).reshape(row_count, -1, head_width)
    beta_rate = jax.nn.sigmoid(beta_raw) * live[:, None]
    mixed = delta_rule(query_unit, key_unit, value_rows, beta_rate, doc_ids)
    norm_scale = lax.rsqrt(lax.optimization_barrier(jnp.mean(mixed * mixed, axis=-1, keepdims=True)) + 1e-05)
    gated = mixed * norm_scale * gain_head * jax.nn.silu(gating_raw.reshape(row_count, -1, head_width))
    gated = gated * live[:, None, None]
    return gated.reshape(row_count, -1)

def project(left, right):
    return jnp.dot(left, right, precision=lax.Precision.HIGHEST)

def layer(input_rows, params, doc_ids, live):
    first_gain, w_query, w_key, w_value, w_gating, w_beta, conv_query, conv_key, conv_value, head_gain, w_project, second_gain, w_gate, w_up, w_down = params
    normed1 = low(input_rows * rms_scale(input_rows) * first_gain)
    query_raw = low_back(project(normed1, w_query))
    key_raw = low_back(project(normed1, w_key))
    value_raw = low_back(project(normed1, w_value))
    gating_raw = low_back(project(normed1, w_gating))
    beta_raw = low_back(project(normed1, w_beta))
    gated = low(mixer(query_raw, key_raw, value_raw, gating_raw, beta_raw, conv_query, conv_key, conv_value, head_gain, doc_ids, live))
    attn_out = low_back(project(gated, w_project))
    resid = input_rows + attn_out
    normed2 = low(resid * rms_scale(resid) * second_gain)
    gate_val = low_back(project(normed2, w_gate))
    up_val = low_back(project(normed2, w_up))
    hidden = low(jax.nn.silu(gate_val) * up_val)
    return resid + low_back(project(hidden, w_down))

def reference(layer_input, first_gain, w_query, w_key, w_value, w_gating, w_beta, conv_query, conv_key, conv_value, head_gain, w_project, second_gain, w_gate, w_up, w_down, doc_starts, seq_lengths, output_grad):
    params = (first_gain, w_query, w_key, w_value, w_gating, w_beta, conv_query, conv_key, conv_value, head_gain, w_project, second_gain, w_gate, w_up, w_down)
    params = tuple((weight.astype(jnp.float32) for weight in params))
    input_seqs = layer_input.astype(jnp.float32).reshape(SEQS, LENGTH, D)
    grad_seqs = output_grad.astype(jnp.float32).reshape(SEQS, LENGTH, D)

    def per_sequence(totals, inputs):
        input_rows, grad_rows, starts, seq_len = inputs
        positions = jnp.arange(LENGTH, dtype=jnp.int32)
        doc_ids = lax.optimization_barrier(jnp.sum((starts[None, :] <= positions[:, None]).astype(jnp.int32), axis=1)).astype(jnp.int32)
        live = (positions < seq_len).astype(input_rows.dtype)

        def forward_rows(row_input, param_set):
            return layer(row_input, param_set, doc_ids, live)
        out_rows, pullback = jax.vjp(forward_rows, input_rows, params)
        back_rows, grads = pullback(grad_rows)
        totals = jax.tree.map(lambda left, right: left + right, totals, grads)
        return (totals, (out_rows.astype(jnp.bfloat16), back_rows))
    zeros = jax.tree.map(jnp.zeros_like, params)
    grads, (out_seqs, back_seqs) = lax.scan(per_sequence, zeros, (input_seqs, grad_seqs, doc_starts, seq_lengths))
    return (out_seqs.reshape(TOKENS, D), back_seqs.reshape(TOKENS, D), grads[0], grads[1], grads[2], grads[3], grads[4], grads[5], grads[6], grads[7], grads[8], grads[9], grads[10], grads[11], grads[12], grads[13], grads[14])
```

```python
import jax, jax.numpy as jnp
from jax import lax
from jax.experimental import pallas as pl
from jax.experimental.pallas import tpu as pltpu
from jax.sharding import PartitionSpec as P

KERNEL = 4
CHUNK = 256
G, Q, K, V = range(4)
F32 = jnp.float32
BF16 = jnp.bfloat16


def dot(left, right):
    return jnp.dot(left, right, preferred_element_type=F32)


def dot_nt(left, right):
    return lax.dot_general(left, right, (((1,), (1,)), ((), ())), preferred_element_type=F32)


def dot_tn(left, right):
    return lax.dot_general(left, right, (((0,), (0,)), ((), ())), preferred_element_type=F32)


def lane_sum(values):
    return jnp.sum(values, axis=-1, keepdims=True)


def document_of(starts_ref, positions):
    total = jnp.zeros_like(positions)
    for entry in range(starts_ref.shape[1]):
        total = total + (positions >= starts_ref[0, entry]).astype(jnp.int32)
    return total


def fill_masks(starts_ref, length_ref, keep_ref, live_ref, carry_ref):
    rows, lanes = live_ref.shape
    place = lax.broadcasted_iota(jnp.int32, (rows, lanes), 0)
    docs = document_of(starts_ref, place)
    for delay in range(1, KERNEL):
        prior = document_of(starts_ref, place - delay)
        keep_ref[delay - 1] = jnp.where((prior == docs) & (place >= delay), 1.0, 0.0)
    live_ref[...] = jnp.where(place < length_ref[0], 1.0, 0.0)
    for edge in range(rows // CHUNK - 1):
        seam = jnp.int32((edge + 1) * CHUNK - 1)
        carry_ref[edge] = jnp.where(docs == document_of(starts_ref, seam), 1.0, 0.0)


def pair_mask(starts_ref, chunk):
    row = lax.broadcasted_iota(jnp.int32, (CHUNK, CHUNK), 0)
    col = lax.broadcasted_iota(jnp.int32, (CHUNK, CHUNK), 1)
    first = chunk * CHUNK
    same = document_of(starts_ref, row + first) == document_of(starts_ref, col + first)
    return same & (row > col), same & (row >= col)


def convolve(raw, taps, keep_ref):
    parts = [raw]
    for delay in range(1, KERNEL):
        parts.append(pltpu.roll(raw, delay, 0) * keep_ref[delay - 1])
    total = parts[0] * taps[KERNEL - 1 : KERNEL]
    for delay in range(1, KERNEL):
        total = total + parts[delay] * taps[KERNEL - 1 - delay : KERNEL - delay]
    return total, parts


def sigmoid(values):
    return 0.5 * jnp.tanh(0.5 * values) + 0.5


def column(values, index):
    lane = lax.broadcasted_iota(jnp.int32, values.shape, 1)
    return lane_sum(jnp.where(lane == index, values, 0.0))


def invert(system):
    size = system[0].shape[0]
    row = lax.broadcasted_iota(jnp.int32, (size, size), 0)
    col = lax.broadcasted_iota(jnp.int32, (size, size), 1)
    apart = row ^ col
    eye = jnp.where(row == col, 1.0, 0.0)
    low = [matrix.astype(BF16) for matrix in system]
    solved = [eye - jnp.where(apart == 1, matrix, 0.0) for matrix in system]
    step = 2
    while step < size:
        level = (apart >= step) & (apart < 2 * step)
        for index, matrix in enumerate(low):
            part = jnp.where(level, matrix, 0.0)
            held = solved[index].astype(BF16)
            solved[index] = solved[index] - dot(dot(held, part).astype(BF16), held)
        step *= 2
    refined = []
    for matrix, high, inverse in zip(system, low, solved):
        rest = (matrix - high.astype(F32)).astype(BF16)
        head = inverse.astype(BF16)
        tail = (inverse - head.astype(F32)).astype(BF16)
        product = dot(high, head) + dot(rest, head) + dot(high, tail)
        residue = eye - inverse - product
        refined.append(inverse + dot(head, residue.astype(BF16)))
    return refined


def unit_rows(conv):
    gate = sigmoid(conv)
    act = conv * gate
    scale = lax.rsqrt(lane_sum(act * act) + 1e-06)
    return gate, act, scale


def forward_kernel(
    starts_ref, length_ref, raw_ref, conv_q_ref, conv_k_ref, conv_v_ref, gain_ref,
    gated_ref, mixed_ref, solve_ref, update_ref, state_ref,
    keep_ref, live_ref, carry_ref, strict_ref, incl_ref,
):
    rows, head_width = live_ref.shape
    width = gated_ref.shape[1]
    chunks = rows // CHUNK
    fill_masks(starts_ref, length_ref, keep_ref, live_ref, carry_ref)
    for chunk in range(chunks):
        strict, incl = pair_mask(starts_ref, chunk)
        strict_ref[chunk] = jnp.where(strict, 1.0, 0.0)
        incl_ref[chunk] = jnp.where(incl, 1.0, 0.0)

    @pl.loop(0, width // head_width)
    def _(head):
        start = pl.multiple_of(head * head_width, head_width)

        def stream(index):
            return raw_ref[:, pl.ds(pl.multiple_of(index * width + start, head_width), head_width)]

        cols = pl.ds(start, head_width)
        conv, _ = convolve(stream(Q), conv_q_ref[:, cols], keep_ref)
        _, act, scale = unit_rows(conv)
        query = (act * scale).astype(BF16)
        conv, _ = convolve(stream(K), conv_k_ref[:, cols], keep_ref)
        _, act, scale = unit_rows(conv)
        keyed = act * scale
        key_low = keyed.astype(BF16)
        conv, _ = convolve(stream(V), conv_v_ref[:, cols], keep_ref)
        valued = conv * sigmoid(conv)
        rate = sigmoid(column(raw_ref[:, 4 * width :], head)) * live_ref[...]
        scaled_value = (valued * rate).astype(BF16)
        scaled_key = keyed * rate
        system = []
        for chunk in range(chunks):
            span = slice(chunk * CHUNK, (chunk + 1) * CHUNK)
            pair = dot_nt(key_low[span], key_low[span])
            wide = jnp.concatenate([rate[span]] * (CHUNK // head_width), axis=1)
            system.append(pair * wide * strict_ref[chunk])
        memory = None
        for chunk, solved in enumerate(invert(system)):
            span = slice(chunk * CHUNK, (chunk + 1) * CHUNK)
            solve_low = solved.astype(BF16)
            solve_ref[head * chunks + chunk] = solve_low
            score = dot_nt(query[span], key_low[span]) * incl_ref[chunk]
            if chunk == 0:
                update = dot(solve_low, scaled_value[span])
                update_low = update.astype(BF16)
                mixed = dot(score.astype(BF16), update_low)
            else:
                carry = carry_ref[chunk - 1][span]
                right = jnp.concatenate(
                    [scaled_value[span], (scaled_key[span] * carry).astype(BF16)], axis=1
                )
                both = dot(solve_low, right)
                memory_low = memory.astype(BF16)
                state_ref[head * (chunks - 1) + chunk - 1] = memory_low
                update = both[:, :head_width] - dot(both[:, head_width:].astype(BF16), memory_low)
                update_low = update.astype(BF16)
                mixed = carry * dot(query[span], memory_low) + dot(score.astype(BF16), update_low)
            update_ref[span, cols] = update_low
            mixed_ref[span, cols] = mixed
            if chunk + 1 < chunks:
                last = (keyed[span] * carry_ref[chunk][span]).astype(BF16)
                fresh = dot_tn(last, update_low)
                if memory is None:
                    memory = fresh
                else:
                    memory = memory * carry_ref[chunk - 1][span][CHUNK - 1 :] + fresh
        mixed = mixed_ref[:, cols]
        norm = lax.rsqrt(lane_sum(mixed * mixed) * (1.0 / head_width) + 1e-05)
        gating = stream(G)
        gated = mixed * norm * gain_ref[...] * (gating * sigmoid(gating)) * live_ref[...]
        gated_ref[:, cols] = gated.astype(BF16)


def delta_forward(starts, length, raw, conv_q, conv_k, conv_v, gain):
    rows = raw.shape[0]
    head_width = gain.shape[-1]
    width = conv_q.shape[1]
    heads, chunks = width // head_width, rows // CHUNK
    vmem = pl.BlockSpec(memory_space=pltpu.VMEM)
    smem = pl.BlockSpec(memory_space=pltpu.SMEM)
    return pl.pallas_call(
        forward_kernel,
        out_shape=(
            jax.ShapeDtypeStruct((rows, width), BF16),
            jax.ShapeDtypeStruct((rows, width), F32),
            jax.ShapeDtypeStruct((heads * chunks, CHUNK, CHUNK), BF16),
            jax.ShapeDtypeStruct((rows, width), BF16),
            jax.ShapeDtypeStruct((heads * (chunks - 1), head_width, head_width), BF16),
        ),
        in_specs=[smem, smem] + [vmem] * 5,
        out_specs=[vmem] * 5,
        scratch_shapes=[
            pltpu.VMEM((KERNEL - 1, rows, head_width), F32),
            pltpu.VMEM((rows, head_width), F32),
            pltpu.VMEM((chunks - 1, rows, head_width), F32),
            pltpu.VMEM((chunks, CHUNK, CHUNK), F32),
            pltpu.VMEM((chunks, CHUNK, CHUNK), F32),
        ],
        compiler_params=pltpu.CompilerParams(vmem_limit_bytes=40 * 1024 * 1024),
        cost_estimate=pl.CostEstimate(
            flops=2 * 24 * heads * chunks * CHUNK**3, bytes_accessed=12 * 2**20, transcendentals=0
        ),
        name="delta_forward",
    )(starts, length, raw, conv_q, conv_k, conv_v, gain)


def backward_kernel(
    starts_ref, length_ref, raw_ref, conv_q_ref, conv_k_ref, conv_v_ref, gain_ref,
    mixed_ref, solve_ref, update_ref, state_ref, grad_ref,
    d_raw_ref, d_conv_ref, d_gain_ref,
    keep_ref, live_ref, carry_ref, strict_ref, incl_ref, d_query_ref, d_key_ref, d_value_ref, d_rate_ref,
):
    rows, head_width = live_ref.shape
    width = mixed_ref.shape[1]
    chunks = rows // CHUNK
    fill_masks(starts_ref, length_ref, keep_ref, live_ref, carry_ref)
    for chunk in range(chunks):
        strict, incl = pair_mask(starts_ref, chunk)
        strict_ref[chunk] = jnp.where(strict, 1.0, 0.0)
        incl_ref[chunk] = jnp.where(incl, 1.0, 0.0)
    d_gain_ref[...] = jnp.zeros_like(d_gain_ref)
    d_raw_ref[:, 4 * width :] = jnp.zeros((rows, head_width), BF16)

    @pl.loop(0, width // head_width)
    def _(head):
        start = pl.multiple_of(head * head_width, head_width)

        def place(index):
            return pl.ds(pl.multiple_of(index * width + start, head_width), head_width)

        cols = pl.ds(start, head_width)
        live = live_ref[...]
        mixed = mixed_ref[:, cols]
        norm = lax.rsqrt(lane_sum(mixed * mixed) * (1.0 / head_width) + 1e-05)
        gating = raw_ref[:, place(G)]
        gate = sigmoid(gating)
        normal = mixed * norm
        grad = grad_ref[:, cols].astype(F32) * live
        grad_gain = grad * gain_ref[...]
        swish = gating * gate
        d_raw_ref[:, place(G)] = (grad_gain * normal * gate * (1.0 + gating - swish)).astype(BF16)
        d_gain_ref[...] += jnp.sum(grad * normal * swish, axis=0, keepdims=True)
        d_normal = grad_gain * swish
        d_mixed = norm * (d_normal - normal * (lane_sum(d_normal * normal) * (1.0 / head_width)))
        d_mixed_low = d_mixed.astype(BF16)

        conv_q, parts_q = convolve(raw_ref[:, place(Q)], conv_q_ref[:, cols], keep_ref)
        gate_q, act_q, scale_q = unit_rows(conv_q)
        unit_q = act_q * scale_q
        query = unit_q.astype(BF16)
        conv_k, parts_k = convolve(raw_ref[:, place(K)], conv_k_ref[:, cols], keep_ref)
        gate_k, act_k, scale_k = unit_rows(conv_k)
        keyed = act_k * scale_k
        key_low = keyed.astype(BF16)
        conv_v, parts_v = convolve(raw_ref[:, place(V)], conv_v_ref[:, cols], keep_ref)
        gate_v = sigmoid(conv_v)
        valued = conv_v * gate_v
        sig = sigmoid(column(raw_ref[:, 4 * width :], head))
        rate = sig * live
        scaled_value = (valued * rate).astype(BF16)
        scaled_key = keyed * rate

        d_memory = None
        for chunk in range(chunks - 1, -1, -1):
            span = slice(chunk * CHUNK, (chunk + 1) * CHUNK)
            key_c, query_c, d_mixed_c = key_low[span], query[span], d_mixed_low[span]
            solve = solve_ref[head * chunks + chunk]
            update = update_ref[span, cols]
            incl, strict = incl_ref[chunk], strict_ref[chunk]
            score = (dot_nt(query_c, key_c) * incl).astype(BF16)
            d_update = dot_tn(score, d_mixed_c)
            d_key = None
            if d_memory is not None:
                last = carry_ref[chunk][span]
                d_memory_low = d_memory.astype(BF16)
                d_update = d_update + dot((keyed[span] * last).astype(BF16), d_memory_low)
                d_key = last * dot_nt(update, d_memory_low)
            d_update_low = d_update.astype(BF16)
            d_score = (dot_nt(d_mixed_c, update) * incl).astype(BF16)
            d_query = dot(d_score, key_c)
            d_key_score = dot_tn(d_score, query_c)
            d_key = d_key_score if d_key is None else d_key + d_key_score
            if chunk == 0:
                right = scaled_value[span]
                solved = dot(solve, right)
                d_right = dot_tn(solve, d_update_low)
                d_value_in = d_right
                d_rate = lane_sum(d_value_in * valued[span])
            else:
                carry = carry_ref[chunk - 1][span]
                state = state_ref[head * (chunks - 1) + chunk - 1]
                right = jnp.concatenate([scaled_value[span], (scaled_key[span] * carry).astype(BF16)], axis=1)
                solved = dot(solve, right)
                d_solved_key = -dot_nt(d_update_low, state)
                d_right = dot_tn(solve, jnp.concatenate([d_update_low, d_solved_key.astype(BF16)], axis=1))
                d_value_in = d_right[:, :head_width]
                d_key_in = d_right[:, head_width:] * carry
                carried = (carry * d_mixed[span]).astype(BF16)
                d_query = d_query + dot_nt(carried, state)
                d_key = d_key + rate[span] * d_key_in
                d_rate = lane_sum(d_value_in * valued[span] + d_key_in * keyed[span])
                fresh = dot_tn(query_c, carried) - dot_tn(solved[:, head_width:].astype(BF16), d_update_low)
                if d_memory is None:
                    d_memory = fresh
                else:
                    d_memory = d_memory * carry[CHUNK - 1 :] + fresh
            d_system = dot_nt(d_right.astype(BF16), solved.astype(BF16)) * -strict
            pair = dot_nt(key_c, key_c)
            d_rate = d_rate + lane_sum(d_system * pair)
            wide = jnp.concatenate([rate[span]] * (CHUNK // head_width), axis=1)
            d_pair = (d_system * wide).astype(BF16)
            d_key = d_key + dot(d_pair, key_c) + dot_tn(d_pair, key_c)
            d_query_ref[span] = d_query
            d_key_ref[span] = d_key
            d_value_ref[span] = rate[span] * d_value_in
            d_rate_ref[span] = jnp.broadcast_to(d_rate, (CHUNK, head_width))

        lane = lax.broadcasted_iota(jnp.int32, (rows, head_width), 1)
        d_beta = d_rate_ref[...] * rate * (1.0 - sig)
        tail = d_raw_ref[:, 4 * width :]
        d_raw_ref[:, 4 * width :] = jnp.where(lane == head, d_beta.astype(BF16), tail)

        def conv_back(index, d_conv, parts, taps):
            sums = [jnp.sum(d_conv * part, axis=0, keepdims=True) for part in parts]
            for delay in range(KERNEL):
                tap = KERNEL - 1 - delay
                d_conv_ref[tap : tap + 1, place(index - 1)] = sums[delay]
            total = d_conv * taps[KERNEL - 1 : KERNEL]
            for delay in range(1, KERNEL):
                tap = KERNEL - 1 - delay
                back = pltpu.roll(d_conv * keep_ref[delay - 1], rows - delay, 0)
                total = total + back * taps[tap : tap + 1]
            d_raw_ref[:, place(index)] = total.astype(BF16)

        def unit_back(d_unit, unit, scale, conv, act, gate):
            d_act = scale * (d_unit - unit * lane_sum(d_unit * unit))
            return d_act * gate * (1.0 + conv - act)

        conv_back(Q, unit_back(d_query_ref[...], unit_q, scale_q, conv_q, act_q, gate_q), parts_q, conv_q_ref[:, cols])
        conv_back(K, unit_back(d_key_ref[...], keyed, scale_k, conv_k, act_k, gate_k), parts_k, conv_k_ref[:, cols])
        d_conv_v = d_value_ref[...] * gate_v * (1.0 + conv_v - valued)
        conv_back(V, d_conv_v, parts_v, conv_v_ref[:, cols])


def delta_backward(starts, length, raw, conv_q, conv_k, conv_v, gain, mixed, solve, update, state, grad):
    rows = raw.shape[0]
    head_width = gain.shape[-1]
    width = conv_q.shape[1]
    heads, chunks = width // head_width, rows // CHUNK
    vmem = pl.BlockSpec(memory_space=pltpu.VMEM)
    smem = pl.BlockSpec(memory_space=pltpu.SMEM)
    return pl.pallas_call(
        backward_kernel,
        out_shape=(
            jax.ShapeDtypeStruct((rows, 4 * width + head_width), BF16),
            jax.ShapeDtypeStruct((KERNEL, 3 * width), F32),
            jax.ShapeDtypeStruct((1, head_width), F32),
        ),
        in_specs=[smem, smem] + [vmem] * 10,
        out_specs=[vmem] * 3,
        scratch_shapes=[
            pltpu.VMEM((KERNEL - 1, rows, head_width), F32),
            pltpu.VMEM((rows, head_width), F32),
            pltpu.VMEM((chunks - 1, rows, head_width), F32),
            pltpu.VMEM((chunks, CHUNK, CHUNK), F32),
            pltpu.VMEM((chunks, CHUNK, CHUNK), F32),
        ]
        + [pltpu.VMEM((rows, head_width), F32)] * 4,
        compiler_params=pltpu.CompilerParams(vmem_limit_bytes=48 * 1024 * 1024),
        cost_estimate=pl.CostEstimate(
            flops=2 * 12 * heads * chunks * CHUNK**3, bytes_accessed=16 * 2**20, transcendentals=0
        ),
        name="delta_backward",
    )(starts, length, raw, conv_q, conv_k, conv_v, gain, mixed, solve, update, state, grad)


def rms_scale(values):
    return lax.rsqrt(jnp.mean(values * values, axis=-1, keepdims=True) + 1e-05)


def rms_back(values, scale_rows, gain, grad):
    scaled_grad = grad * gain
    inner = jnp.mean(scaled_grad * values, axis=-1, keepdims=True)
    return scale_rows * (scaled_grad - values * scale_rows * scale_rows * inner)


def shifted(count, shift):
    return [(index, (index + shift) % count) for index in range(count)]


def gather_rows(rows):
    count = lax.axis_size("tensor")
    mine = lax.axis_index("tensor")
    height = rows.shape[0]
    whole = jnp.zeros((count * height, rows.shape[1]), rows.dtype)
    whole = lax.dynamic_update_slice_in_dim(whole, rows, mine * height, 0)
    for shift in range(1, count):
        came = lax.ppermute(rows, "tensor", shifted(count, shift))
        source = lax.rem(mine + count - shift, count)
        whole = lax.dynamic_update_slice_in_dim(whole, came, source * height, 0)
    return whole


def scatter_rows(partial_rows):
    count = lax.axis_size("tensor")
    mine = lax.axis_index("tensor")
    height = partial_rows.shape[0] // count
    total = lax.dynamic_slice_in_dim(partial_rows, mine * height, height, 0).astype(F32)
    for shift in range(1, count):
        target = lax.rem(mine + shift, count)
        piece = lax.dynamic_slice_in_dim(partial_rows, target * height, height, 0)
        total = total + lax.ppermute(piece, "tensor", shifted(count, shift)).astype(F32)
    return total


def gather_weights(pieces):
    return lax.all_gather(jnp.concatenate(pieces, axis=1), ("fsdp", "dp"), axis=0, tiled=True)


def scatter_grads(grads):
    return lax.psum_scatter(grads, ("dp", "fsdp"), scatter_dimension=0, tiled=True).astype(F32)


def body(
    layer_input,
    first_gain,
    w_query,
    w_key,
    w_value,
    w_gating,
    w_beta,
    conv_query,
    conv_key,
    conv_value,
    head_gain,
    w_project,
    second_gain,
    w_gate,
    w_up,
    w_down,
    doc_starts,
    seq_lengths,
    output_grad,
):
    replicas = lax.axis_size("dp")
    replica = lax.axis_index("dp")
    width = w_query.shape[1]
    units = w_gate.shape[1]
    heads = w_beta.shape[1]
    head_width = head_gain.shape[0]

    def piece(weight, axis):
        size = weight.shape[axis] // replicas
        return lax.dynamic_slice_in_dim(weight, replica * size, size, axis)

    input_float = layer_input.astype(F32)
    conv_q = conv_query.astype(F32)
    conv_k = conv_key.astype(F32)
    conv_v = conv_value.astype(F32)
    gain_head = head_gain.astype(F32)[None, :]
    gains = lax.all_gather(jnp.stack([first_gain, second_gain]), "fsdp", axis=1, tiled=True).astype(F32)
    gain_one, gain_two = gains[0], gains[1]
    beta_piece = jnp.pad(piece(w_beta, 0), ((0, 0), (0, head_width - heads)))
    mix_full = gather_weights(
        [piece(w_gating, 0), piece(w_query, 0), piece(w_key, 0), piece(w_value, 0), beta_piece]
    )
    ffn_full = gather_weights(
        [piece(w_project, 1).T, piece(w_gate, 0), piece(w_up, 0), piece(w_down, 1).T]
    )
    project_t = ffn_full[:, :width]
    gate_up = ffn_full[:, width : width + 2 * units]
    down_t = ffn_full[:, width + 2 * units :]

    scale_one = rms_scale(input_float)
    normed1 = (input_float * scale_one * gain_one).astype(BF16)
    rows_one = gather_rows(normed1)
    raw = dot(rows_one, mix_full)
    gated, mixed, solve, update, state = delta_forward(
        doc_starts, seq_lengths, raw, conv_q, conv_k, conv_v, gain_head
    )
    attn_out = scatter_rows(dot_nt(gated, project_t).astype(BF16))
    resid = input_float + attn_out
    scale_two = rms_scale(resid)
    normed2 = (resid * scale_two * gain_two).astype(BF16)
    rows_two = gather_rows(normed2)
    grad_rows = gather_rows(output_grad)
    d_hidden = dot(grad_rows, down_t)
    both = dot(rows_two, gate_up)
    gate_val, up_val = both[:, :units], both[:, units:]
    gate_sig = jax.nn.sigmoid(gate_val)
    silu_gate = gate_val * gate_sig
    hidden = (silu_gate * up_val).astype(BF16)
    d_gate = (d_hidden * up_val * gate_sig * (1.0 + gate_val * (1.0 - gate_sig))).astype(BF16)
    d_up = (d_hidden * silu_gate).astype(BF16)
    d_both = jnp.concatenate([d_gate, d_up], axis=1)
    d_normed2 = scatter_rows(dot_nt(d_both, gate_up).astype(BF16))
    down_shard = scatter_grads(dot_tn(grad_rows, hidden).astype(BF16))
    ffn_out = scatter_rows(dot_nt(hidden, down_t).astype(BF16))
    result = (resid + ffn_out).astype(BF16)
    both_shard = scatter_grads(dot_tn(rows_two, d_both).astype(BF16))
    grad_second = jnp.sum(d_normed2 * resid * scale_two, axis=0)
    d_resid = output_grad.astype(F32) + rms_back(resid, scale_two, gain_two, d_normed2)
    d_attn = gather_rows(d_resid.astype(BF16))
    d_gated = dot(d_attn, project_t)
    project_shard = scatter_grads(dot_tn(d_attn, gated).astype(BF16))
    d_raw, d_conv, d_head = delta_backward(
        doc_starts, seq_lengths, raw, conv_q, conv_k, conv_v, gain_head, mixed, solve, update, state, d_gated
    )
    d_normed1 = scatter_rows(dot_nt(d_raw, mix_full).astype(BF16))
    mix_shard = scatter_grads(dot_tn(rows_one, d_raw).astype(BF16))
    grad_first = jnp.sum(d_normed1 * input_float * scale_one, axis=0)
    input_grad = d_resid + rms_back(input_float, scale_one, gain_one, d_normed1)
    conv_totals = lax.psum(d_conv, ("dp", "fsdp"))
    group = lax.axis_index("dp") * lax.axis_size("fsdp") + lax.axis_index("fsdp")
    gain_size = grad_first.shape[0] // (replicas * lax.axis_size("fsdp"))
    gain_totals = lax.psum(
        jnp.concatenate([grad_first, grad_second, d_head[0]]), ("dp", "fsdp", "tensor")
    )
    features = grad_first.shape[0]

    def gain_shard(first):
        return lax.dynamic_slice_in_dim(gain_totals, first + group * gain_size, gain_size, 0)

    return (
        result,
        input_grad,
        gain_shard(0),
        mix_shard[:, width : 2 * width],
        mix_shard[:, 2 * width : 3 * width],
        mix_shard[:, 3 * width : 4 * width],
        mix_shard[:, :width],
        mix_shard[:, 4 * width : 4 * width + heads],
        conv_totals[:, :width],
        conv_totals[:, width : 2 * width],
        conv_totals[:, 2 * width :],
        gain_totals[2 * features :],
        project_shard.T,
        gain_shard(features),
        both_shard[:, :units],
        both_shard[:, units:],
        down_shard.T,
    )


def solution(mesh):
    placed = (
        P(("dp", "fsdp", "tensor"), None),
        P("fsdp"),
        P("fsdp", "tensor"),
        P("fsdp", "tensor"),
        P("fsdp", "tensor"),
        P("fsdp", "tensor"),
        P("fsdp", "tensor"),
        P(None, "tensor"),
        P(None, "tensor"),
        P(None, "tensor"),
        P(),
        P("tensor", "fsdp"),
        P("fsdp"),
        P("fsdp", "tensor"),
        P("fsdp", "tensor"),
        P("tensor", "fsdp"),
        P(("dp", "fsdp"), None),
        P(("dp", "fsdp")),
        P(("dp", "fsdp", "tensor"), None),
    )
    return jax.shard_map(
        body,
        mesh=mesh,
        in_specs=placed,
        out_specs=(
            P(("dp", "fsdp", "tensor"), None),
            P(("dp", "fsdp", "tensor"), None),
            P(("dp", "fsdp")),
            P(("dp", "fsdp"), "tensor"),
            P(("dp", "fsdp"), "tensor"),
            P(("dp", "fsdp"), "tensor"),
            P(("dp", "fsdp"), "tensor"),
            P(("dp", "fsdp"), "tensor"),
            P(None, "tensor"),
            P(None, "tensor"),
            P(None, "tensor"),
            P(),
            P("tensor", ("dp", "fsdp")),
            P(("dp", "fsdp")),
            P(("dp", "fsdp"), "tensor"),
            P(("dp", "fsdp"), "tensor"),
            P("tensor", ("dp", "fsdp")),
        ),
        check_vma=False,
    )
```

```python
import functools
import jax, jax.numpy as jnp
from jax import lax
from jax.experimental import pallas as pl
from jax.experimental.pallas import tpu as pltpu
from jax.sharding import PartitionSpec as P

KERNEL = 4
CHUNK = 256
G, Q, K, V = range(4)
MESH = pl.DeviceIdType.MESH
F32 = jnp.float32
BF16 = jnp.bfloat16


def dot(left, right):
    return jnp.dot(left, right, preferred_element_type=F32)


def dot_nt(left, right):
    return lax.dot_general(left, right, (((1,), (1,)), ((), ())), preferred_element_type=F32)


def dot_tn(left, right):
    return lax.dot_general(left, right, (((0,), (0,)), ((), ())), preferred_element_type=F32)


def lane_sum(values):
    return jnp.sum(values, axis=-1, keepdims=True)


def document_of(starts_ref, positions):
    total = jnp.zeros_like(positions)
    for entry in range(starts_ref.shape[1]):
        total = total + (positions >= starts_ref[0, entry]).astype(jnp.int32)
    return total


def fill_masks(starts_ref, length_ref, keep_ref, live_ref, carry_ref):
    rows, lanes = live_ref.shape
    place = lax.broadcasted_iota(jnp.int32, (rows, lanes), 0)
    docs = document_of(starts_ref, place)
    for delay in range(1, KERNEL):
        prior = document_of(starts_ref, place - delay)
        keep_ref[delay - 1] = jnp.where((prior == docs) & (place >= delay), 1.0, 0.0)
    live_ref[...] = jnp.where(place < length_ref[0], 1.0, 0.0)
    for edge in range(rows // CHUNK - 1):
        seam = jnp.int32((edge + 1) * CHUNK - 1)
        carry_ref[edge] = jnp.where(docs == document_of(starts_ref, seam), 1.0, 0.0)


def pair_mask(starts_ref, chunk):
    row = lax.broadcasted_iota(jnp.int32, (CHUNK, CHUNK), 0)
    col = lax.broadcasted_iota(jnp.int32, (CHUNK, CHUNK), 1)
    first = chunk * CHUNK
    same = document_of(starts_ref, row + first) == document_of(starts_ref, col + first)
    return same & (row > col), same & (row >= col)


def convolve(raw, taps, keep_ref):
    parts = [raw]
    for delay in range(1, KERNEL):
        parts.append(pltpu.roll(raw, delay, 0) * keep_ref[delay - 1])
    total = parts[0] * taps[KERNEL - 1 : KERNEL]
    for delay in range(1, KERNEL):
        total = total + parts[delay] * taps[KERNEL - 1 - delay : KERNEL - delay]
    return total, parts


def sigmoid(values):
    return 0.5 * jnp.tanh(0.5 * values) + 0.5


def column(values, index):
    lane = lax.broadcasted_iota(jnp.int32, values.shape, 1)
    return lane_sum(jnp.where(lane == index, values, 0.0))


def invert(system):
    size = system[0].shape[0]
    row = lax.broadcasted_iota(jnp.int32, (size, size), 0)
    col = lax.broadcasted_iota(jnp.int32, (size, size), 1)
    apart = row ^ col
    eye = jnp.where(row == col, 1.0, 0.0)
    low = [matrix.astype(BF16) for matrix in system]
    solved = [eye - jnp.where(apart == 1, matrix, 0.0) for matrix in system]
    step = 2
    while step < size:
        level = (apart >= step) & (apart < 2 * step)
        for index, matrix in enumerate(low):
            part = jnp.where(level, matrix, 0.0)
            held = solved[index].astype(BF16)
            solved[index] = solved[index] - dot(dot(held, part).astype(BF16), held)
        step *= 2
    refined = []
    for matrix, high, inverse in zip(system, low, solved):
        rest = (matrix - high.astype(F32)).astype(BF16)
        head = inverse.astype(BF16)
        tail = (inverse - head.astype(F32)).astype(BF16)
        product = dot(high, head) + dot(rest, head) + dot(high, tail)
        residue = eye - inverse - product
        refined.append(inverse + dot(head, residue.astype(BF16)))
    return refined


def unit_rows(conv):
    gate = sigmoid(conv)
    act = conv * gate
    scale = lax.rsqrt(lane_sum(act * act) + 1e-06)
    return gate, act, scale


def forward_kernel(
    starts_ref, length_ref, raw_ref, conv_q_ref, conv_k_ref, conv_v_ref, gain_ref,
    gated_ref, mixed_ref, solve_ref, update_ref, state_ref,
    keep_ref, live_ref, carry_ref, strict_ref, incl_ref,
):
    rows, head_width = live_ref.shape
    width = gated_ref.shape[1]
    chunks = rows // CHUNK
    fill_masks(starts_ref, length_ref, keep_ref, live_ref, carry_ref)
    for chunk in range(chunks):
        strict, incl = pair_mask(starts_ref, chunk)
        strict_ref[chunk] = jnp.where(strict, 1.0, 0.0)
        incl_ref[chunk] = jnp.where(incl, 1.0, 0.0)

    @pl.loop(0, width // head_width)
    def _(head):
        start = pl.multiple_of(head * head_width, head_width)

        def stream(index):
            return raw_ref[:, pl.ds(pl.multiple_of(index * width + start, head_width), head_width)]

        cols = pl.ds(start, head_width)
        conv, _ = convolve(stream(Q), conv_q_ref[:, cols], keep_ref)
        _, act, scale = unit_rows(conv)
        query = (act * scale).astype(BF16)
        conv, _ = convolve(stream(K), conv_k_ref[:, cols], keep_ref)
        _, act, scale = unit_rows(conv)
        keyed = act * scale
        key_low = keyed.astype(BF16)
        conv, _ = convolve(stream(V), conv_v_ref[:, cols], keep_ref)
        valued = conv * sigmoid(conv)
        rate = sigmoid(column(raw_ref[:, 4 * width :], head)) * live_ref[...]
        scaled_value = (valued * rate).astype(BF16)
        scaled_key = keyed * rate
        system = []
        for chunk in range(chunks):
            span = slice(chunk * CHUNK, (chunk + 1) * CHUNK)
            pair = dot_nt(key_low[span], key_low[span])
            wide = jnp.concatenate([rate[span]] * (CHUNK // head_width), axis=1)
            system.append(pair * wide * strict_ref[chunk])
        memory = None
        for chunk, solved in enumerate(invert(system)):
            span = slice(chunk * CHUNK, (chunk + 1) * CHUNK)
            solve_low = solved.astype(BF16)
            solve_ref[head * chunks + chunk] = solve_low
            score = dot_nt(query[span], key_low[span]) * incl_ref[chunk]
            if chunk == 0:
                update = dot(solve_low, scaled_value[span])
                update_low = update.astype(BF16)
                mixed = dot(score.astype(BF16), update_low)
            else:
                carry = carry_ref[chunk - 1][span]
                right = jnp.concatenate(
                    [scaled_value[span], (scaled_key[span] * carry).astype(BF16)], axis=1
                )
                both = dot(solve_low, right)
                memory_low = memory.astype(BF16)
                state_ref[head * (chunks - 1) + chunk - 1] = memory_low
                update = both[:, :head_width] - dot(both[:, head_width:].astype(BF16), memory_low)
                update_low = update.astype(BF16)
                mixed = carry * dot(query[span], memory_low) + dot(score.astype(BF16), update_low)
            update_ref[span, cols] = update_low
            mixed_ref[span, cols] = mixed
            if chunk + 1 < chunks:
                last = (keyed[span] * carry_ref[chunk][span]).astype(BF16)
                fresh = dot_tn(last, update_low)
                if memory is None:
                    memory = fresh
                else:
                    memory = memory * carry_ref[chunk - 1][span][CHUNK - 1 :] + fresh
        mixed = mixed_ref[:, cols]
        norm = lax.rsqrt(lane_sum(mixed * mixed) * (1.0 / head_width) + 1e-05)
        gating = stream(G)
        gated = mixed * norm * gain_ref[...] * (gating * sigmoid(gating)) * live_ref[...]
        gated_ref[:, cols] = gated.astype(BF16)


def delta_forward(starts, length, raw, conv_q, conv_k, conv_v, gain):
    rows = raw.shape[0]
    head_width = gain.shape[-1]
    width = conv_q.shape[1]
    heads, chunks = width // head_width, rows // CHUNK
    vmem = pl.BlockSpec(memory_space=pltpu.VMEM)
    smem = pl.BlockSpec(memory_space=pltpu.SMEM)
    return pl.pallas_call(
        forward_kernel,
        out_shape=(
            jax.ShapeDtypeStruct((rows, width), BF16),
            jax.ShapeDtypeStruct((rows, width), F32),
            jax.ShapeDtypeStruct((heads * chunks, CHUNK, CHUNK), BF16),
            jax.ShapeDtypeStruct((rows, width), BF16),
            jax.ShapeDtypeStruct((heads * (chunks - 1), head_width, head_width), BF16),
        ),
        in_specs=[smem, smem] + [vmem] * 5,
        out_specs=[vmem] * 5,
        scratch_shapes=[
            pltpu.VMEM((KERNEL - 1, rows, head_width), F32),
            pltpu.VMEM((rows, head_width), F32),
            pltpu.VMEM((chunks - 1, rows, head_width), F32),
            pltpu.VMEM((chunks, CHUNK, CHUNK), F32),
            pltpu.VMEM((chunks, CHUNK, CHUNK), F32),
        ],
        compiler_params=pltpu.CompilerParams(vmem_limit_bytes=40 * 1024 * 1024),
        cost_estimate=pl.CostEstimate(
            flops=2 * 24 * heads * chunks * CHUNK**3, bytes_accessed=12 * 2**20, transcendentals=0
        ),
        name="delta_forward",
    )(starts, length, raw, conv_q, conv_k, conv_v, gain)


def backward_kernel(
    starts_ref, length_ref, raw_ref, conv_q_ref, conv_k_ref, conv_v_ref, gain_ref,
    mixed_ref, solve_ref, update_ref, state_ref, grad_ref,
    d_raw_ref, d_conv_ref, d_gain_ref,
    keep_ref, live_ref, carry_ref, strict_ref, incl_ref, d_query_ref, d_key_ref, d_value_ref, d_rate_ref,
):
    rows, head_width = live_ref.shape
    width = mixed_ref.shape[1]
    chunks = rows // CHUNK
    fill_masks(starts_ref, length_ref, keep_ref, live_ref, carry_ref)
    for chunk in range(chunks):
        strict, incl = pair_mask(starts_ref, chunk)
        strict_ref[chunk] = jnp.where(strict, 1.0, 0.0)
        incl_ref[chunk] = jnp.where(incl, 1.0, 0.0)
    d_gain_ref[...] = jnp.zeros_like(d_gain_ref)
    d_raw_ref[:, 4 * width :] = jnp.zeros((rows, head_width), BF16)

    @pl.loop(0, width // head_width)
    def _(head):
        start = pl.multiple_of(head * head_width, head_width)

        def place(index):
            return pl.ds(pl.multiple_of(index * width + start, head_width), head_width)

        cols = pl.ds(start, head_width)
        live = live_ref[...]
        mixed = mixed_ref[:, cols]
        norm = lax.rsqrt(lane_sum(mixed * mixed) * (1.0 / head_width) + 1e-05)
        gating = raw_ref[:, place(G)]
        gate = sigmoid(gating)
        normal = mixed * norm
        grad = grad_ref[:, cols].astype(F32) * live
        grad_gain = grad * gain_ref[...]
        swish = gating * gate
        d_raw_ref[:, place(G)] = (grad_gain * normal * gate * (1.0 + gating - swish)).astype(BF16)
        d_gain_ref[...] += jnp.sum(grad * normal * swish, axis=0, keepdims=True)
        d_normal = grad_gain * swish
        d_mixed = norm * (d_normal - normal * (lane_sum(d_normal * normal) * (1.0 / head_width)))
        d_mixed_low = d_mixed.astype(BF16)

        conv_q, parts_q = convolve(raw_ref[:, place(Q)], conv_q_ref[:, cols], keep_ref)
        gate_q, act_q, scale_q = unit_rows(conv_q)
        unit_q = act_q * scale_q
        query = unit_q.astype(BF16)
        conv_k, parts_k = convolve(raw_ref[:, place(K)], conv_k_ref[:, cols], keep_ref)
        gate_k, act_k, scale_k = unit_rows(conv_k)
        keyed = act_k * scale_k
        key_low = keyed.astype(BF16)
        conv_v, parts_v = convolve(raw_ref[:, place(V)], conv_v_ref[:, cols], keep_ref)
        gate_v = sigmoid(conv_v)
        valued = conv_v * gate_v
        sig = sigmoid(column(raw_ref[:, 4 * width :], head))
        rate = sig * live
        scaled_value = (valued * rate).astype(BF16)
        scaled_key = keyed * rate

        d_memory = None
        for chunk in range(chunks - 1, -1, -1):
            span = slice(chunk * CHUNK, (chunk + 1) * CHUNK)
            key_c, query_c, d_mixed_c = key_low[span], query[span], d_mixed_low[span]
            solve = solve_ref[head * chunks + chunk]
            update = update_ref[span, cols]
            incl, strict = incl_ref[chunk], strict_ref[chunk]
            score = (dot_nt(query_c, key_c) * incl).astype(BF16)
            d_update = dot_tn(score, d_mixed_c)
            d_key = None
            if d_memory is not None:
                last = carry_ref[chunk][span]
                d_memory_low = d_memory.astype(BF16)
                d_update = d_update + dot((keyed[span] * last).astype(BF16), d_memory_low)
                d_key = last * dot_nt(update, d_memory_low)
            d_update_low = d_update.astype(BF16)
            d_score = (dot_nt(d_mixed_c, update) * incl).astype(BF16)
            d_query = dot(d_score, key_c)
            d_key_score = dot_tn(d_score, query_c)
            d_key = d_key_score if d_key is None else d_key + d_key_score
            if chunk == 0:
                right = scaled_value[span]
                solved = dot(solve, right)
                d_right = dot_tn(solve, d_update_low)
                d_value_in = d_right
                d_rate = lane_sum(d_value_in * valued[span])
            else:
                carry = carry_ref[chunk - 1][span]
                state = state_ref[head * (chunks - 1) + chunk - 1]
                right = jnp.concatenate([scaled_value[span], (scaled_key[span] * carry).astype(BF16)], axis=1)
                solved = dot(solve, right)
                d_solved_key = -dot_nt(d_update_low, state)
                d_right = dot_tn(solve, jnp.concatenate([d_update_low, d_solved_key.astype(BF16)], axis=1))
                d_value_in = d_right[:, :head_width]
                d_key_in = d_right[:, head_width:] * carry
                carried = (carry * d_mixed[span]).astype(BF16)
                d_query = d_query + dot_nt(carried, state)
                d_key = d_key + rate[span] * d_key_in
                d_rate = lane_sum(d_value_in * valued[span] + d_key_in * keyed[span])
                fresh = dot_tn(query_c, carried) - dot_tn(solved[:, head_width:].astype(BF16), d_update_low)
                if d_memory is None:
                    d_memory = fresh
                else:
                    d_memory = d_memory * carry[CHUNK - 1 :] + fresh
            d_system = dot_nt(d_right.astype(BF16), solved.astype(BF16)) * -strict
            pair = dot_nt(key_c, key_c)
            d_rate = d_rate + lane_sum(d_system * pair)
            wide = jnp.concatenate([rate[span]] * (CHUNK // head_width), axis=1)
            d_pair = (d_system * wide).astype(BF16)
            d_key = d_key + dot(d_pair, key_c) + dot_tn(d_pair, key_c)
            d_query_ref[span] = d_query
            d_key_ref[span] = d_key
            d_value_ref[span] = rate[span] * d_value_in
            d_rate_ref[span] = jnp.broadcast_to(d_rate, (CHUNK, head_width))

        lane = lax.broadcasted_iota(jnp.int32, (rows, head_width), 1)
        d_beta = d_rate_ref[...] * rate * (1.0 - sig)
        tail = d_raw_ref[:, 4 * width :]
        d_raw_ref[:, 4 * width :] = jnp.where(lane == head, d_beta.astype(BF16), tail)

        def conv_back(index, d_conv, parts, taps):
            sums = [jnp.sum(d_conv * part, axis=0, keepdims=True) for part in parts]
            for delay in range(KERNEL):
                tap = KERNEL - 1 - delay
                d_conv_ref[tap : tap + 1, place(index - 1)] = sums[delay]
            total = d_conv * taps[KERNEL - 1 : KERNEL]
            for delay in range(1, KERNEL):
                tap = KERNEL - 1 - delay
                back = pltpu.roll(d_conv * keep_ref[delay - 1], rows - delay, 0)
                total = total + back * taps[tap : tap + 1]
            d_raw_ref[:, place(index)] = total.astype(BF16)

        def unit_back(d_unit, unit, scale, conv, act, gate):
            d_act = scale * (d_unit - unit * lane_sum(d_unit * unit))
            return d_act * gate * (1.0 + conv - act)

        conv_back(Q, unit_back(d_query_ref[...], unit_q, scale_q, conv_q, act_q, gate_q), parts_q, conv_q_ref[:, cols])
        conv_back(K, unit_back(d_key_ref[...], keyed, scale_k, conv_k, act_k, gate_k), parts_k, conv_k_ref[:, cols])
        d_conv_v = d_value_ref[...] * gate_v * (1.0 + conv_v - valued)
        conv_back(V, d_conv_v, parts_v, conv_v_ref[:, cols])


def delta_backward(starts, length, raw, conv_q, conv_k, conv_v, gain, mixed, solve, update, state, grad):
    rows = raw.shape[0]
    head_width = gain.shape[-1]
    width = conv_q.shape[1]
    heads, chunks = width // head_width, rows // CHUNK
    vmem = pl.BlockSpec(memory_space=pltpu.VMEM)
    smem = pl.BlockSpec(memory_space=pltpu.SMEM)
    return pl.pallas_call(
        backward_kernel,
        out_shape=(
            jax.ShapeDtypeStruct((rows, 4 * width + head_width), BF16),
            jax.ShapeDtypeStruct((KERNEL, 3 * width), F32),
            jax.ShapeDtypeStruct((1, head_width), F32),
        ),
        in_specs=[smem, smem] + [vmem] * 10,
        out_specs=[vmem] * 3,
        scratch_shapes=[
            pltpu.VMEM((KERNEL - 1, rows, head_width), F32),
            pltpu.VMEM((rows, head_width), F32),
            pltpu.VMEM((chunks - 1, rows, head_width), F32),
            pltpu.VMEM((chunks, CHUNK, CHUNK), F32),
            pltpu.VMEM((chunks, CHUNK, CHUNK), F32),
        ]
        + [pltpu.VMEM((rows, head_width), F32)] * 4,
        compiler_params=pltpu.CompilerParams(vmem_limit_bytes=48 * 1024 * 1024),
        cost_estimate=pl.CostEstimate(
            flops=2 * 12 * heads * chunks * CHUNK**3, bytes_accessed=16 * 2**20, transcendentals=0
        ),
        name="delta_backward",
    )(starts, length, raw, conv_q, conv_k, conv_v, gain, mixed, solve, update, state, grad)


def reduce_kernel(
    group_size, line_size, fsdp_size, gain_ref, head_ref, conv_ref, gain_out, head_out, conv_out,
    line_gain, line_head, stage, group_gain, group_conv,
    line_send, line_recv, group_send, group_recv,
):
    dp, fsdp, tensor = (lax.axis_index(name) for name in ("dp", "fsdp", "tensor"))
    group = dp * fsdp_size + fsdp
    size = gain_out.shape[1]

    def line_peer(shift):
        return (dp, fsdp, lax.rem(tensor + shift, line_size))

    def group_peer(shift):
        peer = lax.rem(group + shift, group_size)
        return peer, (lax.div(peer, fsdp_size), lax.rem(peer, fsdp_size), tensor)

    barrier = pltpu.get_barrier_semaphore()
    for shift in range(1, line_size):
        pl.semaphore_signal(barrier, inc=1, device_id=line_peer(shift), device_id_type=MESH)
    for shift in range(1, group_size):
        pl.semaphore_signal(barrier, inc=1, device_id=group_peer(shift)[1], device_id_type=MESH)
    pl.semaphore_wait(barrier, line_size + group_size - 2)

    copies = []
    for shift in range(1, line_size):
        for part, (source, target) in enumerate(((gain_ref, line_gain), (head_ref, line_head))):
            copy = pltpu.make_async_remote_copy(
                src_ref=source, dst_ref=target.at[shift - 1],
                send_sem=line_send.at[shift - 1, part], recv_sem=line_recv.at[shift - 1, part],
                device_id=line_peer(shift), device_id_type=MESH,
            )
            copy.start()
            copies.append(copy)
    conv_copies = []
    for shift in range(1, group_size):
        copy = pltpu.make_async_remote_copy(
            src_ref=conv_ref, dst_ref=group_conv.at[shift - 1],
            send_sem=group_send.at[shift - 1, 1], recv_sem=group_recv.at[shift - 1, 1],
            device_id=group_peer(shift)[1], device_id_type=MESH,
        )
        copy.start()
        conv_copies.append(copy)
    for copy in copies:
        copy.wait()
    gain = gain_ref[...]
    head = head_ref[...]
    for shift in range(1, line_size):
        gain = gain + line_gain[shift - 1]
        head = head + line_head[shift - 1]
    for peer in range(group_size):
        stage[peer] = jnp.zeros(stage.shape[1:], F32)
        stage[peer, :2, :size] = gain[:, peer * size : (peer + 1) * size]
        stage[peer, 2:3, : head.shape[1]] = head
    for copy in conv_copies:
        copy.wait()
    conv = conv_ref[...]
    for shift in range(1, group_size):
        conv = conv + group_conv[shift - 1]
    conv_out[...] = conv
    copies = []
    for shift in range(1, group_size):
        peer, where = group_peer(shift)
        copy = pltpu.make_async_remote_copy(
            src_ref=stage.at[peer], dst_ref=group_gain.at[shift - 1],
            send_sem=group_send.at[shift - 1, 0], recv_sem=group_recv.at[shift - 1, 0],
            device_id=where, device_id_type=MESH,
        )
        copy.start()
        copies.append(copy)
    for copy in copies:
        copy.wait()
    total = stage[group]
    for shift in range(1, group_size):
        total = total + group_gain[shift - 1]
    gain_out[...] = total[:2, :size]
    head_out[...] = total[2:3, : head.shape[1]]


def reduce_small(gain, head, conv):
    fsdp_size, line_size = lax.axis_size("fsdp"), lax.axis_size("tensor")
    group_size = lax.axis_size("dp") * fsdp_size
    size = gain.shape[1] // group_size
    pad = max(size, head.shape[1])
    vmem = pl.BlockSpec(memory_space=pltpu.VMEM)
    dma = pltpu.SemaphoreType.DMA
    return pl.pallas_call(
        functools.partial(reduce_kernel, group_size, line_size, fsdp_size),
        out_shape=(
            jax.ShapeDtypeStruct((2, size), F32),
            jax.ShapeDtypeStruct(head.shape, F32),
            jax.ShapeDtypeStruct(conv.shape, F32),
        ),
        in_specs=[vmem] * 3,
        out_specs=[vmem] * 3,
        scratch_shapes=[
            pltpu.VMEM((line_size - 1,) + gain.shape, F32),
            pltpu.VMEM((line_size - 1,) + head.shape, F32),
            pltpu.VMEM((group_size, 8, pad), F32),
            pltpu.VMEM((group_size - 1, 8, pad), F32),
            pltpu.VMEM((group_size - 1,) + conv.shape, F32),
            dma((line_size - 1, 2)),
            dma((line_size - 1, 2)),
            dma((group_size - 1, 2)),
            dma((group_size - 1, 2)),
        ],
        compiler_params=pltpu.CompilerParams(collective_id=1, has_side_effects=True, vmem_limit_bytes=16 * 2**20),
        name="reduce_small",
    )(gain, head, conv)


PARTS = 4


def rms_scale(values):
    return lax.rsqrt(jnp.mean(values * values, axis=-1, keepdims=True) + 1e-05)


def rms_back(values, scale_rows, gain, grad):
    scaled_grad = grad * gain
    inner = jnp.mean(scaled_grad * values, axis=-1, keepdims=True)
    return scale_rows * (scaled_grad - values * scale_rows * scale_rows * inner)


class Line:

    def __init__(self, count, rows, sums, rows_out):
        self.count = count
        self.rows = rows
        self.part = rows // PARTS
        self.sums = sums
        self.rows_out = rows_out
        self.dp, self.fsdp, self.place = (lax.axis_index(name) for name in ("dp", "fsdp", "tensor"))

    def device(self, step):
        return (self.dp, self.fsdp, self.place + step)

    def ahead(self, step):
        return self.place < self.count - 1 if step > 0 else self.place > 0

    def behind(self, step):
        return self.ahead(-step)

    def barrier(self):
        barrier = pltpu.get_barrier_semaphore()
        for step in (1, -1):
            @pl.when(self.ahead(step))
            def _():
                pl.semaphore_signal(barrier, inc=1, device_id=self.device(step), device_id_type=MESH)
        ends = (self.place == 0).astype(jnp.int32) + (self.place == self.count - 1).astype(jnp.int32)
        pl.semaphore_wait(barrier, 2 - ends)

    def span(self, owner, part):
        return pl.ds(pl.multiple_of(owner * self.rows + part * self.part, self.part), self.part)

    def sum_copy(self, source, step, slot, part):
        recv, _, send_sem, recv_sem = self.sums[step]
        return pltpu.make_async_remote_copy(
            src_ref=source, dst_ref=recv.at[slot, part],
            send_sem=send_sem.at[slot, part], recv_sem=recv_sem.at[slot, part],
            device_id=self.device(step), device_id_type=MESH,
        )

    def owner_of(self, step, slot):
        return self.count - 1 - slot if step > 0 else slot

    def inject(self, partial_ref, part):
        for step in (1, -1):
            @pl.when(jnp.logical_not(self.behind(step)))
            def _():
                for slot in range(self.count - 1):
                    owner = self.owner_of(step, slot)
                    self.sum_copy(partial_ref.at[self.span(owner, part)], step, slot, part).start()

    def passes(self, step, slot):
        owner = self.owner_of(step, slot)
        further = self.place < owner if step > 0 else self.place > owner
        return jnp.logical_and(self.behind(step), further)

    def forward(self, partial_ref, part):
        for slot in range(self.count - 1):
            for step in (1, -1):
                recv, send, _, _ = self.sums[step]

                @pl.when(self.passes(step, slot))
                def _():
                    self.sum_copy(send.at[slot, part], step, slot, part).wait_recv()
                    mine = partial_ref[self.span(self.owner_of(step, slot), part), :].astype(F32)
                    send[slot, part] = (mine + recv[slot, part].astype(F32)).astype(BF16)
                    self.sum_copy(send.at[slot, part], step, slot, part).start()

    def collect(self, partial_ref, total_ref, part):
        total_ref[...] = partial_ref[self.span(self.place, part), :].astype(F32)
        for step in (1, -1):
            recv, send, _, _ = self.sums[step]
            slot = self.count - 1 - self.place if step > 0 else self.place

            @pl.when(self.behind(step))
            def _():
                self.sum_copy(send.at[0, part], step, slot, part).wait_recv()
                total_ref[...] += recv[slot, part].astype(F32)

    def drain_sums(self, partial_ref):
        for part in range(PARTS):
            for step in (1, -1):
                _, send, _, _ = self.sums[step]
                for slot in range(self.count - 1):
                    owner = self.owner_of(step, slot)
                    further = self.place < owner if step > 0 else self.place > owner

                    @pl.when(further)
                    def _():
                        self.sum_copy(send.at[slot, part], step, slot, part).wait_send()

    def row_copy(self, ref, step, owner, distance, part):
        send_sem, recv_sem = self.rows_out[step]
        where = ref.at[self.span(owner, part)]
        return pltpu.make_async_remote_copy(
            src_ref=where, dst_ref=where,
            send_sem=send_sem.at[distance, part], recv_sem=recv_sem.at[distance, part],
            device_id=self.device(step), device_id_type=MESH,
        )

    def spread(self, ref, part):
        for step in (1, -1):
            @pl.when(self.ahead(step))
            def _():
                self.row_copy(ref, step, self.place, 0, part).start()

    def relay(self, ref, distance, part):
        for step in (1, -1):
            owner = self.place - step * distance
            inside = owner >= 0 if step > 0 else owner < self.count

            @pl.when(inside)
            def _():
                self.row_copy(ref, step, owner, distance - 1, part).wait_recv()

                if distance < self.count - 1:
                    @pl.when(self.ahead(step))
                    def _():
                        self.row_copy(ref, step, owner, distance, part).start()

    def drain_rows(self, ref):
        for part in range(PARTS):
            for step in (1, -1):
                for distance in range(self.count - 1):
                    owner = self.place - step * distance
                    inside = owner >= 0 if step > 0 else owner < self.count

                    @pl.when(jnp.logical_and(inside, self.ahead(step)))
                    def _():
                        self.row_copy(ref, step, owner, distance, part).wait_send()


def line_scratch(count, rows, features, spread):
    dma = pltpu.SemaphoreType.DMA
    slots = (count - 1, PARTS)
    scratch = []
    for _ in range(2):
        scratch += [pltpu.VMEM(slots + (rows // PARTS, features), BF16)] * 2 + [dma(slots)] * 2
    if spread:
        scratch += [dma(slots)] * 4
    return scratch + [pltpu.VMEM((rows // PARTS, features), F32)]


def line_of(count, rows, scratch):
    sums = {1: scratch[0:4], -1: scratch[4:8]}
    rows_out = {1: scratch[8:10], -1: scratch[10:12]} if len(scratch) > 9 else None
    return Line(count, rows, sums, rows_out), scratch[-1]


def run_line(line, partial_ref, total_ref, finish, rows_ref):
    line.barrier()
    line.inject(partial_ref, 0)
    line.inject(partial_ref, 1)
    for turn in range(PARTS + (line.count - 1 if rows_ref is not None else 0)):
        if turn < PARTS:
            line.forward(partial_ref, turn)
            line.collect(partial_ref, total_ref, turn)
            finish(turn, pl.ds(turn * line.part, line.part), line.span(line.place, turn))
            if rows_ref is not None:
                line.spread(rows_ref, turn)
            if turn + 2 < PARTS:
                line.inject(partial_ref, turn + 2)
        if rows_ref is not None:
            for distance in range(1, line.count):
                if 0 <= turn - distance < PARTS:
                    line.relay(rows_ref, distance, turn - distance)
    line.drain_sums(partial_ref)
    if rows_ref is not None:
        line.drain_rows(rows_ref)


def middle_kernel(count, partial_ref, input_ref, gain_ref, rows_ref, resid_ref, *scratch):
    line, total_ref = line_of(count, input_ref.shape[0], scratch)

    def finish(part, local, place):
        resid = input_ref[local, :].astype(F32) + total_ref[...]
        resid_ref[local, :] = resid
        rows_ref[place, :] = (resid * rms_scale(resid) * gain_ref[...]).astype(BF16)

    run_line(line, partial_ref, total_ref, finish, rows_ref)


def turn_kernel(count, partial_ref, resid_ref, grad_ref, gain_ref, rows_ref, d_resid_ref, d_gain_ref, *scratch):
    line, total_ref = line_of(count, resid_ref.shape[0], scratch)

    def finish(part, local, place):
        resid, total = resid_ref[local, :], total_ref[...]
        scale = rms_scale(resid)
        sums = jnp.sum(total * resid * scale, axis=0, keepdims=True)
        d_gain_ref[...] = sums if part == 0 else d_gain_ref[...] + sums
        d_resid = grad_ref[local, :].astype(F32) + rms_back(resid, scale, gain_ref[...], total)
        d_resid_ref[local, :] = d_resid
        rows_ref[place, :] = d_resid.astype(BF16)

    run_line(line, partial_ref, total_ref, finish, rows_ref)


def last_kernel(count, partial_ref, input_ref, d_resid_ref, gain_ref, d_input_ref, d_gain_ref, *scratch):
    line, total_ref = line_of(count, input_ref.shape[0], scratch)

    def finish(part, local, place):
        values, total = input_ref[local, :].astype(F32), total_ref[...]
        scale = rms_scale(values)
        sums = jnp.sum(total * values * scale, axis=0, keepdims=True)
        d_gain_ref[...] = sums if part == 0 else d_gain_ref[...] + sums
        d_input_ref[local, :] = d_resid_ref[local, :] + rms_back(values, scale, gain_ref[...], total)

    run_line(line, partial_ref, total_ref, finish, None)


def line_call(kernel, name, ident, spread, out_shape, operands):
    count = lax.axis_size("tensor")
    partial_rows, features = operands[0].shape
    vmem = pl.BlockSpec(memory_space=pltpu.VMEM)
    return pl.pallas_call(
        functools.partial(kernel, count),
        out_shape=out_shape,
        in_specs=[vmem] * len(operands),
        out_specs=[vmem] * len(out_shape),
        scratch_shapes=line_scratch(count, partial_rows // count, features, spread),
        compiler_params=pltpu.CompilerParams(
            collective_id=ident, has_side_effects=True, vmem_limit_bytes=32 * 2**20
        ),
        cost_estimate=pl.CostEstimate(flops=10**9, bytes_accessed=60 * 2**20, transcendentals=0),
        name=name,
    )(*operands)


def shifted(count, shift):
    return [(index, (index + shift) % count) for index in range(count)]


def gather_rows(rows):
    count = lax.axis_size("tensor")
    mine = lax.axis_index("tensor")
    height = rows.shape[0]
    whole = jnp.zeros((count * height, rows.shape[1]), rows.dtype)
    whole = lax.dynamic_update_slice_in_dim(whole, rows, mine * height, 0)
    for shift in range(1, count):
        came = lax.ppermute(rows, "tensor", shifted(count, shift))
        source = lax.rem(mine + count - shift, count)
        whole = lax.dynamic_update_slice_in_dim(whole, came, source * height, 0)
    return whole


def send_rows(rows):
    count = lax.axis_size("tensor")
    return [lax.ppermute(rows, "tensor", shifted(count, shift)) for shift in range(1, count)]


def place_rows(rows, came):
    count = lax.axis_size("tensor")
    mine = lax.axis_index("tensor")
    height = rows.shape[0]
    whole = jnp.zeros((count * height, rows.shape[1]), rows.dtype)
    whole = lax.dynamic_update_slice_in_dim(whole, rows, mine * height, 0)
    for shift in range(1, count):
        source = lax.rem(mine + count - shift, count)
        whole = lax.dynamic_update_slice_in_dim(whole, came[shift - 1], source * height, 0)
    return whole


def scatter_rows(partial_rows):
    count = lax.axis_size("tensor")
    mine = lax.axis_index("tensor")
    height = partial_rows.shape[0] // count
    total = lax.dynamic_slice_in_dim(partial_rows, mine * height, height, 0).astype(F32)
    for shift in range(1, count):
        target = lax.rem(mine + shift, count)
        piece = lax.dynamic_slice_in_dim(partial_rows, target * height, height, 0)
        total = total + lax.ppermute(piece, "tensor", shifted(count, shift)).astype(F32)
    return total


def gather_weights(pieces):
    return lax.all_gather(jnp.concatenate(pieces, axis=1), ("fsdp", "dp"), axis=0, tiled=True)


def scatter_grads(grads):
    return lax.psum_scatter(grads, ("dp", "fsdp"), scatter_dimension=0, tiled=True).astype(F32)


def body(
    layer_input,
    first_gain,
    w_query,
    w_key,
    w_value,
    w_gating,
    w_beta,
    conv_query,
    conv_key,
    conv_value,
    head_gain,
    w_project,
    second_gain,
    w_gate,
    w_up,
    w_down,
    doc_starts,
    seq_lengths,
    output_grad,
):
    replicas = lax.axis_size("dp")
    replica = lax.axis_index("dp")
    width = w_query.shape[1]
    units = w_gate.shape[1]
    heads = w_beta.shape[1]
    head_width = head_gain.shape[0]

    def piece(weight, axis):
        size = weight.shape[axis] // replicas
        return lax.dynamic_slice_in_dim(weight, replica * size, size, axis)

    input_float = layer_input.astype(F32)
    conv_q = conv_query.astype(F32)
    conv_k = conv_key.astype(F32)
    conv_v = conv_value.astype(F32)
    gain_head = head_gain.astype(F32)[None, :]
    gains = lax.all_gather(jnp.stack([first_gain, second_gain]), "fsdp", axis=1, tiled=True).astype(F32)
    gain_one, gain_two = gains[:1], gains[1:]
    beta_piece = jnp.pad(piece(w_beta, 0), ((0, 0), (0, head_width - heads)))
    mix_full = gather_weights(
        [piece(w_gating, 0), piece(w_query, 0), piece(w_key, 0), piece(w_value, 0), beta_piece, piece(w_project, 1).T]
    )
    ffn_full = gather_weights(
        [piece(w_gate, 0), piece(w_up, 0), piece(w_down, 1).T]
    )
    project_t = mix_full[:, 4 * width + head_width :]
    mix_full = mix_full[:, : 4 * width + head_width]
    gate_up = ffn_full[:, : 2 * units]
    down_t = ffn_full[:, 2 * units :]

    scale_one = rms_scale(input_float)
    normed1 = (input_float * scale_one * gain_one).astype(BF16)
    rows_one = gather_rows(normed1)
    late_grad, rows_one = lax.optimization_barrier((output_grad, rows_one))
    came = send_rows(late_grad)
    raw = dot(rows_one, mix_full)
    gated, mixed, solve, update, state = delta_forward(
        doc_starts, seq_lengths, raw, conv_q, conv_k, conv_v, gain_head
    )
    gated, came = lax.optimization_barrier((gated, came))
    grad_rows = place_rows(output_grad, came)
    attn_partial = dot_nt(gated, project_t).astype(BF16)
    whole_rows = jax.ShapeDtypeStruct(rows_one.shape, BF16)
    own_rows = jax.ShapeDtypeStruct(layer_input.shape, F32)
    gain_sums = jax.ShapeDtypeStruct((1, layer_input.shape[1]), F32)
    rows_two, resid = line_call(
        middle_kernel, "middle", 2, True, (whole_rows, own_rows), (attn_partial, layer_input, gain_two)
    )
    d_hidden = dot(grad_rows, down_t)
    both = dot(rows_two, gate_up)
    gate_val, up_val = both[:, :units], both[:, units:]
    gate_sig = jax.nn.sigmoid(gate_val)
    silu_gate = gate_val * gate_sig
    hidden = (silu_gate * up_val).astype(BF16)
    d_gate = (d_hidden * up_val * gate_sig * (1.0 + gate_val * (1.0 - gate_sig))).astype(BF16)
    d_up = (d_hidden * silu_gate).astype(BF16)
    d_both = jnp.concatenate([d_gate, d_up], axis=1)
    grad_down = dot_tn(grad_rows, hidden).astype(BF16)
    down_shard = scatter_grads(grad_down)
    grad_both = dot_tn(rows_two, d_both).astype(BF16)
    both_shard = scatter_grads(grad_both)
    d_partial, _, _ = lax.optimization_barrier(
        (dot_nt(d_both, gate_up).astype(BF16), grad_down, grad_both)
    )
    d_attn, d_resid, grad_second = line_call(
        turn_kernel, "turn", 3, True, (whole_rows, own_rows, gain_sums), (d_partial, resid, output_grad, gain_two)
    )
    ffn_partial, d_attn, down_shard = lax.optimization_barrier((dot_nt(hidden, down_t).astype(BF16), d_attn, down_shard))
    ffn_out = scatter_rows(ffn_partial)
    result = (resid + ffn_out).astype(BF16)
    d_gated = dot(d_attn, project_t)
    grad_project = dot_tn(d_attn, gated).astype(BF16)
    d_raw, d_conv, d_head = delta_backward(
        doc_starts, seq_lengths, raw, conv_q, conv_k, conv_v, gain_head, mixed, solve, update, state, d_gated
    )
    grad_mix = dot_tn(rows_one, d_raw).astype(BF16)
    mix_shard = scatter_grads(jnp.concatenate([grad_mix, grad_project], axis=1))
    project_shard = mix_shard[:, 4 * width + head_width :]
    mix_partial, result, both_shard = lax.optimization_barrier(
        (dot_nt(d_raw, mix_full).astype(BF16), result, both_shard)
    )
    input_grad, grad_first = line_call(
        last_kernel, "last", 4, False, (own_rows, gain_sums),
        (mix_partial, layer_input, d_resid, gain_one),
    )
    gain_total, head_total, conv_totals = reduce_small(
        jnp.concatenate([grad_first, grad_second], axis=0), d_head, d_conv
    )
    return (
        result,
        input_grad,
        gain_total[0],
        mix_shard[:, width : 2 * width],
        mix_shard[:, 2 * width : 3 * width],
        mix_shard[:, 3 * width : 4 * width],
        mix_shard[:, :width],
        mix_shard[:, 4 * width : 4 * width + heads],
        conv_totals[:, :width],
        conv_totals[:, width : 2 * width],
        conv_totals[:, 2 * width :],
        head_total[0],
        project_shard.T,
        gain_total[1],
        both_shard[:, :units],
        both_shard[:, units:],
        down_shard.T,
    )


def solution(mesh):
    placed = (
        P(("dp", "fsdp", "tensor"), None),
        P("fsdp"),
        P("fsdp", "tensor"),
        P("fsdp", "tensor"),
        P("fsdp", "tensor"),
        P("fsdp", "tensor"),
        P("fsdp", "tensor"),
        P(None, "tensor"),
        P(None, "tensor"),
        P(None, "tensor"),
        P(),
        P("tensor", "fsdp"),
        P("fsdp"),
        P("fsdp", "tensor"),
        P("fsdp", "tensor"),
        P("tensor", "fsdp"),
        P(("dp", "fsdp"), None),
        P(("dp", "fsdp")),
        P(("dp", "fsdp", "tensor"), None),
    )
    return jax.shard_map(
        body,
        mesh=mesh,
        in_specs=placed,
        out_specs=(
            P(("dp", "fsdp", "tensor"), None),
            P(("dp", "fsdp", "tensor"), None),
            P(("dp", "fsdp")),
            P(("dp", "fsdp"), "tensor"),
            P(("dp", "fsdp"), "tensor"),
            P(("dp", "fsdp"), "tensor"),
            P(("dp", "fsdp"), "tensor"),
            P(("dp", "fsdp"), "tensor"),
            P(None, "tensor"),
            P(None, "tensor"),
            P(None, "tensor"),
            P(),
            P("tensor", ("dp", "fsdp")),
            P(("dp", "fsdp")),
            P(("dp", "fsdp"), "tensor"),
            P(("dp", "fsdp"), "tensor"),
            P("tensor", ("dp", "fsdp")),
        ),
        check_vma=False,
    )
```

```python
import functools
import jax, jax.numpy as jnp
from jax import lax
from jax.experimental import pallas as pl
from jax.experimental.pallas import tpu as pltpu
from jax.experimental.layout import Layout, with_layout_constraint
from jax.sharding import PartitionSpec as P

KERNEL = 4
CHUNK = 256
G, Q, K, V = range(4)
MESH = pl.DeviceIdType.MESH
F32 = jnp.float32
BF16 = jnp.bfloat16


def coordinates():
    replica = lax.axis_index("pair") * 2 + lax.axis_index("core")
    return replica, lax.axis_index("fsdp"), lax.axis_index("tensor")


def extents():
    return lax.axis_size("pair") * 2, lax.axis_size("fsdp"), lax.axis_size("tensor")


def device(replica, shard, place):
    return (lax.div(replica, 2), lax.rem(replica, 2), shard, place)


def dot(left, right):
    return jnp.dot(left, right, preferred_element_type=F32)


def dot_nt(left, right):
    return lax.dot_general(left, right, (((1,), (1,)), ((), ())), preferred_element_type=F32)


def dot_tn(left, right):
    return lax.dot_general(left, right, (((0,), (0,)), ((), ())), preferred_element_type=F32)


def lane_sum(values):
    return jnp.sum(values, axis=-1, keepdims=True)


def document_of(starts_ref, positions):
    total = jnp.zeros_like(positions)
    for entry in range(starts_ref.shape[1]):
        total = total + (positions >= starts_ref[0, entry]).astype(jnp.int32)
    return total


def fill_masks(starts_ref, length_ref, keep_ref, live_ref, carry_ref):
    rows, lanes = live_ref.shape
    place = lax.broadcasted_iota(jnp.int32, (rows, lanes), 0)
    docs = document_of(starts_ref, place)
    for delay in range(1, KERNEL):
        prior = document_of(starts_ref, place - delay)
        keep_ref[delay - 1] = jnp.where((prior == docs) & (place >= delay), 1.0, 0.0)
    live_ref[...] = jnp.where(place < length_ref[0], 1.0, 0.0)
    for edge in range(rows // CHUNK - 1):
        seam = jnp.int32((edge + 1) * CHUNK - 1)
        carry_ref[edge] = jnp.where(docs == document_of(starts_ref, seam), 1.0, 0.0)


def pair_mask(starts_ref, chunk):
    row = lax.broadcasted_iota(jnp.int32, (CHUNK, CHUNK), 0)
    col = lax.broadcasted_iota(jnp.int32, (CHUNK, CHUNK), 1)
    first = chunk * CHUNK
    same = document_of(starts_ref, row + first) == document_of(starts_ref, col + first)
    return same & (row > col), same & (row >= col)


def convolve(raw, taps, keep_ref):
    parts = [raw]
    for delay in range(1, KERNEL):
        parts.append(pltpu.roll(raw, delay, 0) * keep_ref[delay - 1])
    total = parts[0] * taps[KERNEL - 1 : KERNEL]
    for delay in range(1, KERNEL):
        total = total + parts[delay] * taps[KERNEL - 1 - delay : KERNEL - delay]
    return total, parts


def sigmoid(values):
    return 0.5 * jnp.tanh(0.5 * values) + 0.5


def column(values, index):
    lane = lax.broadcasted_iota(jnp.int32, values.shape, 1)
    return lane_sum(jnp.where(lane == index, values, 0.0))


def invert(system):
    size = system[0].shape[0]
    row = lax.broadcasted_iota(jnp.int32, (size, size), 0)
    col = lax.broadcasted_iota(jnp.int32, (size, size), 1)
    apart = row ^ col
    eye = jnp.where(row == col, 1.0, 0.0)
    low = [matrix.astype(BF16) for matrix in system]
    solved = [eye - jnp.where(apart == 1, matrix, 0.0) for matrix in system]
    step = 2
    while step < size:
        level = (apart >= step) & (apart < 2 * step)
        for index, matrix in enumerate(low):
            part = jnp.where(level, matrix, 0.0)
            held = solved[index].astype(BF16)
            solved[index] = solved[index] - dot(dot(held, part).astype(BF16), held)
        step *= 2
    refined = []
    for matrix, high, inverse in zip(system, low, solved):
        rest = (matrix - high.astype(F32)).astype(BF16)
        head = inverse.astype(BF16)
        tail = (inverse - head.astype(F32)).astype(BF16)
        product = dot(high, head) + dot(rest, head) + dot(high, tail)
        residue = eye - inverse - product
        refined.append(inverse + dot(head, residue.astype(BF16)))
    return refined


def unit_rows(conv):
    gate = sigmoid(conv)
    act = conv * gate
    scale = lax.rsqrt(lane_sum(act * act) + 1e-06)
    return gate, act, scale


def forward_kernel(
    starts_ref, length_ref, raw_ref, conv_q_ref, conv_k_ref, conv_v_ref, gain_ref,
    gated_ref, mixed_ref, solve_ref, update_ref, state_ref,
    keep_ref, live_ref, carry_ref, strict_ref, incl_ref,
):
    rows, head_width = live_ref.shape
    width = gated_ref.shape[1]
    chunks = rows // CHUNK
    fill_masks(starts_ref, length_ref, keep_ref, live_ref, carry_ref)
    for chunk in range(chunks):
        strict, incl = pair_mask(starts_ref, chunk)
        strict_ref[chunk] = jnp.where(strict, 1.0, 0.0)
        incl_ref[chunk] = jnp.where(incl, 1.0, 0.0)

    @pl.loop(0, width // head_width)
    def _(head):
        start = pl.multiple_of(head * head_width, head_width)

        def stream(index):
            return raw_ref[:, pl.ds(pl.multiple_of(index * width + start, head_width), head_width)]

        cols = pl.ds(start, head_width)
        conv, _ = convolve(stream(Q), conv_q_ref[:, cols], keep_ref)
        _, act, scale = unit_rows(conv)
        query = (act * scale).astype(BF16)
        conv, _ = convolve(stream(K), conv_k_ref[:, cols], keep_ref)
        _, act, scale = unit_rows(conv)
        keyed = act * scale
        key_low = keyed.astype(BF16)
        conv, _ = convolve(stream(V), conv_v_ref[:, cols], keep_ref)
        valued = conv * sigmoid(conv)
        rate = sigmoid(column(raw_ref[:, 4 * width :], head)) * live_ref[...]
        scaled_value = (valued * rate).astype(BF16)
        scaled_key = keyed * rate
        system = []
        for chunk in range(chunks):
            span = slice(chunk * CHUNK, (chunk + 1) * CHUNK)
            pair = dot_nt(key_low[span], key_low[span])
            wide = jnp.concatenate([rate[span]] * (CHUNK // head_width), axis=1)
            system.append(pair * wide * strict_ref[chunk])
        memory = None
        for chunk, solved in enumerate(invert(system)):
            span = slice(chunk * CHUNK, (chunk + 1) * CHUNK)
            solve_low = solved.astype(BF16)
            solve_ref[head * chunks + chunk] = solve_low
            score = dot_nt(query[span], key_low[span]) * incl_ref[chunk]
            if chunk == 0:
                update = dot(solve_low, scaled_value[span])
                update_low = update.astype(BF16)
                mixed = dot(score.astype(BF16), update_low)
            else:
                carry = carry_ref[chunk - 1][span]
                right = jnp.concatenate(
                    [scaled_value[span], (scaled_key[span] * carry).astype(BF16)], axis=1
                )
                both = dot(solve_low, right)
                memory_low = memory.astype(BF16)
                state_ref[head * (chunks - 1) + chunk - 1] = memory_low
                update = both[:, :head_width] - dot(both[:, head_width:].astype(BF16), memory_low)
                update_low = update.astype(BF16)
                mixed = carry * dot(query[span], memory_low) + dot(score.astype(BF16), update_low)
            update_ref[span, cols] = update_low
            mixed_ref[span, cols] = mixed
            if chunk + 1 < chunks:
                last = (keyed[span] * carry_ref[chunk][span]).astype(BF16)
                fresh = dot_tn(last, update_low)
                if memory is None:
                    memory = fresh
                else:
                    memory = memory * carry_ref[chunk - 1][span][CHUNK - 1 :] + fresh
        mixed = mixed_ref[:, cols]
        norm = lax.rsqrt(lane_sum(mixed * mixed) * (1.0 / head_width) + 1e-05)
        gating = stream(G)
        gated = mixed * norm * gain_ref[...] * (gating * sigmoid(gating)) * live_ref[...]
        gated_ref[:, cols] = gated.astype(BF16)


def delta_forward(starts, length, raw, conv_q, conv_k, conv_v, gain):
    rows = raw.shape[0]
    head_width = gain.shape[-1]
    width = conv_q.shape[1]
    heads, chunks = width // head_width, rows // CHUNK
    vmem = pl.BlockSpec(memory_space=pltpu.VMEM)
    smem = pl.BlockSpec(memory_space=pltpu.SMEM)
    return pl.pallas_call(
        forward_kernel,
        out_shape=(
            jax.ShapeDtypeStruct((rows, width), BF16),
            jax.ShapeDtypeStruct((rows, width), F32),
            jax.ShapeDtypeStruct((heads * chunks, CHUNK, CHUNK), BF16),
            jax.ShapeDtypeStruct((rows, width), BF16),
            jax.ShapeDtypeStruct((heads * (chunks - 1), head_width, head_width), BF16),
        ),
        in_specs=[smem, smem] + [vmem] * 5,
        out_specs=[vmem] * 5,
        scratch_shapes=[
            pltpu.VMEM((KERNEL - 1, rows, head_width), F32),
            pltpu.VMEM((rows, head_width), F32),
            pltpu.VMEM((chunks - 1, rows, head_width), F32),
            pltpu.VMEM((chunks, CHUNK, CHUNK), F32),
            pltpu.VMEM((chunks, CHUNK, CHUNK), F32),
        ],
        compiler_params=pltpu.CompilerParams(vmem_limit_bytes=40 * 1024 * 1024),
        cost_estimate=pl.CostEstimate(
            flops=2 * 24 * heads * chunks * CHUNK**3, bytes_accessed=12 * 2**20, transcendentals=0
        ),
        name="delta_forward",
    )(starts, length, raw, conv_q, conv_k, conv_v, gain)


def backward_kernel(
    starts_ref, length_ref, raw_ref, conv_q_ref, conv_k_ref, conv_v_ref, gain_ref,
    mixed_ref, solve_ref, update_ref, state_ref, grad_ref,
    d_raw_ref, d_conv_ref, d_gain_ref,
    keep_ref, live_ref, carry_ref, strict_ref, incl_ref, d_query_ref, d_key_ref, d_value_ref, d_rate_ref,
):
    rows, head_width = live_ref.shape
    width = mixed_ref.shape[1]
    chunks = rows // CHUNK
    fill_masks(starts_ref, length_ref, keep_ref, live_ref, carry_ref)
    for chunk in range(chunks):
        strict, incl = pair_mask(starts_ref, chunk)
        strict_ref[chunk] = jnp.where(strict, 1.0, 0.0)
        incl_ref[chunk] = jnp.where(incl, 1.0, 0.0)
    d_gain_ref[...] = jnp.zeros_like(d_gain_ref)
    d_raw_ref[:, 4 * width :] = jnp.zeros((rows, head_width), BF16)

    @pl.loop(0, width // head_width)
    def _(head):
        start = pl.multiple_of(head * head_width, head_width)

        def place(index):
            return pl.ds(pl.multiple_of(index * width + start, head_width), head_width)

        cols = pl.ds(start, head_width)
        live = live_ref[...]
        mixed = mixed_ref[:, cols]
        norm = lax.rsqrt(lane_sum(mixed * mixed) * (1.0 / head_width) + 1e-05)
        gating = raw_ref[:, place(G)]
        gate = sigmoid(gating)
        normal = mixed * norm
        grad = grad_ref[:, cols].astype(F32) * live
        grad_gain = grad * gain_ref[...]
        swish = gating * gate
        d_raw_ref[:, place(G)] = (grad_gain * normal * gate * (1.0 + gating - swish)).astype(BF16)
        d_gain_ref[...] += jnp.sum(grad * normal * swish, axis=0, keepdims=True)
        d_normal = grad_gain * swish
        d_mixed = norm * (d_normal - normal * (lane_sum(d_normal * normal) * (1.0 / head_width)))
        d_mixed_low = d_mixed.astype(BF16)

        conv_q, parts_q = convolve(raw_ref[:, place(Q)], conv_q_ref[:, cols], keep_ref)
        gate_q, act_q, scale_q = unit_rows(conv_q)
        unit_q = act_q * scale_q
        query = unit_q.astype(BF16)
        conv_k, parts_k = convolve(raw_ref[:, place(K)], conv_k_ref[:, cols], keep_ref)
        gate_k, act_k, scale_k = unit_rows(conv_k)
        keyed = act_k * scale_k
        key_low = keyed.astype(BF16)
        conv_v, parts_v = convolve(raw_ref[:, place(V)], conv_v_ref[:, cols], keep_ref)
        gate_v = sigmoid(conv_v)
        valued = conv_v * gate_v
        sig = sigmoid(column(raw_ref[:, 4 * width :], head))
        rate = sig * live
        scaled_value = (valued * rate).astype(BF16)
        scaled_key = keyed * rate

        d_memory = None
        for chunk in range(chunks - 1, -1, -1):
            span = slice(chunk * CHUNK, (chunk + 1) * CHUNK)
            key_c, query_c, d_mixed_c = key_low[span], query[span], d_mixed_low[span]
            solve = solve_ref[head * chunks + chunk]
            update = update_ref[span, cols]
            incl, strict = incl_ref[chunk], strict_ref[chunk]
            score = (dot_nt(query_c, key_c) * incl).astype(BF16)
            d_update = dot_tn(score, d_mixed_c)
            d_key = None
            if d_memory is not None:
                last = carry_ref[chunk][span]
                d_memory_low = d_memory.astype(BF16)
                d_update = d_update + dot((keyed[span] * last).astype(BF16), d_memory_low)
                d_key = last * dot_nt(update, d_memory_low)
            d_update_low = d_update.astype(BF16)
            d_score = (dot_nt(d_mixed_c, update) * incl).astype(BF16)
            d_query = dot(d_score, key_c)
            d_key_score = dot_tn(d_score, query_c)
            d_key = d_key_score if d_key is None else d_key + d_key_score
            if chunk == 0:
                right = scaled_value[span]
                solved = dot(solve, right)
                d_right = dot_tn(solve, d_update_low)
                d_value_in = d_right
                d_rate = lane_sum(d_value_in * valued[span])
            else:
                carry = carry_ref[chunk - 1][span]
                state = state_ref[head * (chunks - 1) + chunk - 1]
                right = jnp.concatenate([scaled_value[span], (scaled_key[span] * carry).astype(BF16)], axis=1)
                solved = dot(solve, right)
                d_solved_key = -dot_nt(d_update_low, state)
                d_right = dot_tn(solve, jnp.concatenate([d_update_low, d_solved_key.astype(BF16)], axis=1))
                d_value_in = d_right[:, :head_width]
                d_key_in = d_right[:, head_width:] * carry
                carried = (carry * d_mixed[span]).astype(BF16)
                d_query = d_query + dot_nt(carried, state)
                d_key = d_key + rate[span] * d_key_in
                d_rate = lane_sum(d_value_in * valued[span] + d_key_in * keyed[span])
                fresh = dot_tn(query_c, carried) - dot_tn(solved[:, head_width:].astype(BF16), d_update_low)
                if d_memory is None:
                    d_memory = fresh
                else:
                    d_memory = d_memory * carry[CHUNK - 1 :] + fresh
            d_system = dot_nt(d_right.astype(BF16), solved.astype(BF16)) * -strict
            pair = dot_nt(key_c, key_c)
            d_rate = d_rate + lane_sum(d_system * pair)
            wide = jnp.concatenate([rate[span]] * (CHUNK // head_width), axis=1)
            d_pair = (d_system * wide).astype(BF16)
            d_key = d_key + dot(d_pair, key_c) + dot_tn(d_pair, key_c)
            d_query_ref[span] = d_query
            d_key_ref[span] = d_key
            d_value_ref[span] = rate[span] * d_value_in
            d_rate_ref[span] = jnp.broadcast_to(d_rate, (CHUNK, head_width))

        lane = lax.broadcasted_iota(jnp.int32, (rows, head_width), 1)
        d_beta = d_rate_ref[...] * rate * (1.0 - sig)
        tail = d_raw_ref[:, 4 * width :]
        d_raw_ref[:, 4 * width :] = jnp.where(lane == head, d_beta.astype(BF16), tail)

        def conv_back(index, d_conv, parts, taps):
            sums = [jnp.sum(d_conv * part, axis=0, keepdims=True) for part in parts]
            for delay in range(KERNEL):
                tap = KERNEL - 1 - delay
                d_conv_ref[tap : tap + 1, place(index - 1)] = sums[delay]
            total = d_conv * taps[KERNEL - 1 : KERNEL]
            for delay in range(1, KERNEL):
                tap = KERNEL - 1 - delay
                back = pltpu.roll(d_conv * keep_ref[delay - 1], rows - delay, 0)
                total = total + back * taps[tap : tap + 1]
            d_raw_ref[:, place(index)] = total.astype(BF16)

        def unit_back(d_unit, unit, scale, conv, act, gate):
            d_act = scale * (d_unit - unit * lane_sum(d_unit * unit))
            return d_act * gate * (1.0 + conv - act)

        conv_back(Q, unit_back(d_query_ref[...], unit_q, scale_q, conv_q, act_q, gate_q), parts_q, conv_q_ref[:, cols])
        conv_back(K, unit_back(d_key_ref[...], keyed, scale_k, conv_k, act_k, gate_k), parts_k, conv_k_ref[:, cols])
        d_conv_v = d_value_ref[...] * gate_v * (1.0 + conv_v - valued)
        conv_back(V, d_conv_v, parts_v, conv_v_ref[:, cols])


def delta_backward(starts, length, raw, conv_q, conv_k, conv_v, gain, mixed, solve, update, state, grad):
    rows = raw.shape[0]
    head_width = gain.shape[-1]
    width = conv_q.shape[1]
    heads, chunks = width // head_width, rows // CHUNK
    vmem = pl.BlockSpec(memory_space=pltpu.VMEM)
    smem = pl.BlockSpec(memory_space=pltpu.SMEM)
    return pl.pallas_call(
        backward_kernel,
        out_shape=(
            jax.ShapeDtypeStruct((rows, 4 * width + head_width), BF16),
            jax.ShapeDtypeStruct((KERNEL, 3 * width), F32),
            jax.ShapeDtypeStruct((1, head_width), F32),
        ),
        in_specs=[smem, smem] + [vmem] * 10,
        out_specs=[vmem] * 3,
        scratch_shapes=[
            pltpu.VMEM((KERNEL - 1, rows, head_width), F32),
            pltpu.VMEM((rows, head_width), F32),
            pltpu.VMEM((chunks - 1, rows, head_width), F32),
            pltpu.VMEM((chunks, CHUNK, CHUNK), F32),
            pltpu.VMEM((chunks, CHUNK, CHUNK), F32),
        ]
        + [pltpu.VMEM((rows, head_width), F32)] * 4,
        compiler_params=pltpu.CompilerParams(vmem_limit_bytes=48 * 1024 * 1024),
        cost_estimate=pl.CostEstimate(
            flops=2 * 12 * heads * chunks * CHUNK**3, bytes_accessed=16 * 2**20, transcendentals=0
        ),
        name="delta_backward",
    )(starts, length, raw, conv_q, conv_k, conv_v, gain, mixed, solve, update, state, grad)


def reduce_kernel(
    group_size, line_size, fsdp_size, gain_ref, head_ref, conv_ref, gain_out, head_out, conv_out,
    line_gain, line_head, stage, group_gain, group_conv,
    line_send, line_recv, group_send, group_recv,
):
    dp, fsdp, tensor = coordinates()
    group = dp * fsdp_size + fsdp
    size = gain_out.shape[1]

    def line_peer(shift):
        return device(dp, fsdp, lax.rem(tensor + shift, line_size))

    def group_peer(shift):
        peer = lax.rem(group + shift, group_size)
        return peer, device(lax.div(peer, fsdp_size), lax.rem(peer, fsdp_size), tensor)

    barrier = pltpu.get_barrier_semaphore()
    for shift in range(1, line_size):
        pl.semaphore_signal(barrier, inc=1, device_id=line_peer(shift), device_id_type=MESH)
    for shift in range(1, group_size):
        pl.semaphore_signal(barrier, inc=1, device_id=group_peer(shift)[1], device_id_type=MESH)
    pl.semaphore_wait(barrier, line_size + group_size - 2)

    copies = []
    for shift in range(1, line_size):
        for part, (source, target) in enumerate(((gain_ref, line_gain), (head_ref, line_head))):
            copy = pltpu.make_async_remote_copy(
                src_ref=source, dst_ref=target.at[shift - 1],
                send_sem=line_send.at[shift - 1, part], recv_sem=line_recv.at[shift - 1, part],
                device_id=line_peer(shift), device_id_type=MESH,
            )
            copy.start()
            copies.append(copy)
    conv_copies = []
    for shift in range(1, group_size):
        copy = pltpu.make_async_remote_copy(
            src_ref=conv_ref, dst_ref=group_conv.at[shift - 1],
            send_sem=group_send.at[shift - 1, 1], recv_sem=group_recv.at[shift - 1, 1],
            device_id=group_peer(shift)[1], device_id_type=MESH,
        )
        copy.start()
        conv_copies.append(copy)
    for copy in copies:
        copy.wait()
    gain = gain_ref[...]
    head = head_ref[...]
    for shift in range(1, line_size):
        gain = gain + line_gain[shift - 1]
        head = head + line_head[shift - 1]
    for peer in range(group_size):
        stage[peer] = jnp.zeros(stage.shape[1:], F32)
        stage[peer, :2, :size] = gain[:, peer * size : (peer + 1) * size]
        stage[peer, 2:3, : head.shape[1]] = head
    for copy in conv_copies:
        copy.wait()
    conv = conv_ref[...]
    for shift in range(1, group_size):
        conv = conv + group_conv[shift - 1]
    conv_out[...] = conv
    copies = []
    for shift in range(1, group_size):
        peer, where = group_peer(shift)
        copy = pltpu.make_async_remote_copy(
            src_ref=stage.at[peer], dst_ref=group_gain.at[shift - 1],
            send_sem=group_send.at[shift - 1, 0], recv_sem=group_recv.at[shift - 1, 0],
            device_id=where, device_id_type=MESH,
        )
        copy.start()
        copies.append(copy)
    for copy in copies:
        copy.wait()
    total = stage[group]
    for shift in range(1, group_size):
        total = total + group_gain[shift - 1]
    gain_out[...] = total[:2, :size]
    head_out[...] = total[2:3, : head.shape[1]]


def reduce_small(gain, head, conv):
    replicas, fsdp_size, line_size = extents()
    group_size = replicas * fsdp_size
    size = gain.shape[1] // group_size
    pad = max(size, head.shape[1])
    vmem = pl.BlockSpec(memory_space=pltpu.VMEM)
    dma = pltpu.SemaphoreType.DMA
    return pl.pallas_call(
        functools.partial(reduce_kernel, group_size, line_size, fsdp_size),
        out_shape=(
            jax.ShapeDtypeStruct((2, size), F32),
            jax.ShapeDtypeStruct(head.shape, F32),
            jax.ShapeDtypeStruct(conv.shape, F32),
        ),
        in_specs=[vmem] * 3,
        out_specs=[vmem] * 3,
        scratch_shapes=[
            pltpu.VMEM((line_size - 1,) + gain.shape, F32),
            pltpu.VMEM((line_size - 1,) + head.shape, F32),
            pltpu.VMEM((group_size, 8, pad), F32),
            pltpu.VMEM((group_size - 1, 8, pad), F32),
            pltpu.VMEM((group_size - 1,) + conv.shape, F32),
            dma((line_size - 1, 2)),
            dma((line_size - 1, 2)),
            dma((group_size - 1, 2)),
            dma((group_size - 1, 2)),
        ],
        compiler_params=pltpu.CompilerParams(collective_id=1, has_side_effects=True, vmem_limit_bytes=16 * 2**20),
        name="reduce_small",
    )(gain, head, conv)


def plan(count, parts, sums, rows, shared, unit):
    latency, backlog, add, end = 1.5, 1.5, 0.15 + 0.8 / parts, 0.5 + 3.0 / parts
    rank = {"spread": 0, "relay": 0, "finish": 1, "forward": 2, "inject": 3}
    clock = [0.0] * count
    free, come = {}, [{} for _ in range(count)]
    todo = [set() for _ in range(count)]
    done = [0] * count
    at = [0] * count
    tasks = [[[] for _ in range(len(shared) + 1)] for _ in range(count)]
    own_finish = sums and not any(isinstance(step, tuple) for step in shared)
    for place in range(count):
        for part in range(parts):
            for step in (1, -1):
                behind = 0 <= place - step < count
                for slot in range(count - 1) if sums else ():
                    owner = count - 1 - slot if step > 0 else slot
                    if (owner - place) * step > 0:
                        todo[place].add(("forward" if behind else "inject", step, slot, part))
                for distance in range(1, count) if rows else ():
                    if 0 <= place - step * distance < count:
                        todo[place].add(("relay", step, distance, part))
            if rows and not sums:
                todo[place].add(("spread", 0, 0, part))
            if own_finish:
                todo[place].add(("finish", 0, 0, part))

    def ready(place, task):
        kind, step, slot, part = task
        if kind == "inject":
            return max(0.0, free.get((place, step), 0.0) - backlog * unit)
        if kind == "spread":
            return max([0.0] + [free.get((place, way), 0.0) - backlog * unit for way in (1, -1)])
        if kind == "forward":
            return come[place].get(("sum", step, slot, part))
        if kind == "relay":
            return come[place].get(("row", step, slot, part))
        if part != done[place]:
            return None
        times = [0.0]
        for way in (1, -1):
            if 0 <= place - way < count:
                times.append(come[place].get(("sum", way, count - 1 - place if way > 0 else place, part)))
        return None if None in times else max(times)

    def send(place, step, key):
        if 0 <= place + step < count:
            free[place, step] = max(clock[place], free.get((place, step), 0.0)) + unit
            come[place + step][key] = free[place, step] + latency

    def choices(place):
        found = [(ready(place, task), rank[task[0]], task[3], task[2], task[1], task) for task in todo[place]]
        found = [(max(clock[place], entry[0]),) + entry[1:] for entry in found if entry[0] is not None]
        if at[place] < len(shared):
            step = shared[at[place]]
            when = ready(place, ("finish", 0, 0, step[1])) if isinstance(step, tuple) else clock[place]
            if when is not None:
                found.append((max(when, clock[place]), 1 if isinstance(step, tuple) else 9, 0, 0, 0, step))
        return min(found, key=lambda entry: entry[:5]) if found else None

    while True:
        best = None
        for place in range(count):
            choice = choices(place)
            if choice is not None and (best is None or choice[0] < best[0][0]):
                best = (choice, place)
        if best is None:
            return max(clock), tasks
        choice, place = best
        clock[place] = choice[0]
        task = choice[5]
        if isinstance(task, float):
            clock[place] += task
            at[place] += 1
            continue
        if len(task) == 2:
            at[place] += 1
        else:
            todo[place].discard(task)
            tasks[place][at[place]].append(task)
        kind, step, slot, part = task if len(task) == 4 else ("finish", 0, 0, task[1])
        if kind in ("inject", "forward"):
            clock[place] += add if kind == "forward" else 0.02
            send(place, step, ("sum", step, slot, part))
        elif kind == "relay":
            clock[place] += 0.05
            if slot < count - 1:
                send(place, step, ("row", step, slot + 1, part))
        else:
            if kind == "finish":
                done[place] += 1
                clock[place] += end
            if rows:
                for way in (1, -1):
                    send(place, way, ("row", way, 1, part))


PARTS = 4
UNIT = 11.3


def rms_scale(values):
    return lax.rsqrt(jnp.mean(values * values, axis=-1, keepdims=True) + 1e-05)


def rms_back(values, scale_rows, gain, grad):
    scaled_grad = grad * gain
    inner = jnp.mean(scaled_grad * values, axis=-1, keepdims=True)
    return scale_rows * (scaled_grad - values * scale_rows * scale_rows * inner)


class Line:

    def __init__(self, count, rows, scratch, shared, sums, spreads, parts=PARTS):
        self.count, self.rows, self.parts = count, rows, parts
        self.part = rows // parts
        scratch = list(scratch)
        self.sums, self.sends = {}, {}
        if sums:
            for step in (1, -1):
                self.sums[step] = [scratch.pop(0) for _ in range(4)]
            self.total_ref = scratch.pop(0)
        if spreads:
            for step in (1, -1):
                self.sends[step] = [scratch.pop(0) for _ in range(2)]
        self.replica, self.shard, self.place = coordinates()
        self.tasks = plan(count, parts, sums, spreads, shared, UNIT / parts)[1]
        self.started = [[] for _ in range(count)]
        self.partial_ref = self.rows_ref = self.source_ref = self.finish = None

    def greet(self, others=()):
        barrier = pltpu.get_barrier_semaphore()
        for step in (1, -1):
            @pl.when(self.place < self.count - 1 if step > 0 else self.place > 0)
            def _():
                pl.semaphore_signal(
                    barrier, inc=1, device_id=device(self.replica, self.shard, self.place + step), device_id_type=MESH
                )
        for other in others:
            pl.semaphore_signal(barrier, inc=1, device_id=other, device_id_type=MESH)
        ends = (self.place == 0).astype(jnp.int32) + (self.place == self.count - 1).astype(jnp.int32)
        pl.semaphore_wait(barrier, 2 - ends + len(others))

    def span(self, owner, part):
        return pl.ds(pl.multiple_of(owner * self.rows + part * self.part, self.part), self.part)

    def sum_copy(self, source, step, slot, part):
        recv, _, send_sem, recv_sem = self.sums[step]
        return pltpu.make_async_remote_copy(
            src_ref=source, dst_ref=recv.at[slot, part],
            send_sem=send_sem.at[slot, part], recv_sem=recv_sem.at[slot, part],
            device_id=device(self.replica, self.shard, self.place + step), device_id_type=MESH,
        )

    def row_copy(self, step, owner, distance, part, source=None):
        send_sem, recv_sem = self.sends[step]
        where = self.rows_ref.at[self.span(owner, part)]
        return pltpu.make_async_remote_copy(
            src_ref=where if source is None else source, dst_ref=where,
            send_sem=send_sem.at[distance, part], recv_sem=recv_sem.at[distance, part],
            device_id=device(self.replica, self.shard, self.place + step), device_id_type=MESH,
        )

    def emit(self, place, task):
        kind, step, slot, part = task
        if kind in ("inject", "forward"):
            recv, send, _, _ = self.sums[step]
            owner = self.count - 1 - slot if step > 0 else slot
            source = self.partial_ref.at[self.span(owner, part)]
            if kind == "forward":
                self.sum_copy(source, step, slot, part).wait_recv()
                mine = self.partial_ref[self.span(owner, part), :].astype(F32)
                send[slot, part] = (mine + recv[slot, part].astype(F32)).astype(BF16)
                source = send.at[slot, part]
            copy = self.sum_copy(source, step, slot, part)
            copy.start()
        elif kind == "relay":
            owner = place - step * slot
            self.row_copy(step, owner, slot - 1, part).wait_recv()
            if slot < self.count - 1 and 0 <= place + step < self.count:
                self.row_copy(step, owner, slot, part).start()
        elif kind == "spread":
            self.spread_from(place, part)
        else:
            self.collect(part)
            self.finish(part, pl.ds(part * self.part, self.part), None)

    def spread_from(self, place, part):
        for step in (1, -1):
            if 0 <= place + step < self.count:
                source = None if self.source_ref is None else self.source_ref.at[pl.ds(part * self.part, self.part)]
                self.row_copy(step, place, 0, part, source).start()

    def run(self, index):
        for place in range(self.count):
            tasks = self.tasks[place][index]
            if tasks:
                @pl.when(self.place == place)
                def _():
                    for task in tasks:
                        self.emit(place, task)

    def run_at(self, base, step, count):
        for index in range(count):
            if any(tasks[base + index] for tasks in self.tasks):
                @pl.when(step == index)
                def _():
                    self.run(base + index)

    def collect(self, part):
        self.total_ref[...] = self.partial_ref[self.span(self.place, part), :].astype(F32)
        for step in (1, -1):
            recv, send, _, _ = self.sums[step]
            slot = self.count - 1 - self.place if step > 0 else self.place

            @pl.when(self.place > 0 if step > 0 else self.place < self.count - 1)
            def _():
                self.sum_copy(send.at[0, part], step, slot, part).wait_recv()
                self.total_ref[...] += recv[slot, part].astype(F32)

    def finish_all(self):
        for part in range(self.parts):
            self.run(part)
            self.collect(part)
            self.finish(part, pl.ds(part * self.part, self.part), self.span(self.place, part))
            if self.sends:
                for place in range(self.count):
                    @pl.when(self.place == place)
                    def _():
                        self.spread_from(place, part)
        self.run(self.parts)
        self.drain()

    def drain(self):
        for place in range(self.count):
            @pl.when(self.place == place)
            def _():
                for part in range(self.parts):
                    for step in (1, -1):
                        if self.sums:
                            send = self.sums[step][1]
                            for slot in range(self.count - 1):
                                owner = self.count - 1 - slot if step > 0 else slot
                                if (owner - place) * step > 0:
                                    self.sum_copy(send.at[slot, part], step, slot, part).wait_send()
                        if self.sends and 0 <= place + step < self.count:
                            for distance in range(self.count - 1):
                                owner = place - step * distance
                                if 0 <= owner < self.count:
                                    self.row_copy(step, owner, distance, part).wait_send()


def line_scratch(count, rows, features, sums, spreads, parts=PARTS):
    dma = pltpu.SemaphoreType.DMA
    slots = (count - 1, parts)
    scratch = []
    if sums:
        for _ in range(2):
            scratch += [pltpu.VMEM(slots + (rows // parts, features), BF16)] * 2 + [dma(slots)] * 2
        scratch.append(pltpu.VMEM((rows // parts, features), F32))
    if spreads:
        scratch += [dma(slots)] * 4
    return scratch


FINISHES = [("finish", part) for part in range(PARTS)]


def middle_kernel(count, partial_ref, input_ref, gain_ref, rows_ref, resid_ref, *scratch):
    line = Line(count, input_ref.shape[0], scratch, FINISHES, True, True)

    def finish(part, local, place):
        resid = input_ref[local, :].astype(F32) + line.total_ref[...]
        resid_ref[local, :] = resid
        rows_ref[place, :] = (resid * rms_scale(resid) * gain_ref[...]).astype(BF16)

    line.partial_ref, line.rows_ref, line.finish = partial_ref, rows_ref, finish
    line.greet()
    line.finish_all()


def turn_kernel(count, partial_ref, resid_ref, grad_ref, gain_ref, rows_ref, d_resid_ref, d_gain_ref, *scratch):
    line = Line(count, resid_ref.shape[0], scratch, FINISHES, True, True)

    def finish(part, local, place):
        resid, total = resid_ref[local, :], line.total_ref[...]
        scale = rms_scale(resid)
        sums = jnp.sum(total * resid * scale, axis=0, keepdims=True)
        d_gain_ref[...] = sums if part == 0 else d_gain_ref[...] + sums
        d_resid = grad_ref[local, :].astype(F32) + rms_back(resid, scale, gain_ref[...], total)
        d_resid_ref[local, :] = d_resid
        rows_ref[place, :] = d_resid.astype(BF16)

    line.partial_ref, line.rows_ref, line.finish = partial_ref, rows_ref, finish
    line.greet()
    line.finish_all()


def last_kernel(count, partial_ref, input_ref, d_resid_ref, gain_ref, d_input_ref, d_gain_ref, *scratch):
    line = Line(count, input_ref.shape[0], scratch, FINISHES, True, False)

    def finish(part, local, place):
        values, total = input_ref[local, :].astype(F32), line.total_ref[...]
        scale = rms_scale(values)
        sums = jnp.sum(total * values * scale, axis=0, keepdims=True)
        d_gain_ref[...] = sums if part == 0 else d_gain_ref[...] + sums
        d_input_ref[local, :] = d_resid_ref[local, :] + rms_back(values, scale, gain_ref[...], total)

    line.partial_ref, line.finish = partial_ref, finish
    line.greet()
    line.finish_all()


def line_call(kernel, name, ident, spreads, out_shape, operands):
    count = lax.axis_size("tensor")
    partial_rows, features = operands[0].shape
    vmem = pl.BlockSpec(memory_space=pltpu.VMEM)
    return pl.pallas_call(
        functools.partial(kernel, count),
        out_shape=out_shape,
        in_specs=[vmem] * len(operands),
        out_specs=[vmem] * len(out_shape),
        scratch_shapes=line_scratch(count, partial_rows // count, features, True, spreads),
        compiler_params=pltpu.CompilerParams(
            collective_id=ident, has_side_effects=True, vmem_limit_bytes=32 * 2**20
        ),
        cost_estimate=pl.CostEstimate(flops=10**9, bytes_accessed=60 * 2**20, transcendentals=0),
        name=name,
    )(*operands)


def enter_kernel(
    sizes, input_ref, gain_one_ref, gain_two_ref, beta_ref, gating_ref, query_ref, key_ref, value_ref, project_ref,
    rows_ref, mix_ref, whole_project_ref, gains_ref,
    all_rows, all_one, all_two, all_beta, local_sem, small_send, small_recv,
    first_send, first_recv, second_send, second_recv, third_send, third_recv, *row_sems,
):
    replicas, shards, count = sizes
    rows = input_ref.shape[0]
    width = query_ref.shape[1]
    heads = beta_ref.shape[0]
    share = query_ref.shape[0]
    sources = (gating_ref, query_ref, key_ref, value_ref, project_ref)
    streams = len(sources)
    pairs = replicas // 2
    line = Line(count, rows, row_sems, [], False, True, parts=2)
    line.rows_ref, line.source_ref = all_rows, input_ref
    replica, shard, place = line.replica, line.shard, line.place
    partner = replica + 1 - 2 * lax.rem(replica, 2)

    def across(step):
        return lax.rem(replica + 2 * step, replicas)

    def shard_at(shift):
        return lax.rem(shard + shift, shards)

    def piece(ref, stream, row, col, part):
        if stream < 4:
            size = share // replicas
            return ref.at[
                pl.ds(pl.multiple_of(row + part * size, size), size),
                pl.ds(col + stream * width if col is not None else 0, width),
            ]
        size = width // replicas
        return ref.at[
            pl.ds(pl.multiple_of(part * size, size), size),
            pl.ds(pl.multiple_of(row, 128), share),
        ]

    def held(stream, owner, part):
        ref = mix_ref if stream < 4 else whole_project_ref
        return piece(ref, stream, owner * share, 0, part)

    def own(stream, part):
        ref = sources[stream]
        if stream < 4:
            return piece(ref, stream, 0, None, part)
        return piece(ref, stream, 0, None, part)

    def remote(source, target, send, recv, where):
        return pltpu.make_async_remote_copy(
            src_ref=source, dst_ref=target, send_sem=send, recv_sem=recv, device_id=where, device_id_type=MESH
        )

    def first(shift, stream, owner):
        return remote(
            own(stream, replica), held(stream, owner, replica),
            first_send.at[shift - 1, stream], first_recv.at[shift - 1, stream],
            device(replica, shard_at(shift), place),
        )

    def second(shift, step, stream, part):
        where = held(stream, shard_at(shards - shift), part)
        return remote(
            where, where, second_send.at[shift - 1, step - 1, stream], second_recv.at[shift - 1, step - 1, stream],
            device(across(step), shard, place),
        )

    def third(shift, step, stream, part):
        where = held(stream, shard_at(shards - shift), part)
        return remote(
            where, where, third_send.at[shift - 1, step, stream], third_recv.at[shift - 1, step, stream],
            device(partner, shard, place),
        )

    def spread(part):
        for there in range(count):
            @pl.when(place == there)
            def _():
                line.spread_from(there, part)

    def relay(distance, part):
        for there in range(count):
            @pl.when(place == there)
            def _():
                for step in (1, -1):
                    if 0 <= there - step * distance < count:
                        line.emit(there, ("relay", step, distance, part))

    features = share * shards
    cols = pl.ds(pl.multiple_of(shard * share, 128), share)
    smalls = ((gain_one_ref, all_one.at[:, cols]), (gain_two_ref, all_two.at[:, cols]), (beta_ref, all_beta.at[:, cols]))

    def small(shift, index):
        source, target = smalls[index]
        return remote(
            source, target, small_send.at[shift - 1, index], small_recv.at[shift - 1, index],
            device(replica, shard_at(shift), place),
        )

    others = [device(replica, shard_at(shift), place) for shift in range(1, shards)]
    others += [device(across(step), shard, place) for step in range(1, pairs)] + [device(partner, shard, place)]
    line.greet(others)
    for shift in range(1, shards):
        for index in range(len(smalls)):
            small(shift, index).start()
    for part in range(2):
        spread(part)
    for stream in range(streams):
        for shift in range(1, shards):
            first(shift, stream, shard).start()
    locals_ = [pltpu.make_async_copy(source, target, local_sem.at[index]) for index, (source, target) in enumerate(smalls)]
    for stream in range(4):
        locals_.append(pltpu.make_async_copy(
            sources[stream],
            mix_ref.at[pl.ds(pl.multiple_of(shard * share, share), share), pl.ds(stream * width, width)],
            local_sem.at[3 + stream],
        ))
    locals_.append(pltpu.make_async_copy(project_ref, whole_project_ref.at[:, cols], local_sem.at[7]))
    for copy in locals_:
        copy.start()
    for copy in locals_[:3]:
        copy.wait()
    for shift in range(1, shards):
        for index in range(len(smalls)):
            small(shift, index).wait()
    gains_ref[...] = jnp.concatenate([all_one[...].astype(F32), all_two[...].astype(F32)], axis=0)
    lanes = mix_ref.shape[1] - 4 * width
    beta = jnp.concatenate([all_beta[...].astype(F32), jnp.zeros((lanes - heads, features), F32)], axis=0)
    mix_ref[:, 4 * width :] = beta.T.astype(BF16)

    def normalize(source, start, size):
        values = source[pl.ds(start, size), :].astype(F32)
        return (values * rms_scale(values) * gains_ref[0:1, :]).astype(BF16)

    rows_ref[line.span(place, 0), :] = normalize(input_ref, 0, line.part)
    rows_ref[line.span(place, 1), :] = normalize(input_ref, line.part, line.part)

    for turn in range(max(streams + 2, 2 * (count - 1))):
        if turn < streams:
            for shift in range(1, shards):
                first(shift, turn, shard_at(shards - shift)).wait_recv()
                for step in range(1, pairs):
                    second(shift, step, turn, replica).start()
                third(shift, 0, turn, replica).start()
        distance, part = turn // 2 + 1, turn % 2
        if distance < count:
            relay(distance, part)
        if 0 <= turn - 1 < streams:
            for shift in range(1, shards):
                for step in range(1, pairs):
                    came = across(pairs - step)
                    second(shift, step, turn - 1, came).wait_recv()
                    third(shift, step, turn - 1, came).start()
        if distance < count:
            for step in (1, -1):
                owner = place - step * distance
                inside = owner >= 0 if step > 0 else owner < count

                @pl.when(inside)
                def _():
                    start = pl.multiple_of(owner * rows + part * line.part, line.part)
                    rows_ref[line.span(owner, part), :] = normalize(all_rows, start, line.part)
        if 0 <= turn - 2 < streams:
            for shift in range(1, shards):
                for step in range(pairs):
                    third(shift, step, turn - 2, replica).wait_recv()
    for copy in locals_[3:]:
        copy.wait()
    for stream in range(streams):
        for shift in range(1, shards):
            first(shift, stream, shard).wait_send()
            for step in range(1, pairs):
                second(shift, step, stream, replica).wait_send()
            for step in range(pairs):
                third(shift, step, stream, replica).wait_send()
    line.drain()


def enter(layer_input, first_gain, second_gain, w_beta, mixers, w_project):
    replicas, shards, count = extents()
    rows, features = layer_input.shape
    width = mixers[0].shape[1]
    share = mixers[0].shape[0]
    heads = w_beta.shape[1]
    pairs = replicas // 2
    vmem = pl.BlockSpec(memory_space=pltpu.VMEM)
    hbm = pl.BlockSpec(memory_space=pl.ANY)
    dma = pltpu.SemaphoreType.DMA
    far = max(shards - 1, 1)
    out_shape = (
        jax.ShapeDtypeStruct((count * rows, features), BF16),
        jax.ShapeDtypeStruct((features, 4 * width + 128), BF16),
        jax.ShapeDtypeStruct((width, features), BF16),
        jax.ShapeDtypeStruct((2, features), F32),
    )
    return pl.pallas_call(
        functools.partial(enter_kernel, (replicas, shards, count)),
        out_shape=out_shape,
        in_specs=[vmem] * 4 + [hbm] * 5,
        out_specs=[vmem] * 4,
        scratch_shapes=[
            pltpu.VMEM((count * rows, features), BF16),
            pltpu.VMEM((1, features), BF16),
            pltpu.VMEM((1, features), BF16),
            pltpu.VMEM((heads, features), BF16),
            dma((8,)),
            dma((far, 3)),
            dma((far, 3)),
            dma((far, 5)),
            dma((far, 5)),
            dma((far, max(pairs - 1, 1), 5)),
            dma((far, max(pairs - 1, 1), 5)),
            dma((far, pairs, 5)),
            dma((far, pairs, 5)),
        ]
        + [dma((count - 1, 2))] * 4,
        compiler_params=pltpu.CompilerParams(collective_id=5, has_side_effects=True, vmem_limit_bytes=40 * 2**20),
        cost_estimate=pl.CostEstimate(flops=10**9, bytes_accessed=60 * 2**20, transcendentals=0),
        name="enter",
    )(layer_input, first_gain[None, :], second_gain[None, :], w_beta.T, *mixers, w_project)


class Pair:

    def __init__(self, features, owners, left_ref, right_ref, grad_refs, out_ref, scratch):
        self.owners, self.left_ref, self.right_ref, self.grad_refs = owners, left_ref, right_ref, grad_refs
        self.out_ref = out_ref
        self.tiles, self.came, self.send_sem, self.recv_sem = scratch
        self.core = lax.axis_index("core")
        replica, shard, place = coordinates()
        self.partner = device(replica + 1 - 2 * self.core, shard, place)
        self.blocks, self.size = out_ref.shape[:2]
        self.share = features // (2 * lax.axis_size("pair"))

    def copy(self, block):
        return pltpu.make_async_remote_copy(
            src_ref=self.tiles.at[block], dst_ref=self.came.at[block], send_sem=self.send_sem.at[block],
            recv_sem=self.recv_sem.at[block], device_id=self.partner, device_id_type=MESH,
        )

    def product(self, block, core):
        steps = self.share // self.size
        start = (lax.div(block, steps) * 2 + core) * self.share + lax.rem(block, steps) * self.size
        cols = pl.ds(pl.multiple_of(start, self.size), self.size)
        start = 0
        for owner, grad_ref in zip(self.owners, self.grad_refs):
            wide = grad_ref.shape[1]
            values = dot_tn((self.left_ref if owner == 0 else self.right_ref)[:, cols], grad_ref[...])
            yield slice(start, start + wide), values
            start += wide

    def theirs(self, block):
        for span, values in self.product(block, 1 - self.core):
            self.tiles[block, :, span] = values.astype(BF16)
        self.copy(block).start()

    def ours(self, block):
        self.copy(block).wait_recv()
        for span, values in self.product(block, self.core):
            self.out_ref[block, :, span] = (values + self.came[block, :, span].astype(F32)).astype(BF16)

    def drain(self):
        for block in range(self.blocks):
            self.copy(block).wait_send()


def pair_shape(left, grads):
    features = left.shape[1]
    return features // (2 * CHUNK), CHUNK, sum(grad.shape[1] for grad in grads)


def pair_scratch(shape):
    dma = pltpu.SemaphoreType.DMA
    return [pltpu.VMEM(shape, BF16), pltpu.VMEM(shape, BF16), dma(shape[:1]), dma(shape[:1])]


def mix_grads_kernel(features, left_ref, right_ref, first_ref, second_ref, out_ref, *scratch):
    pair = Pair(features, (0, 1), left_ref, right_ref, (first_ref, second_ref), out_ref, scratch)
    barrier = pltpu.get_barrier_semaphore()
    pl.semaphore_signal(barrier, inc=1, device_id=pair.partner, device_id_type=MESH)
    pl.semaphore_wait(barrier, 1)
    pl.loop(0, pair.blocks)(pair.theirs)
    pl.loop(0, pair.blocks)(pair.ours)
    pair.drain()


def mix_grads(left, right, grads):
    shape = pair_shape(left, grads)
    vmem = pl.BlockSpec(memory_space=pltpu.VMEM)
    out = pl.pallas_call(
        functools.partial(mix_grads_kernel, left.shape[1]),
        out_shape=jax.ShapeDtypeStruct(shape, BF16),
        in_specs=[vmem] * 4,
        out_specs=vmem,
        scratch_shapes=pair_scratch(shape),
        compiler_params=pltpu.CompilerParams(collective_id=7, has_side_effects=True, vmem_limit_bytes=40 * 2**20),
        cost_estimate=pl.CostEstimate(
            flops=2 * left.shape[0] * left.shape[1] * shape[2], bytes_accessed=30 * 2**20, transcendentals=0
        ),
        name="mix_grads",
    )(left, right, *grads)
    return out.reshape(shape[0] * shape[1], shape[2])


BLOCK_TIME = 2.8


def ffn_grads_kernel(
    count, features, left_ref, right_ref, d_gate_ref, d_up_ref, hidden_ref, partial_ref, resid_ref,
    out_ref, result_ref, *scratch,
):
    pair = Pair(features, (0, 0, 1), left_ref, right_ref, (d_gate_ref, d_up_ref, hidden_ref), out_ref, scratch[:4])
    line = Line(count, resid_ref.shape[0], scratch[4:], [BLOCK_TIME] * (2 * pair.blocks), True, False)

    def finish(part, local, place):
        result_ref[local, :] = (resid_ref[local, :] + line.total_ref[...]).astype(BF16)

    line.partial_ref, line.finish = partial_ref, finish
    line.greet([pair.partner])

    @pl.loop(0, pair.blocks)
    def _(block):
        line.run_at(0, block, pair.blocks)
        pair.theirs(block)

    @pl.loop(0, pair.blocks)
    def _(block):
        line.run_at(pair.blocks, block, pair.blocks)
        pair.ours(block)

    line.run(2 * pair.blocks)
    line.drain()
    pair.drain()


def ffn_grads(left, right, grads, ffn_partial, resid):
    count = lax.axis_size("tensor")
    shape = pair_shape(left, grads)
    vmem = pl.BlockSpec(memory_space=pltpu.VMEM)
    sums, result = pl.pallas_call(
        functools.partial(ffn_grads_kernel, count, left.shape[1]),
        out_shape=(jax.ShapeDtypeStruct(shape, BF16), jax.ShapeDtypeStruct(resid.shape, BF16)),
        in_specs=[vmem] * 7,
        out_specs=[vmem] * 2,
        scratch_shapes=pair_scratch(shape) + line_scratch(count, resid.shape[0], resid.shape[1], True, False),
        compiler_params=pltpu.CompilerParams(collective_id=6, has_side_effects=True, vmem_limit_bytes=58 * 2**20),
        cost_estimate=pl.CostEstimate(
            flops=2 * left.shape[0] * left.shape[1] * shape[2], bytes_accessed=50 * 2**20, transcendentals=0
        ),
        name="ffn_grads",
    )(left, right, *grads, ffn_partial, resid)
    return sums.reshape(shape[0] * shape[1], shape[2]), result


def group_scatter(sums):
    shard = lax.psum_scatter(sums, ("pair", "fsdp"), scatter_dimension=0, tiled=True)
    return with_layout_constraint(shard, Layout(major_to_minor=(0, 1))).astype(F32)


def shifted(count, shift):
    return [(index, (index + shift) % count) for index in range(count)]


def gather_rows(rows):
    count = lax.axis_size("tensor")
    mine = lax.axis_index("tensor")
    height = rows.shape[0]
    whole = jnp.zeros((count * height, rows.shape[1]), rows.dtype)
    whole = lax.dynamic_update_slice_in_dim(whole, rows, mine * height, 0)
    for shift in range(1, count):
        came = lax.ppermute(rows, "tensor", shifted(count, shift))
        source = lax.rem(mine + count - shift, count)
        whole = lax.dynamic_update_slice_in_dim(whole, came, source * height, 0)
    return whole


def send_rows(rows):
    count = lax.axis_size("tensor")
    return [lax.ppermute(rows, "tensor", shifted(count, shift)) for shift in range(1, count)]


def place_rows(rows, came):
    count = lax.axis_size("tensor")
    mine = lax.axis_index("tensor")
    height = rows.shape[0]
    whole = jnp.zeros((count * height, rows.shape[1]), rows.dtype)
    whole = lax.dynamic_update_slice_in_dim(whole, rows, mine * height, 0)
    for shift in range(1, count):
        source = lax.rem(mine + count - shift, count)
        whole = lax.dynamic_update_slice_in_dim(whole, came[shift - 1], source * height, 0)
    return whole


def gather_weights(pieces, axis):
    return lax.all_gather(jnp.concatenate(pieces, axis=1), ("fsdp", "pair", "core"), axis=axis, tiled=True)


def scatter_grads(grads, axis=0):
    return lax.psum_scatter(grads, ("pair", "core", "fsdp"), scatter_dimension=axis, tiled=True).astype(F32)


def body(
    layer_input,
    first_gain,
    w_query,
    w_key,
    w_value,
    w_gating,
    w_beta,
    conv_query,
    conv_key,
    conv_value,
    head_gain,
    w_project,
    second_gain,
    w_gate,
    w_up,
    w_down,
    doc_starts,
    seq_lengths,
    output_grad,
):
    replicas, replica = extents()[0], coordinates()[0]
    width = w_query.shape[1]
    units = w_gate.shape[1]
    heads = w_beta.shape[1]
    head_width = head_gain.shape[0]

    def piece(weight, axis):
        size = weight.shape[axis] // replicas
        return lax.dynamic_slice_in_dim(weight, replica * size, size, axis)

    input_float = layer_input.astype(F32)
    conv_q = conv_query.astype(F32)
    conv_k = conv_key.astype(F32)
    conv_v = conv_value.astype(F32)
    gain_head = head_gain.astype(F32)[None, :]
    rows_one, mix_full, project_full, gains = enter(
        layer_input, first_gain, second_gain, w_beta, (w_gating, w_query, w_key, w_value), w_project
    )
    gain_one, gain_two = gains[:1], gains[1:]
    late, rows_one = lax.optimization_barrier(((w_gate, w_up, w_down), rows_one))
    gate_up = gather_weights([piece(late[0], 0), piece(late[1], 0)], 0)
    down = gather_weights([piece(late[2], 1)], 1)
    late_grad, rows_one = lax.optimization_barrier((output_grad, rows_one))
    came = send_rows(late_grad)
    raw = dot(rows_one, mix_full)
    gated, mixed, solve, update, state = delta_forward(
        doc_starts, seq_lengths, raw, conv_q, conv_k, conv_v, gain_head
    )
    gated, came = lax.optimization_barrier((gated, came))
    grad_rows = place_rows(output_grad, came)
    attn_partial = dot(gated, project_full).astype(BF16)
    whole_rows = jax.ShapeDtypeStruct(rows_one.shape, BF16)
    own_rows = jax.ShapeDtypeStruct(layer_input.shape, F32)
    gain_sums = jax.ShapeDtypeStruct((1, layer_input.shape[1]), F32)
    rows_two, resid = line_call(
        middle_kernel, "middle", 2, True, (whole_rows, own_rows), (attn_partial, layer_input, gain_two)
    )
    d_hidden = dot_nt(grad_rows, down)
    both = dot(rows_two, gate_up)
    gate_val, up_val = both[:, :units], both[:, units:]
    gate_sig = jax.nn.sigmoid(gate_val)
    silu_gate = gate_val * gate_sig
    hidden = (silu_gate * up_val).astype(BF16)
    d_gate = (d_hidden * up_val * gate_sig * (1.0 + gate_val * (1.0 - gate_sig))).astype(BF16)
    d_up = (d_hidden * silu_gate).astype(BF16)
    d_both = jnp.concatenate([d_gate, d_up], axis=1)
    ffn_partial = dot(hidden, down).astype(BF16)
    ffn_sums, result = ffn_grads(rows_two, grad_rows, (d_gate, d_up, hidden), ffn_partial, resid)
    ffn_shard = group_scatter(ffn_sums)
    d_partial, _ = lax.optimization_barrier((dot_nt(d_both, gate_up).astype(BF16), ffn_sums))
    d_attn, d_resid, grad_second = line_call(
        turn_kernel, "turn", 3, True, (whole_rows, own_rows, gain_sums), (d_partial, resid, output_grad, gain_two)
    )
    d_gated = dot_nt(d_attn, project_full)
    d_raw, d_conv, d_head = delta_backward(
        doc_starts, seq_lengths, raw, conv_q, conv_k, conv_v, gain_head, mixed, solve, update, state, d_gated
    )
    mix_sums, ffn_shard = lax.optimization_barrier(
        (mix_grads(rows_one, d_attn, (d_raw, gated)), ffn_shard)
    )
    mix_shard = group_scatter(mix_sums)
    project_shard = mix_shard[:, 4 * width + head_width :]
    mix_partial = dot_nt(d_raw, mix_full).astype(BF16)
    input_grad, grad_first = line_call(
        last_kernel, "last", 4, False, (own_rows, gain_sums),
        (mix_partial, layer_input, d_resid, gain_one),
    )
    gain_total, head_total, conv_totals = reduce_small(
        jnp.concatenate([grad_first, grad_second], axis=0), d_head, d_conv
    )
    return (
        result,
        input_grad,
        gain_total[0],
        mix_shard[:, width : 2 * width],
        mix_shard[:, 2 * width : 3 * width],
        mix_shard[:, 3 * width : 4 * width],
        mix_shard[:, :width],
        mix_shard[:, 4 * width : 4 * width + heads],
        conv_totals[:, :width],
        conv_totals[:, width : 2 * width],
        conv_totals[:, 2 * width :],
        head_total[0],
        project_shard.T,
        gain_total[1],
        ffn_shard[:, :units],
        ffn_shard[:, units : 2 * units],
        ffn_shard[:, 2 * units :].T,
    )


def solution(mesh):
    replicas, shards, count = (mesh.shape[name] for name in ("dp", "fsdp", "tensor"))
    mesh = jax.sharding.Mesh(
        mesh.devices.reshape(replicas // 2, 2, shards, count), ("pair", "core", "fsdp", "tensor")
    )
    placed = (
        P(("pair", "core", "fsdp", "tensor"), None),
        P("fsdp"),
        P("fsdp", "tensor"),
        P("fsdp", "tensor"),
        P("fsdp", "tensor"),
        P("fsdp", "tensor"),
        P("fsdp", "tensor"),
        P(None, "tensor"),
        P(None, "tensor"),
        P(None, "tensor"),
        P(),
        P("tensor", "fsdp"),
        P("fsdp"),
        P("fsdp", "tensor"),
        P("fsdp", "tensor"),
        P("tensor", "fsdp"),
        P(("pair", "core", "fsdp"), None),
        P(("pair", "core", "fsdp")),
        P(("pair", "core", "fsdp", "tensor"), None),
    )
    return jax.shard_map(
        body,
        mesh=mesh,
        in_specs=placed,
        out_specs=(
            P(("pair", "core", "fsdp", "tensor"), None),
            P(("pair", "core", "fsdp", "tensor"), None),
            P(("pair", "core", "fsdp")),
            P(("pair", "core", "fsdp"), "tensor"),
            P(("pair", "core", "fsdp"), "tensor"),
            P(("pair", "core", "fsdp"), "tensor"),
            P(("pair", "core", "fsdp"), "tensor"),
            P(("pair", "core", "fsdp"), "tensor"),
            P(None, "tensor"),
            P(None, "tensor"),
            P(None, "tensor"),
            P(),
            P("tensor", ("pair", "core", "fsdp")),
            P(("pair", "core", "fsdp")),
            P(("pair", "core", "fsdp"), "tensor"),
            P(("pair", "core", "fsdp"), "tensor"),
            P("tensor", ("pair", "core", "fsdp")),
        ),
        check_vma=False,
    )
```

```python
import functools
import jax, jax.numpy as jnp
from jax import lax
from jax.experimental import pallas as pl
from jax.experimental.pallas import tpu as pltpu
from jax.experimental.layout import Layout, with_layout_constraint
from jax.sharding import PartitionSpec as P

KERNEL = 4
CHUNK = 256
G, Q, K, V = range(4)
MESH = pl.DeviceIdType.MESH
F32 = jnp.float32
BF16 = jnp.bfloat16


def coordinates():
    replica = lax.axis_index("pair") * 2 + lax.axis_index("core")
    return replica, lax.axis_index("fsdp"), lax.axis_index("tensor")


def extents():
    return lax.axis_size("pair") * 2, lax.axis_size("fsdp"), lax.axis_size("tensor")


def device(replica, shard, place):
    return (lax.div(replica, 2), lax.rem(replica, 2), shard, place)


def dot(left, right):
    return jnp.dot(left, right, preferred_element_type=F32)


def dot_nt(left, right):
    return lax.dot_general(left, right, (((1,), (1,)), ((), ())), preferred_element_type=F32)


def dot_tn(left, right):
    return lax.dot_general(left, right, (((0,), (0,)), ((), ())), preferred_element_type=F32)


def lane_sum(values):
    return jnp.sum(values, axis=-1, keepdims=True)


def document_of(starts_ref, positions):
    total = jnp.zeros_like(positions)
    for entry in range(starts_ref.shape[1]):
        total = total + (positions >= starts_ref[0, entry]).astype(jnp.int32)
    return total


def fill_masks(starts_ref, length_ref, keep_ref, live_ref, carry_ref):
    rows, lanes = live_ref.shape
    place = lax.broadcasted_iota(jnp.int32, (rows, lanes), 0)
    docs = document_of(starts_ref, place)
    for delay in range(1, KERNEL):
        prior = document_of(starts_ref, place - delay)
        keep_ref[delay - 1] = jnp.where((prior == docs) & (place >= delay), 1.0, 0.0)
    live_ref[...] = jnp.where(place < length_ref[0], 1.0, 0.0)
    for edge in range(rows // CHUNK - 1):
        seam = jnp.int32((edge + 1) * CHUNK - 1)
        carry_ref[edge] = jnp.where(docs == document_of(starts_ref, seam), 1.0, 0.0)


def pair_mask(starts_ref, chunk):
    row = lax.broadcasted_iota(jnp.int32, (CHUNK, CHUNK), 0)
    col = lax.broadcasted_iota(jnp.int32, (CHUNK, CHUNK), 1)
    first = chunk * CHUNK
    same = document_of(starts_ref, row + first) == document_of(starts_ref, col + first)
    return same & (row > col), same & (row >= col)


def convolve(raw, taps, keep_ref):
    parts = [raw]
    for delay in range(1, KERNEL):
        parts.append(pltpu.roll(raw, delay, 0) * keep_ref[delay - 1])
    total = parts[0] * taps[KERNEL - 1 : KERNEL]
    for delay in range(1, KERNEL):
        total = total + parts[delay] * taps[KERNEL - 1 - delay : KERNEL - delay]
    return total, parts


def sigmoid(values):
    return 0.5 * jnp.tanh(0.5 * values) + 0.5


def column(values, index):
    lane = lax.broadcasted_iota(jnp.int32, values.shape, 1)
    return lane_sum(jnp.where(lane == index, values, 0.0))


def invert(system):
    size = system[0].shape[0]
    row = lax.broadcasted_iota(jnp.int32, (size, size), 0)
    col = lax.broadcasted_iota(jnp.int32, (size, size), 1)
    apart = row ^ col
    eye = jnp.where(row == col, 1.0, 0.0)
    low = [matrix.astype(BF16) for matrix in system]
    solved = [eye - jnp.where(apart == 1, matrix, 0.0) for matrix in system]
    step = 2
    while step < size:
        level = (apart >= step) & (apart < 2 * step)
        for index, matrix in enumerate(low):
            part = jnp.where(level, matrix, 0.0)
            held = solved[index].astype(BF16)
            solved[index] = solved[index] - dot(dot(held, part).astype(BF16), held)
        step *= 2
    refined = []
    for matrix, high, inverse in zip(system, low, solved):
        rest = (matrix - high.astype(F32)).astype(BF16)
        head = inverse.astype(BF16)
        tail = (inverse - head.astype(F32)).astype(BF16)
        product = dot(high, head) + dot(rest, head) + dot(high, tail)
        residue = eye - inverse - product
        refined.append(inverse + dot(head, residue.astype(BF16)))
    return refined


def unit_rows(conv):
    gate = sigmoid(conv)
    act = conv * gate
    scale = lax.rsqrt(lane_sum(act * act) + 1e-06)
    return gate, act, scale


TILE = 256
PROJECT_TILE = 512
ATTEND_TIMES = (1.2, 1.5, 0.9)


def forward_kernel(
    count, starts_ref, length_ref, rows_ref, mix_ref, project_ref, own_grad_ref, conv_q_ref, conv_k_ref, conv_v_ref, gain_ref,
    raw_ref, gated_ref, mixed_ref, solve_ref, update_ref, state_ref, partial_ref, grad_rows_ref,
    keep_ref, live_ref, carry_ref, strict_ref, incl_ref, *sems,
):
    rows, head_width = live_ref.shape
    width = gated_ref.shape[1]
    chunks = rows // CHUNK
    heads = width // head_width
    tiles, ends = 4 * width // TILE, project_ref.shape[1] // PROJECT_TILE
    shared = [ATTEND_TIMES[0]] * tiles + [ATTEND_TIMES[1]] * (3 * heads) + [ATTEND_TIMES[2]] * ends
    line = Line(count, rows // count, sems, shared, False, True, ATTEND_PARTS, ATTEND_LATENCY)
    line.rows_ref, line.source_ref = grad_rows_ref, own_grad_ref
    line.greet()
    own = pl.ds(pl.multiple_of(line.place * line.rows, line.rows), line.rows)
    grad_rows_ref[own, :] = own_grad_ref[...]

    @pl.loop(0, tiles)
    def _(tile):
        line.run_at(0, tile, tiles)
        cols = pl.ds(pl.multiple_of(tile * TILE, TILE), TILE)
        raw_ref[:, cols] = dot(rows_ref[...], mix_ref[:, cols])

    raw_ref[:, 4 * width :] = dot(rows_ref[...], mix_ref[:, 4 * width :])
    fill_masks(starts_ref, length_ref, keep_ref, live_ref, carry_ref)
    for chunk in range(chunks):
        strict, incl = pair_mask(starts_ref, chunk)
        strict_ref[chunk] = jnp.where(strict, 1.0, 0.0)
        incl_ref[chunk] = jnp.where(incl, 1.0, 0.0)

    @pl.loop(0, heads)
    def _(head):
        line.run_at(tiles, head, heads, 3)
        start = pl.multiple_of(head * head_width, head_width)

        def stream(index):
            return raw_ref[:, pl.ds(pl.multiple_of(index * width + start, head_width), head_width)]

        cols = pl.ds(start, head_width)
        conv, _ = convolve(stream(Q), conv_q_ref[:, cols], keep_ref)
        _, act, scale = unit_rows(conv)
        query = (act * scale).astype(BF16)
        conv, _ = convolve(stream(K), conv_k_ref[:, cols], keep_ref)
        _, act, scale = unit_rows(conv)
        keyed = act * scale
        key_low = keyed.astype(BF16)
        conv, _ = convolve(stream(V), conv_v_ref[:, cols], keep_ref)
        valued = conv * sigmoid(conv)
        rate = sigmoid(column(raw_ref[:, 4 * width :], head)) * live_ref[...]
        scaled_value = (valued * rate).astype(BF16)
        scaled_key = keyed * rate
        system = []
        for chunk in range(chunks):
            span = slice(chunk * CHUNK, (chunk + 1) * CHUNK)
            pair = dot_nt(key_low[span], key_low[span])
            wide = jnp.concatenate([rate[span]] * (CHUNK // head_width), axis=1)
            system.append(pair * wide * strict_ref[chunk])
        line.run_at(tiles + 1, head, heads, 3)
        memory = None
        inverses = invert(system)
        line.run_at(tiles + 2, head, heads, 3)
        for chunk, solved in enumerate(inverses):
            span = slice(chunk * CHUNK, (chunk + 1) * CHUNK)
            solve_low = solved.astype(BF16)
            solve_ref[head * chunks + chunk] = solve_low
            score = dot_nt(query[span], key_low[span]) * incl_ref[chunk]
            if chunk == 0:
                update = dot(solve_low, scaled_value[span])
                update_low = update.astype(BF16)
                mixed = dot(score.astype(BF16), update_low)
            else:
                carry = carry_ref[chunk - 1][span]
                right = jnp.concatenate(
                    [scaled_value[span], (scaled_key[span] * carry).astype(BF16)], axis=1
                )
                both = dot(solve_low, right)
                memory_low = memory.astype(BF16)
                state_ref[head * (chunks - 1) + chunk - 1] = memory_low
                update = both[:, :head_width] - dot(both[:, head_width:].astype(BF16), memory_low)
                update_low = update.astype(BF16)
                mixed = carry * dot(query[span], memory_low) + dot(score.astype(BF16), update_low)
            update_ref[span, cols] = update_low
            mixed_ref[span, cols] = mixed
            if chunk + 1 < chunks:
                last = (keyed[span] * carry_ref[chunk][span]).astype(BF16)
                fresh = dot_tn(last, update_low)
                if memory is None:
                    memory = fresh
                else:
                    memory = memory * carry_ref[chunk - 1][span][CHUNK - 1 :] + fresh
        mixed = mixed_ref[:, cols]
        norm = lax.rsqrt(lane_sum(mixed * mixed) * (1.0 / head_width) + 1e-05)
        gating = stream(G)
        gated = mixed * norm * gain_ref[...] * (gating * sigmoid(gating)) * live_ref[...]
        gated_ref[:, cols] = gated.astype(BF16)

    @pl.loop(0, ends)
    def _(tile):
        line.run_at(tiles + 3 * heads, tile, ends)
        cols = pl.ds(pl.multiple_of(tile * PROJECT_TILE, PROJECT_TILE), PROJECT_TILE)
        partial_ref[:, cols] = dot(gated_ref[...], project_ref[:, cols]).astype(BF16)

    line.run(tiles + 3 * heads + ends)
    line.drain()


def attend(starts, length, rows_one, mix_full, project_full, own_grad, conv_q, conv_k, conv_v, gain):
    rows, features = rows_one.shape
    head_width = gain.shape[-1]
    width = conv_q.shape[1]
    heads, chunks = width // head_width, rows // CHUNK
    count = lax.axis_size("tensor")
    vmem = pl.BlockSpec(memory_space=pltpu.VMEM)
    smem = pl.BlockSpec(memory_space=pltpu.SMEM)
    return pl.pallas_call(
        functools.partial(forward_kernel, count),
        out_shape=(
            jax.ShapeDtypeStruct((rows, mix_full.shape[1]), F32),
            jax.ShapeDtypeStruct((rows, width), BF16),
            jax.ShapeDtypeStruct((rows, width), F32),
            jax.ShapeDtypeStruct((heads * chunks, CHUNK, CHUNK), BF16),
            jax.ShapeDtypeStruct((rows, width), BF16),
            jax.ShapeDtypeStruct((heads * (chunks - 1), head_width, head_width), BF16),
            jax.ShapeDtypeStruct((rows, features), BF16),
            jax.ShapeDtypeStruct((rows, features), BF16),
        ),
        in_specs=[smem, smem] + [vmem] * 8,
        out_specs=[vmem] * 8,
        scratch_shapes=[
            pltpu.VMEM((KERNEL - 1, rows, head_width), F32),
            pltpu.VMEM((rows, head_width), F32),
            pltpu.VMEM((chunks - 1, rows, head_width), F32),
            pltpu.VMEM((chunks, CHUNK, CHUNK), F32),
            pltpu.VMEM((chunks, CHUNK, CHUNK), F32),
        ]
        + line_scratch(count, rows // count, features, False, True, ATTEND_PARTS),
        compiler_params=pltpu.CompilerParams(collective_id=8, has_side_effects=True, vmem_limit_bytes=48 * 2**20),
        cost_estimate=pl.CostEstimate(
            flops=2 * 24 * heads * chunks * CHUNK**3, bytes_accessed=40 * 2**20, transcendentals=0
        ),
        name="attend",
    )(starts, length, rows_one, mix_full, project_full, own_grad, conv_q, conv_k, conv_v, gain)


def backward_kernel(
    starts_ref, length_ref, raw_ref, conv_q_ref, conv_k_ref, conv_v_ref, gain_ref,
    mixed_ref, solve_ref, update_ref, state_ref, grad_ref,
    d_raw_ref, d_conv_ref, d_gain_ref,
    keep_ref, live_ref, carry_ref, strict_ref, incl_ref, d_query_ref, d_key_ref, d_value_ref, d_rate_ref,
):
    rows, head_width = live_ref.shape
    width = mixed_ref.shape[1]
    chunks = rows // CHUNK
    fill_masks(starts_ref, length_ref, keep_ref, live_ref, carry_ref)
    for chunk in range(chunks):
        strict, incl = pair_mask(starts_ref, chunk)
        strict_ref[chunk] = jnp.where(strict, 1.0, 0.0)
        incl_ref[chunk] = jnp.where(incl, 1.0, 0.0)
    d_gain_ref[...] = jnp.zeros_like(d_gain_ref)
    d_raw_ref[:, 4 * width :] = jnp.zeros((rows, head_width), BF16)

    @pl.loop(0, width // head_width)
    def _(head):
        start = pl.multiple_of(head * head_width, head_width)

        def place(index):
            return pl.ds(pl.multiple_of(index * width + start, head_width), head_width)

        cols = pl.ds(start, head_width)
        live = live_ref[...]
        mixed = mixed_ref[:, cols]
        norm = lax.rsqrt(lane_sum(mixed * mixed) * (1.0 / head_width) + 1e-05)
        gating = raw_ref[:, place(G)]
        gate = sigmoid(gating)
        normal = mixed * norm
        grad = grad_ref[:, cols].astype(F32) * live
        grad_gain = grad * gain_ref[...]
        swish = gating * gate
        d_raw_ref[:, place(G)] = (grad_gain * normal * gate * (1.0 + gating - swish)).astype(BF16)
        d_gain_ref[...] += jnp.sum(grad * normal * swish, axis=0, keepdims=True)
        d_normal = grad_gain * swish
        d_mixed = norm * (d_normal - normal * (lane_sum(d_normal * normal) * (1.0 / head_width)))
        d_mixed_low = d_mixed.astype(BF16)

        conv_q, parts_q = convolve(raw_ref[:, place(Q)], conv_q_ref[:, cols], keep_ref)
        gate_q, act_q, scale_q = unit_rows(conv_q)
        unit_q = act_q * scale_q
        query = unit_q.astype(BF16)
        conv_k, parts_k = convolve(raw_ref[:, place(K)], conv_k_ref[:, cols], keep_ref)
        gate_k, act_k, scale_k = unit_rows(conv_k)
        keyed = act_k * scale_k
        key_low = keyed.astype(BF16)
        conv_v, parts_v = convolve(raw_ref[:, place(V)], conv_v_ref[:, cols], keep_ref)
        gate_v = sigmoid(conv_v)
        valued = conv_v * gate_v
        sig = sigmoid(column(raw_ref[:, 4 * width :], head))
        rate = sig * live
        scaled_value = (valued * rate).astype(BF16)
        scaled_key = keyed * rate

        d_memory = None
        for chunk in range(chunks - 1, -1, -1):
            span = slice(chunk * CHUNK, (chunk + 1) * CHUNK)
            key_c, query_c, d_mixed_c = key_low[span], query[span], d_mixed_low[span]
            solve = solve_ref[head * chunks + chunk]
            update = update_ref[span, cols]
            incl, strict = incl_ref[chunk], strict_ref[chunk]
            score = (dot_nt(query_c, key_c) * incl).astype(BF16)
            d_update = dot_tn(score, d_mixed_c)
            d_key = None
            if d_memory is not None:
                last = carry_ref[chunk][span]
                d_memory_low = d_memory.astype(BF16)
                d_update = d_update + dot((keyed[span] * last).astype(BF16), d_memory_low)
                d_key = last * dot_nt(update, d_memory_low)
            d_update_low = d_update.astype(BF16)
            d_score = (dot_nt(d_mixed_c, update) * incl).astype(BF16)
            d_query = dot(d_score, key_c)
            d_key_score = dot_tn(d_score, query_c)
            d_key = d_key_score if d_key is None else d_key + d_key_score
            if chunk == 0:
                right = scaled_value[span]
                solved = dot(solve, right)
                d_right = dot_tn(solve, d_update_low)
                d_value_in = d_right
                d_rate = lane_sum(d_value_in * valued[span])
            else:
                carry = carry_ref[chunk - 1][span]
                state = state_ref[head * (chunks - 1) + chunk - 1]
                right = jnp.concatenate([scaled_value[span], (scaled_key[span] * carry).astype(BF16)], axis=1)
                solved = dot(solve, right)
                d_solved_key = -dot_nt(d_update_low, state)
                d_right = dot_tn(solve, jnp.concatenate([d_update_low, d_solved_key.astype(BF16)], axis=1))
                d_value_in = d_right[:, :head_width]
                d_key_in = d_right[:, head_width:] * carry
                carried = (carry * d_mixed[span]).astype(BF16)
                d_query = d_query + dot_nt(carried, state)
                d_key = d_key + rate[span] * d_key_in
                d_rate = lane_sum(d_value_in * valued[span] + d_key_in * keyed[span])
                fresh = dot_tn(query_c, carried) - dot_tn(solved[:, head_width:].astype(BF16), d_update_low)
                if d_memory is None:
                    d_memory = fresh
                else:
                    d_memory = d_memory * carry[CHUNK - 1 :] + fresh
            d_system = dot_nt(d_right.astype(BF16), solved.astype(BF16)) * -strict
            pair = dot_nt(key_c, key_c)
            d_rate = d_rate + lane_sum(d_system * pair)
            wide = jnp.concatenate([rate[span]] * (CHUNK // head_width), axis=1)
            d_pair = (d_system * wide).astype(BF16)
            d_key = d_key + dot(d_pair, key_c) + dot_tn(d_pair, key_c)
            d_query_ref[span] = d_query
            d_key_ref[span] = d_key
            d_value_ref[span] = rate[span] * d_value_in
            d_rate_ref[span] = jnp.broadcast_to(d_rate, (CHUNK, head_width))

        lane = lax.broadcasted_iota(jnp.int32, (rows, head_width), 1)
        d_beta = d_rate_ref[...] * rate * (1.0 - sig)
        tail = d_raw_ref[:, 4 * width :]
        d_raw_ref[:, 4 * width :] = jnp.where(lane == head, d_beta.astype(BF16), tail)

        def conv_back(index, d_conv, parts, taps):
            sums = [jnp.sum(d_conv * part, axis=0, keepdims=True) for part in parts]
            for delay in range(KERNEL):
                tap = KERNEL - 1 - delay
                d_conv_ref[tap : tap + 1, place(index - 1)] = sums[delay]
            total = d_conv * taps[KERNEL - 1 : KERNEL]
            for delay in range(1, KERNEL):
                tap = KERNEL - 1 - delay
                back = pltpu.roll(d_conv * keep_ref[delay - 1], rows - delay, 0)
                total = total + back * taps[tap : tap + 1]
            d_raw_ref[:, place(index)] = total.astype(BF16)

        def unit_back(d_unit, unit, scale, conv, act, gate):
            d_act = scale * (d_unit - unit * lane_sum(d_unit * unit))
            return d_act * gate * (1.0 + conv - act)

        conv_back(Q, unit_back(d_query_ref[...], unit_q, scale_q, conv_q, act_q, gate_q), parts_q, conv_q_ref[:, cols])
        conv_back(K, unit_back(d_key_ref[...], keyed, scale_k, conv_k, act_k, gate_k), parts_k, conv_k_ref[:, cols])
        d_conv_v = d_value_ref[...] * gate_v * (1.0 + conv_v - valued)
        conv_back(V, d_conv_v, parts_v, conv_v_ref[:, cols])


def delta_backward(starts, length, raw, conv_q, conv_k, conv_v, gain, mixed, solve, update, state, grad):
    rows = raw.shape[0]
    head_width = gain.shape[-1]
    width = conv_q.shape[1]
    heads, chunks = width // head_width, rows // CHUNK
    vmem = pl.BlockSpec(memory_space=pltpu.VMEM)
    smem = pl.BlockSpec(memory_space=pltpu.SMEM)
    return pl.pallas_call(
        backward_kernel,
        out_shape=(
            jax.ShapeDtypeStruct((rows, 4 * width + head_width), BF16),
            jax.ShapeDtypeStruct((KERNEL, 3 * width), F32),
            jax.ShapeDtypeStruct((1, head_width), F32),
        ),
        in_specs=[smem, smem] + [vmem] * 10,
        out_specs=[vmem] * 3,
        scratch_shapes=[
            pltpu.VMEM((KERNEL - 1, rows, head_width), F32),
            pltpu.VMEM((rows, head_width), F32),
            pltpu.VMEM((chunks - 1, rows, head_width), F32),
            pltpu.VMEM((chunks, CHUNK, CHUNK), F32),
            pltpu.VMEM((chunks, CHUNK, CHUNK), F32),
        ]
        + [pltpu.VMEM((rows, head_width), F32)] * 4,
        compiler_params=pltpu.CompilerParams(vmem_limit_bytes=48 * 1024 * 1024),
        cost_estimate=pl.CostEstimate(
            flops=2 * 12 * heads * chunks * CHUNK**3, bytes_accessed=16 * 2**20, transcendentals=0
        ),
        name="delta_backward",
    )(starts, length, raw, conv_q, conv_k, conv_v, gain, mixed, solve, update, state, grad)


def reduce_kernel(
    group_size, line_size, fsdp_size, gain_ref, head_ref, conv_ref, gain_out, head_out, conv_out,
    line_gain, line_head, stage, group_gain, group_conv,
    line_send, line_recv, group_send, group_recv,
):
    dp, fsdp, tensor = coordinates()
    group = dp * fsdp_size + fsdp
    size = gain_out.shape[1]

    def line_peer(shift):
        return device(dp, fsdp, lax.rem(tensor + shift, line_size))

    def group_peer(shift):
        peer = lax.rem(group + shift, group_size)
        return peer, device(lax.div(peer, fsdp_size), lax.rem(peer, fsdp_size), tensor)

    barrier = pltpu.get_barrier_semaphore()
    for shift in range(1, line_size):
        pl.semaphore_signal(barrier, inc=1, device_id=line_peer(shift), device_id_type=MESH)
    for shift in range(1, group_size):
        pl.semaphore_signal(barrier, inc=1, device_id=group_peer(shift)[1], device_id_type=MESH)
    pl.semaphore_wait(barrier, line_size + group_size - 2)

    copies = []
    for shift in range(1, line_size):
        for part, (source, target) in enumerate(((gain_ref, line_gain), (head_ref, line_head))):
            copy = pltpu.make_async_remote_copy(
                src_ref=source, dst_ref=target.at[shift - 1],
                send_sem=line_send.at[shift - 1, part], recv_sem=line_recv.at[shift - 1, part],
                device_id=line_peer(shift), device_id_type=MESH,
            )
            copy.start()
            copies.append(copy)
    conv_copies = []
    for shift in range(1, group_size):
        copy = pltpu.make_async_remote_copy(
            src_ref=conv_ref, dst_ref=group_conv.at[shift - 1],
            send_sem=group_send.at[shift - 1, 1], recv_sem=group_recv.at[shift - 1, 1],
            device_id=group_peer(shift)[1], device_id_type=MESH,
        )
        copy.start()
        conv_copies.append(copy)
    for copy in copies:
        copy.wait()
    gain = gain_ref[...]
    head = head_ref[...]
    for shift in range(1, line_size):
        gain = gain + line_gain[shift - 1]
        head = head + line_head[shift - 1]
    for peer in range(group_size):
        stage[peer] = jnp.zeros(stage.shape[1:], F32)
        stage[peer, :2, :size] = gain[:, peer * size : (peer + 1) * size]
        stage[peer, 2:3, : head.shape[1]] = head
    for copy in conv_copies:
        copy.wait()
    conv = conv_ref[...]
    for shift in range(1, group_size):
        conv = conv + group_conv[shift - 1]
    conv_out[...] = conv
    copies = []
    for shift in range(1, group_size):
        peer, where = group_peer(shift)
        copy = pltpu.make_async_remote_copy(
            src_ref=stage.at[peer], dst_ref=group_gain.at[shift - 1],
            send_sem=group_send.at[shift - 1, 0], recv_sem=group_recv.at[shift - 1, 0],
            device_id=where, device_id_type=MESH,
        )
        copy.start()
        copies.append(copy)
    for copy in copies:
        copy.wait()
    total = stage[group]
    for shift in range(1, group_size):
        total = total + group_gain[shift - 1]
    gain_out[...] = total[:2, :size]
    head_out[...] = total[2:3, : head.shape[1]]


def reduce_small(gain, head, conv):
    replicas, fsdp_size, line_size = extents()
    group_size = replicas * fsdp_size
    size = gain.shape[1] // group_size
    pad = max(size, head.shape[1])
    vmem = pl.BlockSpec(memory_space=pltpu.VMEM)
    dma = pltpu.SemaphoreType.DMA
    return pl.pallas_call(
        functools.partial(reduce_kernel, group_size, line_size, fsdp_size),
        out_shape=(
            jax.ShapeDtypeStruct((2, size), F32),
            jax.ShapeDtypeStruct(head.shape, F32),
            jax.ShapeDtypeStruct(conv.shape, F32),
        ),
        in_specs=[vmem] * 3,
        out_specs=[vmem] * 3,
        scratch_shapes=[
            pltpu.VMEM((line_size - 1,) + gain.shape, F32),
            pltpu.VMEM((line_size - 1,) + head.shape, F32),
            pltpu.VMEM((group_size, 8, pad), F32),
            pltpu.VMEM((group_size - 1, 8, pad), F32),
            pltpu.VMEM((group_size - 1,) + conv.shape, F32),
            dma((line_size - 1, 2)),
            dma((line_size - 1, 2)),
            dma((group_size - 1, 2)),
            dma((group_size - 1, 2)),
        ],
        compiler_params=pltpu.CompilerParams(collective_id=1, has_side_effects=True, vmem_limit_bytes=16 * 2**20),
        name="reduce_small",
    )(gain, head, conv)


def plan(count, parts, sums, rows, shared, unit, latency=1.5):
    backlog, add, end = 1.5, 0.15 + 0.8 / parts, 0.5 + 3.0 / parts
    rank = {"spread": 0, "relay": 0, "finish": 1, "forward": 2, "inject": 3}
    clock = [0.0] * count
    free, come = {}, [{} for _ in range(count)]
    todo = [set() for _ in range(count)]
    done = [0] * count
    at = [0] * count
    tasks = [[[] for _ in range(len(shared) + 1)] for _ in range(count)]
    own_finish = sums and not any(isinstance(step, tuple) for step in shared)
    for place in range(count):
        for part in range(parts):
            for step in (1, -1):
                behind = 0 <= place - step < count
                for slot in range(count - 1) if sums else ():
                    owner = count - 1 - slot if step > 0 else slot
                    if (owner - place) * step > 0:
                        todo[place].add(("forward" if behind else "inject", step, slot, part))
                for distance in range(1, count) if rows else ():
                    if 0 <= place - step * distance < count:
                        todo[place].add(("relay", step, distance, part))
            if rows and not sums:
                todo[place].add(("spread", 0, 0, part))
            if own_finish:
                todo[place].add(("finish", 0, 0, part))

    def ready(place, task):
        kind, step, slot, part = task
        if kind == "inject":
            return max(0.0, free.get((place, step), 0.0) - backlog * unit)
        if kind == "spread":
            return max([0.0] + [free.get((place, way), 0.0) - backlog * unit for way in (1, -1)])
        if kind == "forward":
            return come[place].get(("sum", step, slot, part))
        if kind == "relay":
            return come[place].get(("row", step, slot, part))
        if part != done[place]:
            return None
        times = [0.0]
        for way in (1, -1):
            if 0 <= place - way < count:
                times.append(come[place].get(("sum", way, count - 1 - place if way > 0 else place, part)))
        return None if None in times else max(times)

    def send(place, step, key):
        if 0 <= place + step < count:
            free[place, step] = max(clock[place], free.get((place, step), 0.0)) + unit
            come[place + step][key] = free[place, step] + latency

    def choices(place):
        found = [(ready(place, task), rank[task[0]], task[3], task[2], task[1], task) for task in todo[place]]
        found = [(max(clock[place], entry[0]),) + entry[1:] for entry in found if entry[0] is not None]
        if at[place] < len(shared):
            step = shared[at[place]]
            when = ready(place, ("finish", 0, 0, step[1])) if isinstance(step, tuple) else clock[place]
            if when is not None:
                found.append((max(when, clock[place]), 1 if isinstance(step, tuple) else 9, 0, 0, 0, step))
        return min(found, key=lambda entry: entry[:5]) if found else None

    while True:
        best = None
        for place in range(count):
            choice = choices(place)
            if choice is not None and (best is None or choice[0] < best[0][0]):
                best = (choice, place)
        if best is None:
            return max(clock), tasks
        choice, place = best
        clock[place] = choice[0]
        task = choice[5]
        if isinstance(task, float):
            clock[place] += task
            at[place] += 1
            continue
        if len(task) == 2:
            at[place] += 1
        else:
            todo[place].discard(task)
            tasks[place][at[place]].append(task)
        kind, step, slot, part = task if len(task) == 4 else ("finish", 0, 0, task[1])
        if kind in ("inject", "forward"):
            clock[place] += add if kind == "forward" else 0.02
            send(place, step, ("sum", step, slot, part))
        elif kind == "relay":
            clock[place] += 0.05
            if slot < count - 1:
                send(place, step, ("row", step, slot + 1, part))
        else:
            if kind == "finish":
                done[place] += 1
                clock[place] += end
            if rows:
                for way in (1, -1):
                    send(place, way, ("row", way, 1, part))


PARTS = 4
TURN_PARTS = 4
ATTEND_PARTS = 4
ATTEND_LATENCY, FFN_LATENCY = 1.5, 1.5
UNIT = 11.3


def rms_scale(values):
    return lax.rsqrt(jnp.mean(values * values, axis=-1, keepdims=True) + 1e-05)


def rms_back(values, scale_rows, gain, grad):
    scaled_grad = grad * gain
    inner = jnp.mean(scaled_grad * values, axis=-1, keepdims=True)
    return scale_rows * (scaled_grad - values * scale_rows * scale_rows * inner)


class Line:

    def __init__(self, count, rows, scratch, shared, sums, spreads, parts=PARTS, latency=1.5):
        self.count, self.rows, self.parts = count, rows, parts
        self.part = rows // parts
        scratch = list(scratch)
        self.sums, self.sends = {}, {}
        if sums:
            for step in (1, -1):
                self.sums[step] = [scratch.pop(0) for _ in range(4)]
            self.total_ref = scratch.pop(0)
        if spreads:
            for step in (1, -1):
                self.sends[step] = [scratch.pop(0) for _ in range(2)]
        self.replica, self.shard, self.place = coordinates()
        self.tasks = plan(count, parts, sums, spreads, shared, UNIT / parts, latency)[1]
        self.started = [[] for _ in range(count)]
        self.partial_ref = self.rows_ref = self.source_ref = self.finish = None

    def greet(self, others=()):
        barrier = pltpu.get_barrier_semaphore()
        for step in (1, -1):
            @pl.when(self.place < self.count - 1 if step > 0 else self.place > 0)
            def _():
                pl.semaphore_signal(
                    barrier, inc=1, device_id=device(self.replica, self.shard, self.place + step), device_id_type=MESH
                )
        for other in others:
            pl.semaphore_signal(barrier, inc=1, device_id=other, device_id_type=MESH)
        ends = (self.place == 0).astype(jnp.int32) + (self.place == self.count - 1).astype(jnp.int32)
        pl.semaphore_wait(barrier, 2 - ends + len(others))

    def span(self, owner, part):
        return pl.ds(pl.multiple_of(owner * self.rows + part * self.part, self.part), self.part)

    def sum_copy(self, source, step, slot, part):
        recv, _, send_sem, recv_sem = self.sums[step]
        return pltpu.make_async_remote_copy(
            src_ref=source, dst_ref=recv.at[slot, part],
            send_sem=send_sem.at[slot, part], recv_sem=recv_sem.at[slot, part],
            device_id=device(self.replica, self.shard, self.place + step), device_id_type=MESH,
        )

    def row_copy(self, step, owner, distance, part, source=None):
        send_sem, recv_sem = self.sends[step]
        where = self.rows_ref.at[self.span(owner, part)]
        return pltpu.make_async_remote_copy(
            src_ref=where if source is None else source, dst_ref=where,
            send_sem=send_sem.at[distance, part], recv_sem=recv_sem.at[distance, part],
            device_id=device(self.replica, self.shard, self.place + step), device_id_type=MESH,
        )

    def emit(self, place, task):
        kind, step, slot, part = task
        if kind in ("inject", "forward"):
            recv, send, _, _ = self.sums[step]
            owner = self.count - 1 - slot if step > 0 else slot
            source = self.partial_ref.at[self.span(owner, part)]
            if kind == "forward":
                self.sum_copy(source, step, slot, part).wait_recv()
                mine = self.partial_ref[self.span(owner, part), :].astype(F32)
                send[slot, part] = (mine + recv[slot, part].astype(F32)).astype(BF16)
                source = send.at[slot, part]
            copy = self.sum_copy(source, step, slot, part)
            copy.start()
        elif kind == "relay":
            owner = place - step * slot
            self.row_copy(step, owner, slot - 1, part).wait_recv()
            if slot < self.count - 1 and 0 <= place + step < self.count:
                self.row_copy(step, owner, slot, part).start()
        elif kind == "spread":
            self.spread_from(place, part)
        else:
            self.collect(part)
            self.finish(part, pl.ds(part * self.part, self.part), None)

    def spread_from(self, place, part):
        for step in (1, -1):
            if 0 <= place + step < self.count:
                source = None if self.source_ref is None else self.source_ref.at[pl.ds(part * self.part, self.part)]
                self.row_copy(step, place, 0, part, source).start()

    def run(self, index):
        for place in range(self.count):
            tasks = self.tasks[place][index]
            if tasks:
                @pl.when(self.place == place)
                def _():
                    for task in tasks:
                        self.emit(place, task)

    def run_at(self, base, step, count, stride=1):
        for index in range(count):
            if any(tasks[base + stride * index] for tasks in self.tasks):
                @pl.when(step == index)
                def _():
                    self.run(base + stride * index)

    def collect(self, part):
        self.total_ref[...] = self.partial_ref[self.span(self.place, part), :].astype(F32)
        for step in (1, -1):
            recv, send, _, _ = self.sums[step]
            slot = self.count - 1 - self.place if step > 0 else self.place

            @pl.when(self.place > 0 if step > 0 else self.place < self.count - 1)
            def _():
                self.sum_copy(send.at[0, part], step, slot, part).wait_recv()
                self.total_ref[...] += recv[slot, part].astype(F32)

    def finish_all(self):
        for part in range(self.parts):
            self.run(part)
            self.collect(part)
            self.finish(part, pl.ds(part * self.part, self.part), self.span(self.place, part))
            if self.sends:
                for place in range(self.count):
                    @pl.when(self.place == place)
                    def _():
                        self.spread_from(place, part)
        self.run(self.parts)
        self.drain()

    def drain(self):
        for place in range(self.count):
            @pl.when(self.place == place)
            def _():
                for part in range(self.parts):
                    for step in (1, -1):
                        if self.sums:
                            send = self.sums[step][1]
                            for slot in range(self.count - 1):
                                owner = self.count - 1 - slot if step > 0 else slot
                                if (owner - place) * step > 0:
                                    self.sum_copy(send.at[slot, part], step, slot, part).wait_send()
                        if self.sends and 0 <= place + step < self.count:
                            for distance in range(self.count - 1):
                                owner = place - step * distance
                                if 0 <= owner < self.count:
                                    self.row_copy(step, owner, distance, part).wait_send()


def line_scratch(count, rows, features, sums, spreads, parts=PARTS):
    dma = pltpu.SemaphoreType.DMA
    slots = (count - 1, parts)
    scratch = []
    if sums:
        for _ in range(2):
            scratch += [pltpu.VMEM(slots + (rows // parts, features), BF16)] * 2 + [dma(slots)] * 2
        scratch.append(pltpu.VMEM((rows // parts, features), F32))
    if spreads:
        scratch += [dma(slots)] * 4
    return scratch


def finishes(parts):
    return [("finish", part) for part in range(parts)]


def middle_kernel(count, partial_ref, input_ref, gain_ref, rows_ref, resid_ref, *scratch):
    line = Line(count, input_ref.shape[0], scratch, finishes(TURN_PARTS), True, True, TURN_PARTS)

    def finish(part, local, place):
        resid = input_ref[local, :].astype(F32) + line.total_ref[...]
        resid_ref[local, :] = resid
        rows_ref[place, :] = (resid * rms_scale(resid) * gain_ref[...]).astype(BF16)

    line.partial_ref, line.rows_ref, line.finish = partial_ref, rows_ref, finish
    line.greet()
    line.finish_all()


def turn_kernel(count, partial_ref, resid_ref, grad_ref, gain_ref, rows_ref, d_resid_ref, d_gain_ref, *scratch):
    line = Line(count, resid_ref.shape[0], scratch, finishes(TURN_PARTS), True, True, TURN_PARTS)

    def finish(part, local, place):
        resid, total = resid_ref[local, :], line.total_ref[...]
        scale = rms_scale(resid)
        sums = jnp.sum(total * resid * scale, axis=0, keepdims=True)
        d_gain_ref[...] = sums if part == 0 else d_gain_ref[...] + sums
        d_resid = grad_ref[local, :].astype(F32) + rms_back(resid, scale, gain_ref[...], total)
        d_resid_ref[local, :] = d_resid
        rows_ref[place, :] = d_resid.astype(BF16)

    line.partial_ref, line.rows_ref, line.finish = partial_ref, rows_ref, finish
    line.greet()
    line.finish_all()


def last_kernel(count, partial_ref, input_ref, d_resid_ref, gain_ref, d_input_ref, d_gain_ref, *scratch):
    line = Line(count, input_ref.shape[0], scratch, finishes(PARTS), True, False)

    def finish(part, local, place):
        values, total = input_ref[local, :].astype(F32), line.total_ref[...]
        scale = rms_scale(values)
        sums = jnp.sum(total * values * scale, axis=0, keepdims=True)
        d_gain_ref[...] = sums if part == 0 else d_gain_ref[...] + sums
        d_input_ref[local, :] = d_resid_ref[local, :] + rms_back(values, scale, gain_ref[...], total)

    line.partial_ref, line.finish = partial_ref, finish
    line.greet()
    line.finish_all()


def line_call(kernel, name, ident, spreads, out_shape, operands):
    count = lax.axis_size("tensor")
    partial_rows, features = operands[0].shape
    vmem = pl.BlockSpec(memory_space=pltpu.VMEM)
    return pl.pallas_call(
        functools.partial(kernel, count),
        out_shape=out_shape,
        in_specs=[vmem] * len(operands),
        out_specs=[vmem] * len(out_shape),
        scratch_shapes=line_scratch(
            count, partial_rows // count, features, True, spreads, TURN_PARTS if spreads else PARTS
        ),
        compiler_params=pltpu.CompilerParams(
            collective_id=ident, has_side_effects=True, vmem_limit_bytes=32 * 2**20
        ),
        cost_estimate=pl.CostEstimate(flops=10**9, bytes_accessed=60 * 2**20, transcendentals=0),
        name=name,
    )(*operands)


def enter_kernel(
    sizes, input_ref, gain_one_ref, gain_two_ref, beta_ref, gating_ref, query_ref, key_ref, value_ref, project_ref,
    rows_ref, mix_ref, whole_project_ref, gains_ref,
    all_rows, all_one, all_two, all_beta, local_sem, small_send, small_recv,
    first_send, first_recv, second_send, second_recv, third_send, third_recv, *row_sems,
):
    replicas, shards, count = sizes
    rows = input_ref.shape[0]
    width = query_ref.shape[1]
    heads = beta_ref.shape[0]
    share = query_ref.shape[0]
    sources = (gating_ref, query_ref, key_ref, value_ref, project_ref)
    streams = len(sources)
    pairs = replicas // 2
    line = Line(count, rows, row_sems, [], False, True, parts=2)
    line.rows_ref, line.source_ref = all_rows, input_ref
    replica, shard, place = line.replica, line.shard, line.place
    partner = replica + 1 - 2 * lax.rem(replica, 2)

    def across(step):
        return lax.rem(replica + 2 * step, replicas)

    def shard_at(shift):
        return lax.rem(shard + shift, shards)

    def piece(ref, stream, row, col, part):
        if stream < 4:
            size = share // replicas
            return ref.at[
                pl.ds(pl.multiple_of(row + part * size, size), size),
                pl.ds(col + stream * width if col is not None else 0, width),
            ]
        size = width // replicas
        return ref.at[
            pl.ds(pl.multiple_of(part * size, size), size),
            pl.ds(pl.multiple_of(row, 128), share),
        ]

    def held(stream, owner, part):
        ref = mix_ref if stream < 4 else whole_project_ref
        return piece(ref, stream, owner * share, 0, part)

    def own(stream, part):
        ref = sources[stream]
        if stream < 4:
            return piece(ref, stream, 0, None, part)
        return piece(ref, stream, 0, None, part)

    def remote(source, target, send, recv, where):
        return pltpu.make_async_remote_copy(
            src_ref=source, dst_ref=target, send_sem=send, recv_sem=recv, device_id=where, device_id_type=MESH
        )

    def first(shift, stream, owner):
        return remote(
            own(stream, replica), held(stream, owner, replica),
            first_send.at[shift - 1, stream], first_recv.at[shift - 1, stream],
            device(replica, shard_at(shift), place),
        )

    def second(shift, step, stream, part):
        where = held(stream, shard_at(shards - shift), part)
        return remote(
            where, where, second_send.at[shift - 1, step - 1, stream], second_recv.at[shift - 1, step - 1, stream],
            device(across(step), shard, place),
        )

    def third(shift, step, stream, part):
        where = held(stream, shard_at(shards - shift), part)
        return remote(
            where, where, third_send.at[shift - 1, step, stream], third_recv.at[shift - 1, step, stream],
            device(partner, shard, place),
        )

    def spread(part):
        for there in range(count):
            @pl.when(place == there)
            def _():
                line.spread_from(there, part)

    def relay(distance, part):
        for there in range(count):
            @pl.when(place == there)
            def _():
                for step in (1, -1):
                    if 0 <= there - step * distance < count:
                        line.emit(there, ("relay", step, distance, part))

    features = share * shards
    cols = pl.ds(pl.multiple_of(shard * share, 128), share)
    smalls = ((gain_one_ref, all_one.at[:, cols]), (gain_two_ref, all_two.at[:, cols]), (beta_ref, all_beta.at[:, cols]))

    def small(shift, index):
        source, target = smalls[index]
        return remote(
            source, target, small_send.at[shift - 1, index], small_recv.at[shift - 1, index],
            device(replica, shard_at(shift), place),
        )

    others = [device(replica, shard_at(shift), place) for shift in range(1, shards)]
    others += [device(across(step), shard, place) for step in range(1, pairs)] + [device(partner, shard, place)]
    line.greet(others)
    for shift in range(1, shards):
        for index in range(len(smalls)):
            small(shift, index).start()
    for part in range(2):
        spread(part)
    for stream in range(streams):
        for shift in range(1, shards):
            first(shift, stream, shard).start()
    locals_ = [pltpu.make_async_copy(source, target, local_sem.at[index]) for index, (source, target) in enumerate(smalls)]
    for stream in range(4):
        locals_.append(pltpu.make_async_copy(
            sources[stream],
            mix_ref.at[pl.ds(pl.multiple_of(shard * share, share), share), pl.ds(stream * width, width)],
            local_sem.at[3 + stream],
        ))
    locals_.append(pltpu.make_async_copy(project_ref, whole_project_ref.at[:, cols], local_sem.at[7]))
    for copy in locals_:
        copy.start()
    for copy in locals_[:3]:
        copy.wait()
    for shift in range(1, shards):
        for index in range(len(smalls)):
            small(shift, index).wait()
    gains_ref[...] = jnp.concatenate([all_one[...].astype(F32), all_two[...].astype(F32)], axis=0)
    lanes = mix_ref.shape[1] - 4 * width
    beta = jnp.concatenate([all_beta[...].astype(F32), jnp.zeros((lanes - heads, features), F32)], axis=0)
    mix_ref[:, 4 * width :] = beta.T.astype(BF16)

    def normalize(source, start, size):
        values = source[pl.ds(start, size), :].astype(F32)
        return (values * rms_scale(values) * gains_ref[0:1, :]).astype(BF16)

    rows_ref[line.span(place, 0), :] = normalize(input_ref, 0, line.part)
    rows_ref[line.span(place, 1), :] = normalize(input_ref, line.part, line.part)

    for turn in range(max(streams + 2, 2 * (count - 1))):
        if turn < streams:
            for shift in range(1, shards):
                first(shift, turn, shard_at(shards - shift)).wait_recv()
                for step in range(1, pairs):
                    second(shift, step, turn, replica).start()
                third(shift, 0, turn, replica).start()
        distance, part = turn // 2 + 1, turn % 2
        if distance < count:
            relay(distance, part)
        if 0 <= turn - 1 < streams:
            for shift in range(1, shards):
                for step in range(1, pairs):
                    came = across(pairs - step)
                    second(shift, step, turn - 1, came).wait_recv()
                    third(shift, step, turn - 1, came).start()
        if distance < count:
            for step in (1, -1):
                owner = place - step * distance
                inside = owner >= 0 if step > 0 else owner < count

                @pl.when(inside)
                def _():
                    start = pl.multiple_of(owner * rows + part * line.part, line.part)
                    rows_ref[line.span(owner, part), :] = normalize(all_rows, start, line.part)
        if 0 <= turn - 2 < streams:
            for shift in range(1, shards):
                for step in range(pairs):
                    third(shift, step, turn - 2, replica).wait_recv()
    for copy in locals_[3:]:
        copy.wait()
    for stream in range(streams):
        for shift in range(1, shards):
            first(shift, stream, shard).wait_send()
            for step in range(1, pairs):
                second(shift, step, stream, replica).wait_send()
            for step in range(pairs):
                third(shift, step, stream, replica).wait_send()
    line.drain()


def enter(layer_input, first_gain, second_gain, w_beta, mixers, w_project):
    replicas, shards, count = extents()
    rows, features = layer_input.shape
    width = mixers[0].shape[1]
    share = mixers[0].shape[0]
    heads = w_beta.shape[1]
    pairs = replicas // 2
    vmem = pl.BlockSpec(memory_space=pltpu.VMEM)
    hbm = pl.BlockSpec(memory_space=pltpu.HBM)
    dma = pltpu.SemaphoreType.DMA
    far = max(shards - 1, 1)
    out_shape = (
        jax.ShapeDtypeStruct((count * rows, features), BF16),
        jax.ShapeDtypeStruct((features, 4 * width + 128), BF16),
        jax.ShapeDtypeStruct((width, features), BF16),
        jax.ShapeDtypeStruct((2, features), F32),
    )
    return pl.pallas_call(
        functools.partial(enter_kernel, (replicas, shards, count)),
        out_shape=out_shape,
        in_specs=[vmem] * 4 + [hbm] * 5,
        out_specs=[vmem] * 4,
        scratch_shapes=[
            pltpu.VMEM((count * rows, features), BF16),
            pltpu.VMEM((1, features), BF16),
            pltpu.VMEM((1, features), BF16),
            pltpu.VMEM((heads, features), BF16),
            dma((8,)),
            dma((far, 3)),
            dma((far, 3)),
            dma((far, 5)),
            dma((far, 5)),
            dma((far, max(pairs - 1, 1), 5)),
            dma((far, max(pairs - 1, 1), 5)),
            dma((far, pairs, 5)),
            dma((far, pairs, 5)),
        ]
        + [dma((count - 1, 2))] * 4,
        compiler_params=pltpu.CompilerParams(collective_id=5, has_side_effects=True, vmem_limit_bytes=40 * 2**20),
        cost_estimate=pl.CostEstimate(flops=10**9, bytes_accessed=60 * 2**20, transcendentals=0),
        name="enter",
    )(layer_input, first_gain[None, :], second_gain[None, :], w_beta.T, *mixers, w_project)


class Pair:

    def __init__(self, features, owners, left_ref, right_ref, grad_refs, out_ref, scratch):
        self.owners, self.left_ref, self.right_ref, self.grad_refs = owners, left_ref, right_ref, grad_refs
        self.out_ref = out_ref
        self.tiles, self.came, self.send_sem, self.recv_sem, self.out_sem = scratch
        self.core = lax.axis_index("core")
        replica, shard, place = coordinates()
        self.partner = device(replica + 1 - 2 * self.core, shard, place)
        self.blocks, self.size = out_ref.shape[:2]
        self.share = features // (2 * lax.axis_size("pair"))

    def copy(self, block):
        return pltpu.make_async_remote_copy(
            src_ref=self.tiles.at[block], dst_ref=self.came.at[block], send_sem=self.send_sem.at[block],
            recv_sem=self.recv_sem.at[block], device_id=self.partner, device_id_type=MESH,
        )

    def product(self, block, core):
        steps = self.share // self.size
        start = (lax.div(block, steps) * 2 + core) * self.share + lax.rem(block, steps) * self.size
        cols = pl.ds(pl.multiple_of(start, self.size), self.size)
        start = 0
        for owner, grad_ref in zip(self.owners, self.grad_refs):
            wide = grad_ref.shape[1]
            values = dot_tn((self.left_ref if owner == 0 else self.right_ref)[:, cols], grad_ref[...])
            yield slice(start, start + wide), values
            start += wide

    def theirs(self, block):
        for span, values in self.product(block, 1 - self.core):
            self.tiles[block, :, span] = values.astype(BF16)
        self.copy(block).start()

    def store(self, block):
        return pltpu.make_async_copy(self.tiles.at[block], self.out_ref.at[block], self.out_sem.at[block])

    def ours(self, block):
        self.copy(block).wait()
        for span, values in self.product(block, self.core):
            self.tiles[block, :, span] = (values + self.came[block, :, span].astype(F32)).astype(BF16)
        self.store(block).start()

    def drain(self):
        for block in range(self.blocks):
            self.store(block).wait()


def pair_shape(left, grads):
    features = left.shape[1]
    return features // (2 * CHUNK), CHUNK, sum(grad.shape[1] for grad in grads)


def pair_scratch(shape):
    dma = pltpu.SemaphoreType.DMA
    return [pltpu.VMEM(shape, BF16), pltpu.VMEM(shape, BF16)] + [dma(shape[:1])] * 3


def mix_grads_kernel(features, left_ref, right_ref, first_ref, second_ref, out_ref, *scratch):
    pair = Pair(features, (0, 1), left_ref, right_ref, (first_ref, second_ref), out_ref, scratch)
    barrier = pltpu.get_barrier_semaphore()
    pl.semaphore_signal(barrier, inc=1, device_id=pair.partner, device_id_type=MESH)
    pl.semaphore_wait(barrier, 1)
    pl.loop(0, pair.blocks)(pair.theirs)
    pl.loop(0, pair.blocks)(pair.ours)
    pair.drain()


def mix_grads(left, right, grads):
    shape = pair_shape(left, grads)
    vmem = pl.BlockSpec(memory_space=pltpu.VMEM)
    out = pl.pallas_call(
        functools.partial(mix_grads_kernel, left.shape[1]),
        out_shape=jax.ShapeDtypeStruct(shape, BF16),
        in_specs=[vmem] * 4,
        out_specs=pl.BlockSpec(memory_space=pltpu.HBM),
        scratch_shapes=pair_scratch(shape),
        compiler_params=pltpu.CompilerParams(collective_id=7, has_side_effects=True, vmem_limit_bytes=40 * 2**20),
        cost_estimate=pl.CostEstimate(
            flops=2 * left.shape[0] * left.shape[1] * shape[2], bytes_accessed=30 * 2**20, transcendentals=0
        ),
        name="mix_grads",
    )(left, right, *grads)
    return out.reshape(shape[0] * shape[1], shape[2])


BLOCK_TIME, TILE_TIME = 2.8, 1.3


def ffn_grads_kernel(
    count, features, left_ref, right_ref, d_gate_ref, d_up_ref, hidden_ref, partial_ref, resid_ref, gate_up_ref,
    out_ref, result_ref, d_partial_ref, *scratch,
):
    pair = Pair(features, (0, 0, 1), left_ref, right_ref, (d_gate_ref, d_up_ref, hidden_ref), out_ref, scratch[:5])
    tiles = features // TILE
    units = d_gate_ref.shape[1]
    shared = [BLOCK_TIME] * (2 * pair.blocks) + [TILE_TIME] * tiles
    line = Line(count, resid_ref.shape[0], scratch[5:], shared, True, False, latency=FFN_LATENCY)

    def finish(part, local, place):
        result_ref[local, :] = (resid_ref[local, :] + line.total_ref[...]).astype(BF16)

    line.partial_ref, line.finish = partial_ref, finish
    line.greet([pair.partner])

    @pl.loop(0, pair.blocks)
    def _(block):
        line.run_at(0, block, pair.blocks)
        pair.theirs(block)

    @pl.loop(0, pair.blocks)
    def _(block):
        line.run_at(pair.blocks, block, pair.blocks)
        pair.ours(block)

    @pl.loop(0, tiles)
    def _(tile):
        line.run_at(2 * pair.blocks, tile, tiles)
        cols = pl.ds(pl.multiple_of(tile * TILE, TILE), TILE)
        values = dot_nt(d_gate_ref[...], gate_up_ref[cols, :units]) + dot_nt(d_up_ref[...], gate_up_ref[cols, units:])
        d_partial_ref[:, cols] = values.astype(BF16)

    line.run(2 * pair.blocks + tiles)
    line.drain()
    pair.drain()


def ffn_grads(left, right, grads, ffn_partial, resid, gate_up):
    count = lax.axis_size("tensor")
    shape = pair_shape(left, grads)
    vmem = pl.BlockSpec(memory_space=pltpu.VMEM)
    sums, result, d_partial = pl.pallas_call(
        functools.partial(ffn_grads_kernel, count, left.shape[1]),
        out_shape=(jax.ShapeDtypeStruct(shape, BF16), jax.ShapeDtypeStruct(resid.shape, BF16), jax.ShapeDtypeStruct(left.shape, BF16)),
        in_specs=[vmem] * 8,
        out_specs=[pl.BlockSpec(memory_space=pltpu.HBM), vmem, vmem],
        scratch_shapes=pair_scratch(shape) + line_scratch(count, resid.shape[0], resid.shape[1], True, False),
        compiler_params=pltpu.CompilerParams(collective_id=6, has_side_effects=True, vmem_limit_bytes=58 * 2**20),
        cost_estimate=pl.CostEstimate(
            flops=2 * left.shape[0] * left.shape[1] * shape[2], bytes_accessed=50 * 2**20, transcendentals=0
        ),
        name="ffn_grads",
    )(left, right, *grads, ffn_partial, resid, gate_up)
    return sums.reshape(shape[0] * shape[1], shape[2]), result, d_partial


def group_scatter(sums):
    shard = lax.psum_scatter(sums, ("pair", "fsdp"), scatter_dimension=0, tiled=True)
    return with_layout_constraint(shard, Layout(major_to_minor=(0, 1))).astype(F32)


def gather_weights(pieces, axis):
    return lax.all_gather(jnp.concatenate(pieces, axis=1), ("fsdp", "pair", "core"), axis=axis, tiled=True)


def scatter_grads(grads, axis=0):
    return lax.psum_scatter(grads, ("pair", "core", "fsdp"), scatter_dimension=axis, tiled=True).astype(F32)


def body(
    layer_input,
    first_gain,
    w_query,
    w_key,
    w_value,
    w_gating,
    w_beta,
    conv_query,
    conv_key,
    conv_value,
    head_gain,
    w_project,
    second_gain,
    w_gate,
    w_up,
    w_down,
    doc_starts,
    seq_lengths,
    output_grad,
):
    replicas, replica = extents()[0], coordinates()[0]
    width = w_query.shape[1]
    units = w_gate.shape[1]
    heads = w_beta.shape[1]
    head_width = head_gain.shape[0]

    def piece(weight, axis):
        size = weight.shape[axis] // replicas
        return lax.dynamic_slice_in_dim(weight, replica * size, size, axis)

    input_float = layer_input.astype(F32)
    conv_q = conv_query.astype(F32)
    conv_k = conv_key.astype(F32)
    conv_v = conv_value.astype(F32)
    gain_head = head_gain.astype(F32)[None, :]
    rows_one, mix_full, project_full, gains = enter(
        layer_input, first_gain, second_gain, w_beta, (w_gating, w_query, w_key, w_value), w_project
    )
    gain_one, gain_two = gains[:1], gains[1:]
    late, rows_one = lax.optimization_barrier(((w_gate, w_up, w_down), rows_one))
    gate_up = gather_weights([piece(late[0], 0), piece(late[1], 0)], 0)
    down = gather_weights([piece(late[2], 1)], 1)
    raw, gated, mixed, solve, update, state, attn_partial, grad_rows = attend(
        doc_starts, seq_lengths, rows_one, mix_full, project_full, output_grad, conv_q, conv_k, conv_v, gain_head
    )
    whole_rows = jax.ShapeDtypeStruct(rows_one.shape, BF16)
    own_rows = jax.ShapeDtypeStruct(layer_input.shape, F32)
    gain_sums = jax.ShapeDtypeStruct((1, layer_input.shape[1]), F32)
    rows_two, resid = line_call(
        middle_kernel, "middle", 2, True, (whole_rows, own_rows), (attn_partial, layer_input, gain_two)
    )
    d_hidden = dot_nt(grad_rows, down)
    both = dot(rows_two, gate_up)
    gate_val, up_val = both[:, :units], both[:, units:]
    gate_sig = jax.nn.sigmoid(gate_val)
    silu_gate = gate_val * gate_sig
    hidden = (silu_gate * up_val).astype(BF16)
    d_gate = (d_hidden * up_val * gate_sig * (1.0 + gate_val * (1.0 - gate_sig))).astype(BF16)
    d_up = (d_hidden * silu_gate).astype(BF16)
    ffn_partial = dot(hidden, down).astype(BF16)
    ffn_sums, result, d_partial = ffn_grads(rows_two, grad_rows, (d_gate, d_up, hidden), ffn_partial, resid, gate_up)
    ffn_shard = group_scatter(ffn_sums)
    d_attn, d_resid, grad_second = line_call(
        turn_kernel, "turn", 3, True, (whole_rows, own_rows, gain_sums), (d_partial, resid, output_grad, gain_two)
    )
    d_gated = dot_nt(d_attn, project_full)
    d_raw, d_conv, d_head = delta_backward(
        doc_starts, seq_lengths, raw, conv_q, conv_k, conv_v, gain_head, mixed, solve, update, state, d_gated
    )
    mix_sums, ffn_shard = lax.optimization_barrier(
        (mix_grads(rows_one, d_attn, (d_raw, gated)), ffn_shard)
    )
    mix_shard = group_scatter(mix_sums)
    project_shard = mix_shard[:, 4 * width + head_width :]
    mix_partial = dot_nt(d_raw, mix_full).astype(BF16)
    input_grad, grad_first = line_call(
        last_kernel, "last", 4, False, (own_rows, gain_sums),
        (mix_partial, layer_input, d_resid, gain_one),
    )
    gain_total, head_total, conv_totals = reduce_small(
        jnp.concatenate([grad_first, grad_second], axis=0), d_head, d_conv
    )
    return (
        result,
        input_grad,
        gain_total[0],
        mix_shard[:, width : 2 * width],
        mix_shard[:, 2 * width : 3 * width],
        mix_shard[:, 3 * width : 4 * width],
        mix_shard[:, :width],
        mix_shard[:, 4 * width : 4 * width + heads],
        conv_totals[:, :width],
        conv_totals[:, width : 2 * width],
        conv_totals[:, 2 * width :],
        head_total[0],
        project_shard.T,
        gain_total[1],
        ffn_shard[:, :units],
        ffn_shard[:, units : 2 * units],
        ffn_shard[:, 2 * units :].T,
    )


def solution(mesh):
    replicas, shards, count = (mesh.shape[name] for name in ("dp", "fsdp", "tensor"))
    mesh = jax.sharding.Mesh(
        mesh.devices.reshape(replicas // 2, 2, shards, count), ("pair", "core", "fsdp", "tensor")
    )
    placed = (
        P(("pair", "core", "fsdp", "tensor"), None),
        P("fsdp"),
        P("fsdp", "tensor"),
        P("fsdp", "tensor"),
        P("fsdp", "tensor"),
        P("fsdp", "tensor"),
        P("fsdp", "tensor"),
        P(None, "tensor"),
        P(None, "tensor"),
        P(None, "tensor"),
        P(),
        P("tensor", "fsdp"),
        P("fsdp"),
        P("fsdp", "tensor"),
        P("fsdp", "tensor"),
        P("tensor", "fsdp"),
        P(("pair", "core", "fsdp"), None),
        P(("pair", "core", "fsdp")),
        P(("pair", "core", "fsdp", "tensor"), None),
    )
    return jax.shard_map(
        body,
        mesh=mesh,
        in_specs=placed,
        out_specs=(
            P(("pair", "core", "fsdp", "tensor"), None),
            P(("pair", "core", "fsdp", "tensor"), None),
            P(("pair", "core", "fsdp")),
            P(("pair", "core", "fsdp"), "tensor"),
            P(("pair", "core", "fsdp"), "tensor"),
            P(("pair", "core", "fsdp"), "tensor"),
            P(("pair", "core", "fsdp"), "tensor"),
            P(("pair", "core", "fsdp"), "tensor"),
            P(None, "tensor"),
            P(None, "tensor"),
            P(None, "tensor"),
            P(),
            P("tensor", ("pair", "core", "fsdp")),
            P(("pair", "core", "fsdp")),
            P(("pair", "core", "fsdp"), "tensor"),
            P(("pair", "core", "fsdp"), "tensor"),
            P("tensor", ("pair", "core", "fsdp")),
        ),
        check_vma=False,
    )
```

```python
import functools
import jax, jax.numpy as jnp
from jax import lax
from jax.experimental import pallas as pl
from jax.experimental.pallas import tpu as pltpu
from jax.experimental.layout import Layout, with_layout_constraint
from jax.sharding import PartitionSpec as P

KERNEL = 4
CHUNK = 256
G, Q, K, V = range(4)
MESH = pl.DeviceIdType.MESH
F32 = jnp.float32
BF16 = jnp.bfloat16


def coordinates():
    replica = lax.axis_index("pair") * 2 + lax.axis_index("core")
    return replica, lax.axis_index("fsdp"), lax.axis_index("tensor")


def extents():
    return lax.axis_size("pair") * 2, lax.axis_size("fsdp"), lax.axis_size("tensor")


def device(replica, shard, place):
    return (lax.div(replica, 2), lax.rem(replica, 2), shard, place)


def dot(left, right):
    return jnp.dot(left, right, preferred_element_type=F32)


def dot_nt(left, right):
    return lax.dot_general(left, right, (((1,), (1,)), ((), ())), preferred_element_type=F32)


def dot_tn(left, right):
    return lax.dot_general(left, right, (((0,), (0,)), ((), ())), preferred_element_type=F32)


def lane_sum(values):
    return jnp.sum(values, axis=-1, keepdims=True)


def document_of(starts_ref, positions):
    total = jnp.zeros_like(positions)
    for entry in range(starts_ref.shape[1]):
        total = total + (positions >= starts_ref[0, entry]).astype(jnp.int32)
    return total


def fill_masks(starts_ref, length_ref, keep_ref, live_ref, carry_ref):
    rows, lanes = live_ref.shape
    place = lax.broadcasted_iota(jnp.int32, (rows, lanes), 0)
    docs = document_of(starts_ref, place)
    for delay in range(1, KERNEL):
        prior = document_of(starts_ref, place - delay)
        keep_ref[delay - 1] = jnp.where((prior == docs) & (place >= delay), 1.0, 0.0)
    live_ref[...] = jnp.where(place < length_ref[0], 1.0, 0.0)
    for edge in range(rows // CHUNK - 1):
        seam = jnp.int32((edge + 1) * CHUNK - 1)
        carry_ref[edge] = jnp.where(docs == document_of(starts_ref, seam), 1.0, 0.0)


def pair_mask(starts_ref, chunk):
    row = lax.broadcasted_iota(jnp.int32, (CHUNK, CHUNK), 0)
    col = lax.broadcasted_iota(jnp.int32, (CHUNK, CHUNK), 1)
    first = chunk * CHUNK
    same = document_of(starts_ref, row + first) == document_of(starts_ref, col + first)
    return same & (row > col), same & (row >= col)


def convolve(raw, taps, keep_ref):
    parts = [raw]
    for delay in range(1, KERNEL):
        parts.append(pltpu.roll(raw, delay, 0) * keep_ref[delay - 1])
    total = parts[0] * taps[KERNEL - 1 : KERNEL]
    for delay in range(1, KERNEL):
        total = total + parts[delay] * taps[KERNEL - 1 - delay : KERNEL - delay]
    return total, parts


def sigmoid(values):
    return 0.5 * jnp.tanh(0.5 * values) + 0.5


def column(values, index):
    lane = lax.broadcasted_iota(jnp.int32, values.shape, 1)
    return lane_sum(jnp.where(lane == index, values, 0.0))


def invert(system):
    size = system[0].shape[0]
    row = lax.broadcasted_iota(jnp.int32, (size, size), 0)
    col = lax.broadcasted_iota(jnp.int32, (size, size), 1)
    apart = row ^ col
    eye = jnp.where(row == col, 1.0, 0.0)
    low = [matrix.astype(BF16) for matrix in system]
    solved = [eye - jnp.where(apart == 1, matrix, 0.0) for matrix in system]
    step = 2
    while step < size:
        level = (apart >= step) & (apart < 2 * step)
        for index, matrix in enumerate(low):
            part = jnp.where(level, matrix, 0.0)
            held = solved[index].astype(BF16)
            solved[index] = solved[index] - dot(dot(held, part).astype(BF16), held)
        step *= 2
    refined = []
    for matrix, high, inverse in zip(system, low, solved):
        rest = (matrix - high.astype(F32)).astype(BF16)
        head = inverse.astype(BF16)
        tail = (inverse - head.astype(F32)).astype(BF16)
        product = dot(high, head) + dot(rest, head) + dot(high, tail)
        residue = eye - inverse - product
        refined.append(inverse + dot(head, residue.astype(BF16)))
    return refined


def unit_rows(conv):
    gate = sigmoid(conv)
    act = conv * gate
    scale = lax.rsqrt(lane_sum(act * act) + 1e-06)
    return gate, act, scale


TILE = 256
PROJECT_TILE = 512
ATTEND_TIMES = (1.2, 1.5, 0.9)


def backward_kernel(
    starts_ref, length_ref, raw_ref, conv_q_ref, conv_k_ref, conv_v_ref, gain_ref,
    mixed_ref, solve_ref, update_ref, state_ref, grad_ref,
    d_raw_ref, d_conv_ref, d_gain_ref,
    keep_ref, live_ref, carry_ref, strict_ref, incl_ref, d_query_ref, d_key_ref, d_value_ref, d_rate_ref,
):
    rows, head_width = live_ref.shape
    width = mixed_ref.shape[1]
    chunks = rows // CHUNK
    fill_masks(starts_ref, length_ref, keep_ref, live_ref, carry_ref)
    for chunk in range(chunks):
        strict, incl = pair_mask(starts_ref, chunk)
        strict_ref[chunk] = jnp.where(strict, 1.0, 0.0)
        incl_ref[chunk] = jnp.where(incl, 1.0, 0.0)
    d_gain_ref[...] = jnp.zeros_like(d_gain_ref)
    d_raw_ref[:, 4 * width :] = jnp.zeros((rows, head_width), BF16)

    @pl.loop(0, width // head_width)
    def _(head):
        start = pl.multiple_of(head * head_width, head_width)

        def place(index):
            return pl.ds(pl.multiple_of(index * width + start, head_width), head_width)

        cols = pl.ds(start, head_width)
        live = live_ref[...]
        mixed = mixed_ref[:, cols]
        norm = lax.rsqrt(lane_sum(mixed * mixed) * (1.0 / head_width) + 1e-05)
        gating = raw_ref[:, place(G)]
        gate = sigmoid(gating)
        normal = mixed * norm
        grad = grad_ref[:, cols].astype(F32) * live
        grad_gain = grad * gain_ref[...]
        swish = gating * gate
        d_raw_ref[:, place(G)] = (grad_gain * normal * gate * (1.0 + gating - swish)).astype(BF16)
        d_gain_ref[...] += jnp.sum(grad * normal * swish, axis=0, keepdims=True)
        d_normal = grad_gain * swish
        d_mixed = norm * (d_normal - normal * (lane_sum(d_normal * normal) * (1.0 / head_width)))
        d_mixed_low = d_mixed.astype(BF16)

        conv_q, parts_q = convolve(raw_ref[:, place(Q)], conv_q_ref[:, cols].astype(F32), keep_ref)
        gate_q, act_q, scale_q = unit_rows(conv_q)
        unit_q = act_q * scale_q
        query = unit_q.astype(BF16)
        conv_k, parts_k = convolve(raw_ref[:, place(K)], conv_k_ref[:, cols].astype(F32), keep_ref)
        gate_k, act_k, scale_k = unit_rows(conv_k)
        keyed = act_k * scale_k
        key_low = keyed.astype(BF16)
        conv_v, parts_v = convolve(raw_ref[:, place(V)], conv_v_ref[:, cols].astype(F32), keep_ref)
        gate_v = sigmoid(conv_v)
        valued = conv_v * gate_v
        sig = sigmoid(column(raw_ref[:, 4 * width :], head))
        rate = sig * live
        scaled_value = (valued * rate).astype(BF16)
        scaled_key = keyed * rate

        d_memory = None
        for chunk in range(chunks - 1, -1, -1):
            span = slice(chunk * CHUNK, (chunk + 1) * CHUNK)
            key_c, query_c, d_mixed_c = key_low[span], query[span], d_mixed_low[span]
            solve = solve_ref[head * chunks + chunk]
            update = update_ref[span, cols]
            incl, strict = incl_ref[chunk], strict_ref[chunk]
            score = (dot_nt(query_c, key_c) * incl).astype(BF16)
            d_update = dot_tn(score, d_mixed_c)
            d_key = None
            if d_memory is not None:
                last = carry_ref[chunk][span]
                d_memory_low = d_memory.astype(BF16)
                d_update = d_update + dot((keyed[span] * last).astype(BF16), d_memory_low)
                d_key = last * dot_nt(update, d_memory_low)
            d_update_low = d_update.astype(BF16)
            d_score = (dot_nt(d_mixed_c, update) * incl).astype(BF16)
            d_query = dot(d_score, key_c)
            d_key_score = dot_tn(d_score, query_c)
            d_key = d_key_score if d_key is None else d_key + d_key_score
            if chunk == 0:
                right = scaled_value[span]
                solved = dot(solve, right)
                d_right = dot_tn(solve, d_update_low)
                d_value_in = d_right
                d_rate = lane_sum(d_value_in * valued[span])
            else:
                carry = carry_ref[chunk - 1][span]
                state = state_ref[head * (chunks - 1) + chunk - 1]
                right = jnp.concatenate([scaled_value[span], (scaled_key[span] * carry).astype(BF16)], axis=1)
                solved = dot(solve, right)
                d_solved_key = -dot_nt(d_update_low, state)
                d_right = dot_tn(solve, jnp.concatenate([d_update_low, d_solved_key.astype(BF16)], axis=1))
                d_value_in = d_right[:, :head_width]
                d_key_in = d_right[:, head_width:] * carry
                carried = (carry * d_mixed[span]).astype(BF16)
                d_query = d_query + dot_nt(carried, state)
                d_key = d_key + rate[span] * d_key_in
                d_rate = lane_sum(d_value_in * valued[span] + d_key_in * keyed[span])
                fresh = dot_tn(query_c, carried) - dot_tn(solved[:, head_width:].astype(BF16), d_update_low)
                if d_memory is None:
                    d_memory = fresh
                else:
                    d_memory = d_memory * carry[CHUNK - 1 :] + fresh
            d_system = dot_nt(d_right.astype(BF16), solved.astype(BF16)) * -strict
            pair = dot_nt(key_c, key_c)
            d_rate = d_rate + lane_sum(d_system * pair)
            wide = jnp.concatenate([rate[span]] * (CHUNK // head_width), axis=1)
            d_pair = (d_system * wide).astype(BF16)
            d_key = d_key + dot(d_pair, key_c) + dot_tn(d_pair, key_c)
            d_query_ref[span] = d_query
            d_key_ref[span] = d_key
            d_value_ref[span] = rate[span] * d_value_in
            d_rate_ref[span] = jnp.broadcast_to(d_rate, (CHUNK, head_width))

        lane = lax.broadcasted_iota(jnp.int32, (rows, head_width), 1)
        d_beta = d_rate_ref[...] * rate * (1.0 - sig)
        tail = d_raw_ref[:, 4 * width :]
        d_raw_ref[:, 4 * width :] = jnp.where(lane == head, d_beta.astype(BF16), tail)

        def conv_back(index, d_conv, parts, taps):
            sums = [jnp.sum(d_conv * part, axis=0, keepdims=True) for part in parts]
            for delay in range(KERNEL):
                tap = KERNEL - 1 - delay
                d_conv_ref[tap : tap + 1, place(index - 1)] = sums[delay]
            total = d_conv * taps[KERNEL - 1 : KERNEL]
            for delay in range(1, KERNEL):
                tap = KERNEL - 1 - delay
                back = pltpu.roll(d_conv * keep_ref[delay - 1], rows - delay, 0)
                total = total + back * taps[tap : tap + 1]
            d_raw_ref[:, place(index)] = total.astype(BF16)

        def unit_back(d_unit, unit, scale, conv, act, gate):
            d_act = scale * (d_unit - unit * lane_sum(d_unit * unit))
            return d_act * gate * (1.0 + conv - act)

        conv_back(Q, unit_back(d_query_ref[...], unit_q, scale_q, conv_q, act_q, gate_q), parts_q, conv_q_ref[:, cols].astype(F32))
        conv_back(K, unit_back(d_key_ref[...], keyed, scale_k, conv_k, act_k, gate_k), parts_k, conv_k_ref[:, cols].astype(F32))
        d_conv_v = d_value_ref[...] * gate_v * (1.0 + conv_v - valued)
        conv_back(V, d_conv_v, parts_v, conv_v_ref[:, cols].astype(F32))


def delta_backward(starts, length, raw, conv_q, conv_k, conv_v, gain, mixed, solve, update, state, grad):
    rows = raw.shape[0]
    head_width = gain.shape[-1]
    width = conv_q.shape[1]
    heads, chunks = width // head_width, rows // CHUNK
    vmem = pl.BlockSpec(memory_space=pltpu.VMEM)
    smem = pl.BlockSpec(memory_space=pltpu.SMEM)
    return pl.pallas_call(
        backward_kernel,
        out_shape=(
            jax.ShapeDtypeStruct((rows, 4 * width + head_width), BF16),
            jax.ShapeDtypeStruct((KERNEL, 3 * width), F32),
            jax.ShapeDtypeStruct((1, head_width), F32),
        ),
        in_specs=[smem, smem] + [vmem] * 10,
        out_specs=[vmem] * 3,
        scratch_shapes=[
            pltpu.VMEM((KERNEL - 1, rows, head_width), F32),
            pltpu.VMEM((rows, head_width), F32),
            pltpu.VMEM((chunks - 1, rows, head_width), F32),
            pltpu.VMEM((chunks, CHUNK, CHUNK), F32),
            pltpu.VMEM((chunks, CHUNK, CHUNK), F32),
        ]
        + [pltpu.VMEM((rows, head_width), F32)] * 4,
        compiler_params=pltpu.CompilerParams(vmem_limit_bytes=18 * 2**20),
        cost_estimate=pl.CostEstimate(
            flops=2 * 12 * heads * chunks * CHUNK**3, bytes_accessed=16 * 2**20, transcendentals=0
        ),
        name="delta_backward",
    )(starts, length, raw, conv_q, conv_k, conv_v, gain, mixed, solve, update, state, grad)


def reduce_kernel(
    group_size, line_size, fsdp_size, gain_ref, head_ref, conv_ref, gain_out, head_out, conv_out,
    line_gain, line_head, stage, group_gain, group_conv,
    line_send, line_recv, group_send, group_recv,
):
    dp, fsdp, tensor = coordinates()
    group = dp * fsdp_size + fsdp
    size = gain_out.shape[1]

    def line_peer(shift):
        return device(dp, fsdp, lax.rem(tensor + shift, line_size))

    def group_peer(shift):
        peer = lax.rem(group + shift, group_size)
        return peer, device(lax.div(peer, fsdp_size), lax.rem(peer, fsdp_size), tensor)

    barrier = pltpu.get_barrier_semaphore()
    for shift in range(1, line_size):
        pl.semaphore_signal(barrier, inc=1, device_id=line_peer(shift), device_id_type=MESH)
    for shift in range(1, group_size):
        pl.semaphore_signal(barrier, inc=1, device_id=group_peer(shift)[1], device_id_type=MESH)
    pl.semaphore_wait(barrier, line_size + group_size - 2)

    copies = []
    for shift in range(1, line_size):
        for part, (source, target) in enumerate(((gain_ref, line_gain), (head_ref, line_head))):
            copy = pltpu.make_async_remote_copy(
                src_ref=source, dst_ref=target.at[shift - 1],
                send_sem=line_send.at[shift - 1, part], recv_sem=line_recv.at[shift - 1, part],
                device_id=line_peer(shift), device_id_type=MESH,
            )
            copy.start()
            copies.append(copy)
    conv_copies = []
    for shift in range(1, group_size):
        copy = pltpu.make_async_remote_copy(
            src_ref=conv_ref, dst_ref=group_conv.at[shift - 1],
            send_sem=group_send.at[shift - 1, 1], recv_sem=group_recv.at[shift - 1, 1],
            device_id=group_peer(shift)[1], device_id_type=MESH,
        )
        copy.start()
        conv_copies.append(copy)
    for copy in copies:
        copy.wait()
    gain = gain_ref[...]
    head = head_ref[...]
    for shift in range(1, line_size):
        gain = gain + line_gain[shift - 1]
        head = head + line_head[shift - 1]
    for peer in range(group_size):
        stage[peer] = jnp.zeros(stage.shape[1:], F32)
        stage[peer, :2, :size] = gain[:, peer * size : (peer + 1) * size]
        stage[peer, 2:3, : head.shape[1]] = head
    for copy in conv_copies:
        copy.wait()
    conv = conv_ref[...]
    for shift in range(1, group_size):
        conv = conv + group_conv[shift - 1]
    conv_out[...] = conv
    copies = []
    for shift in range(1, group_size):
        peer, where = group_peer(shift)
        copy = pltpu.make_async_remote_copy(
            src_ref=stage.at[peer], dst_ref=group_gain.at[shift - 1],
            send_sem=group_send.at[shift - 1, 0], recv_sem=group_recv.at[shift - 1, 0],
            device_id=where, device_id_type=MESH,
        )
        copy.start()
        copies.append(copy)
    for copy in copies:
        copy.wait()
    total = stage[group]
    for shift in range(1, group_size):
        total = total + group_gain[shift - 1]
    gain_out[...] = total[:2, :size]
    head_out[...] = total[2:3, : head.shape[1]]


def reduce_small(gain, head, conv):
    replicas, fsdp_size, line_size = extents()
    group_size = replicas * fsdp_size
    size = gain.shape[1] // group_size
    pad = max(size, head.shape[1])
    vmem = pl.BlockSpec(memory_space=pltpu.VMEM)
    dma = pltpu.SemaphoreType.DMA
    return pl.pallas_call(
        functools.partial(reduce_kernel, group_size, line_size, fsdp_size),
        out_shape=(
            jax.ShapeDtypeStruct((2, size), F32),
            jax.ShapeDtypeStruct(head.shape, F32),
            jax.ShapeDtypeStruct(conv.shape, F32),
        ),
        in_specs=[vmem] * 3,
        out_specs=[vmem] * 3,
        scratch_shapes=[
            pltpu.VMEM((line_size - 1,) + gain.shape, F32),
            pltpu.VMEM((line_size - 1,) + head.shape, F32),
            pltpu.VMEM((group_size, 8, pad), F32),
            pltpu.VMEM((group_size - 1, 8, pad), F32),
            pltpu.VMEM((group_size - 1,) + conv.shape, F32),
            dma((line_size - 1, 2)),
            dma((line_size - 1, 2)),
            dma((group_size - 1, 2)),
            dma((group_size - 1, 2)),
        ],
        compiler_params=pltpu.CompilerParams(collective_id=1, has_side_effects=True, vmem_limit_bytes=8 * 2**20),
        name="reduce_small",
    )(gain, head, conv)


def plan(count, parts, sums, rows, shared, unit, latency=1.5):
    backlog, add, end = 1.5, 0.15 + 0.8 / parts, 0.5 + 3.0 / parts
    rank = {"spread": 0, "relay": 0, "finish": 1, "forward": 2, "inject": 3}
    clock = [0.0] * count
    free, come = {}, [{} for _ in range(count)]
    todo = [set() for _ in range(count)]
    done = [0] * count
    at = [0] * count
    tasks = [[[] for _ in range(len(shared) + 1)] for _ in range(count)]
    own_finish = sums and not any(isinstance(step, tuple) for step in shared)
    for place in range(count):
        for part in range(parts):
            for step in (1, -1):
                behind = 0 <= place - step < count
                for slot in range(count - 1) if sums else ():
                    owner = count - 1 - slot if step > 0 else slot
                    if (owner - place) * step > 0:
                        todo[place].add(("forward" if behind else "inject", step, slot, part))
                for distance in range(1, count) if rows else ():
                    if 0 <= place - step * distance < count:
                        todo[place].add(("relay", step, distance, part))
            if rows and not sums:
                todo[place].add(("spread", 0, 0, part))
            if own_finish:
                todo[place].add(("finish", 0, 0, part))

    def ready(place, task):
        kind, step, slot, part = task
        if kind == "inject":
            return max(0.0, free.get((place, step), 0.0) - backlog * unit)
        if kind == "spread":
            return max([0.0] + [free.get((place, way), 0.0) - backlog * unit for way in (1, -1)])
        if kind == "forward":
            return come[place].get(("sum", step, slot, part))
        if kind == "relay":
            return come[place].get(("row", step, slot, part))
        if part != done[place]:
            return None
        times = [0.0]
        for way in (1, -1):
            if 0 <= place - way < count:
                times.append(come[place].get(("sum", way, count - 1 - place if way > 0 else place, part)))
        return None if None in times else max(times)

    def send(place, step, key):
        if 0 <= place + step < count:
            free[place, step] = max(clock[place], free.get((place, step), 0.0)) + unit
            come[place + step][key] = free[place, step] + latency

    def choices(place):
        found = [(ready(place, task), rank[task[0]], task[3], task[2], task[1], task) for task in todo[place]]
        found = [(max(clock[place], entry[0]),) + entry[1:] for entry in found if entry[0] is not None]
        if at[place] < len(shared):
            step = shared[at[place]]
            when = ready(place, ("finish", 0, 0, step[1])) if isinstance(step, tuple) else clock[place]
            if when is not None:
                found.append((max(when, clock[place]), 1 if isinstance(step, tuple) else 9, 0, 0, 0, step))
        return min(found, key=lambda entry: entry[:5]) if found else None

    while True:
        best = None
        for place in range(count):
            choice = choices(place)
            if choice is not None and (best is None or choice[0] < best[0][0]):
                best = (choice, place)
        if best is None:
            return max(clock), tasks
        choice, place = best
        clock[place] = choice[0]
        task = choice[5]
        if isinstance(task, float):
            clock[place] += task
            at[place] += 1
            continue
        if len(task) == 2:
            at[place] += 1
        else:
            todo[place].discard(task)
            tasks[place][at[place]].append(task)
        kind, step, slot, part = task if len(task) == 4 else ("finish", 0, 0, task[1])
        if kind in ("inject", "forward"):
            clock[place] += add if kind == "forward" else 0.02
            send(place, step, ("sum", step, slot, part))
        elif kind == "relay":
            clock[place] += 0.05
            if slot < count - 1:
                send(place, step, ("row", step, slot + 1, part))
        else:
            if kind == "finish":
                done[place] += 1
                clock[place] += end
            if rows:
                for way in (1, -1):
                    send(place, way, ("row", way, 1, part))


PARTS = 4
LANES = 512
FFN_MEMORY = 52 * 2**20
TURN_PARTS = 4
ATTEND_PARTS = 4
ATTEND_LATENCY, FFN_LATENCY = 1.5, 1.5
UNIT = 11.3


def rms_scale(values):
    return lax.rsqrt(jnp.mean(values * values, axis=-1, keepdims=True) + 1e-05)


def rms_back(values, scale_rows, gain, grad):
    scaled_grad = grad * gain
    inner = jnp.mean(scaled_grad * values, axis=-1, keepdims=True)
    return scale_rows * (scaled_grad - values * scale_rows * scale_rows * inner)


class Line:

    def __init__(self, count, rows, scratch, shared, sums, spreads, parts=PARTS, latency=1.5):
        self.count, self.rows, self.parts = count, rows, parts
        self.part = rows // parts
        scratch = list(scratch)
        self.sums, self.sends = {}, {}
        if sums:
            for step in (1, -1):
                self.sums[step] = [scratch.pop(0) for _ in range(4)]
            self.total_ref = scratch.pop(0)
        if spreads:
            for step in (1, -1):
                self.sends[step] = [scratch.pop(0) for _ in range(2)]
        self.replica, self.shard, self.place = coordinates()
        self.tasks = plan(count, parts, sums, spreads, shared, UNIT / parts, latency)[1]
        self.started = [[] for _ in range(count)]
        self.partial_ref = self.rows_ref = self.source_ref = self.finish = None

    def greet(self, others=()):
        barrier = pltpu.get_barrier_semaphore()
        for step in (1, -1):
            @pl.when(self.place < self.count - 1 if step > 0 else self.place > 0)
            def _():
                pl.semaphore_signal(
                    barrier, inc=1, device_id=device(self.replica, self.shard, self.place + step), device_id_type=MESH
                )
        for other in others:
            pl.semaphore_signal(barrier, inc=1, device_id=other, device_id_type=MESH)
        ends = (self.place == 0).astype(jnp.int32) + (self.place == self.count - 1).astype(jnp.int32)
        pl.semaphore_wait(barrier, 2 - ends + len(others))

    def span(self, owner, part):
        return pl.ds(pl.multiple_of(owner * self.rows + part * self.part, self.part), self.part)

    def sum_copy(self, source, step, slot, part):
        recv, _, send_sem, recv_sem = self.sums[step]
        return pltpu.make_async_remote_copy(
            src_ref=source, dst_ref=recv.at[slot, part],
            send_sem=send_sem.at[slot, part], recv_sem=recv_sem.at[slot, part],
            device_id=device(self.replica, self.shard, self.place + step), device_id_type=MESH,
        )

    def row_copy(self, step, owner, distance, part, source=None):
        send_sem, recv_sem = self.sends[step]
        where = self.rows_ref.at[self.span(owner, part)]
        return pltpu.make_async_remote_copy(
            src_ref=where if source is None else source, dst_ref=where,
            send_sem=send_sem.at[distance, part], recv_sem=recv_sem.at[distance, part],
            device_id=device(self.replica, self.shard, self.place + step), device_id_type=MESH,
        )

    def emit(self, place, task):
        kind, step, slot, part = task
        if kind in ("inject", "forward"):
            recv, send, _, _ = self.sums[step]
            owner = self.count - 1 - slot if step > 0 else slot
            source = self.partial_ref.at[self.span(owner, part)]
            if kind == "forward":
                self.sum_copy(source, step, slot, part).wait_recv()

                @pl.loop(0, self.partial_ref.shape[1] // LANES)
                def _(step_index):
                    cols = pl.ds(pl.multiple_of(step_index * LANES, LANES), LANES)
                    mine = self.partial_ref[self.span(owner, part), cols].astype(F32)
                    send[slot, part, :, cols] = (mine + recv[slot, part, :, cols].astype(F32)).astype(BF16)

                source = send.at[slot, part]
            copy = self.sum_copy(source, step, slot, part)
            copy.start()
        elif kind == "relay":
            owner = place - step * slot
            self.row_copy(step, owner, slot - 1, part).wait_recv()
            if slot < self.count - 1 and 0 <= place + step < self.count:
                self.row_copy(step, owner, slot, part).start()
        elif kind == "spread":
            self.spread_from(place, part)
        else:
            self.collect(part)
            self.finish(part, pl.ds(part * self.part, self.part), None)

    def spread_from(self, place, part):
        for step in (1, -1):
            if 0 <= place + step < self.count:
                source = None if self.source_ref is None else self.source_ref.at[pl.ds(part * self.part, self.part)]
                self.row_copy(step, place, 0, part, source).start()

    def run(self, index):
        for place in range(self.count):
            tasks = self.tasks[place][index]
            if tasks:
                @pl.when(self.place == place)
                def _():
                    for task in tasks:
                        self.emit(place, task)

    def run_at(self, base, step, count, stride=1):
        for index in range(count):
            if any(tasks[base + stride * index] for tasks in self.tasks):
                @pl.when(step == index)
                def _():
                    self.run(base + stride * index)

    def collect(self, part):
        places = []
        for step in (1, -1):
            recv, send, _, _ = self.sums[step]
            slot = self.count - 1 - self.place if step > 0 else self.place
            has = self.place > 0 if step > 0 else self.place < self.count - 1

            @pl.when(has)
            def _():
                self.sum_copy(send.at[0, part], step, slot, part).wait_recv()

            places.append((recv, slot, has))

        @pl.loop(0, self.partial_ref.shape[1] // LANES)
        def _(index):
            cols = pl.ds(pl.multiple_of(index * LANES, LANES), LANES)
            self.total_ref[:, cols] = self.partial_ref[self.span(self.place, part), cols].astype(F32)
            for recv, slot, has in places:
                @pl.when(has)
                def _():
                    self.total_ref[:, cols] += recv[slot, part, :, cols].astype(F32)

    def finish_all(self):
        @pl.loop(0, self.parts)
        def _(part):
            self.run_at(0, part, self.parts)
            self.collect(part)
            local = pl.ds(pl.multiple_of(part * self.part, self.part), self.part)
            self.finish(part, local, self.span(self.place, part))
            if self.sends:
                for place in range(self.count):
                    @pl.when(self.place == place)
                    def _():
                        self.spread_from(place, part)

        self.run(self.parts)
        self.drain()

    def drain(self):
        for place in range(self.count):
            @pl.when(self.place == place)
            def _():
                for part in range(self.parts):
                    for step in (1, -1):
                        if self.sums:
                            send = self.sums[step][1]
                            for slot in range(self.count - 1):
                                owner = self.count - 1 - slot if step > 0 else slot
                                if (owner - place) * step > 0:
                                    self.sum_copy(send.at[slot, part], step, slot, part).wait_send()
                        if self.sends and 0 <= place + step < self.count:
                            for distance in range(self.count - 1):
                                owner = place - step * distance
                                if 0 <= owner < self.count:
                                    self.row_copy(step, owner, distance, part).wait_send()


def line_scratch(count, rows, features, sums, spreads, parts=PARTS):
    dma = pltpu.SemaphoreType.DMA
    slots = (count - 1, parts)
    scratch = []
    if sums:
        for _ in range(2):
            scratch += [pltpu.VMEM(slots + (rows // parts, features), BF16)] * 2 + [dma(slots)] * 2
        scratch.append(pltpu.VMEM((rows // parts, features), F32))
    if spreads:
        scratch += [dma(slots)] * 4
    return scratch


def finishes(parts):
    return [("finish", part) for part in range(parts)]


def middle_kernel(count, partial_ref, input_ref, gain_ref, rows_ref, resid_ref, *scratch):
    line = Line(count, input_ref.shape[0], scratch, finishes(TURN_PARTS), True, True, TURN_PARTS)

    def finish(part, local, place):
        resid = input_ref[local, :].astype(F32) + line.total_ref[...]
        resid_ref[local, :] = resid
        rows_ref[place, :] = (resid * rms_scale(resid) * gain_ref[...]).astype(BF16)

    line.partial_ref, line.rows_ref, line.finish = partial_ref, rows_ref, finish
    line.greet()
    line.finish_all()


def turn_kernel(count, partial_ref, resid_ref, grad_ref, gain_ref, rows_ref, d_resid_ref, d_gain_ref, *scratch):
    line = Line(count, resid_ref.shape[0], scratch, finishes(TURN_PARTS), True, True, TURN_PARTS)

    def finish(part, local, place):
        resid, total = resid_ref[local, :], line.total_ref[...]
        scale = rms_scale(resid)
        sums = jnp.sum(total * resid * scale, axis=0, keepdims=True)
        d_gain_ref[...] += sums
        d_resid = grad_ref[local, :].astype(F32) + rms_back(resid, scale, gain_ref[...], total)
        d_resid_ref[local, :] = d_resid
        rows_ref[place, :] = d_resid.astype(BF16)

    d_gain_ref[...] = jnp.zeros_like(d_gain_ref)
    line.partial_ref, line.rows_ref, line.finish = partial_ref, rows_ref, finish
    line.greet()
    line.finish_all()


def last_kernel(count, partial_ref, input_ref, d_resid_ref, gain_ref, d_input_ref, d_gain_ref, *scratch):
    line = Line(count, input_ref.shape[0], scratch, finishes(PARTS), True, False)

    def finish(part, local, place):
        values, total = input_ref[local, :].astype(F32), line.total_ref[...]
        scale = rms_scale(values)
        sums = jnp.sum(total * values * scale, axis=0, keepdims=True)
        d_gain_ref[...] += sums
        d_input_ref[local, :] = d_resid_ref[local, :] + rms_back(values, scale, gain_ref[...], total)

    d_gain_ref[...] = jnp.zeros_like(d_gain_ref)
    line.partial_ref, line.finish = partial_ref, finish
    line.greet()
    line.finish_all()


def line_call(kernel, name, ident, spreads, out_shape, operands):
    count = lax.axis_size("tensor")
    partial_rows, features = operands[0].shape
    vmem = pl.BlockSpec(memory_space=pltpu.VMEM)
    return pl.pallas_call(
        functools.partial(kernel, count),
        out_shape=out_shape,
        in_specs=[vmem] * len(operands),
        out_specs=[vmem] * len(out_shape),
        scratch_shapes=line_scratch(
            count, partial_rows // count, features, True, spreads, TURN_PARTS if spreads else PARTS
        ),
        compiler_params=pltpu.CompilerParams(
            collective_id=ident, has_side_effects=True, vmem_limit_bytes=16 * 2**20
        ),
        cost_estimate=pl.CostEstimate(flops=10**9, bytes_accessed=60 * 2**20, transcendentals=0),
        name=name,
    )(*operands)


def begin_kernel(
    sizes, starts_ref, length_ref, input_ref, own_gains_ref, beta_ref, own_grad_ref,
    conv_q_ref, conv_k_ref, conv_v_ref, gain_ref,
    gating_ref, query_ref, key_ref, value_ref, project_ref, gate_ref, up_ref,
    gains_ref, partial_ref, grad_rows_ref, rows_ref, mix_ref, whole_project_ref, gate_up_ref,
    raw_ref, gated_ref, mixed_ref, solve_ref, update_ref, state_ref,
    all_rows, normed, mix_all, project_all, ffn_all, raw_all, gated_all, mixed_all, solve_all, update_all, state_all,
    keep_ref, live_ref, carry_ref, strict_ref, incl_ref,
    all_gains, all_beta, local_sem, store_sem, small_send, small_recv,
    first_send, first_recv, second_send, second_recv, third_send, third_recv, *row_sems,
):
    replicas, shards, count = sizes
    rows = input_ref.shape[0]
    width = query_ref.shape[1]
    heads = beta_ref.shape[0]
    share = query_ref.shape[0]
    units = gate_ref.shape[1]
    half = share // 2
    streams = [(ref, mix_all, False, 0, share, index * width) for index, ref in enumerate((gating_ref, query_ref, key_ref, value_ref))]
    streams.append((project_ref, project_all, True, 0, width, 0))
    for first_row in (0, half):
        for index, ref in enumerate((gate_ref, up_ref)):
            streams.append((ref, ffn_all, False, first_row, half, index * units))
    count_streams = len(streams)
    pairs = replicas // 2
    line = Line(count, rows, row_sems[:4], [], False, True, parts=2)
    line.rows_ref, line.source_ref = all_rows, input_ref
    replica, shard, place = line.replica, line.shard, line.place
    partner = replica + 1 - 2 * lax.rem(replica, 2)

    def across(step):
        return lax.rem(replica + 2 * step, replicas)

    def shard_at(shift):
        return lax.rem(shard + shift, shards)

    def held(stream, owner, part):
        ref, whole, spread_cols, first_row, height, col = streams[stream]
        size = height // replicas
        if spread_cols:
            return whole.at[
                pl.ds(pl.multiple_of(part * size, size), size), pl.ds(pl.multiple_of(owner * share, 128), share)
            ]
        start = owner * share + first_row + part * size
        return whole.at[pl.ds(pl.multiple_of(start, size), size), pl.ds(col, ref.shape[1])]

    def own(stream, part):
        ref, _, spread_cols, first_row, height, _ = streams[stream]
        size = height // replicas
        return ref.at[pl.ds(pl.multiple_of(first_row + part * size, size), size), :]

    def remote(source, target, send, recv, where):
        return pltpu.make_async_remote_copy(
            src_ref=source, dst_ref=target, send_sem=send, recv_sem=recv, device_id=where, device_id_type=MESH
        )

    def first(shift, stream, owner):
        return remote(
            own(stream, replica), held(stream, owner, replica),
            first_send.at[shift - 1, stream], first_recv.at[shift - 1, stream],
            device(replica, shard_at(shift), place),
        )

    def second(shift, step, stream, part):
        where = held(stream, shard_at(shards - shift), part)
        return remote(
            where, where, second_send.at[shift - 1, step - 1, stream], second_recv.at[shift - 1, step - 1, stream],
            device(across(step), shard, place),
        )

    def third(shift, step, stream, part):
        where = held(stream, shard_at(shards - shift), part)
        return remote(
            where, where, third_send.at[shift - 1, step, stream], third_recv.at[shift - 1, step, stream],
            device(partner, shard, place),
        )

    def spread(part):
        for there in range(count):
            @pl.when(place == there)
            def _():
                line.spread_from(there, part)

    def relay(distance, part):
        for there in range(count):
            @pl.when(place == there)
            def _():
                for step in (1, -1):
                    if 0 <= there - step * distance < count:
                        line.emit(there, ("relay", step, distance, part))

    features = share * shards
    cols = pl.ds(pl.multiple_of(shard * share, 128), share)
    smalls = ((own_gains_ref, all_gains.at[:, cols]), (beta_ref, all_beta.at[:, cols]))

    def small(shift, index):
        source, target = smalls[index]
        return remote(
            source, target, small_send.at[shift - 1, index], small_recv.at[shift - 1, index],
            device(replica, shard_at(shift), place),
        )

    others = [device(replica, shard_at(shift), place) for shift in range(1, shards)]
    others += [device(across(step), shard, place) for step in range(1, pairs)] + [device(partner, shard, place)]
    line.greet(others)
    for shift in range(1, shards):
        for index in range(len(smalls)):
            small(shift, index).start()
    for part in range(2):
        spread(part)
    for stream in range(count_streams):
        for shift in range(1, shards):
            first(shift, stream, shard).start()
    locals_ = [pltpu.make_async_copy(source, target, local_sem.at[index]) for index, (source, target) in enumerate(smalls)]
    own_rows = pl.ds(pl.multiple_of(shard * share, share), share)
    for index, ref in enumerate((gating_ref, query_ref, key_ref, value_ref)):
        locals_.append(pltpu.make_async_copy(
            ref, mix_all.at[own_rows, pl.ds(index * width, width)], local_sem.at[2 + index],
        ))
    locals_.append(pltpu.make_async_copy(project_ref, project_all.at[:, cols], local_sem.at[6]))
    for index, ref in enumerate((gate_ref, up_ref)):
        locals_.append(pltpu.make_async_copy(
            ref, ffn_all.at[own_rows, pl.ds(index * units, units)], local_sem.at[7 + index],
        ))
    for copy in locals_:
        copy.start()
    for copy in locals_[:2]:
        copy.wait()
    for shift in range(1, shards):
        for index in range(len(smalls)):
            small(shift, index).wait()
    gains_ref[...] = all_gains[...].astype(F32)
    lanes = mix_all.shape[1] - 4 * width
    beta = jnp.concatenate([all_beta[...].astype(F32), jnp.zeros((lanes - heads, features), F32)], axis=0)
    mix_all[:, 4 * width :] = beta.T.astype(BF16)

    def normalize(source, start, size):
        values = source[pl.ds(start, size), :].astype(F32)
        return (values * rms_scale(values) * gains_ref[0:1, :]).astype(BF16)

    normed[line.span(place, 0), :] = normalize(input_ref, 0, line.part)
    normed[line.span(place, 1), :] = normalize(input_ref, line.part, line.part)

    def serve(turn):
        if turn < count_streams:
            for shift in range(1, shards):
                first(shift, turn, shard_at(shards - shift)).wait_recv()
                for step in range(1, pairs):
                    second(shift, step, turn, replica).start()
                third(shift, 0, turn, replica).start()
        distance, part = turn // 2 + 1, turn % 2
        if distance < count:
            relay(distance, part)
        if 0 <= turn - 1 < count_streams:
            for shift in range(1, shards):
                for step in range(1, pairs):
                    came = across(pairs - step)
                    second(shift, step, turn - 1, came).wait_recv()
                    third(shift, step, turn - 1, came).start()
        if distance < count:
            for step in (1, -1):
                owner = place - step * distance
                inside = owner >= 0 if step > 0 else owner < count

                @pl.when(inside)
                def _():
                    start = pl.multiple_of(owner * rows + part * line.part, line.part)
                    normed[line.span(owner, part), :] = normalize(all_rows, start, line.part)
        if 0 <= turn - 2 < count_streams:
            for shift in range(1, shards):
                for step in range(pairs):
                    third(shift, step, turn - 2, replica).wait_recv()
    ready = max(6, 2 * (count - 1))
    for turn in range(ready):
        serve(turn)
    for copy in locals_[2:]:
        copy.wait()

    rows, head_width = live_ref.shape
    chunks = rows // CHUNK
    heads = width // head_width
    tiles, ends = 4 * width // TILE, features // PROJECT_TILE
    shared = [ATTEND_TIMES[0]] * tiles + [ATTEND_TIMES[1]] * (3 * heads) + [ATTEND_TIMES[2]] * ends
    first_line, line = line, Line(count, rows // count, row_sems[4:], shared, False, True, ATTEND_PARTS, ATTEND_LATENCY)
    line.rows_ref, line.source_ref = grad_rows_ref, own_grad_ref
    grad_rows_ref[pl.ds(pl.multiple_of(place * line.rows, line.rows), line.rows), :] = own_grad_ref[...]
    stores = [(normed, rows_ref), (mix_all, mix_ref), (ffn_all.at[own_rows], gate_up_ref.at[own_rows])]

    def store(index):
        return pltpu.make_async_copy(*stores[index], store_sem.at[index])

    for index in range(len(stores)):
        store(index).start()

    @pl.loop(0, tiles)
    def _(tile):
        line.run_at(0, tile, tiles)

        @pl.when(tile == tiles // 2)
        def _():
            serve(ready)

        cols = pl.ds(pl.multiple_of(tile * TILE, TILE), TILE)
        raw_all[:, cols] = dot(normed[...], mix_all[:, cols])

    raw_all[:, 4 * width :] = dot(normed[...], mix_all[:, 4 * width :])
    stores.append((raw_all, raw_ref))
    store(len(stores) - 1).start()
    serve(ready + 1)
    fill_masks(starts_ref, length_ref, keep_ref, live_ref, carry_ref)
    for chunk in range(chunks):
        strict, incl = pair_mask(starts_ref, chunk)
        strict_ref[chunk] = jnp.where(strict, 1.0, 0.0)
        incl_ref[chunk] = jnp.where(incl, 1.0, 0.0)

    @pl.loop(0, heads)
    def _(head):
        line.run_at(tiles, head, heads, 3)
        start = pl.multiple_of(head * head_width, head_width)

        def stream(index):
            return raw_all[:, pl.ds(pl.multiple_of(index * width + start, head_width), head_width)]

        cols = pl.ds(start, head_width)
        conv, _ = convolve(stream(Q), conv_q_ref[:, cols].astype(F32), keep_ref)
        _, act, scale = unit_rows(conv)
        query = (act * scale).astype(BF16)
        conv, _ = convolve(stream(K), conv_k_ref[:, cols].astype(F32), keep_ref)
        _, act, scale = unit_rows(conv)
        keyed = act * scale
        key_low = keyed.astype(BF16)
        conv, _ = convolve(stream(V), conv_v_ref[:, cols].astype(F32), keep_ref)
        valued = conv * sigmoid(conv)
        rate = sigmoid(column(raw_all[:, 4 * width :], head)) * live_ref[...]
        scaled_value = (valued * rate).astype(BF16)
        scaled_key = keyed * rate
        system = []
        for chunk in range(chunks):
            span = slice(chunk * CHUNK, (chunk + 1) * CHUNK)
            pair = dot_nt(key_low[span], key_low[span])
            wide = jnp.concatenate([rate[span]] * (CHUNK // head_width), axis=1)
            system.append(pair * wide * strict_ref[chunk])
        line.run_at(tiles + 1, head, heads, 3)
        memory = None
        inverses = invert(system)
        line.run_at(tiles + 2, head, heads, 3)
        for chunk, solved in enumerate(inverses):
            span = slice(chunk * CHUNK, (chunk + 1) * CHUNK)
            solve_low = solved.astype(BF16)
            solve_all[head * chunks + chunk] = solve_low
            score = dot_nt(query[span], key_low[span]) * incl_ref[chunk]
            if chunk == 0:
                update = dot(solve_low, scaled_value[span])
                update_low = update.astype(BF16)
                mixed = dot(score.astype(BF16), update_low)
            else:
                carry = carry_ref[chunk - 1][span]
                right = jnp.concatenate(
                    [scaled_value[span], (scaled_key[span] * carry).astype(BF16)], axis=1
                )
                both = dot(solve_low, right)
                memory_low = memory.astype(BF16)
                state_all[head * (chunks - 1) + chunk - 1] = memory_low
                update = both[:, :head_width] - dot(both[:, head_width:].astype(BF16), memory_low)
                update_low = update.astype(BF16)
                mixed = carry * dot(query[span], memory_low) + dot(score.astype(BF16), update_low)
            update_all[span, cols] = update_low
            mixed_all[span, cols] = mixed
            if chunk + 1 < chunks:
                last = (keyed[span] * carry_ref[chunk][span]).astype(BF16)
                fresh = dot_tn(last, update_low)
                if memory is None:
                    memory = fresh
                else:
                    memory = memory * carry_ref[chunk - 1][span][CHUNK - 1 :] + fresh
        mixed = mixed_all[:, cols]
        norm = lax.rsqrt(lane_sum(mixed * mixed) * (1.0 / head_width) + 1e-05)
        gating = stream(G)
        gated = mixed * norm * gain_ref[...] * (gating * sigmoid(gating)) * live_ref[...]
        gated_all[:, cols] = gated.astype(BF16)
        for index in range(1, heads, 2):
            @pl.when(head == index)
            def _():
                serve(ready + 2 + index // 2)

    stores += [
        (project_all, whole_project_ref), (gated_all, gated_ref), (mixed_all, mixed_ref), (solve_all, solve_ref),
        (update_all, update_ref), (state_all, state_ref),
    ]
    for shift in range(1, shards):
        there = pl.ds(pl.multiple_of(shard_at(shift) * share, half), half)
        stores.append((ffn_all.at[there], gate_up_ref.at[there]))
    for index in range(3 + 1, len(stores)):
        store(index).start()

    @pl.loop(0, ends)
    def _(tile):
        line.run_at(tiles + 3 * heads, tile, ends)
        cols = pl.ds(pl.multiple_of(tile * PROJECT_TILE, PROJECT_TILE), PROJECT_TILE)
        partial_ref[:, cols] = dot(gated_all[...], project_all[:, cols]).astype(BF16)

    line.run(tiles + 3 * heads + ends)
    line.drain()
    for turn in range(ready + 2 + heads // 2, count_streams + 2):
        serve(turn)
    for shift in range(1, shards):
        there = pl.ds(pl.multiple_of(shard_at(shift) * share + half, half), half)
        stores.append((ffn_all.at[there], gate_up_ref.at[there]))
        store(len(stores) - 1).start()
    for index in range(len(stores)):
        store(index).wait()

    for stream in range(count_streams):
        for shift in range(1, shards):
            first(shift, stream, shard).wait_send()
            for step in range(1, pairs):
                second(shift, step, stream, replica).wait_send()
            for step in range(pairs):
                third(shift, step, stream, replica).wait_send()
    first_line.drain()


def begin(starts, length, layer_input, first_gain, second_gain, w_beta, output_grad, convs, gain, mixers, w_project, ffn):
    replicas, shards, count = extents()
    rows, features = layer_input.shape
    share, width = mixers[0].shape
    heads_here = w_beta.shape[1]
    head_width = gain.shape[-1]
    seq_rows = count * rows
    heads, chunks = width // head_width, seq_rows // CHUNK
    pairs, far = replicas // 2, max(shards - 1, 1)
    streams = 9
    wide = 4 * width + head_width
    hbm_out = [
        ((seq_rows, features), BF16),
        ((features, wide), BF16),
        ((width, features), BF16),
        ((features, 2 * ffn[0].shape[1]), BF16),
        ((seq_rows, wide), F32),
        ((seq_rows, width), BF16),
        ((seq_rows, width), F32),
        ((heads * chunks, CHUNK, CHUNK), BF16),
        ((seq_rows, width), BF16),
        ((heads * (chunks - 1), head_width, head_width), BF16),
    ]
    vmem_out = [((2, features), F32), ((seq_rows, features), BF16), ((seq_rows, features), BF16)]
    vmem = pl.BlockSpec(memory_space=pltpu.VMEM)
    hbm = pl.BlockSpec(memory_space=pltpu.HBM)
    smem = pl.BlockSpec(memory_space=pltpu.SMEM)
    dma = pltpu.SemaphoreType.DMA
    weights = [pltpu.with_memory_space_constraint(weight, pltpu.HBM) for weight in (*mixers, w_project, *ffn)]
    return pl.pallas_call(
        functools.partial(begin_kernel, (replicas, shards, count)),
        out_shape=[jax.ShapeDtypeStruct(*entry) for entry in vmem_out] + [pltpu.HBM(*entry) for entry in hbm_out],
        in_specs=[smem] * 2 + [vmem] * 8 + [hbm] * 7,
        out_specs=[vmem] * 3 + [hbm] * len(hbm_out),
        scratch_shapes=[pltpu.VMEM((seq_rows, features), BF16)]
        + [pltpu.VMEM(*entry) for entry in hbm_out]
        + [
            pltpu.VMEM((KERNEL - 1, seq_rows, head_width), F32),
            pltpu.VMEM((seq_rows, head_width), F32),
            pltpu.VMEM((chunks - 1, seq_rows, head_width), F32),
            pltpu.VMEM((chunks, CHUNK, CHUNK), F32),
            pltpu.VMEM((chunks, CHUNK, CHUNK), F32),
            pltpu.VMEM((2, features), BF16),
            pltpu.VMEM((heads_here, features), BF16),
            dma((9,)),
            dma((10 + 2 * far,)),
            dma((far, 2)),
            dma((far, 2)),
            dma((far, streams)),
            dma((far, streams)),
            dma((far, max(pairs - 1, 1), streams)),
            dma((far, max(pairs - 1, 1), streams)),
            dma((far, pairs, streams)),
            dma((far, pairs, streams)),
        ]
        + line_scratch(count, rows, features, False, True, 2)
        + line_scratch(count, rows, features, False, True, ATTEND_PARTS),
        compiler_params=pltpu.CompilerParams(collective_id=5, has_side_effects=True, vmem_limit_bytes=56 * 2**20),
        cost_estimate=pl.CostEstimate(
            flops=2 * 36 * heads * chunks * CHUNK**3, bytes_accessed=60 * 2**20, transcendentals=0
        ),
        name="begin",
    )(
        starts, length, layer_input, jnp.stack([first_gain, second_gain]), w_beta.T, output_grad, *convs, gain, *weights
    )


class Pair:

    def __init__(self, features, owners, left_ref, right_ref, grad_refs, out_ref, scratch):
        self.owners, self.left_ref, self.right_ref, self.grad_refs = owners, left_ref, right_ref, grad_refs
        self.out_ref = out_ref
        self.tiles, self.came, self.send_sem, self.recv_sem, self.out_sem = scratch
        self.core = lax.axis_index("core")
        replica, shard, place = coordinates()
        self.partner = device(replica + 1 - 2 * self.core, shard, place)
        self.blocks, self.size = out_ref.shape[:2]
        self.share = features // (2 * lax.axis_size("pair"))

    def copy(self, block):
        return pltpu.make_async_remote_copy(
            src_ref=self.tiles.at[block], dst_ref=self.came.at[block], send_sem=self.send_sem.at[block],
            recv_sem=self.recv_sem.at[block], device_id=self.partner, device_id_type=MESH,
        )

    def product(self, block, core):
        steps = self.share // self.size
        start = (lax.div(block, steps) * 2 + core) * self.share + lax.rem(block, steps) * self.size
        cols = pl.ds(pl.multiple_of(start, self.size), self.size)
        start = 0
        for owner, grad_ref in zip(self.owners, self.grad_refs):
            wide = grad_ref.shape[1]
            values = dot_tn((self.left_ref if owner == 0 else self.right_ref)[:, cols], grad_ref[...])
            yield slice(start, start + wide), values
            start += wide

    def theirs(self, block):
        for span, values in self.product(block, 1 - self.core):
            self.tiles[block, :, span] = values.astype(BF16)
        self.copy(block).start()

    def store(self, block):
        return pltpu.make_async_copy(self.tiles.at[block], self.out_ref.at[block], self.out_sem.at[block])

    def ours(self, block):
        self.copy(block).wait()
        for span, values in self.product(block, self.core):
            self.tiles[block, :, span] = (values + self.came[block, :, span].astype(F32)).astype(BF16)
        self.store(block).start()

    def drain(self):
        for block in range(self.blocks):
            self.store(block).wait()


def pair_shape(left, grads):
    features = left.shape[1]
    return features // (2 * CHUNK), CHUNK, sum(grad.shape[1] for grad in grads)


def pair_scratch(shape):
    dma = pltpu.SemaphoreType.DMA
    return [pltpu.VMEM(shape, BF16), pltpu.VMEM(shape, BF16)] + [dma(shape[:1])] * 3


def mix_grads_kernel(features, left_ref, right_ref, first_ref, second_ref, out_ref, *scratch):
    pair = Pair(features, (0, 1), left_ref, right_ref, (first_ref, second_ref), out_ref, scratch)
    barrier = pltpu.get_barrier_semaphore()
    pl.semaphore_signal(barrier, inc=1, device_id=pair.partner, device_id_type=MESH)
    pl.semaphore_wait(barrier, 1)
    pl.loop(0, pair.blocks)(pair.theirs)
    pl.loop(0, pair.blocks)(pair.ours)
    pair.drain()


def mix_grads(left, right, grads):
    shape = pair_shape(left, grads)
    vmem = pl.BlockSpec(memory_space=pltpu.VMEM)
    out = pl.pallas_call(
        functools.partial(mix_grads_kernel, left.shape[1]),
        out_shape=pltpu.HBM(shape, BF16),
        in_specs=[vmem] * 4,
        out_specs=pl.BlockSpec(memory_space=pltpu.HBM),
        scratch_shapes=pair_scratch(shape),
        compiler_params=pltpu.CompilerParams(collective_id=7, has_side_effects=True, vmem_limit_bytes=24 * 2**20),
        cost_estimate=pl.CostEstimate(
            flops=2 * left.shape[0] * left.shape[1] * shape[2], bytes_accessed=30 * 2**20, transcendentals=0
        ),
        name="mix_grads",
    )(left, right, *grads)
    return out.reshape(shape[0] * shape[1], shape[2])


BLOCK_TIME, TILE_TIME = 2.8, 1.3


def ffn_grads_kernel(
    count, features, left_ref, right_ref, d_gate_ref, d_up_ref, hidden_ref, partial_ref, resid_ref, gate_up_ref,
    out_ref, result_ref, d_partial_ref, *scratch,
):
    *scratch, weights, weights_sem = scratch
    load = pltpu.make_async_copy(gate_up_ref, weights, weights_sem)
    load.start()
    pair = Pair(features, (0, 0, 1), left_ref, right_ref, (d_gate_ref, d_up_ref, hidden_ref), out_ref, scratch[:5])
    tiles = features // TILE
    units = d_gate_ref.shape[1]
    shared = [BLOCK_TIME] * (2 * pair.blocks) + [TILE_TIME] * tiles
    line = Line(count, resid_ref.shape[0], scratch[5:], shared, True, False, latency=FFN_LATENCY)

    def finish(part, local, place):
        result_ref[local, :] = (resid_ref[local, :] + line.total_ref[...]).astype(BF16)

    line.partial_ref, line.finish = partial_ref, finish
    line.greet([pair.partner])

    @pl.loop(0, pair.blocks)
    def _(block):
        line.run_at(0, block, pair.blocks)
        pair.theirs(block)

    @pl.loop(0, pair.blocks)
    def _(block):
        line.run_at(pair.blocks, block, pair.blocks)
        pair.ours(block)

    load.wait()

    @pl.loop(0, tiles)
    def _(tile):
        line.run_at(2 * pair.blocks, tile, tiles)
        cols = pl.ds(pl.multiple_of(tile * TILE, TILE), TILE)
        values = dot_nt(d_gate_ref[...], weights[cols, :units]) + dot_nt(d_up_ref[...], weights[cols, units:])
        d_partial_ref[:, cols] = values.astype(BF16)

    line.run(2 * pair.blocks + tiles)
    line.drain()
    pair.drain()


def ffn_grads(left, right, grads, ffn_partial, resid, gate_up):
    count = lax.axis_size("tensor")
    shape = pair_shape(left, grads)
    vmem = pl.BlockSpec(memory_space=pltpu.VMEM)
    sums, result, d_partial = pl.pallas_call(
        functools.partial(ffn_grads_kernel, count, left.shape[1]),
        out_shape=(jax.ShapeDtypeStruct(shape, BF16), jax.ShapeDtypeStruct(resid.shape, BF16), jax.ShapeDtypeStruct(left.shape, BF16)),
        in_specs=[vmem] * 7 + [pl.BlockSpec(memory_space=pltpu.HBM)],
        out_specs=[pl.BlockSpec(memory_space=pltpu.HBM), vmem, vmem],
        scratch_shapes=pair_scratch(shape)
        + line_scratch(count, resid.shape[0], resid.shape[1], True, False)
        + [pltpu.VMEM(gate_up.shape, BF16), pltpu.SemaphoreType.DMA],
        compiler_params=pltpu.CompilerParams(collective_id=6, has_side_effects=True, vmem_limit_bytes=FFN_MEMORY),
        cost_estimate=pl.CostEstimate(
            flops=2 * left.shape[0] * left.shape[1] * shape[2], bytes_accessed=50 * 2**20, transcendentals=0
        ),
        name="ffn_grads",
    )(left, right, *grads, ffn_partial, resid, pltpu.with_memory_space_constraint(gate_up, pltpu.HBM))
    return sums.reshape(shape[0] * shape[1], shape[2]), result, d_partial


def group_scatter(sums):
    shard = lax.psum_scatter(sums, ("pair", "fsdp"), scatter_dimension=0, tiled=True)
    return with_layout_constraint(shard, Layout(major_to_minor=(0, 1))).astype(F32)


def gather_weights(pieces, axis):
    return lax.all_gather(jnp.concatenate(pieces, axis=1), ("fsdp", "pair", "core"), axis=axis, tiled=True)


def scatter_grads(grads, axis=0):
    return lax.psum_scatter(grads, ("pair", "core", "fsdp"), scatter_dimension=axis, tiled=True).astype(F32)


def body(
    layer_input,
    first_gain,
    w_query,
    w_key,
    w_value,
    w_gating,
    w_beta,
    conv_query,
    conv_key,
    conv_value,
    head_gain,
    w_project,
    second_gain,
    w_gate,
    w_up,
    w_down,
    doc_starts,
    seq_lengths,
    output_grad,
):
    replicas, replica = extents()[0], coordinates()[0]
    width = w_query.shape[1]
    units = w_gate.shape[1]
    heads = w_beta.shape[1]
    head_width = head_gain.shape[0]

    def piece(weight, axis):
        size = weight.shape[axis] // replicas
        return lax.dynamic_slice_in_dim(weight, replica * size, size, axis)

    input_float = layer_input.astype(F32)
    conv_q, conv_k, conv_v = conv_query, conv_key, conv_value
    gain_head = head_gain.astype(F32)[None, :]
    (
        gains, attn_partial, grad_rows, rows_one, mix_full, project_full, gate_up,
        raw, gated, mixed, solve, update, state,
    ) = begin(
        doc_starts, seq_lengths, layer_input, first_gain, second_gain, w_beta, output_grad, (conv_q, conv_k, conv_v),
        gain_head, (w_gating, w_query, w_key, w_value), w_project, (w_gate, w_up),
    )
    gain_one, gain_two = gains[:1], gains[1:]
    late, attn_partial = lax.optimization_barrier((w_down, attn_partial))
    down = gather_weights([piece(late, 1)], 1)
    whole_rows = jax.ShapeDtypeStruct(rows_one.shape, BF16)
    own_rows = jax.ShapeDtypeStruct(layer_input.shape, F32)
    gain_sums = jax.ShapeDtypeStruct((1, layer_input.shape[1]), F32)
    rows_two, resid = line_call(
        middle_kernel, "middle", 2, True, (whole_rows, own_rows), (attn_partial, layer_input, gain_two)
    )
    d_hidden = dot_nt(grad_rows, down)
    both = dot(rows_two, gate_up)
    gate_val, up_val = both[:, :units], both[:, units:]
    gate_sig = jax.nn.sigmoid(gate_val)
    silu_gate = gate_val * gate_sig
    hidden = (silu_gate * up_val).astype(BF16)
    d_gate = (d_hidden * up_val * gate_sig * (1.0 + gate_val * (1.0 - gate_sig))).astype(BF16)
    d_up = (d_hidden * silu_gate).astype(BF16)
    ffn_partial = dot(hidden, down).astype(BF16)
    ffn_sums, result, d_partial = ffn_grads(rows_two, grad_rows, (d_gate, d_up, hidden), ffn_partial, resid, gate_up)
    ffn_shard = group_scatter(ffn_sums)
    d_attn, d_resid, grad_second = line_call(
        turn_kernel, "turn", 3, True, (whole_rows, own_rows, gain_sums), (d_partial, resid, output_grad, gain_two)
    )
    d_gated = dot_nt(d_attn, project_full)
    d_raw, d_conv, d_head = delta_backward(
        doc_starts, seq_lengths, raw, conv_q, conv_k, conv_v, gain_head, mixed, solve, update, state, d_gated
    )
    mix_sums, ffn_shard = lax.optimization_barrier(
        (mix_grads(rows_one, d_attn, (d_raw, gated)), ffn_shard)
    )
    mix_shard = group_scatter(mix_sums)
    project_shard = mix_shard[:, 4 * width + head_width :]
    mix_partial = dot_nt(d_raw, mix_full).astype(BF16)
    input_grad, grad_first = line_call(
        last_kernel, "last", 4, False, (own_rows, gain_sums),
        (mix_partial, layer_input, d_resid, gain_one),
    )
    gain_total, head_total, conv_totals = reduce_small(
        jnp.concatenate([grad_first, grad_second], axis=0), d_head, d_conv
    )
    return (
        result,
        input_grad,
        gain_total[0],
        mix_shard[:, width : 2 * width],
        mix_shard[:, 2 * width : 3 * width],
        mix_shard[:, 3 * width : 4 * width],
        mix_shard[:, :width],
        mix_shard[:, 4 * width : 4 * width + heads],
        conv_totals[:, :width],
        conv_totals[:, width : 2 * width],
        conv_totals[:, 2 * width :],
        head_total[0],
        project_shard.T,
        gain_total[1],
        ffn_shard[:, :units],
        ffn_shard[:, units : 2 * units],
        ffn_shard[:, 2 * units :].T,
    )


def solution(mesh):
    replicas, shards, count = (mesh.shape[name] for name in ("dp", "fsdp", "tensor"))
    mesh = jax.sharding.Mesh(
        mesh.devices.reshape(replicas // 2, 2, shards, count), ("pair", "core", "fsdp", "tensor")
    )
    placed = (
        P(("pair", "core", "fsdp", "tensor"), None),
        P("fsdp"),
        P("fsdp", "tensor"),
        P("fsdp", "tensor"),
        P("fsdp", "tensor"),
        P("fsdp", "tensor"),
        P("fsdp", "tensor"),
        P(None, "tensor"),
        P(None, "tensor"),
        P(None, "tensor"),
        P(),
        P("tensor", "fsdp"),
        P("fsdp"),
        P("fsdp", "tensor"),
        P("fsdp", "tensor"),
        P("tensor", "fsdp"),
        P(("pair", "core", "fsdp"), None),
        P(("pair", "core", "fsdp")),
        P(("pair", "core", "fsdp", "tensor"), None),
    )
    return jax.shard_map(
        body,
        mesh=mesh,
        in_specs=placed,
        out_specs=(
            P(("pair", "core", "fsdp", "tensor"), None),
            P(("pair", "core", "fsdp", "tensor"), None),
            P(("pair", "core", "fsdp")),
            P(("pair", "core", "fsdp"), "tensor"),
            P(("pair", "core", "fsdp"), "tensor"),
            P(("pair", "core", "fsdp"), "tensor"),
            P(("pair", "core", "fsdp"), "tensor"),
            P(("pair", "core", "fsdp"), "tensor"),
            P(None, "tensor"),
            P(None, "tensor"),
            P(None, "tensor"),
            P(),
            P("tensor", ("pair", "core", "fsdp")),
            P(("pair", "core", "fsdp")),
            P(("pair", "core", "fsdp"), "tensor"),
            P(("pair", "core", "fsdp"), "tensor"),
            P("tensor", ("pair", "core", "fsdp")),
        ),
        check_vma=False,
    )
```

```python
import functools
import jax, jax.numpy as jnp
from jax import lax
from jax.experimental import pallas as pl
from jax.experimental.pallas import tpu as pltpu
from jax.sharding import PartitionSpec as P

KERNEL = 4
CHUNK = 256
G, Q, K, V = range(4)
MESH = pl.DeviceIdType.MESH
F32 = jnp.float32
BF16 = jnp.bfloat16


def coordinates():
    replica = lax.axis_index("pair") * 2 + lax.axis_index("core")
    return replica, lax.axis_index("fsdp"), lax.axis_index("tensor")


def extents():
    return lax.axis_size("pair") * 2, lax.axis_size("fsdp"), lax.axis_size("tensor")


def device(replica, shard, place):
    return (lax.div(replica, 2), lax.rem(replica, 2), shard, place)


def dot(left, right):
    return jnp.dot(left, right, preferred_element_type=F32)


def dot_nt(left, right):
    return lax.dot_general(left, right, (((1,), (1,)), ((), ())), preferred_element_type=F32)


def dot_tn(left, right):
    return lax.dot_general(left, right, (((0,), (0,)), ((), ())), preferred_element_type=F32)


def lane_sum(values):
    return jnp.sum(values, axis=-1, keepdims=True)


def document_of(starts_ref, positions):
    total = jnp.zeros_like(positions)
    for entry in range(starts_ref.shape[1]):
        total = total + (positions >= starts_ref[0, entry]).astype(jnp.int32)
    return total


def fill_masks(starts_ref, length_ref, keep_ref, live_ref, carry_ref):
    rows, lanes = live_ref.shape
    place = lax.broadcasted_iota(jnp.int32, (rows, lanes), 0)
    docs = document_of(starts_ref, place)
    for delay in range(1, KERNEL):
        prior = document_of(starts_ref, place - delay)
        keep_ref[delay - 1] = jnp.where((prior == docs) & (place >= delay), 1.0, 0.0)
    live_ref[...] = jnp.where(place < length_ref[0], 1.0, 0.0)
    for edge in range(rows // CHUNK - 1):
        seam = jnp.int32((edge + 1) * CHUNK - 1)
        carry_ref[edge] = jnp.where(docs == document_of(starts_ref, seam), 1.0, 0.0)


def pair_mask(starts_ref, chunk):
    row = lax.broadcasted_iota(jnp.int32, (CHUNK, CHUNK), 0)
    col = lax.broadcasted_iota(jnp.int32, (CHUNK, CHUNK), 1)
    first = chunk * CHUNK
    same = document_of(starts_ref, row + first) == document_of(starts_ref, col + first)
    return same & (row > col), same & (row >= col)


def convolve(raw, taps, keep_ref):
    parts = [raw]
    for delay in range(1, KERNEL):
        parts.append(pltpu.roll(raw, delay, 0) * keep_ref[delay - 1])
    total = parts[0] * taps[KERNEL - 1 : KERNEL]
    for delay in range(1, KERNEL):
        total = total + parts[delay] * taps[KERNEL - 1 - delay : KERNEL - delay]
    return total, parts


def sigmoid(values):
    return 0.5 * jnp.tanh(0.5 * values) + 0.5


def column(values, index):
    lane = lax.broadcasted_iota(jnp.int32, values.shape, 1)
    return lane_sum(jnp.where(lane == index, values, 0.0))


def invert(system):
    size = system[0].shape[0]
    row = lax.broadcasted_iota(jnp.int32, (size, size), 0)
    col = lax.broadcasted_iota(jnp.int32, (size, size), 1)
    apart = row ^ col
    eye = jnp.where(row == col, 1.0, 0.0)
    low = [matrix.astype(BF16) for matrix in system]
    solved = [eye - jnp.where(apart == 1, matrix, 0.0) for matrix in system]
    step = 2
    while step < size:
        level = (apart >= step) & (apart < 2 * step)
        for index, matrix in enumerate(low):
            part = jnp.where(level, matrix, 0.0)
            held = solved[index].astype(BF16)
            solved[index] = solved[index] - dot(dot(held, part).astype(BF16), held)
        step *= 2
    refined = []
    for matrix, high, inverse in zip(system, low, solved):
        rest = (matrix - high.astype(F32)).astype(BF16)
        head = inverse.astype(BF16)
        tail = (inverse - head.astype(F32)).astype(BF16)
        product = dot(high, head) + dot(rest, head) + dot(high, tail)
        residue = eye - inverse - product
        refined.append(inverse + dot(head, residue.astype(BF16)))
    return refined


def unit_rows(conv):
    gate = sigmoid(conv)
    act = conv * gate
    scale = lax.rsqrt(lane_sum(act * act) + 1e-06)
    return gate, act, scale


TILE = 256
PROJECT_TILE = 512
ATTEND_TIMES = (1.2, 1.5, 0.9)


def backward_kernel(
    starts_ref, length_ref, raw_ref, conv_q_ref, conv_k_ref, conv_v_ref, gain_ref,
    mixed_ref, solve_ref, update_ref, state_ref, grad_ref,
    d_raw_ref, d_conv_ref, d_gain_ref,
    keep_ref, live_ref, carry_ref, strict_ref, incl_ref, d_query_ref, d_key_ref, d_value_ref, d_rate_ref,
):
    rows, head_width = live_ref.shape
    width = mixed_ref.shape[1]
    chunks = rows // CHUNK
    fill_masks(starts_ref, length_ref, keep_ref, live_ref, carry_ref)
    for chunk in range(chunks):
        strict, incl = pair_mask(starts_ref, chunk)
        strict_ref[chunk] = jnp.where(strict, 1.0, 0.0)
        incl_ref[chunk] = jnp.where(incl, 1.0, 0.0)
    d_gain_ref[...] = jnp.zeros_like(d_gain_ref)
    d_raw_ref[:, 4 * width :] = jnp.zeros((rows, head_width), BF16)

    @pl.loop(0, width // head_width)
    def _(head):
        start = pl.multiple_of(head * head_width, head_width)

        def place(index):
            return pl.ds(pl.multiple_of(index * width + start, head_width), head_width)

        cols = pl.ds(start, head_width)
        live = live_ref[...]
        mixed = mixed_ref[:, cols]
        norm = lax.rsqrt(lane_sum(mixed * mixed) * (1.0 / head_width) + 1e-05)
        gating = raw_ref[:, place(G)]
        gate = sigmoid(gating)
        normal = mixed * norm
        grad = grad_ref[:, cols].astype(F32) * live
        grad_gain = grad * gain_ref[...]
        swish = gating * gate
        d_raw_ref[:, place(G)] = (grad_gain * normal * gate * (1.0 + gating - swish)).astype(BF16)
        d_gain_ref[...] += jnp.sum(grad * normal * swish, axis=0, keepdims=True)
        d_normal = grad_gain * swish
        d_mixed = norm * (d_normal - normal * (lane_sum(d_normal * normal) * (1.0 / head_width)))
        d_mixed_low = d_mixed.astype(BF16)

        conv_q, parts_q = convolve(raw_ref[:, place(Q)], conv_q_ref[:, cols].astype(F32), keep_ref)
        gate_q, act_q, scale_q = unit_rows(conv_q)
        unit_q = act_q * scale_q
        query = unit_q.astype(BF16)
        conv_k, parts_k = convolve(raw_ref[:, place(K)], conv_k_ref[:, cols].astype(F32), keep_ref)
        gate_k, act_k, scale_k = unit_rows(conv_k)
        keyed = act_k * scale_k
        key_low = keyed.astype(BF16)
        conv_v, parts_v = convolve(raw_ref[:, place(V)], conv_v_ref[:, cols].astype(F32), keep_ref)
        gate_v = sigmoid(conv_v)
        valued = conv_v * gate_v
        sig = sigmoid(column(raw_ref[:, 4 * width :], head))
        rate = sig * live
        scaled_value = (valued * rate).astype(BF16)
        scaled_key = keyed * rate

        d_memory = None
        for chunk in range(chunks - 1, -1, -1):
            span = slice(chunk * CHUNK, (chunk + 1) * CHUNK)
            key_c, query_c, d_mixed_c = key_low[span], query[span], d_mixed_low[span]
            solve = solve_ref[head * chunks + chunk]
            update = update_ref[span, cols]
            incl, strict = incl_ref[chunk], strict_ref[chunk]
            score = (dot_nt(query_c, key_c) * incl).astype(BF16)
            d_update = dot_tn(score, d_mixed_c)
            d_key = None
            if d_memory is not None:
                last = carry_ref[chunk][span]
                d_memory_low = d_memory.astype(BF16)
                d_update = d_update + dot((keyed[span] * last).astype(BF16), d_memory_low)
                d_key = last * dot_nt(update, d_memory_low)
            d_update_low = d_update.astype(BF16)
            d_score = (dot_nt(d_mixed_c, update) * incl).astype(BF16)
            d_query = dot(d_score, key_c)
            d_key_score = dot_tn(d_score, query_c)
            d_key = d_key_score if d_key is None else d_key + d_key_score
            if chunk == 0:
                right = scaled_value[span]
                solved = dot(solve, right)
                d_right = dot_tn(solve, d_update_low)
                d_value_in = d_right
                d_rate = lane_sum(d_value_in * valued[span])
            else:
                carry = carry_ref[chunk - 1][span]
                state = state_ref[head * (chunks - 1) + chunk - 1]
                right = jnp.concatenate([scaled_value[span], (scaled_key[span] * carry).astype(BF16)], axis=1)
                solved = dot(solve, right)
                d_solved_key = -dot_nt(d_update_low, state)
                d_right = dot_tn(solve, jnp.concatenate([d_update_low, d_solved_key.astype(BF16)], axis=1))
                d_value_in = d_right[:, :head_width]
                d_key_in = d_right[:, head_width:] * carry
                carried = (carry * d_mixed[span]).astype(BF16)
                d_query = d_query + dot_nt(carried, state)
                d_key = d_key + rate[span] * d_key_in
                d_rate = lane_sum(d_value_in * valued[span] + d_key_in * keyed[span])
                fresh = dot_tn(query_c, carried) - dot_tn(solved[:, head_width:].astype(BF16), d_update_low)
                if d_memory is None:
                    d_memory = fresh
                else:
                    d_memory = d_memory * carry[CHUNK - 1 :] + fresh
            d_system = dot_nt(d_right.astype(BF16), solved.astype(BF16)) * -strict
            pair = dot_nt(key_c, key_c)
            d_rate = d_rate + lane_sum(d_system * pair)
            wide = jnp.concatenate([rate[span]] * (CHUNK // head_width), axis=1)
            d_pair = (d_system * wide).astype(BF16)
            d_key = d_key + dot(d_pair, key_c) + dot_tn(d_pair, key_c)
            d_query_ref[span] = d_query
            d_key_ref[span] = d_key
            d_value_ref[span] = rate[span] * d_value_in
            d_rate_ref[span] = jnp.broadcast_to(d_rate, (CHUNK, head_width))

        lane = lax.broadcasted_iota(jnp.int32, (rows, head_width), 1)
        d_beta = d_rate_ref[...] * rate * (1.0 - sig)
        tail = d_raw_ref[:, 4 * width :]
        d_raw_ref[:, 4 * width :] = jnp.where(lane == head, d_beta.astype(BF16), tail)

        def conv_back(index, d_conv, parts, taps):
            sums = [jnp.sum(d_conv * part, axis=0, keepdims=True) for part in parts]
            for delay in range(KERNEL):
                tap = KERNEL - 1 - delay
                d_conv_ref[tap : tap + 1, place(index - 1)] = sums[delay]
            total = d_conv * taps[KERNEL - 1 : KERNEL]
            for delay in range(1, KERNEL):
                tap = KERNEL - 1 - delay
                back = pltpu.roll(d_conv * keep_ref[delay - 1], rows - delay, 0)
                total = total + back * taps[tap : tap + 1]
            d_raw_ref[:, place(index)] = total.astype(BF16)

        def unit_back(d_unit, unit, scale, conv, act, gate):
            d_act = scale * (d_unit - unit * lane_sum(d_unit * unit))
            return d_act * gate * (1.0 + conv - act)

        conv_back(Q, unit_back(d_query_ref[...], unit_q, scale_q, conv_q, act_q, gate_q), parts_q, conv_q_ref[:, cols].astype(F32))
        conv_back(K, unit_back(d_key_ref[...], keyed, scale_k, conv_k, act_k, gate_k), parts_k, conv_k_ref[:, cols].astype(F32))
        d_conv_v = d_value_ref[...] * gate_v * (1.0 + conv_v - valued)
        conv_back(V, d_conv_v, parts_v, conv_v_ref[:, cols].astype(F32))


def delta_backward(starts, length, raw, conv_q, conv_k, conv_v, gain, mixed, solve, update, state, grad):
    rows = raw.shape[0]
    head_width = gain.shape[-1]
    width = conv_q.shape[1]
    heads, chunks = width // head_width, rows // CHUNK
    vmem = pl.BlockSpec(memory_space=pltpu.VMEM)
    smem = pl.BlockSpec(memory_space=pltpu.SMEM)
    return pl.pallas_call(
        backward_kernel,
        out_shape=(
            jax.ShapeDtypeStruct((rows, 4 * width + head_width), BF16),
            jax.ShapeDtypeStruct((KERNEL, 3 * width), F32),
            jax.ShapeDtypeStruct((1, head_width), F32),
        ),
        in_specs=[smem, smem] + [vmem] * 10,
        out_specs=[vmem] * 3,
        scratch_shapes=[
            pltpu.VMEM((KERNEL - 1, rows, head_width), F32),
            pltpu.VMEM((rows, head_width), F32),
            pltpu.VMEM((chunks - 1, rows, head_width), F32),
            pltpu.VMEM((chunks, CHUNK, CHUNK), F32),
            pltpu.VMEM((chunks, CHUNK, CHUNK), F32),
        ]
        + [pltpu.VMEM((rows, head_width), F32)] * 4,
        compiler_params=pltpu.CompilerParams(vmem_limit_bytes=18 * 2**20),
        cost_estimate=pl.CostEstimate(
            flops=2 * 12 * heads * chunks * CHUNK**3, bytes_accessed=16 * 2**20, transcendentals=0
        ),
        name="delta_backward",
    )(starts, length, raw, conv_q, conv_k, conv_v, gain, mixed, solve, update, state, grad)


def reduce_kernel(
    group_size, line_size, fsdp_size, gain_ref, head_ref, conv_ref, gain_out, head_out, conv_out,
    line_gain, line_head, stage, group_gain, group_conv,
    line_send, line_recv, group_send, group_recv,
):
    dp, fsdp, tensor = coordinates()
    group = dp * fsdp_size + fsdp
    size = gain_out.shape[1]

    def line_peer(shift):
        return device(dp, fsdp, lax.rem(tensor + shift, line_size))

    def group_peer(shift):
        peer = lax.rem(group + shift, group_size)
        return peer, device(lax.div(peer, fsdp_size), lax.rem(peer, fsdp_size), tensor)

    barrier = pltpu.get_barrier_semaphore()
    for shift in range(1, line_size):
        pl.semaphore_signal(barrier, inc=1, device_id=line_peer(shift), device_id_type=MESH)
    for shift in range(1, group_size):
        pl.semaphore_signal(barrier, inc=1, device_id=group_peer(shift)[1], device_id_type=MESH)
    pl.semaphore_wait(barrier, line_size + group_size - 2)

    copies = []
    for shift in range(1, line_size):
        for part, (source, target) in enumerate(((gain_ref, line_gain), (head_ref, line_head))):
            copy = pltpu.make_async_remote_copy(
                src_ref=source, dst_ref=target.at[shift - 1],
                send_sem=line_send.at[shift - 1, part], recv_sem=line_recv.at[shift - 1, part],
                device_id=line_peer(shift), device_id_type=MESH,
            )
            copy.start()
            copies.append(copy)
    conv_copies = []
    for shift in range(1, group_size):
        copy = pltpu.make_async_remote_copy(
            src_ref=conv_ref, dst_ref=group_conv.at[shift - 1],
            send_sem=group_send.at[shift - 1, 1], recv_sem=group_recv.at[shift - 1, 1],
            device_id=group_peer(shift)[1], device_id_type=MESH,
        )
        copy.start()
        conv_copies.append(copy)
    for copy in copies:
        copy.wait()
    gain = gain_ref[...]
    head = head_ref[...]
    for shift in range(1, line_size):
        gain = gain + line_gain[shift - 1]
        head = head + line_head[shift - 1]
    for peer in range(group_size):
        stage[peer] = jnp.zeros(stage.shape[1:], F32)
        stage[peer, :2, :size] = gain[:, peer * size : (peer + 1) * size]
        stage[peer, 2:3, : head.shape[1]] = head
    for copy in conv_copies:
        copy.wait()
    conv = conv_ref[...]
    for shift in range(1, group_size):
        conv = conv + group_conv[shift - 1]
    conv_out[...] = conv
    copies = []
    for shift in range(1, group_size):
        peer, where = group_peer(shift)
        copy = pltpu.make_async_remote_copy(
            src_ref=stage.at[peer], dst_ref=group_gain.at[shift - 1],
            send_sem=group_send.at[shift - 1, 0], recv_sem=group_recv.at[shift - 1, 0],
            device_id=where, device_id_type=MESH,
        )
        copy.start()
        copies.append(copy)
    for copy in copies:
        copy.wait()
    total = stage[group]
    for shift in range(1, group_size):
        total = total + group_gain[shift - 1]
    gain_out[...] = total[:2, :size]
    head_out[...] = total[2:3, : head.shape[1]]


def reduce_small(gain, head, conv):
    replicas, fsdp_size, line_size = extents()
    group_size = replicas * fsdp_size
    size = gain.shape[1] // group_size
    pad = max(size, head.shape[1])
    vmem = pl.BlockSpec(memory_space=pltpu.VMEM)
    dma = pltpu.SemaphoreType.DMA
    return pl.pallas_call(
        functools.partial(reduce_kernel, group_size, line_size, fsdp_size),
        out_shape=(
            jax.ShapeDtypeStruct((2, size), F32),
            jax.ShapeDtypeStruct(head.shape, F32),
            jax.ShapeDtypeStruct(conv.shape, F32),
        ),
        in_specs=[vmem] * 3,
        out_specs=[vmem] * 3,
        scratch_shapes=[
            pltpu.VMEM((line_size - 1,) + gain.shape, F32),
            pltpu.VMEM((line_size - 1,) + head.shape, F32),
            pltpu.VMEM((group_size, 8, pad), F32),
            pltpu.VMEM((group_size - 1, 8, pad), F32),
            pltpu.VMEM((group_size - 1,) + conv.shape, F32),
            dma((line_size - 1, 2)),
            dma((line_size - 1, 2)),
            dma((group_size - 1, 2)),
            dma((group_size - 1, 2)),
        ],
        compiler_params=pltpu.CompilerParams(collective_id=1, has_side_effects=True, vmem_limit_bytes=8 * 2**20),
        name="reduce_small",
    )(gain, head, conv)


def plan(count, parts, sums, rows, shared, unit, latency=1.5):
    backlog, add, end = 1.5, 0.15 + 0.8 / parts, 0.5 + 3.0 / parts
    rank = {"spread": 0, "relay": 0, "finish": 1, "forward": 2, "inject": 3}
    clock = [0.0] * count
    free, come = {}, [{} for _ in range(count)]
    todo = [set() for _ in range(count)]
    done = [0] * count
    at = [0] * count
    tasks = [[[] for _ in range(len(shared) + 1)] for _ in range(count)]
    own_finish = sums and not any(isinstance(step, tuple) for step in shared)
    for place in range(count):
        for part in range(parts):
            for step in (1, -1):
                behind = 0 <= place - step < count
                for slot in range(count - 1) if sums else ():
                    owner = count - 1 - slot if step > 0 else slot
                    if (owner - place) * step > 0:
                        todo[place].add(("forward" if behind else "inject", step, slot, part))
                for distance in range(1, count) if rows else ():
                    if 0 <= place - step * distance < count:
                        todo[place].add(("relay", step, distance, part))
            if rows and not sums:
                todo[place].add(("spread", 0, 0, part))
            if own_finish:
                todo[place].add(("finish", 0, 0, part))

    def ready(place, task):
        kind, step, slot, part = task
        if kind == "inject":
            return max(0.0, free.get((place, step), 0.0) - backlog * unit)
        if kind == "spread":
            return max([0.0] + [free.get((place, way), 0.0) - backlog * unit for way in (1, -1)])
        if kind == "forward":
            return come[place].get(("sum", step, slot, part))
        if kind == "relay":
            return come[place].get(("row", step, slot, part))
        if part != done[place]:
            return None
        times = [0.0]
        for way in (1, -1):
            if 0 <= place - way < count:
                times.append(come[place].get(("sum", way, count - 1 - place if way > 0 else place, part)))
        return None if None in times else max(times)

    def send(place, step, key):
        if 0 <= place + step < count:
            free[place, step] = max(clock[place], free.get((place, step), 0.0)) + unit
            come[place + step][key] = free[place, step] + latency

    def choices(place):
        found = [(ready(place, task), rank[task[0]], task[3], task[2], task[1], task) for task in todo[place]]
        found = [(max(clock[place], entry[0]),) + entry[1:] for entry in found if entry[0] is not None]
        if at[place] < len(shared):
            step = shared[at[place]]
            when = ready(place, ("finish", 0, 0, step[1])) if isinstance(step, tuple) else clock[place]
            if when is not None:
                found.append((max(when, clock[place]), 1 if isinstance(step, tuple) else 9, 0, 0, 0, step))
        return min(found, key=lambda entry: entry[:5]) if found else None

    while True:
        best = None
        for place in range(count):
            choice = choices(place)
            if choice is not None and (best is None or choice[0] < best[0][0]):
                best = (choice, place)
        if best is None:
            return max(clock), tasks
        choice, place = best
        clock[place] = choice[0]
        task = choice[5]
        if isinstance(task, float):
            clock[place] += task
            at[place] += 1
            continue
        if len(task) == 2:
            at[place] += 1
        else:
            todo[place].discard(task)
            tasks[place][at[place]].append(task)
        kind, step, slot, part = task if len(task) == 4 else ("finish", 0, 0, task[1])
        if kind in ("inject", "forward"):
            clock[place] += add if kind == "forward" else 0.02
            send(place, step, ("sum", step, slot, part))
        elif kind == "relay":
            clock[place] += 0.05
            if slot < count - 1:
                send(place, step, ("row", step, slot + 1, part))
        else:
            if kind == "finish":
                done[place] += 1
                clock[place] += end
            if rows:
                for way in (1, -1):
                    send(place, way, ("row", way, 1, part))


PARTS = 4
LANES = 512
FFN_MEMORY = 52 * 2**20
TURN_PARTS = 4
ATTEND_PARTS = 4
ATTEND_LATENCY, FFN_LATENCY = 1.5, 1.5
UNIT = 11.3


def rms_scale(values):
    return lax.rsqrt(jnp.mean(values * values, axis=-1, keepdims=True) + 1e-05)


def rms_back(values, scale_rows, gain, grad):
    scaled_grad = grad * gain
    inner = jnp.mean(scaled_grad * values, axis=-1, keepdims=True)
    return scale_rows * (scaled_grad - values * scale_rows * scale_rows * inner)


class Line:

    def __init__(self, count, rows, scratch, shared, sums, spreads, parts=PARTS, latency=1.5):
        self.count, self.rows, self.parts = count, rows, parts
        self.part = rows // parts
        scratch = list(scratch)
        self.sums, self.sends = {}, {}
        if sums:
            for step in (1, -1):
                self.sums[step] = [scratch.pop(0) for _ in range(4)]
            self.total_ref = scratch.pop(0)
        if spreads:
            for step in (1, -1):
                self.sends[step] = [scratch.pop(0) for _ in range(2)]
        self.replica, self.shard, self.place = coordinates()
        self.tasks = plan(count, parts, sums, spreads, shared, UNIT / parts, latency)[1]
        self.started = [[] for _ in range(count)]
        self.partial_ref = self.rows_ref = self.source_ref = self.finish = None

    def greet(self, others=()):
        barrier = pltpu.get_barrier_semaphore()
        for step in (1, -1):
            @pl.when(self.place < self.count - 1 if step > 0 else self.place > 0)
            def _():
                pl.semaphore_signal(
                    barrier, inc=1, device_id=device(self.replica, self.shard, self.place + step), device_id_type=MESH
                )
        for other in others:
            pl.semaphore_signal(barrier, inc=1, device_id=other, device_id_type=MESH)
        ends = (self.place == 0).astype(jnp.int32) + (self.place == self.count - 1).astype(jnp.int32)
        pl.semaphore_wait(barrier, 2 - ends + len(others))

    def span(self, owner, part):
        return pl.ds(pl.multiple_of(owner * self.rows + part * self.part, self.part), self.part)

    def sum_copy(self, source, step, slot, part):
        recv, _, send_sem, recv_sem = self.sums[step]
        return pltpu.make_async_remote_copy(
            src_ref=source, dst_ref=recv.at[slot, part],
            send_sem=send_sem.at[slot, part], recv_sem=recv_sem.at[slot, part],
            device_id=device(self.replica, self.shard, self.place + step), device_id_type=MESH,
        )

    def row_copy(self, step, owner, distance, part, source=None):
        send_sem, recv_sem = self.sends[step]
        where = self.rows_ref.at[self.span(owner, part)]
        return pltpu.make_async_remote_copy(
            src_ref=where if source is None else source, dst_ref=where,
            send_sem=send_sem.at[distance, part], recv_sem=recv_sem.at[distance, part],
            device_id=device(self.replica, self.shard, self.place + step), device_id_type=MESH,
        )

    def emit(self, place, task):
        kind, step, slot, part = task
        if kind in ("inject", "forward"):
            recv, send, _, _ = self.sums[step]
            owner = self.count - 1 - slot if step > 0 else slot
            source = self.partial_ref.at[self.span(owner, part)]
            if kind == "forward":
                self.sum_copy(source, step, slot, part).wait_recv()

                @pl.loop(0, self.partial_ref.shape[1] // LANES)
                def _(step_index):
                    cols = pl.ds(pl.multiple_of(step_index * LANES, LANES), LANES)
                    mine = self.partial_ref[self.span(owner, part), cols].astype(F32)
                    send[slot, part, :, cols] = (mine + recv[slot, part, :, cols].astype(F32)).astype(BF16)

                source = send.at[slot, part]
            copy = self.sum_copy(source, step, slot, part)
            copy.start()
        elif kind == "relay":
            owner = place - step * slot
            self.row_copy(step, owner, slot - 1, part).wait_recv()
            if slot < self.count - 1 and 0 <= place + step < self.count:
                self.row_copy(step, owner, slot, part).start()
        elif kind == "spread":
            self.spread_from(place, part)
        else:
            self.collect(part)
            self.finish(part, pl.ds(part * self.part, self.part), None)

    def spread_from(self, place, part):
        for step in (1, -1):
            if 0 <= place + step < self.count:
                source = None if self.source_ref is None else self.source_ref.at[pl.ds(part * self.part, self.part)]
                self.row_copy(step, place, 0, part, source).start()

    def run(self, index):
        for place in range(self.count):
            tasks = self.tasks[place][index]
            if tasks:
                @pl.when(self.place == place)
                def _():
                    for task in tasks:
                        self.emit(place, task)

    def run_at(self, base, step, count, stride=1):
        for index in range(count):
            if any(tasks[base + stride * index] for tasks in self.tasks):
                @pl.when(step == index)
                def _():
                    self.run(base + stride * index)

    def collect(self, part):
        places = []
        for step in (1, -1):
            recv, send, _, _ = self.sums[step]
            slot = self.count - 1 - self.place if step > 0 else self.place
            has = self.place > 0 if step > 0 else self.place < self.count - 1

            @pl.when(has)
            def _():
                self.sum_copy(send.at[0, part], step, slot, part).wait_recv()

            places.append((recv, slot, has))

        @pl.loop(0, self.partial_ref.shape[1] // LANES)
        def _(index):
            cols = pl.ds(pl.multiple_of(index * LANES, LANES), LANES)
            self.total_ref[:, cols] = self.partial_ref[self.span(self.place, part), cols].astype(F32)
            for recv, slot, has in places:
                @pl.when(has)
                def _():
                    self.total_ref[:, cols] += recv[slot, part, :, cols].astype(F32)

    def finish_all(self):
        @pl.loop(0, self.parts)
        def _(part):
            self.run_at(0, part, self.parts)
            self.collect(part)
            local = pl.ds(pl.multiple_of(part * self.part, self.part), self.part)
            self.finish(part, local, self.span(self.place, part))
            if self.sends:
                for place in range(self.count):
                    @pl.when(self.place == place)
                    def _():
                        self.spread_from(place, part)

        self.run(self.parts)
        self.drain()

    def drain(self):
        for place in range(self.count):
            @pl.when(self.place == place)
            def _():
                for part in range(self.parts):
                    for step in (1, -1):
                        if self.sums:
                            send = self.sums[step][1]
                            for slot in range(self.count - 1):
                                owner = self.count - 1 - slot if step > 0 else slot
                                if (owner - place) * step > 0:
                                    self.sum_copy(send.at[slot, part], step, slot, part).wait_send()
                        if self.sends and 0 <= place + step < self.count:
                            for distance in range(self.count - 1):
                                owner = place - step * distance
                                if 0 <= owner < self.count:
                                    self.row_copy(step, owner, distance, part).wait_send()


def line_scratch(count, rows, features, sums, spreads, parts=PARTS):
    dma = pltpu.SemaphoreType.DMA
    slots = (count - 1, parts)
    scratch = []
    if sums:
        for _ in range(2):
            scratch += [pltpu.VMEM(slots + (rows // parts, features), BF16)] * 2 + [dma(slots)] * 2
        scratch.append(pltpu.VMEM((rows // parts, features), F32))
    if spreads:
        scratch += [dma(slots)] * 4
    return scratch


def finishes(parts):
    return [("finish", part) for part in range(parts)]


def middle_kernel(count, partial_ref, input_ref, gain_ref, rows_ref, resid_ref, *scratch):
    line = Line(count, input_ref.shape[0], scratch, finishes(TURN_PARTS), True, True, TURN_PARTS)

    def finish(part, local, place):
        resid = input_ref[local, :].astype(F32) + line.total_ref[...]
        resid_ref[local, :] = resid
        rows_ref[place, :] = (resid * rms_scale(resid) * gain_ref[...]).astype(BF16)

    line.partial_ref, line.rows_ref, line.finish = partial_ref, rows_ref, finish
    line.greet()
    line.finish_all()


def turn_kernel(count, partial_ref, resid_ref, grad_ref, gain_ref, rows_ref, d_resid_ref, d_gain_ref, *scratch):
    line = Line(count, resid_ref.shape[0], scratch, finishes(TURN_PARTS), True, True, TURN_PARTS)

    def finish(part, local, place):
        resid, total = resid_ref[local, :], line.total_ref[...]
        scale = rms_scale(resid)
        sums = jnp.sum(total * resid * scale, axis=0, keepdims=True)
        d_gain_ref[...] += sums
        d_resid = grad_ref[local, :].astype(F32) + rms_back(resid, scale, gain_ref[...], total)
        d_resid_ref[local, :] = d_resid
        rows_ref[place, :] = d_resid.astype(BF16)

    d_gain_ref[...] = jnp.zeros_like(d_gain_ref)
    line.partial_ref, line.rows_ref, line.finish = partial_ref, rows_ref, finish
    line.greet()
    line.finish_all()


def last_kernel(count, partial_ref, input_ref, d_resid_ref, gain_ref, d_input_ref, d_gain_ref, *scratch):
    line = Line(count, input_ref.shape[0], scratch, finishes(PARTS), True, False)

    def finish(part, local, place):
        values, total = input_ref[local, :].astype(F32), line.total_ref[...]
        scale = rms_scale(values)
        sums = jnp.sum(total * values * scale, axis=0, keepdims=True)
        d_gain_ref[...] += sums
        d_input_ref[local, :] = d_resid_ref[local, :] + rms_back(values, scale, gain_ref[...], total)

    d_gain_ref[...] = jnp.zeros_like(d_gain_ref)
    line.partial_ref, line.finish = partial_ref, finish
    line.greet()
    line.finish_all()


def line_call(kernel, name, ident, spreads, out_shape, operands):
    count = lax.axis_size("tensor")
    partial_rows, features = operands[0].shape
    vmem = pl.BlockSpec(memory_space=pltpu.VMEM)
    return pl.pallas_call(
        functools.partial(kernel, count),
        out_shape=out_shape,
        in_specs=[vmem] * len(operands),
        out_specs=[vmem] * len(out_shape),
        scratch_shapes=line_scratch(
            count, partial_rows // count, features, True, spreads, TURN_PARTS if spreads else PARTS
        ),
        compiler_params=pltpu.CompilerParams(
            collective_id=ident, has_side_effects=True, vmem_limit_bytes=16 * 2**20
        ),
        cost_estimate=pl.CostEstimate(flops=10**9, bytes_accessed=60 * 2**20, transcendentals=0),
        name=name,
    )(*operands)


def begin_kernel(
    sizes, starts_ref, length_ref, input_ref, own_gains_ref, beta_ref, own_grad_ref,
    conv_q_ref, conv_k_ref, conv_v_ref, gain_ref,
    gating_ref, query_ref, key_ref, value_ref, project_ref, gate_ref, up_ref,
    gains_ref, partial_ref, grad_rows_ref, rows_ref, mix_ref, whole_project_ref, gate_up_ref,
    raw_ref, gated_ref, mixed_ref, solve_ref, update_ref, state_ref,
    all_rows, normed, mix_all, project_all, ffn_all, raw_all, gated_all, mixed_all, solve_all, update_all, state_all,
    keep_ref, live_ref, carry_ref, strict_ref, incl_ref,
    all_gains, all_beta, local_sem, store_sem, small_send, small_recv,
    first_send, first_recv, second_send, second_recv, third_send, third_recv, *row_sems,
):
    replicas, shards, count = sizes
    rows = input_ref.shape[0]
    width = query_ref.shape[1]
    heads = beta_ref.shape[0]
    share = query_ref.shape[0]
    units = gate_ref.shape[1]
    half = share // 2
    streams = [(ref, mix_all, False, 0, share, index * width) for index, ref in enumerate((gating_ref, query_ref, key_ref, value_ref))]
    streams.append((project_ref, project_all, True, 0, width, 0))
    for first_row in (0, half):
        for index, ref in enumerate((gate_ref, up_ref)):
            streams.append((ref, ffn_all, False, first_row, half, index * units))
    count_streams = len(streams)
    pairs = replicas // 2
    line = Line(count, rows, row_sems[:4], [], False, True, parts=2)
    line.rows_ref, line.source_ref = all_rows, input_ref
    replica, shard, place = line.replica, line.shard, line.place
    partner = replica + 1 - 2 * lax.rem(replica, 2)

    def across(step):
        return lax.rem(replica + 2 * step, replicas)

    def shard_at(shift):
        return lax.rem(shard + shift, shards)

    def held(stream, owner, part):
        ref, whole, spread_cols, first_row, height, col = streams[stream]
        size = height // replicas
        if spread_cols:
            return whole.at[
                pl.ds(pl.multiple_of(part * size, size), size), pl.ds(pl.multiple_of(owner * share, 128), share)
            ]
        start = owner * share + first_row + part * size
        return whole.at[pl.ds(pl.multiple_of(start, size), size), pl.ds(col, ref.shape[1])]

    def own(stream, part):
        ref, _, spread_cols, first_row, height, _ = streams[stream]
        size = height // replicas
        return ref.at[pl.ds(pl.multiple_of(first_row + part * size, size), size), :]

    def remote(source, target, send, recv, where):
        return pltpu.make_async_remote_copy(
            src_ref=source, dst_ref=target, send_sem=send, recv_sem=recv, device_id=where, device_id_type=MESH
        )

    def first(shift, stream, owner):
        return remote(
            own(stream, replica), held(stream, owner, replica),
            first_send.at[shift - 1, stream], first_recv.at[shift - 1, stream],
            device(replica, shard_at(shift), place),
        )

    def second(shift, step, stream, part):
        where = held(stream, shard_at(shards - shift), part)
        return remote(
            where, where, second_send.at[shift - 1, step - 1, stream], second_recv.at[shift - 1, step - 1, stream],
            device(across(step), shard, place),
        )

    def third(shift, step, stream, part):
        where = held(stream, shard_at(shards - shift), part)
        return remote(
            where, where, third_send.at[shift - 1, step, stream], third_recv.at[shift - 1, step, stream],
            device(partner, shard, place),
        )

    def spread(part):
        for there in range(count):
            @pl.when(place == there)
            def _():
                line.spread_from(there, part)

    def relay(distance, part):
        for there in range(count):
            @pl.when(place == there)
            def _():
                for step in (1, -1):
                    if 0 <= there - step * distance < count:
                        line.emit(there, ("relay", step, distance, part))

    features = share * shards
    cols = pl.ds(pl.multiple_of(shard * share, 128), share)
    smalls = ((own_gains_ref, all_gains.at[:, cols]), (beta_ref, all_beta.at[:, cols]))

    def small(shift, index):
        source, target = smalls[index]
        return remote(
            source, target, small_send.at[shift - 1, index], small_recv.at[shift - 1, index],
            device(replica, shard_at(shift), place),
        )

    others = [device(replica, shard_at(shift), place) for shift in range(1, shards)]
    others += [device(across(step), shard, place) for step in range(1, pairs)] + [device(partner, shard, place)]
    line.greet(others)
    for shift in range(1, shards):
        for index in range(len(smalls)):
            small(shift, index).start()
    for part in range(2):
        spread(part)
    for stream in range(count_streams):
        for shift in range(1, shards):
            first(shift, stream, shard).start()
    locals_ = [pltpu.make_async_copy(source, target, local_sem.at[index]) for index, (source, target) in enumerate(smalls)]
    own_rows = pl.ds(pl.multiple_of(shard * share, share), share)
    for index, ref in enumerate((gating_ref, query_ref, key_ref, value_ref)):
        locals_.append(pltpu.make_async_copy(
            ref, mix_all.at[own_rows, pl.ds(index * width, width)], local_sem.at[2 + index],
        ))
    locals_.append(pltpu.make_async_copy(project_ref, project_all.at[:, cols], local_sem.at[6]))
    for index, ref in enumerate((gate_ref, up_ref)):
        locals_.append(pltpu.make_async_copy(
            ref, ffn_all.at[own_rows, pl.ds(index * units, units)], local_sem.at[7 + index],
        ))
    for copy in locals_:
        copy.start()
    for copy in locals_[:2]:
        copy.wait()
    for shift in range(1, shards):
        for index in range(len(smalls)):
            small(shift, index).wait()
    gains_ref[...] = all_gains[...].astype(F32)
    lanes = mix_all.shape[1] - 4 * width
    beta = jnp.concatenate([all_beta[...].astype(F32), jnp.zeros((lanes - heads, features), F32)], axis=0)
    mix_all[:, 4 * width :] = beta.T.astype(BF16)

    def normalize(source, start, size):
        values = source[pl.ds(start, size), :].astype(F32)
        return (values * rms_scale(values) * gains_ref[0:1, :]).astype(BF16)

    normed[line.span(place, 0), :] = normalize(input_ref, 0, line.part)
    normed[line.span(place, 1), :] = normalize(input_ref, line.part, line.part)

    def serve(turn):
        if turn < count_streams:
            for shift in range(1, shards):
                first(shift, turn, shard_at(shards - shift)).wait_recv()
                for step in range(1, pairs):
                    second(shift, step, turn, replica).start()
                third(shift, 0, turn, replica).start()
        distance, part = turn // 2 + 1, turn % 2
        if distance < count:
            relay(distance, part)
        if 0 <= turn - 1 < count_streams:
            for shift in range(1, shards):
                for step in range(1, pairs):
                    came = across(pairs - step)
                    second(shift, step, turn - 1, came).wait_recv()
                    third(shift, step, turn - 1, came).start()
        if distance < count:
            for step in (1, -1):
                owner = place - step * distance
                inside = owner >= 0 if step > 0 else owner < count

                @pl.when(inside)
                def _():
                    start = pl.multiple_of(owner * rows + part * line.part, line.part)
                    normed[line.span(owner, part), :] = normalize(all_rows, start, line.part)
        if 0 <= turn - 2 < count_streams:
            for shift in range(1, shards):
                for step in range(pairs):
                    third(shift, step, turn - 2, replica).wait_recv()
    ready = max(6, 2 * (count - 1))
    for turn in range(ready):
        serve(turn)
    for copy in locals_[2:]:
        copy.wait()

    rows, head_width = live_ref.shape
    chunks = rows // CHUNK
    heads = width // head_width
    tiles, ends = 4 * width // TILE, features // PROJECT_TILE
    shared = [ATTEND_TIMES[0]] * tiles + [ATTEND_TIMES[1]] * (3 * heads) + [ATTEND_TIMES[2]] * ends
    first_line, line = line, Line(count, rows // count, row_sems[4:], shared, False, True, ATTEND_PARTS, ATTEND_LATENCY)
    line.rows_ref, line.source_ref = grad_rows_ref, own_grad_ref
    grad_rows_ref[pl.ds(pl.multiple_of(place * line.rows, line.rows), line.rows), :] = own_grad_ref[...]
    stores = [(normed, rows_ref), (mix_all, mix_ref), (ffn_all.at[own_rows], gate_up_ref.at[own_rows])]

    def store(index):
        return pltpu.make_async_copy(*stores[index], store_sem.at[index])

    for index in range(len(stores)):
        store(index).start()

    @pl.loop(0, tiles)
    def _(tile):
        line.run_at(0, tile, tiles)

        @pl.when(tile == tiles // 2)
        def _():
            serve(ready)

        cols = pl.ds(pl.multiple_of(tile * TILE, TILE), TILE)
        raw_all[:, cols] = dot(normed[...], mix_all[:, cols])

    raw_all[:, 4 * width :] = dot(normed[...], mix_all[:, 4 * width :])
    stores.append((raw_all, raw_ref))
    store(len(stores) - 1).start()
    serve(ready + 1)
    fill_masks(starts_ref, length_ref, keep_ref, live_ref, carry_ref)
    for chunk in range(chunks):
        strict, incl = pair_mask(starts_ref, chunk)
        strict_ref[chunk] = jnp.where(strict, 1.0, 0.0)
        incl_ref[chunk] = jnp.where(incl, 1.0, 0.0)

    @pl.loop(0, heads)
    def _(head):
        line.run_at(tiles, head, heads, 3)
        start = pl.multiple_of(head * head_width, head_width)

        def stream(index):
            return raw_all[:, pl.ds(pl.multiple_of(index * width + start, head_width), head_width)]

        cols = pl.ds(start, head_width)
        conv, _ = convolve(stream(Q), conv_q_ref[:, cols].astype(F32), keep_ref)
        _, act, scale = unit_rows(conv)
        query = (act * scale).astype(BF16)
        conv, _ = convolve(stream(K), conv_k_ref[:, cols].astype(F32), keep_ref)
        _, act, scale = unit_rows(conv)
        keyed = act * scale
        key_low = keyed.astype(BF16)
        conv, _ = convolve(stream(V), conv_v_ref[:, cols].astype(F32), keep_ref)
        valued = conv * sigmoid(conv)
        rate = sigmoid(column(raw_all[:, 4 * width :], head)) * live_ref[...]
        scaled_value = (valued * rate).astype(BF16)
        scaled_key = keyed * rate
        system = []
        for chunk in range(chunks):
            span = slice(chunk * CHUNK, (chunk + 1) * CHUNK)
            pair = dot_nt(key_low[span], key_low[span])
            wide = jnp.concatenate([rate[span]] * (CHUNK // head_width), axis=1)
            system.append(pair * wide * strict_ref[chunk])
        line.run_at(tiles + 1, head, heads, 3)
        memory = None
        inverses = invert(system)
        line.run_at(tiles + 2, head, heads, 3)
        for chunk, solved in enumerate(inverses):
            span = slice(chunk * CHUNK, (chunk + 1) * CHUNK)
            solve_low = solved.astype(BF16)
            solve_all[head * chunks + chunk] = solve_low
            score = dot_nt(query[span], key_low[span]) * incl_ref[chunk]
            if chunk == 0:
                update = dot(solve_low, scaled_value[span])
                update_low = update.astype(BF16)
                mixed = dot(score.astype(BF16), update_low)
            else:
                carry = carry_ref[chunk - 1][span]
                right = jnp.concatenate(
                    [scaled_value[span], (scaled_key[span] * carry).astype(BF16)], axis=1
                )
                both = dot(solve_low, right)
                memory_low = memory.astype(BF16)
                state_all[head * (chunks - 1) + chunk - 1] = memory_low
                update = both[:, :head_width] - dot(both[:, head_width:].astype(BF16), memory_low)
                update_low = update.astype(BF16)
                mixed = carry * dot(query[span], memory_low) + dot(score.astype(BF16), update_low)
            update_all[span, cols] = update_low
            mixed_all[span, cols] = mixed
            if chunk + 1 < chunks:
                last = (keyed[span] * carry_ref[chunk][span]).astype(BF16)
                fresh = dot_tn(last, update_low)
                if memory is None:
                    memory = fresh
                else:
                    memory = memory * carry_ref[chunk - 1][span][CHUNK - 1 :] + fresh
        mixed = mixed_all[:, cols]
        norm = lax.rsqrt(lane_sum(mixed * mixed) * (1.0 / head_width) + 1e-05)
        gating = stream(G)
        gated = mixed * norm * gain_ref[...] * (gating * sigmoid(gating)) * live_ref[...]
        gated_all[:, cols] = gated.astype(BF16)
        for index in range(1, heads, 2):
            @pl.when(head == index)
            def _():
                serve(ready + 2 + index // 2)

    stores += [
        (project_all, whole_project_ref), (gated_all, gated_ref), (mixed_all, mixed_ref), (solve_all, solve_ref),
        (update_all, update_ref), (state_all, state_ref),
    ]
    for shift in range(1, shards):
        there = pl.ds(pl.multiple_of(shard_at(shift) * share, half), half)
        stores.append((ffn_all.at[there], gate_up_ref.at[there]))
    for index in range(3 + 1, len(stores)):
        store(index).start()

    @pl.loop(0, ends)
    def _(tile):
        line.run_at(tiles + 3 * heads, tile, ends)
        cols = pl.ds(pl.multiple_of(tile * PROJECT_TILE, PROJECT_TILE), PROJECT_TILE)
        partial_ref[:, cols] = dot(gated_all[...], project_all[:, cols]).astype(BF16)

    line.run(tiles + 3 * heads + ends)
    line.drain()
    for turn in range(ready + 2 + heads // 2, count_streams + 2):
        serve(turn)
    for shift in range(1, shards):
        there = pl.ds(pl.multiple_of(shard_at(shift) * share + half, half), half)
        stores.append((ffn_all.at[there], gate_up_ref.at[there]))
        store(len(stores) - 1).start()
    for index in range(len(stores)):
        store(index).wait()

    for stream in range(count_streams):
        for shift in range(1, shards):
            first(shift, stream, shard).wait_send()
            for step in range(1, pairs):
                second(shift, step, stream, replica).wait_send()
            for step in range(pairs):
                third(shift, step, stream, replica).wait_send()
    first_line.drain()


def begin(starts, length, layer_input, first_gain, second_gain, w_beta, output_grad, convs, gain, mixers, w_project, ffn):
    replicas, shards, count = extents()
    rows, features = layer_input.shape
    share, width = mixers[0].shape
    heads_here = w_beta.shape[1]
    head_width = gain.shape[-1]
    seq_rows = count * rows
    heads, chunks = width // head_width, seq_rows // CHUNK
    pairs, far = replicas // 2, max(shards - 1, 1)
    streams = 9
    wide = 4 * width + head_width
    hbm_out = [
        ((seq_rows, features), BF16),
        ((features, wide), BF16),
        ((width, features), BF16),
        ((features, 2 * ffn[0].shape[1]), BF16),
        ((seq_rows, wide), F32),
        ((seq_rows, width), BF16),
        ((seq_rows, width), F32),
        ((heads * chunks, CHUNK, CHUNK), BF16),
        ((seq_rows, width), BF16),
        ((heads * (chunks - 1), head_width, head_width), BF16),
    ]
    vmem_out = [((2, features), F32), ((seq_rows, features), BF16), ((seq_rows, features), BF16)]
    vmem = pl.BlockSpec(memory_space=pltpu.VMEM)
    hbm = pl.BlockSpec(memory_space=pltpu.HBM)
    smem = pl.BlockSpec(memory_space=pltpu.SMEM)
    dma = pltpu.SemaphoreType.DMA
    weights = [pltpu.with_memory_space_constraint(weight, pltpu.HBM) for weight in (*mixers, w_project, *ffn)]
    return pl.pallas_call(
        functools.partial(begin_kernel, (replicas, shards, count)),
        out_shape=[jax.ShapeDtypeStruct(*entry) for entry in vmem_out] + [pltpu.HBM(*entry) for entry in hbm_out],
        in_specs=[smem] * 2 + [vmem] * 8 + [hbm] * 7,
        out_specs=[vmem] * 3 + [hbm] * len(hbm_out),
        scratch_shapes=[pltpu.VMEM((seq_rows, features), BF16)]
        + [pltpu.VMEM(*entry) for entry in hbm_out]
        + [
            pltpu.VMEM((KERNEL - 1, seq_rows, head_width), F32),
            pltpu.VMEM((seq_rows, head_width), F32),
            pltpu.VMEM((chunks - 1, seq_rows, head_width), F32),
            pltpu.VMEM((chunks, CHUNK, CHUNK), F32),
            pltpu.VMEM((chunks, CHUNK, CHUNK), F32),
            pltpu.VMEM((2, features), BF16),
            pltpu.VMEM((heads_here, features), BF16),
            dma((9,)),
            dma((10 + 2 * far,)),
            dma((far, 2)),
            dma((far, 2)),
            dma((far, streams)),
            dma((far, streams)),
            dma((far, max(pairs - 1, 1), streams)),
            dma((far, max(pairs - 1, 1), streams)),
            dma((far, pairs, streams)),
            dma((far, pairs, streams)),
        ]
        + line_scratch(count, rows, features, False, True, 2)
        + line_scratch(count, rows, features, False, True, ATTEND_PARTS),
        compiler_params=pltpu.CompilerParams(collective_id=5, has_side_effects=True, vmem_limit_bytes=56 * 2**20),
        cost_estimate=pl.CostEstimate(
            flops=2 * 36 * heads * chunks * CHUNK**3, bytes_accessed=60 * 2**20, transcendentals=0
        ),
        name="begin",
    )(
        starts, length, layer_input, jnp.stack([first_gain, second_gain]), w_beta.T, output_grad, *convs, gain, *weights
    )


class Pair:

    def __init__(self, features, owners, left_ref, right_ref, grad_refs, out_ref, scratch):
        self.owners, self.left_ref, self.right_ref, self.grad_refs = owners, left_ref, right_ref, grad_refs
        self.out_ref = out_ref
        self.tiles, self.came, self.send_sem, self.recv_sem, self.out_sem = scratch
        self.core = lax.axis_index("core")
        replica, shard, place = coordinates()
        self.partner = device(replica + 1 - 2 * self.core, shard, place)
        self.blocks, self.size = out_ref.shape[:2]
        self.share = features // (2 * lax.axis_size("pair"))

    def copy(self, block):
        return pltpu.make_async_remote_copy(
            src_ref=self.tiles.at[block], dst_ref=self.came.at[block], send_sem=self.send_sem.at[block],
            recv_sem=self.recv_sem.at[block], device_id=self.partner, device_id_type=MESH,
        )

    def product(self, block, core):
        steps = self.share // self.size
        start = (lax.div(block, steps) * 2 + core) * self.share + lax.rem(block, steps) * self.size
        cols = pl.ds(pl.multiple_of(start, self.size), self.size)
        start = 0
        for owner, grad_ref in zip(self.owners, self.grad_refs):
            wide = grad_ref.shape[1]
            values = dot_tn((self.left_ref if owner == 0 else self.right_ref)[:, cols], grad_ref[...])
            yield slice(start, start + wide), values
            start += wide

    def theirs(self, block):
        for span, values in self.product(block, 1 - self.core):
            self.tiles[block, :, span] = values.astype(BF16)
        self.copy(block).start()

    def store(self, block):
        return pltpu.make_async_copy(self.tiles.at[block], self.out_ref.at[block], self.out_sem.at[block])

    def ours(self, block):
        self.copy(block).wait()
        for span, values in self.product(block, self.core):
            self.tiles[block, :, span] = (values + self.came[block, :, span].astype(F32)).astype(BF16)
        self.store(block).start()

    def drain(self):
        for block in range(self.blocks):
            self.store(block).wait()


def pair_shape(left, grads):
    features = left.shape[1]
    return features // (2 * CHUNK), CHUNK, sum(grad.shape[1] for grad in grads)


def pair_scratch(shape):
    dma = pltpu.SemaphoreType.DMA
    return [pltpu.VMEM(shape, BF16), pltpu.VMEM(shape, BF16)] + [dma(shape[:1])] * 3


def mix_grads_kernel(features, left_ref, right_ref, first_ref, second_ref, out_ref, *scratch):
    pair = Pair(features, (0, 1), left_ref, right_ref, (first_ref, second_ref), out_ref, scratch)
    barrier = pltpu.get_barrier_semaphore()
    pl.semaphore_signal(barrier, inc=1, device_id=pair.partner, device_id_type=MESH)
    pl.semaphore_wait(barrier, 1)
    pl.loop(0, pair.blocks)(pair.theirs)
    pl.loop(0, pair.blocks)(pair.ours)
    pair.drain()


def mix_grads(left, right, grads):
    shape = pair_shape(left, grads)
    vmem = pl.BlockSpec(memory_space=pltpu.VMEM)
    out = pl.pallas_call(
        functools.partial(mix_grads_kernel, left.shape[1]),
        out_shape=pltpu.HBM(shape, BF16),
        in_specs=[vmem] * 4,
        out_specs=pl.BlockSpec(memory_space=pltpu.HBM),
        scratch_shapes=pair_scratch(shape),
        compiler_params=pltpu.CompilerParams(collective_id=7, has_side_effects=True, vmem_limit_bytes=24 * 2**20),
        cost_estimate=pl.CostEstimate(
            flops=2 * left.shape[0] * left.shape[1] * shape[2], bytes_accessed=30 * 2**20, transcendentals=0
        ),
        name="mix_grads",
    )(left, right, *grads)
    return out.reshape(shape[0] * shape[1], shape[2])


BLOCK_TIME, TILE_TIME = 2.8, 1.3


def ffn_grads_kernel(
    count, features, left_ref, right_ref, d_gate_ref, d_up_ref, hidden_ref, partial_ref, resid_ref, gate_up_ref,
    out_ref, result_ref, d_partial_ref, *scratch,
):
    *scratch, weights, weights_sem = scratch
    load = pltpu.make_async_copy(gate_up_ref, weights, weights_sem)
    load.start()
    pair = Pair(features, (0, 0, 1), left_ref, right_ref, (d_gate_ref, d_up_ref, hidden_ref), out_ref, scratch[:5])
    tiles = features // TILE
    units = d_gate_ref.shape[1]
    shared = [BLOCK_TIME] * (2 * pair.blocks) + [TILE_TIME] * tiles
    line = Line(count, resid_ref.shape[0], scratch[5:], shared, True, False, latency=FFN_LATENCY)

    def finish(part, local, place):
        result_ref[local, :] = (resid_ref[local, :] + line.total_ref[...]).astype(BF16)

    line.partial_ref, line.finish = partial_ref, finish
    line.greet([pair.partner])

    @pl.loop(0, pair.blocks)
    def _(block):
        line.run_at(0, block, pair.blocks)
        pair.theirs(block)

    @pl.loop(0, pair.blocks)
    def _(block):
        line.run_at(pair.blocks, block, pair.blocks)
        pair.ours(block)

    load.wait()

    @pl.loop(0, tiles)
    def _(tile):
        line.run_at(2 * pair.blocks, tile, tiles)
        cols = pl.ds(pl.multiple_of(tile * TILE, TILE), TILE)
        values = dot_nt(d_gate_ref[...], weights[cols, :units]) + dot_nt(d_up_ref[...], weights[cols, units:])
        d_partial_ref[:, cols] = values.astype(BF16)

    line.run(2 * pair.blocks + tiles)
    line.drain()
    pair.drain()


def ffn_grads(left, right, grads, ffn_partial, resid, gate_up):
    count = lax.axis_size("tensor")
    shape = pair_shape(left, grads)
    vmem = pl.BlockSpec(memory_space=pltpu.VMEM)
    sums, result, d_partial = pl.pallas_call(
        functools.partial(ffn_grads_kernel, count, left.shape[1]),
        out_shape=(jax.ShapeDtypeStruct(shape, BF16), jax.ShapeDtypeStruct(resid.shape, BF16), jax.ShapeDtypeStruct(left.shape, BF16)),
        in_specs=[vmem] * 7 + [pl.BlockSpec(memory_space=pltpu.HBM)],
        out_specs=[pl.BlockSpec(memory_space=pltpu.HBM), vmem, vmem],
        scratch_shapes=pair_scratch(shape)
        + line_scratch(count, resid.shape[0], resid.shape[1], True, False)
        + [pltpu.VMEM(gate_up.shape, BF16), pltpu.SemaphoreType.DMA],
        compiler_params=pltpu.CompilerParams(collective_id=6, has_side_effects=True, vmem_limit_bytes=FFN_MEMORY),
        cost_estimate=pl.CostEstimate(
            flops=2 * left.shape[0] * left.shape[1] * shape[2], bytes_accessed=50 * 2**20, transcendentals=0
        ),
        name="ffn_grads",
    )(left, right, *grads, ffn_partial, resid, pltpu.with_memory_space_constraint(gate_up, pltpu.HBM))
    return sums.reshape(shape[0] * shape[1], shape[2]), result, d_partial


def group_scatter(sums):
    return lax.psum_scatter(sums, ("pair", "fsdp"), scatter_dimension=0, tiled=True)


def widen_kernel(parts, shard_ref, *out_refs):
    for (start, stop, flip), out_ref in zip(parts, out_refs):
        values = shard_ref[:, start:stop].astype(F32)
        out_ref[...] = values.T if flip else values


def widen(shard, parts, name):
    rows = shard.shape[0]
    shapes = [(stop - start, rows) if flip else (rows, stop - start) for start, stop, flip in parts]
    vmem = pl.BlockSpec(memory_space=pltpu.VMEM)
    return pl.pallas_call(
        functools.partial(widen_kernel, parts),
        out_shape=[jax.ShapeDtypeStruct(shape, F32) for shape in shapes],
        in_specs=[vmem],
        out_specs=[vmem] * len(parts),
        compiler_params=pltpu.CompilerParams(vmem_limit_bytes=16 * 2**20),
        cost_estimate=pl.CostEstimate(flops=10**6, bytes_accessed=8 * 2**20, transcendentals=0),
        name=name,
    )(shard)


def gather_weights(pieces, axis):
    return lax.all_gather(jnp.concatenate(pieces, axis=1), ("fsdp", "pair", "core"), axis=axis, tiled=True)


def scatter_grads(grads, axis=0):
    return lax.psum_scatter(grads, ("pair", "core", "fsdp"), scatter_dimension=axis, tiled=True).astype(F32)


def body(
    layer_input,
    first_gain,
    w_query,
    w_key,
    w_value,
    w_gating,
    w_beta,
    conv_query,
    conv_key,
    conv_value,
    head_gain,
    w_project,
    second_gain,
    w_gate,
    w_up,
    w_down,
    doc_starts,
    seq_lengths,
    output_grad,
):
    replicas, replica = extents()[0], coordinates()[0]
    width = w_query.shape[1]
    units = w_gate.shape[1]
    heads = w_beta.shape[1]
    head_width = head_gain.shape[0]

    def piece(weight, axis):
        size = weight.shape[axis] // replicas
        return lax.dynamic_slice_in_dim(weight, replica * size, size, axis)

    input_float = layer_input.astype(F32)
    conv_q, conv_k, conv_v = conv_query, conv_key, conv_value
    gain_head = head_gain.astype(F32)[None, :]
    (
        gains, attn_partial, grad_rows, rows_one, mix_full, project_full, gate_up,
        raw, gated, mixed, solve, update, state,
    ) = begin(
        doc_starts, seq_lengths, layer_input, first_gain, second_gain, w_beta, output_grad, (conv_q, conv_k, conv_v),
        gain_head, (w_gating, w_query, w_key, w_value), w_project, (w_gate, w_up),
    )
    gain_one, gain_two = gains[:1], gains[1:]
    late, attn_partial = lax.optimization_barrier((w_down, attn_partial))
    down = gather_weights([piece(late, 1)], 1)
    whole_rows = jax.ShapeDtypeStruct(rows_one.shape, BF16)
    own_rows = jax.ShapeDtypeStruct(layer_input.shape, F32)
    gain_sums = jax.ShapeDtypeStruct((1, layer_input.shape[1]), F32)
    rows_two, resid = line_call(
        middle_kernel, "middle", 2, True, (whole_rows, own_rows), (attn_partial, layer_input, gain_two)
    )
    d_hidden = dot_nt(grad_rows, down)
    both = dot(rows_two, gate_up)
    gate_val, up_val = both[:, :units], both[:, units:]
    gate_sig = jax.nn.sigmoid(gate_val)
    silu_gate = gate_val * gate_sig
    hidden = (silu_gate * up_val).astype(BF16)
    d_gate = (d_hidden * up_val * gate_sig * (1.0 + gate_val * (1.0 - gate_sig))).astype(BF16)
    d_up = (d_hidden * silu_gate).astype(BF16)
    ffn_partial = dot(hidden, down).astype(BF16)
    ffn_sums, result, d_partial = ffn_grads(rows_two, grad_rows, (d_gate, d_up, hidden), ffn_partial, resid, gate_up)
    ffn_shard = group_scatter(ffn_sums)
    d_attn, d_resid, grad_second = line_call(
        turn_kernel, "turn", 3, True, (whole_rows, own_rows, gain_sums), (d_partial, resid, output_grad, gain_two)
    )
    d_gated = dot_nt(d_attn, project_full)
    d_raw, d_conv, d_head = delta_backward(
        doc_starts, seq_lengths, raw, conv_q, conv_k, conv_v, gain_head, mixed, solve, update, state, d_gated
    )
    mix_sums, ffn_shard = lax.optimization_barrier(
        (mix_grads(rows_one, d_attn, (d_raw, gated)), ffn_shard)
    )
    mix_shard = group_scatter(mix_sums)
    beta_start = 4 * width
    project_start = beta_start + head_width
    grad_gating, grad_query, grad_key, grad_value, grad_beta, grad_project = widen(
        mix_shard,
        [(index * width, (index + 1) * width, False) for index in range(4)]
        + [(beta_start, beta_start + heads, False), (project_start, project_start + width, True)],
        "widen_mix",
    )
    grad_gate, grad_up, grad_down = widen(
        ffn_shard, [(0, units, False), (units, 2 * units, False), (2 * units, 3 * units, True)], "widen_ffn"
    )
    mix_partial = dot_nt(d_raw, mix_full).astype(BF16)
    input_grad, grad_first = line_call(
        last_kernel, "last", 4, False, (own_rows, gain_sums),
        (mix_partial, layer_input, d_resid, gain_one),
    )
    gain_total, head_total, conv_totals = reduce_small(
        jnp.concatenate([grad_first, grad_second], axis=0), d_head, d_conv
    )
    return (
        result,
        input_grad,
        gain_total[0],
        grad_query,
        grad_key,
        grad_value,
        grad_gating,
        grad_beta,
        conv_totals[:, :width],
        conv_totals[:, width : 2 * width],
        conv_totals[:, 2 * width :],
        head_total[0],
        grad_project,
        gain_total[1],
        grad_gate,
        grad_up,
        grad_down,
    )


def solution(mesh):
    replicas, shards, count = (mesh.shape[name] for name in ("dp", "fsdp", "tensor"))
    mesh = jax.sharding.Mesh(
        mesh.devices.reshape(replicas // 2, 2, shards, count), ("pair", "core", "fsdp", "tensor")
    )
    placed = (
        P(("pair", "core", "fsdp", "tensor"), None),
        P("fsdp"),
        P("fsdp", "tensor"),
        P("fsdp", "tensor"),
        P("fsdp", "tensor"),
        P("fsdp", "tensor"),
        P("fsdp", "tensor"),
        P(None, "tensor"),
        P(None, "tensor"),
        P(None, "tensor"),
        P(),
        P("tensor", "fsdp"),
        P("fsdp"),
        P("fsdp", "tensor"),
        P("fsdp", "tensor"),
        P("tensor", "fsdp"),
        P(("pair", "core", "fsdp"), None),
        P(("pair", "core", "fsdp")),
        P(("pair", "core", "fsdp", "tensor"), None),
    )
    return jax.shard_map(
        body,
        mesh=mesh,
        in_specs=placed,
        out_specs=(
            P(("pair", "core", "fsdp", "tensor"), None),
            P(("pair", "core", "fsdp", "tensor"), None),
            P(("pair", "core", "fsdp")),
            P(("pair", "core", "fsdp"), "tensor"),
            P(("pair", "core", "fsdp"), "tensor"),
            P(("pair", "core", "fsdp"), "tensor"),
            P(("pair", "core", "fsdp"), "tensor"),
            P(("pair", "core", "fsdp"), "tensor"),
            P(None, "tensor"),
            P(None, "tensor"),
            P(None, "tensor"),
            P(),
            P("tensor", ("pair", "core", "fsdp")),
            P(("pair", "core", "fsdp")),
            P(("pair", "core", "fsdp"), "tensor"),
            P(("pair", "core", "fsdp"), "tensor"),
            P("tensor", ("pair", "core", "fsdp")),
        ),
        check_vma=False,
    )
```

```python
import functools
import jax, jax.numpy as jnp
from jax import lax
from jax.experimental import pallas as pl
from jax.experimental.pallas import tpu as pltpu
from jax.sharding import PartitionSpec as P

KERNEL = 4
CHUNK = 256
G, Q, K, V = range(4)
MESH = pl.DeviceIdType.MESH
F32 = jnp.float32
BF16 = jnp.bfloat16


def coordinates():
    replica = lax.axis_index("pair") * 2 + lax.axis_index("core")
    return replica, lax.axis_index("fsdp"), lax.axis_index("tensor")


def extents():
    return lax.axis_size("pair") * 2, lax.axis_size("fsdp"), lax.axis_size("tensor")


def device(replica, shard, place):
    return (lax.div(replica, 2), lax.rem(replica, 2), shard, place)


def dot(left, right):
    return jnp.dot(left, right, preferred_element_type=F32)


def dot_nt(left, right):
    return lax.dot_general(left, right, (((1,), (1,)), ((), ())), preferred_element_type=F32)


def dot_tn(left, right):
    return lax.dot_general(left, right, (((0,), (0,)), ((), ())), preferred_element_type=F32)


def lane_sum(values):
    return jnp.sum(values, axis=-1, keepdims=True)


def document_of(starts_ref, positions):
    total = jnp.zeros_like(positions)
    for entry in range(starts_ref.shape[1]):
        total = total + (positions >= starts_ref[0, entry]).astype(jnp.int32)
    return total


def fill_masks(starts_ref, length_ref, keep_ref, live_ref, carry_ref):
    rows, lanes = live_ref.shape
    place = lax.broadcasted_iota(jnp.int32, (rows, lanes), 0)
    docs = document_of(starts_ref, place)
    for delay in range(1, KERNEL):
        prior = document_of(starts_ref, place - delay)
        keep_ref[delay - 1] = jnp.where((prior == docs) & (place >= delay), 1.0, 0.0)
    live_ref[...] = jnp.where(place < length_ref[0], 1.0, 0.0)
    for edge in range(rows // CHUNK - 1):
        seam = jnp.int32((edge + 1) * CHUNK - 1)
        carry_ref[edge] = jnp.where(docs == document_of(starts_ref, seam), 1.0, 0.0)


def pair_mask(starts_ref, chunk):
    row = lax.broadcasted_iota(jnp.int32, (CHUNK, CHUNK), 0)
    col = lax.broadcasted_iota(jnp.int32, (CHUNK, CHUNK), 1)
    first = chunk * CHUNK
    same = document_of(starts_ref, row + first) == document_of(starts_ref, col + first)
    return same & (row > col), same & (row >= col)


def convolve(raw, taps, keep_ref):
    parts = [raw]
    for delay in range(1, KERNEL):
        parts.append(pltpu.roll(raw, delay, 0) * keep_ref[delay - 1])
    total = parts[0] * taps[KERNEL - 1 : KERNEL]
    for delay in range(1, KERNEL):
        total = total + parts[delay] * taps[KERNEL - 1 - delay : KERNEL - delay]
    return total, parts


def sigmoid(values):
    return 0.5 * jnp.tanh(0.5 * values) + 0.5


def column(values, index):
    lane = lax.broadcasted_iota(jnp.int32, values.shape, 1)
    return lane_sum(jnp.where(lane == index, values, 0.0))


def invert(system):
    size = system[0].shape[0]
    row = lax.broadcasted_iota(jnp.int32, (size, size), 0)
    col = lax.broadcasted_iota(jnp.int32, (size, size), 1)
    apart = row ^ col
    eye = jnp.where(row == col, 1.0, 0.0)
    low = [matrix.astype(BF16) for matrix in system]
    solved = [eye - jnp.where(apart == 1, matrix, 0.0) for matrix in system]
    step = 2
    while step < size:
        level = (apart >= step) & (apart < 2 * step)
        for index, matrix in enumerate(low):
            part = jnp.where(level, matrix, 0.0)
            held = solved[index].astype(BF16)
            solved[index] = solved[index] - dot(dot(held, part).astype(BF16), held)
        step *= 2
    refined = []
    for matrix, high, inverse in zip(system, low, solved):
        rest = (matrix - high.astype(F32)).astype(BF16)
        head = inverse.astype(BF16)
        tail = (inverse - head.astype(F32)).astype(BF16)
        product = dot(high, head) + dot(rest, head) + dot(high, tail)
        residue = eye - inverse - product
        refined.append(inverse + dot(head, residue.astype(BF16)))
    return refined


def unit_rows(conv):
    gate = sigmoid(conv)
    act = conv * gate
    scale = lax.rsqrt(lane_sum(act * act) + 1e-06)
    return gate, act, scale


TILE = 256
PROJECT_TILE = 512
ATTEND_TIMES = (1.2, 1.5, 0.9)


def backward_kernel(
    starts_ref, length_ref, raw_ref, conv_q_ref, conv_k_ref, conv_v_ref, gain_ref,
    mixed_ref, solve_ref, update_ref, state_ref, grad_ref,
    d_raw_ref, d_conv_ref, d_gain_ref,
    keep_ref, live_ref, carry_ref, strict_ref, incl_ref, d_query_ref, d_key_ref, d_value_ref, d_rate_ref,
):
    rows, head_width = live_ref.shape
    width = mixed_ref.shape[1]
    chunks = rows // CHUNK
    fill_masks(starts_ref, length_ref, keep_ref, live_ref, carry_ref)
    for chunk in range(chunks):
        strict, incl = pair_mask(starts_ref, chunk)
        strict_ref[chunk] = jnp.where(strict, 1.0, 0.0)
        incl_ref[chunk] = jnp.where(incl, 1.0, 0.0)
    d_gain_ref[...] = jnp.zeros_like(d_gain_ref)
    d_raw_ref[:, 4 * width :] = jnp.zeros((rows, head_width), BF16)

    @pl.loop(0, width // head_width)
    def _(head):
        start = pl.multiple_of(head * head_width, head_width)

        def place(index):
            return pl.ds(pl.multiple_of(index * width + start, head_width), head_width)

        cols = pl.ds(start, head_width)
        live = live_ref[...]
        mixed = mixed_ref[:, cols]
        norm = lax.rsqrt(lane_sum(mixed * mixed) * (1.0 / head_width) + 1e-05)
        gating = raw_ref[:, place(G)]
        gate = sigmoid(gating)
        normal = mixed * norm
        grad = grad_ref[:, cols].astype(F32) * live
        grad_gain = grad * gain_ref[...]
        swish = gating * gate
        d_raw_ref[:, place(G)] = (grad_gain * normal * gate * (1.0 + gating - swish)).astype(BF16)
        d_gain_ref[...] += jnp.sum(grad * normal * swish, axis=0, keepdims=True)
        d_normal = grad_gain * swish
        d_mixed = norm * (d_normal - normal * (lane_sum(d_normal * normal) * (1.0 / head_width)))
        d_mixed_low = d_mixed.astype(BF16)

        conv_q, parts_q = convolve(raw_ref[:, place(Q)], conv_q_ref[:, cols].astype(F32), keep_ref)
        gate_q, act_q, scale_q = unit_rows(conv_q)
        unit_q = act_q * scale_q
        query = unit_q.astype(BF16)
        conv_k, parts_k = convolve(raw_ref[:, place(K)], conv_k_ref[:, cols].astype(F32), keep_ref)
        gate_k, act_k, scale_k = unit_rows(conv_k)
        keyed = act_k * scale_k
        key_low = keyed.astype(BF16)
        conv_v, parts_v = convolve(raw_ref[:, place(V)], conv_v_ref[:, cols].astype(F32), keep_ref)
        gate_v = sigmoid(conv_v)
        valued = conv_v * gate_v
        sig = sigmoid(column(raw_ref[:, 4 * width :], head))
        rate = sig * live
        scaled_value = (valued * rate).astype(BF16)
        scaled_key = keyed * rate

        d_memory = None
        for chunk in range(chunks - 1, -1, -1):
            span = slice(chunk * CHUNK, (chunk + 1) * CHUNK)
            key_c, query_c, d_mixed_c = key_low[span], query[span], d_mixed_low[span]
            solve = solve_ref[head * chunks + chunk]
            update = update_ref[span, cols]
            incl, strict = incl_ref[chunk], strict_ref[chunk]
            score = (dot_nt(query_c, key_c) * incl).astype(BF16)
            d_update = dot_tn(score, d_mixed_c)
            d_key = None
            if d_memory is not None:
                last = carry_ref[chunk][span]
                d_memory_low = d_memory.astype(BF16)
                d_update = d_update + dot((keyed[span] * last).astype(BF16), d_memory_low)
                d_key = last * dot_nt(update, d_memory_low)
            d_update_low = d_update.astype(BF16)
            d_score = (dot_nt(d_mixed_c, update) * incl).astype(BF16)
            d_query = dot(d_score, key_c)
            d_key_score = dot_tn(d_score, query_c)
            d_key = d_key_score if d_key is None else d_key + d_key_score
            if chunk == 0:
                right = scaled_value[span]
                solved = dot(solve, right)
                d_right = dot_tn(solve, d_update_low)
                d_value_in = d_right
                d_rate = lane_sum(d_value_in * valued[span])
            else:
                carry = carry_ref[chunk - 1][span]
                state = state_ref[head * (chunks - 1) + chunk - 1]
                right = jnp.concatenate([scaled_value[span], (scaled_key[span] * carry).astype(BF16)], axis=1)
                solved = dot(solve, right)
                d_solved_key = -dot_nt(d_update_low, state)
                d_right = dot_tn(solve, jnp.concatenate([d_update_low, d_solved_key.astype(BF16)], axis=1))
                d_value_in = d_right[:, :head_width]
                d_key_in = d_right[:, head_width:] * carry
                carried = (carry * d_mixed[span]).astype(BF16)
                d_query = d_query + dot_nt(carried, state)
                d_key = d_key + rate[span] * d_key_in
                d_rate = lane_sum(d_value_in * valued[span] + d_key_in * keyed[span])
                fresh = dot_tn(query_c, carried) - dot_tn(solved[:, head_width:].astype(BF16), d_update_low)
                if d_memory is None:
                    d_memory = fresh
                else:
                    d_memory = d_memory * carry[CHUNK - 1 :] + fresh
            d_system = dot_nt(d_right.astype(BF16), solved.astype(BF16)) * -strict
            pair = dot_nt(key_c, key_c)
            d_rate = d_rate + lane_sum(d_system * pair)
            wide = jnp.concatenate([rate[span]] * (CHUNK // head_width), axis=1)
            d_pair = (d_system * wide).astype(BF16)
            d_key = d_key + dot(d_pair, key_c) + dot_tn(d_pair, key_c)
            d_query_ref[span] = d_query
            d_key_ref[span] = d_key
            d_value_ref[span] = rate[span] * d_value_in
            d_rate_ref[span] = jnp.broadcast_to(d_rate, (CHUNK, head_width))

        lane = lax.broadcasted_iota(jnp.int32, (rows, head_width), 1)
        d_beta = d_rate_ref[...] * rate * (1.0 - sig)
        tail = d_raw_ref[:, 4 * width :]
        d_raw_ref[:, 4 * width :] = jnp.where(lane == head, d_beta.astype(BF16), tail)

        def conv_back(index, d_conv, parts, taps):
            sums = [jnp.sum(d_conv * part, axis=0, keepdims=True) for part in parts]
            for delay in range(KERNEL):
                tap = KERNEL - 1 - delay
                d_conv_ref[tap : tap + 1, place(index - 1)] = sums[delay]
            total = d_conv * taps[KERNEL - 1 : KERNEL]
            for delay in range(1, KERNEL):
                tap = KERNEL - 1 - delay
                back = pltpu.roll(d_conv * keep_ref[delay - 1], rows - delay, 0)
                total = total + back * taps[tap : tap + 1]
            d_raw_ref[:, place(index)] = total.astype(BF16)

        def unit_back(d_unit, unit, scale, conv, act, gate):
            d_act = scale * (d_unit - unit * lane_sum(d_unit * unit))
            return d_act * gate * (1.0 + conv - act)

        conv_back(Q, unit_back(d_query_ref[...], unit_q, scale_q, conv_q, act_q, gate_q), parts_q, conv_q_ref[:, cols].astype(F32))
        conv_back(K, unit_back(d_key_ref[...], keyed, scale_k, conv_k, act_k, gate_k), parts_k, conv_k_ref[:, cols].astype(F32))
        d_conv_v = d_value_ref[...] * gate_v * (1.0 + conv_v - valued)
        conv_back(V, d_conv_v, parts_v, conv_v_ref[:, cols].astype(F32))


def delta_backward(starts, length, raw, conv_q, conv_k, conv_v, gain, mixed, solve, update, state, grad):
    rows = raw.shape[0]
    head_width = gain.shape[-1]
    width = conv_q.shape[1]
    heads, chunks = width // head_width, rows // CHUNK
    vmem = pl.BlockSpec(memory_space=pltpu.VMEM)
    smem = pl.BlockSpec(memory_space=pltpu.SMEM)
    return pl.pallas_call(
        backward_kernel,
        out_shape=(
            jax.ShapeDtypeStruct((rows, 4 * width + head_width), BF16),
            jax.ShapeDtypeStruct((KERNEL, 3 * width), F32),
            jax.ShapeDtypeStruct((1, head_width), F32),
        ),
        in_specs=[smem, smem] + [vmem] * 10,
        out_specs=[vmem] * 3,
        scratch_shapes=[
            pltpu.VMEM((KERNEL - 1, rows, head_width), F32),
            pltpu.VMEM((rows, head_width), F32),
            pltpu.VMEM((chunks - 1, rows, head_width), F32),
            pltpu.VMEM((chunks, CHUNK, CHUNK), F32),
            pltpu.VMEM((chunks, CHUNK, CHUNK), F32),
        ]
        + [pltpu.VMEM((rows, head_width), F32)] * 4,
        compiler_params=pltpu.CompilerParams(vmem_limit_bytes=18 * 2**20),
        cost_estimate=pl.CostEstimate(
            flops=2 * 12 * heads * chunks * CHUNK**3, bytes_accessed=16 * 2**20, transcendentals=0
        ),
        name="delta_backward",
    )(starts, length, raw, conv_q, conv_k, conv_v, gain, mixed, solve, update, state, grad)


def reduce_kernel(
    group_size, line_size, fsdp_size, gain_ref, head_ref, conv_ref, gain_out, head_out, conv_out,
    line_gain, line_head, stage, group_gain, group_conv,
    line_send, line_recv, group_send, group_recv,
):
    dp, fsdp, tensor = coordinates()
    group = dp * fsdp_size + fsdp
    size = gain_out.shape[1]

    def line_peer(shift):
        return device(dp, fsdp, lax.rem(tensor + shift, line_size))

    def group_peer(shift):
        peer = lax.rem(group + shift, group_size)
        return peer, device(lax.div(peer, fsdp_size), lax.rem(peer, fsdp_size), tensor)

    barrier = pltpu.get_barrier_semaphore()
    for shift in range(1, line_size):
        pl.semaphore_signal(barrier, inc=1, device_id=line_peer(shift), device_id_type=MESH)
    for shift in range(1, group_size):
        pl.semaphore_signal(barrier, inc=1, device_id=group_peer(shift)[1], device_id_type=MESH)
    pl.semaphore_wait(barrier, line_size + group_size - 2)

    copies = []
    for shift in range(1, line_size):
        for part, (source, target) in enumerate(((gain_ref, line_gain), (head_ref, line_head))):
            copy = pltpu.make_async_remote_copy(
                src_ref=source, dst_ref=target.at[shift - 1],
                send_sem=line_send.at[shift - 1, part], recv_sem=line_recv.at[shift - 1, part],
                device_id=line_peer(shift), device_id_type=MESH,
            )
            copy.start()
            copies.append(copy)
    conv_copies = []
    for shift in range(1, group_size):
        copy = pltpu.make_async_remote_copy(
            src_ref=conv_ref, dst_ref=group_conv.at[shift - 1],
            send_sem=group_send.at[shift - 1, 1], recv_sem=group_recv.at[shift - 1, 1],
            device_id=group_peer(shift)[1], device_id_type=MESH,
        )
        copy.start()
        conv_copies.append(copy)
    for copy in copies:
        copy.wait()
    gain = gain_ref[...]
    head = head_ref[...]
    for shift in range(1, line_size):
        gain = gain + line_gain[shift - 1]
        head = head + line_head[shift - 1]
    for peer in range(group_size):
        stage[peer] = jnp.zeros(stage.shape[1:], F32)
        stage[peer, :2, :size] = gain[:, peer * size : (peer + 1) * size]
        stage[peer, 2:3, : head.shape[1]] = head
    for copy in conv_copies:
        copy.wait()
    conv = conv_ref[...]
    for shift in range(1, group_size):
        conv = conv + group_conv[shift - 1]
    conv_out[...] = conv
    copies = []
    for shift in range(1, group_size):
        peer, where = group_peer(shift)
        copy = pltpu.make_async_remote_copy(
            src_ref=stage.at[peer], dst_ref=group_gain.at[shift - 1],
            send_sem=group_send.at[shift - 1, 0], recv_sem=group_recv.at[shift - 1, 0],
            device_id=where, device_id_type=MESH,
        )
        copy.start()
        copies.append(copy)
    for copy in copies:
        copy.wait()
    total = stage[group]
    for shift in range(1, group_size):
        total = total + group_gain[shift - 1]
    gain_out[...] = total[:2, :size]
    head_out[...] = total[2:3, : head.shape[1]]


def reduce_small(gain, head, conv):
    replicas, fsdp_size, line_size = extents()
    group_size = replicas * fsdp_size
    size = gain.shape[1] // group_size
    pad = max(size, head.shape[1])
    vmem = pl.BlockSpec(memory_space=pltpu.VMEM)
    dma = pltpu.SemaphoreType.DMA
    return pl.pallas_call(
        functools.partial(reduce_kernel, group_size, line_size, fsdp_size),
        out_shape=(
            jax.ShapeDtypeStruct((2, size), F32),
            jax.ShapeDtypeStruct(head.shape, F32),
            jax.ShapeDtypeStruct(conv.shape, F32),
        ),
        in_specs=[vmem] * 3,
        out_specs=[vmem] * 3,
        scratch_shapes=[
            pltpu.VMEM((line_size - 1,) + gain.shape, F32),
            pltpu.VMEM((line_size - 1,) + head.shape, F32),
            pltpu.VMEM((group_size, 8, pad), F32),
            pltpu.VMEM((group_size - 1, 8, pad), F32),
            pltpu.VMEM((group_size - 1,) + conv.shape, F32),
            dma((line_size - 1, 2)),
            dma((line_size - 1, 2)),
            dma((group_size - 1, 2)),
            dma((group_size - 1, 2)),
        ],
        compiler_params=pltpu.CompilerParams(collective_id=1, has_side_effects=True, vmem_limit_bytes=8 * 2**20),
        name="reduce_small",
    )(gain, head, conv)


def plan(count, parts, sums, rows, shared, unit, latency=1.5):
    backlog, add, end = 1.5, 0.15 + 0.8 / parts, 0.5 + 3.0 / parts
    rank = {"spread": 0, "relay": 0, "finish": 1, "forward": 2, "inject": 3}
    clock = [0.0] * count
    free, come = {}, [{} for _ in range(count)]
    todo = [set() for _ in range(count)]
    done = [0] * count
    at = [0] * count
    tasks = [[[] for _ in range(len(shared) + 1)] for _ in range(count)]
    own_finish = sums and not any(isinstance(step, tuple) for step in shared)
    for place in range(count):
        for part in range(parts):
            for step in (1, -1):
                behind = 0 <= place - step < count
                for slot in range(count - 1) if sums else ():
                    owner = count - 1 - slot if step > 0 else slot
                    if (owner - place) * step > 0:
                        todo[place].add(("forward" if behind else "inject", step, slot, part))
                for distance in range(1, count) if rows else ():
                    if 0 <= place - step * distance < count:
                        todo[place].add(("relay", step, distance, part))
            if rows and not sums:
                todo[place].add(("spread", 0, 0, part))
            if own_finish:
                todo[place].add(("finish", 0, 0, part))

    def ready(place, task):
        kind, step, slot, part = task
        if kind == "inject":
            return max(0.0, free.get((place, step), 0.0) - backlog * unit)
        if kind == "spread":
            return max([0.0] + [free.get((place, way), 0.0) - backlog * unit for way in (1, -1)])
        if kind == "forward":
            return come[place].get(("sum", step, slot, part))
        if kind == "relay":
            return come[place].get(("row", step, slot, part))
        if part != done[place]:
            return None
        times = [0.0]
        for way in (1, -1):
            if 0 <= place - way < count:
                times.append(come[place].get(("sum", way, count - 1 - place if way > 0 else place, part)))
        return None if None in times else max(times)

    def send(place, step, key):
        if 0 <= place + step < count:
            free[place, step] = max(clock[place], free.get((place, step), 0.0)) + unit
            come[place + step][key] = free[place, step] + latency

    def choices(place):
        found = [(ready(place, task), rank[task[0]], task[3], task[2], task[1], task) for task in todo[place]]
        found = [(max(clock[place], entry[0]),) + entry[1:] for entry in found if entry[0] is not None]
        if at[place] < len(shared):
            step = shared[at[place]]
            when = ready(place, ("finish", 0, 0, step[1])) if isinstance(step, tuple) else clock[place]
            if when is not None:
                found.append((max(when, clock[place]), 1 if isinstance(step, tuple) else 9, 0, 0, 0, step))
        return min(found, key=lambda entry: entry[:5]) if found else None

    while True:
        best = None
        for place in range(count):
            choice = choices(place)
            if choice is not None and (best is None or choice[0] < best[0][0]):
                best = (choice, place)
        if best is None:
            return max(clock), tasks
        choice, place = best
        clock[place] = choice[0]
        task = choice[5]
        if isinstance(task, float):
            clock[place] += task
            at[place] += 1
            continue
        if len(task) == 2:
            at[place] += 1
        else:
            todo[place].discard(task)
            tasks[place][at[place]].append(task)
        kind, step, slot, part = task if len(task) == 4 else ("finish", 0, 0, task[1])
        if kind in ("inject", "forward"):
            clock[place] += add if kind == "forward" else 0.02
            send(place, step, ("sum", step, slot, part))
        elif kind == "relay":
            clock[place] += 0.05
            if slot < count - 1:
                send(place, step, ("row", step, slot + 1, part))
        else:
            if kind == "finish":
                done[place] += 1
                clock[place] += end
            if rows:
                for way in (1, -1):
                    send(place, way, ("row", way, 1, part))


PARTS = 4
LANES = 512
FFN_MEMORY = 52 * 2**20
TURN_PARTS = 4
ATTEND_PARTS = 4
ATTEND_LATENCY, FFN_LATENCY = 1.5, 1.5
UNIT = 11.3


def rms_scale(values):
    return lax.rsqrt(jnp.mean(values * values, axis=-1, keepdims=True) + 1e-05)


def rms_back(values, scale_rows, gain, grad):
    scaled_grad = grad * gain
    inner = jnp.mean(scaled_grad * values, axis=-1, keepdims=True)
    return scale_rows * (scaled_grad - values * scale_rows * scale_rows * inner)


class Line:

    def __init__(self, count, rows, scratch, shared, sums, spreads, parts=PARTS, latency=1.5):
        self.count, self.rows, self.parts = count, rows, parts
        self.part = rows // parts
        scratch = list(scratch)
        self.sums, self.sends = {}, {}
        if sums:
            for step in (1, -1):
                self.sums[step] = [scratch.pop(0) for _ in range(4)]
            self.total_ref = scratch.pop(0)
        if spreads:
            for step in (1, -1):
                self.sends[step] = [scratch.pop(0) for _ in range(2)]
        self.replica, self.shard, self.place = coordinates()
        self.tasks = plan(count, parts, sums, spreads, shared, UNIT / parts, latency)[1]
        self.started = [[] for _ in range(count)]
        self.partial_ref = self.rows_ref = self.source_ref = self.finish = None

    def greet(self, others=()):
        barrier = pltpu.get_barrier_semaphore()
        for step in (1, -1):
            @pl.when(self.place < self.count - 1 if step > 0 else self.place > 0)
            def _():
                pl.semaphore_signal(
                    barrier, inc=1, device_id=device(self.replica, self.shard, self.place + step), device_id_type=MESH
                )
        for other in others:
            pl.semaphore_signal(barrier, inc=1, device_id=other, device_id_type=MESH)
        ends = (self.place == 0).astype(jnp.int32) + (self.place == self.count - 1).astype(jnp.int32)
        pl.semaphore_wait(barrier, 2 - ends + len(others))

    def span(self, owner, part):
        return pl.ds(pl.multiple_of(owner * self.rows + part * self.part, self.part), self.part)

    def sum_copy(self, source, step, slot, part):
        recv, _, send_sem, recv_sem = self.sums[step]
        return pltpu.make_async_remote_copy(
            src_ref=source, dst_ref=recv.at[slot, part],
            send_sem=send_sem.at[slot, part], recv_sem=recv_sem.at[slot, part],
            device_id=device(self.replica, self.shard, self.place + step), device_id_type=MESH,
        )

    def row_copy(self, step, owner, distance, part, source=None):
        send_sem, recv_sem = self.sends[step]
        where = self.rows_ref.at[self.span(owner, part)]
        return pltpu.make_async_remote_copy(
            src_ref=where if source is None else source, dst_ref=where,
            send_sem=send_sem.at[distance, part], recv_sem=recv_sem.at[distance, part],
            device_id=device(self.replica, self.shard, self.place + step), device_id_type=MESH,
        )

    def emit(self, place, task):
        kind, step, slot, part = task
        if kind in ("inject", "forward"):
            recv, send, _, _ = self.sums[step]
            owner = self.count - 1 - slot if step > 0 else slot
            source = self.partial_ref.at[self.span(owner, part)]
            if kind == "forward":
                self.sum_copy(source, step, slot, part).wait_recv()

                @pl.loop(0, self.partial_ref.shape[1] // LANES)
                def _(step_index):
                    cols = pl.ds(pl.multiple_of(step_index * LANES, LANES), LANES)
                    mine = self.partial_ref[self.span(owner, part), cols].astype(F32)
                    send[slot, part, :, cols] = (mine + recv[slot, part, :, cols].astype(F32)).astype(BF16)

                source = send.at[slot, part]
            copy = self.sum_copy(source, step, slot, part)
            copy.start()
        elif kind == "relay":
            owner = place - step * slot
            self.row_copy(step, owner, slot - 1, part).wait_recv()
            if slot < self.count - 1 and 0 <= place + step < self.count:
                self.row_copy(step, owner, slot, part).start()
        elif kind == "spread":
            self.spread_from(place, part)
        else:
            self.collect(part)
            self.finish(part, pl.ds(part * self.part, self.part), None)

    def spread_from(self, place, part):
        for step in (1, -1):
            if 0 <= place + step < self.count:
                source = None if self.source_ref is None else self.source_ref.at[pl.ds(part * self.part, self.part)]
                self.row_copy(step, place, 0, part, source).start()

    def run(self, index):
        for place in range(self.count):
            tasks = self.tasks[place][index]
            if tasks:
                @pl.when(self.place == place)
                def _():
                    for task in tasks:
                        self.emit(place, task)

    def run_at(self, base, step, count, stride=1):
        for index in range(count):
            if any(tasks[base + stride * index] for tasks in self.tasks):
                @pl.when(step == index)
                def _():
                    self.run(base + stride * index)

    def collect(self, part):
        places = []
        for step in (1, -1):
            recv, send, _, _ = self.sums[step]
            slot = self.count - 1 - self.place if step > 0 else self.place
            has = self.place > 0 if step > 0 else self.place < self.count - 1

            @pl.when(has)
            def _():
                self.sum_copy(send.at[0, part], step, slot, part).wait_recv()

            places.append((recv, slot, has))

        @pl.loop(0, self.partial_ref.shape[1] // LANES)
        def _(index):
            cols = pl.ds(pl.multiple_of(index * LANES, LANES), LANES)
            self.total_ref[:, cols] = self.partial_ref[self.span(self.place, part), cols].astype(F32)
            for recv, slot, has in places:
                @pl.when(has)
                def _():
                    self.total_ref[:, cols] += recv[slot, part, :, cols].astype(F32)

    def finish_all(self):
        @pl.loop(0, self.parts)
        def _(part):
            self.run_at(0, part, self.parts)
            self.collect(part)
            local = pl.ds(pl.multiple_of(part * self.part, self.part), self.part)
            self.finish(part, local, self.span(self.place, part))
            if self.sends:
                for place in range(self.count):
                    @pl.when(self.place == place)
                    def _():
                        self.spread_from(place, part)

        self.run(self.parts)
        self.drain()

    def drain(self):
        for place in range(self.count):
            @pl.when(self.place == place)
            def _():
                for part in range(self.parts):
                    for step in (1, -1):
                        if self.sums:
                            send = self.sums[step][1]
                            for slot in range(self.count - 1):
                                owner = self.count - 1 - slot if step > 0 else slot
                                if (owner - place) * step > 0:
                                    self.sum_copy(send.at[slot, part], step, slot, part).wait_send()
                        if self.sends and 0 <= place + step < self.count:
                            for distance in range(self.count - 1):
                                owner = place - step * distance
                                if 0 <= owner < self.count:
                                    self.row_copy(step, owner, distance, part).wait_send()


def line_scratch(count, rows, features, sums, spreads, parts=PARTS):
    dma = pltpu.SemaphoreType.DMA
    slots = (count - 1, parts)
    scratch = []
    if sums:
        for _ in range(2):
            scratch += [pltpu.VMEM(slots + (rows // parts, features), BF16)] * 2 + [dma(slots)] * 2
        scratch.append(pltpu.VMEM((rows // parts, features), F32))
    if spreads:
        scratch += [dma(slots)] * 4
    return scratch


def finishes(parts):
    return [("finish", part) for part in range(parts)]


def middle_kernel(count, partial_ref, input_ref, gain_ref, rows_ref, resid_ref, *scratch):
    line = Line(count, input_ref.shape[0], scratch, finishes(TURN_PARTS), True, True, TURN_PARTS)

    def finish(part, local, place):
        resid = input_ref[local, :].astype(F32) + line.total_ref[...]
        resid_ref[local, :] = resid
        rows_ref[place, :] = (resid * rms_scale(resid) * gain_ref[...]).astype(BF16)

    line.partial_ref, line.rows_ref, line.finish = partial_ref, rows_ref, finish
    line.greet()
    line.finish_all()


def turn_kernel(count, partial_ref, resid_ref, grad_ref, gain_ref, rows_ref, d_resid_ref, d_gain_ref, *scratch):
    line = Line(count, resid_ref.shape[0], scratch, finishes(TURN_PARTS), True, True, TURN_PARTS)

    def finish(part, local, place):
        resid, total = resid_ref[local, :], line.total_ref[...]
        scale = rms_scale(resid)
        sums = jnp.sum(total * resid * scale, axis=0, keepdims=True)
        d_gain_ref[...] += sums
        d_resid = grad_ref[local, :].astype(F32) + rms_back(resid, scale, gain_ref[...], total)
        d_resid_ref[local, :] = d_resid
        rows_ref[place, :] = d_resid.astype(BF16)

    d_gain_ref[...] = jnp.zeros_like(d_gain_ref)
    line.partial_ref, line.rows_ref, line.finish = partial_ref, rows_ref, finish
    line.greet()
    line.finish_all()


def last_kernel(count, partial_ref, input_ref, d_resid_ref, gain_ref, d_input_ref, d_gain_ref, *scratch):
    line = Line(count, input_ref.shape[0], scratch, finishes(PARTS), True, False)

    def finish(part, local, place):
        values, total = input_ref[local, :].astype(F32), line.total_ref[...]
        scale = rms_scale(values)
        sums = jnp.sum(total * values * scale, axis=0, keepdims=True)
        d_gain_ref[...] += sums
        d_input_ref[local, :] = d_resid_ref[local, :] + rms_back(values, scale, gain_ref[...], total)

    d_gain_ref[...] = jnp.zeros_like(d_gain_ref)
    line.partial_ref, line.finish = partial_ref, finish
    line.greet()
    line.finish_all()


def line_call(kernel, name, ident, spreads, out_shape, operands):
    count = lax.axis_size("tensor")
    partial_rows, features = operands[0].shape
    vmem = pl.BlockSpec(memory_space=pltpu.VMEM)
    return pl.pallas_call(
        functools.partial(kernel, count),
        out_shape=out_shape,
        in_specs=[vmem] * len(operands),
        out_specs=[vmem] * len(out_shape),
        scratch_shapes=line_scratch(
            count, partial_rows // count, features, True, spreads, TURN_PARTS if spreads else PARTS
        ),
        compiler_params=pltpu.CompilerParams(
            collective_id=ident, has_side_effects=True, vmem_limit_bytes=16 * 2**20
        ),
        cost_estimate=pl.CostEstimate(flops=10**9, bytes_accessed=60 * 2**20, transcendentals=0),
        name=name,
    )(*operands)


def begin_kernel(
    sizes, starts_ref, length_ref, input_ref, own_gains_ref, beta_ref, own_grad_ref,
    conv_q_ref, conv_k_ref, conv_v_ref, gain_ref,
    gating_ref, query_ref, key_ref, value_ref, project_ref, gate_ref, up_ref,
    gains_ref, partial_ref, grad_rows_ref, rows_ref, mix_ref, whole_project_ref, gate_up_ref,
    raw_ref, gated_ref, mixed_ref, solve_ref, update_ref, state_ref,
    all_rows, normed, mix_all, project_all, ffn_all, raw_all, gated_all, mixed_all, solve_all, update_all, state_all,
    keep_ref, live_ref, carry_ref, strict_ref, incl_ref,
    all_gains, all_beta, local_sem, store_sem, small_send, small_recv,
    first_send, first_recv, second_send, second_recv, third_send, third_recv, *row_sems,
):
    replicas, shards, count = sizes
    rows = input_ref.shape[0]
    width = query_ref.shape[1]
    heads = beta_ref.shape[0]
    share = query_ref.shape[0]
    units = gate_ref.shape[1]
    half = share // 2
    streams = [(ref, mix_all, False, 0, share, index * width) for index, ref in enumerate((gating_ref, query_ref, key_ref, value_ref))]
    streams.append((project_ref, project_all, True, 0, width, 0))
    for first_row in (0, half):
        for index, ref in enumerate((gate_ref, up_ref)):
            streams.append((ref, ffn_all, False, first_row, half, index * units))
    count_streams = len(streams)
    pairs = replicas // 2
    line = Line(count, rows, row_sems[:4], [], False, True, parts=2)
    line.rows_ref, line.source_ref = all_rows, input_ref
    replica, shard, place = line.replica, line.shard, line.place
    partner = replica + 1 - 2 * lax.rem(replica, 2)

    def across(step):
        return lax.rem(replica + 2 * step, replicas)

    def shard_at(shift):
        return lax.rem(shard + shift, shards)

    def held(stream, owner, part):
        ref, whole, spread_cols, first_row, height, col = streams[stream]
        size = height // replicas
        if spread_cols:
            return whole.at[
                pl.ds(pl.multiple_of(part * size, size), size), pl.ds(pl.multiple_of(owner * share, 128), share)
            ]
        start = owner * share + first_row + part * size
        return whole.at[pl.ds(pl.multiple_of(start, size), size), pl.ds(col, ref.shape[1])]

    def own(stream, part):
        ref, _, spread_cols, first_row, height, _ = streams[stream]
        size = height // replicas
        return ref.at[pl.ds(pl.multiple_of(first_row + part * size, size), size), :]

    def remote(source, target, send, recv, where):
        return pltpu.make_async_remote_copy(
            src_ref=source, dst_ref=target, send_sem=send, recv_sem=recv, device_id=where, device_id_type=MESH
        )

    def first(shift, stream, owner):
        return remote(
            own(stream, replica), held(stream, owner, replica),
            first_send.at[shift - 1, stream], first_recv.at[shift - 1, stream],
            device(replica, shard_at(shift), place),
        )

    def second(shift, step, stream, part):
        where = held(stream, shard_at(shards - shift), part)
        return remote(
            where, where, second_send.at[shift - 1, step - 1, stream], second_recv.at[shift - 1, step - 1, stream],
            device(across(step), shard, place),
        )

    def third(shift, step, stream, part):
        where = held(stream, shard_at(shards - shift), part)
        return remote(
            where, where, third_send.at[shift - 1, step, stream], third_recv.at[shift - 1, step, stream],
            device(partner, shard, place),
        )

    def spread(part):
        for there in range(count):
            @pl.when(place == there)
            def _():
                line.spread_from(there, part)

    def relay(distance, part):
        for there in range(count):
            @pl.when(place == there)
            def _():
                for step in (1, -1):
                    if 0 <= there - step * distance < count:
                        line.emit(there, ("relay", step, distance, part))

    features = share * shards
    cols = pl.ds(pl.multiple_of(shard * share, 128), share)
    smalls = ((own_gains_ref, all_gains.at[:, cols]), (beta_ref, all_beta.at[:, cols]))

    def small(shift, index):
        source, target = smalls[index]
        return remote(
            source, target, small_send.at[shift - 1, index], small_recv.at[shift - 1, index],
            device(replica, shard_at(shift), place),
        )

    others = [device(replica, shard_at(shift), place) for shift in range(1, shards)]
    others += [device(across(step), shard, place) for step in range(1, pairs)] + [device(partner, shard, place)]
    line.greet(others)
    for shift in range(1, shards):
        for index in range(len(smalls)):
            small(shift, index).start()
    for part in range(2):
        spread(part)
    for stream in range(count_streams):
        for shift in range(1, shards):
            first(shift, stream, shard).start()
    locals_ = [pltpu.make_async_copy(source, target, local_sem.at[index]) for index, (source, target) in enumerate(smalls)]
    own_rows = pl.ds(pl.multiple_of(shard * share, share), share)
    for index, ref in enumerate((gating_ref, query_ref, key_ref, value_ref)):
        locals_.append(pltpu.make_async_copy(
            ref, mix_all.at[own_rows, pl.ds(index * width, width)], local_sem.at[2 + index],
        ))
    locals_.append(pltpu.make_async_copy(project_ref, project_all.at[:, cols], local_sem.at[6]))
    for index, ref in enumerate((gate_ref, up_ref)):
        locals_.append(pltpu.make_async_copy(
            ref, ffn_all.at[own_rows, pl.ds(index * units, units)], local_sem.at[7 + index],
        ))
    for copy in locals_:
        copy.start()
    for copy in locals_[:2]:
        copy.wait()
    for shift in range(1, shards):
        for index in range(len(smalls)):
            small(shift, index).wait()
    gains_ref[...] = all_gains[...].astype(F32)
    lanes = mix_all.shape[1] - 4 * width
    beta = jnp.concatenate([all_beta[...].astype(F32), jnp.zeros((lanes - heads, features), F32)], axis=0)
    mix_all[:, 4 * width :] = beta.T.astype(BF16)

    def normalize(source, start, size):
        values = source[pl.ds(start, size), :].astype(F32)
        return (values * rms_scale(values) * gains_ref[0:1, :]).astype(BF16)

    normed[line.span(place, 0), :] = normalize(input_ref, 0, line.part)
    normed[line.span(place, 1), :] = normalize(input_ref, line.part, line.part)

    def serve(turn):
        if turn < count_streams:
            for shift in range(1, shards):
                first(shift, turn, shard_at(shards - shift)).wait_recv()
                for step in range(1, pairs):
                    second(shift, step, turn, replica).start()
                third(shift, 0, turn, replica).start()
        distance, part = turn // 2 + 1, turn % 2
        if distance < count:
            relay(distance, part)
        if 0 <= turn - 1 < count_streams:
            for shift in range(1, shards):
                for step in range(1, pairs):
                    came = across(pairs - step)
                    second(shift, step, turn - 1, came).wait_recv()
                    third(shift, step, turn - 1, came).start()
        if distance < count:
            for step in (1, -1):
                owner = place - step * distance
                inside = owner >= 0 if step > 0 else owner < count

                @pl.when(inside)
                def _():
                    start = pl.multiple_of(owner * rows + part * line.part, line.part)
                    normed[line.span(owner, part), :] = normalize(all_rows, start, line.part)
        if 0 <= turn - 2 < count_streams:
            for shift in range(1, shards):
                for step in range(pairs):
                    third(shift, step, turn - 2, replica).wait_recv()
    ready = max(6, 2 * (count - 1))
    for turn in range(ready):
        serve(turn)
    for copy in locals_[2:]:
        copy.wait()

    rows, head_width = live_ref.shape
    chunks = rows // CHUNK
    heads = width // head_width
    tiles, ends = 4 * width // TILE, features // PROJECT_TILE
    shared = [ATTEND_TIMES[0]] * tiles + [ATTEND_TIMES[1]] * (3 * heads) + [ATTEND_TIMES[2]] * ends
    first_line, line = line, Line(count, rows // count, row_sems[4:], shared, False, True, ATTEND_PARTS, ATTEND_LATENCY)
    line.rows_ref, line.source_ref = grad_rows_ref, own_grad_ref
    grad_rows_ref[pl.ds(pl.multiple_of(place * line.rows, line.rows), line.rows), :] = own_grad_ref[...]
    stores = [(normed, rows_ref), (mix_all, mix_ref), (ffn_all.at[own_rows], gate_up_ref.at[own_rows])]

    def store(index):
        return pltpu.make_async_copy(*stores[index], store_sem.at[index])

    for index in range(len(stores)):
        store(index).start()

    @pl.loop(0, tiles)
    def _(tile):
        line.run_at(0, tile, tiles)

        @pl.when(tile == tiles // 2)
        def _():
            serve(ready)

        cols = pl.ds(pl.multiple_of(tile * TILE, TILE), TILE)
        raw_all[:, cols] = dot(normed[...], mix_all[:, cols])

    raw_all[:, 4 * width :] = dot(normed[...], mix_all[:, 4 * width :])
    stores.append((raw_all, raw_ref))
    store(len(stores) - 1).start()
    serve(ready + 1)
    fill_masks(starts_ref, length_ref, keep_ref, live_ref, carry_ref)
    for chunk in range(chunks):
        strict, incl = pair_mask(starts_ref, chunk)
        strict_ref[chunk] = jnp.where(strict, 1.0, 0.0)
        incl_ref[chunk] = jnp.where(incl, 1.0, 0.0)

    @pl.loop(0, heads)
    def _(head):
        line.run_at(tiles, head, heads, 3)
        start = pl.multiple_of(head * head_width, head_width)

        def stream(index):
            return raw_all[:, pl.ds(pl.multiple_of(index * width + start, head_width), head_width)]

        cols = pl.ds(start, head_width)
        conv, _ = convolve(stream(Q), conv_q_ref[:, cols].astype(F32), keep_ref)
        _, act, scale = unit_rows(conv)
        query = (act * scale).astype(BF16)
        conv, _ = convolve(stream(K), conv_k_ref[:, cols].astype(F32), keep_ref)
        _, act, scale = unit_rows(conv)
        keyed = act * scale
        key_low = keyed.astype(BF16)
        conv, _ = convolve(stream(V), conv_v_ref[:, cols].astype(F32), keep_ref)
        valued = conv * sigmoid(conv)
        rate = sigmoid(column(raw_all[:, 4 * width :], head)) * live_ref[...]
        scaled_value = (valued * rate).astype(BF16)
        scaled_key = keyed * rate
        system = []
        for chunk in range(chunks):
            span = slice(chunk * CHUNK, (chunk + 1) * CHUNK)
            pair = dot_nt(key_low[span], key_low[span])
            wide = jnp.concatenate([rate[span]] * (CHUNK // head_width), axis=1)
            system.append(pair * wide * strict_ref[chunk])
        line.run_at(tiles + 1, head, heads, 3)
        memory = None
        inverses = invert(system)
        line.run_at(tiles + 2, head, heads, 3)
        for chunk, solved in enumerate(inverses):
            span = slice(chunk * CHUNK, (chunk + 1) * CHUNK)
            solve_low = solved.astype(BF16)
            solve_all[head * chunks + chunk] = solve_low
            score = dot_nt(query[span], key_low[span]) * incl_ref[chunk]
            if chunk == 0:
                update = dot(solve_low, scaled_value[span])
                update_low = update.astype(BF16)
                mixed = dot(score.astype(BF16), update_low)
            else:
                carry = carry_ref[chunk - 1][span]
                right = jnp.concatenate(
                    [scaled_value[span], (scaled_key[span] * carry).astype(BF16)], axis=1
                )
                both = dot(solve_low, right)
                memory_low = memory.astype(BF16)
                state_all[head * (chunks - 1) + chunk - 1] = memory_low
                update = both[:, :head_width] - dot(both[:, head_width:].astype(BF16), memory_low)
                update_low = update.astype(BF16)
                mixed = carry * dot(query[span], memory_low) + dot(score.astype(BF16), update_low)
            update_all[span, cols] = update_low
            mixed_all[span, cols] = mixed
            if chunk + 1 < chunks:
                last = (keyed[span] * carry_ref[chunk][span]).astype(BF16)
                fresh = dot_tn(last, update_low)
                if memory is None:
                    memory = fresh
                else:
                    memory = memory * carry_ref[chunk - 1][span][CHUNK - 1 :] + fresh
        mixed = mixed_all[:, cols]
        norm = lax.rsqrt(lane_sum(mixed * mixed) * (1.0 / head_width) + 1e-05)
        gating = stream(G)
        gated = mixed * norm * gain_ref[...] * (gating * sigmoid(gating)) * live_ref[...]
        gated_all[:, cols] = gated.astype(BF16)
        for index in range(1, heads, 2):
            @pl.when(head == index)
            def _():
                serve(ready + 2 + index // 2)

    stores += [
        (project_all, whole_project_ref), (gated_all, gated_ref), (mixed_all, mixed_ref), (solve_all, solve_ref),
        (update_all, update_ref), (state_all, state_ref),
    ]
    for shift in range(1, shards):
        there = pl.ds(pl.multiple_of(shard_at(shift) * share, half), half)
        stores.append((ffn_all.at[there], gate_up_ref.at[there]))
    for index in range(3 + 1, len(stores)):
        store(index).start()

    @pl.loop(0, ends)
    def _(tile):
        line.run_at(tiles + 3 * heads, tile, ends)
        cols = pl.ds(pl.multiple_of(tile * PROJECT_TILE, PROJECT_TILE), PROJECT_TILE)
        partial_ref[:, cols] = dot(gated_all[...], project_all[:, cols]).astype(BF16)

    line.run(tiles + 3 * heads + ends)
    line.drain()
    for turn in range(ready + 2 + heads // 2, count_streams + 2):
        serve(turn)
    for shift in range(1, shards):
        there = pl.ds(pl.multiple_of(shard_at(shift) * share + half, half), half)
        stores.append((ffn_all.at[there], gate_up_ref.at[there]))
        store(len(stores) - 1).start()
    for index in range(len(stores)):
        store(index).wait()

    for stream in range(count_streams):
        for shift in range(1, shards):
            first(shift, stream, shard).wait_send()
            for step in range(1, pairs):
                second(shift, step, stream, replica).wait_send()
            for step in range(pairs):
                third(shift, step, stream, replica).wait_send()
    first_line.drain()


def begin(starts, length, layer_input, first_gain, second_gain, w_beta, output_grad, convs, gain, mixers, w_project, ffn):
    replicas, shards, count = extents()
    rows, features = layer_input.shape
    share, width = mixers[0].shape
    heads_here = w_beta.shape[1]
    head_width = gain.shape[-1]
    seq_rows = count * rows
    heads, chunks = width // head_width, seq_rows // CHUNK
    pairs, far = replicas // 2, max(shards - 1, 1)
    streams = 9
    wide = 4 * width + head_width
    hbm_out = [
        ((seq_rows, features), BF16),
        ((features, wide), BF16),
        ((width, features), BF16),
        ((features, 2 * ffn[0].shape[1]), BF16),
        ((seq_rows, wide), F32),
        ((seq_rows, width), BF16),
        ((seq_rows, width), F32),
        ((heads * chunks, CHUNK, CHUNK), BF16),
        ((seq_rows, width), BF16),
        ((heads * (chunks - 1), head_width, head_width), BF16),
    ]
    vmem_out = [((2, features), F32), ((seq_rows, features), BF16), ((seq_rows, features), BF16)]
    vmem = pl.BlockSpec(memory_space=pltpu.VMEM)
    hbm = pl.BlockSpec(memory_space=pltpu.HBM)
    smem = pl.BlockSpec(memory_space=pltpu.SMEM)
    dma = pltpu.SemaphoreType.DMA
    weights = [pltpu.with_memory_space_constraint(weight, pltpu.HBM) for weight in (*mixers, w_project, *ffn)]
    return pl.pallas_call(
        functools.partial(begin_kernel, (replicas, shards, count)),
        out_shape=[jax.ShapeDtypeStruct(*entry) for entry in vmem_out] + [pltpu.HBM(*entry) for entry in hbm_out],
        in_specs=[smem] * 2 + [vmem] * 8 + [hbm] * 7,
        out_specs=[vmem] * 3 + [hbm] * len(hbm_out),
        scratch_shapes=[pltpu.VMEM((seq_rows, features), BF16)]
        + [pltpu.VMEM(*entry) for entry in hbm_out]
        + [
            pltpu.VMEM((KERNEL - 1, seq_rows, head_width), F32),
            pltpu.VMEM((seq_rows, head_width), F32),
            pltpu.VMEM((chunks - 1, seq_rows, head_width), F32),
            pltpu.VMEM((chunks, CHUNK, CHUNK), F32),
            pltpu.VMEM((chunks, CHUNK, CHUNK), F32),
            pltpu.VMEM((2, features), BF16),
            pltpu.VMEM((heads_here, features), BF16),
            dma((9,)),
            dma((10 + 2 * far,)),
            dma((far, 2)),
            dma((far, 2)),
            dma((far, streams)),
            dma((far, streams)),
            dma((far, max(pairs - 1, 1), streams)),
            dma((far, max(pairs - 1, 1), streams)),
            dma((far, pairs, streams)),
            dma((far, pairs, streams)),
        ]
        + line_scratch(count, rows, features, False, True, 2)
        + line_scratch(count, rows, features, False, True, ATTEND_PARTS),
        compiler_params=pltpu.CompilerParams(collective_id=5, has_side_effects=True, vmem_limit_bytes=56 * 2**20),
        cost_estimate=pl.CostEstimate(
            flops=2 * 36 * heads * chunks * CHUNK**3, bytes_accessed=60 * 2**20, transcendentals=0
        ),
        name="begin",
    )(
        starts, length, layer_input, jnp.stack([first_gain, second_gain]), w_beta.T, output_grad, *convs, gain, *weights
    )


def fetched(far_refs, scratch):
    count = len(far_refs)
    near, sems, rest = scratch[:count], scratch[count], scratch[count + 1 :]
    loads = [pltpu.make_async_copy(far, ref, sems.at[index]) for index, (far, ref) in enumerate(zip(far_refs, near))]
    for load in loads:
        load.start()
    return near, rest, loads


class Pair:

    def __init__(self, features, owners, left_ref, right_ref, grad_refs, out_ref, scratch):
        self.owners, self.left_ref, self.right_ref, self.grad_refs = owners, left_ref, right_ref, grad_refs
        self.out_ref = out_ref
        self.tiles, self.came, self.send_sem, self.recv_sem, self.out_sem = scratch
        self.core = lax.axis_index("core")
        replica, shard, place = coordinates()
        self.partner = device(replica + 1 - 2 * self.core, shard, place)
        self.blocks, self.size = out_ref.shape[:2]
        self.share = features // (2 * lax.axis_size("pair"))

    def copy(self, block):
        return pltpu.make_async_remote_copy(
            src_ref=self.tiles.at[block], dst_ref=self.came.at[block], send_sem=self.send_sem.at[block],
            recv_sem=self.recv_sem.at[block], device_id=self.partner, device_id_type=MESH,
        )

    def product(self, block, core):
        steps = self.share // self.size
        start = (lax.div(block, steps) * 2 + core) * self.share + lax.rem(block, steps) * self.size
        cols = pl.ds(pl.multiple_of(start, self.size), self.size)
        start = 0
        for owner, grad_ref in zip(self.owners, self.grad_refs):
            wide = grad_ref.shape[1]
            values = dot_tn((self.left_ref if owner == 0 else self.right_ref)[:, cols], grad_ref[...])
            yield slice(start, start + wide), values
            start += wide

    def theirs(self, block):
        for span, values in self.product(block, 1 - self.core):
            self.tiles[block, :, span] = values.astype(BF16)
        self.copy(block).start()

    def store(self, block):
        return pltpu.make_async_copy(self.tiles.at[block], self.out_ref.at[block], self.out_sem.at[block])

    def ours(self, block):
        self.copy(block).wait()
        for span, values in self.product(block, self.core):
            self.tiles[block, :, span] = (values + self.came[block, :, span].astype(F32)).astype(BF16)
        self.store(block).start()

    def drain(self):
        for block in range(self.blocks):
            self.store(block).wait()


def pair_shape(left, grads):
    features = left.shape[1]
    return features // (2 * CHUNK), CHUNK, sum(grad.shape[1] for grad in grads)


def pair_scratch(shape):
    dma = pltpu.SemaphoreType.DMA
    return [pltpu.VMEM(shape, BF16), pltpu.VMEM(shape, BF16)] + [dma(shape[:1])] * 3


def mix_grads_kernel(features, left_ref, right_ref, first_ref, second_ref, out_ref, *scratch):
    pair = Pair(features, (0, 1), left_ref, right_ref, (first_ref, second_ref), out_ref, scratch)
    barrier = pltpu.get_barrier_semaphore()
    pl.semaphore_signal(barrier, inc=1, device_id=pair.partner, device_id_type=MESH)
    pl.semaphore_wait(barrier, 1)
    pl.loop(0, pair.blocks)(pair.theirs)
    pl.loop(0, pair.blocks)(pair.ours)
    pair.drain()


def mix_grads(left, right, grads):
    shape = pair_shape(left, grads)
    vmem = pl.BlockSpec(memory_space=pltpu.VMEM)
    out = pl.pallas_call(
        functools.partial(mix_grads_kernel, left.shape[1]),
        out_shape=pltpu.HBM(shape, BF16),
        in_specs=[vmem] * 4,
        out_specs=pl.BlockSpec(memory_space=pltpu.HBM),
        scratch_shapes=pair_scratch(shape),
        compiler_params=pltpu.CompilerParams(collective_id=7, has_side_effects=True, vmem_limit_bytes=24 * 2**20),
        cost_estimate=pl.CostEstimate(
            flops=2 * left.shape[0] * left.shape[1] * shape[2], bytes_accessed=30 * 2**20, transcendentals=0
        ),
        name="mix_grads",
    )(left, right, *grads)
    return out.reshape(shape[0] * shape[1], shape[2])


BLOCK_TIME, TILE_TIME = 2.8, 1.3


def ffn_grads_kernel(
    count, features, partial_ref, gate_up_ref, left_far, right_far, d_gate_far, d_up_far, hidden_far, resid_far,
    out_ref, result_ref, d_partial_ref, *scratch,
):
    *scratch, weights, weights_sem = scratch
    near, scratch, loads = fetched((left_far, right_far, d_gate_far, d_up_far, hidden_far, resid_far), scratch)
    left_ref, right_ref, d_gate_ref, d_up_ref, hidden_ref, resid_ref = near
    weights_load = pltpu.make_async_copy(gate_up_ref, weights, weights_sem)
    pair = Pair(features, (0, 0, 1), left_ref, right_ref, (d_gate_ref, d_up_ref, hidden_ref), out_ref, scratch[:5])
    tiles = features // TILE
    units = d_gate_ref.shape[1]
    shared = [BLOCK_TIME] * (2 * pair.blocks) + [TILE_TIME] * tiles
    line = Line(count, resid_ref.shape[0], scratch[5:], shared, True, False, latency=FFN_LATENCY)

    def finish(part, local, place):
        result_ref[local, :] = (resid_ref[local, :] + line.total_ref[...]).astype(BF16)

    line.partial_ref, line.finish = partial_ref, finish
    line.greet([pair.partner])

    @pl.loop(0, pair.blocks)
    def _(block):
        line.run_at(0, block, pair.blocks)

        @pl.when(block == 0)
        def _():
            for load in loads:
                load.wait()
            weights_load.start()

        pair.theirs(block)

    @pl.loop(0, pair.blocks)
    def _(block):
        line.run_at(pair.blocks, block, pair.blocks)
        pair.ours(block)

    weights_load.wait()

    @pl.loop(0, tiles)
    def _(tile):
        line.run_at(2 * pair.blocks, tile, tiles)
        cols = pl.ds(pl.multiple_of(tile * TILE, TILE), TILE)
        values = dot_nt(d_gate_ref[...], weights[cols, :units]) + dot_nt(d_up_ref[...], weights[cols, units:])
        d_partial_ref[:, cols] = values.astype(BF16)

    line.run(2 * pair.blocks + tiles)
    line.drain()
    pair.drain()


def ffn_grads(left, right, grads, ffn_partial, resid, gate_up):
    count = lax.axis_size("tensor")
    far = (left, right, *grads, resid)
    shape = pair_shape(left, grads)
    vmem = pl.BlockSpec(memory_space=pltpu.VMEM)
    sums, result, d_partial = pl.pallas_call(
        functools.partial(ffn_grads_kernel, count, left.shape[1]),
        out_shape=(jax.ShapeDtypeStruct(shape, BF16), jax.ShapeDtypeStruct(resid.shape, BF16), jax.ShapeDtypeStruct(left.shape, BF16)),
        in_specs=[vmem] + [pl.BlockSpec(memory_space=pltpu.HBM)] * (1 + len(far)),
        out_specs=[pl.BlockSpec(memory_space=pltpu.HBM), vmem, vmem],
        scratch_shapes=[pltpu.VMEM(operand.shape, operand.dtype) for operand in far]
        + [pltpu.SemaphoreType.DMA((len(far),))]
        + pair_scratch(shape)
        + line_scratch(count, resid.shape[0], resid.shape[1], True, False)
        + [pltpu.VMEM(gate_up.shape, BF16), pltpu.SemaphoreType.DMA],
        compiler_params=pltpu.CompilerParams(collective_id=6, has_side_effects=True, vmem_limit_bytes=FFN_MEMORY),
        cost_estimate=pl.CostEstimate(
            flops=2 * left.shape[0] * left.shape[1] * shape[2], bytes_accessed=50 * 2**20, transcendentals=0
        ),
        name="ffn_grads",
    )(ffn_partial, *[pltpu.with_memory_space_constraint(operand, pltpu.HBM) for operand in (gate_up, *far)])
    return sums.reshape(shape[0] * shape[1], shape[2]), result, d_partial


def group_scatter(sums):
    return lax.psum_scatter(sums, ("pair", "fsdp"), scatter_dimension=0, tiled=True)


def widen_kernel(parts, shard_ref, *out_refs):
    for (start, stop, flip), out_ref in zip(parts, out_refs):
        values = shard_ref[:, start:stop].astype(F32)
        out_ref[...] = values.T if flip else values


def widen(shard, parts, name):
    rows = shard.shape[0]
    shapes = [(stop - start, rows) if flip else (rows, stop - start) for start, stop, flip in parts]
    vmem = pl.BlockSpec(memory_space=pltpu.VMEM)
    return pl.pallas_call(
        functools.partial(widen_kernel, parts),
        out_shape=[jax.ShapeDtypeStruct(shape, F32) for shape in shapes],
        in_specs=[vmem],
        out_specs=[vmem] * len(parts),
        compiler_params=pltpu.CompilerParams(vmem_limit_bytes=16 * 2**20),
        cost_estimate=pl.CostEstimate(flops=10**6, bytes_accessed=8 * 2**20, transcendentals=0),
        name=name,
    )(shard)


def gather_weights(pieces, axis):
    return lax.all_gather(jnp.concatenate(pieces, axis=1), ("fsdp", "pair", "core"), axis=axis, tiled=True)


def scatter_grads(grads, axis=0):
    return lax.psum_scatter(grads, ("pair", "core", "fsdp"), scatter_dimension=axis, tiled=True).astype(F32)


def body(
    layer_input,
    first_gain,
    w_query,
    w_key,
    w_value,
    w_gating,
    w_beta,
    conv_query,
    conv_key,
    conv_value,
    head_gain,
    w_project,
    second_gain,
    w_gate,
    w_up,
    w_down,
    doc_starts,
    seq_lengths,
    output_grad,
):
    replicas, replica = extents()[0], coordinates()[0]
    width = w_query.shape[1]
    units = w_gate.shape[1]
    heads = w_beta.shape[1]
    head_width = head_gain.shape[0]

    def piece(weight, axis):
        size = weight.shape[axis] // replicas
        return lax.dynamic_slice_in_dim(weight, replica * size, size, axis)

    input_float = layer_input.astype(F32)
    conv_q, conv_k, conv_v = conv_query, conv_key, conv_value
    gain_head = head_gain.astype(F32)[None, :]
    (
        gains, attn_partial, grad_rows, rows_one, mix_full, project_full, gate_up,
        raw, gated, mixed, solve, update, state,
    ) = begin(
        doc_starts, seq_lengths, layer_input, first_gain, second_gain, w_beta, output_grad, (conv_q, conv_k, conv_v),
        gain_head, (w_gating, w_query, w_key, w_value), w_project, (w_gate, w_up),
    )
    gain_one, gain_two = gains[:1], gains[1:]
    late, attn_partial = lax.optimization_barrier((w_down, attn_partial))
    down = gather_weights([piece(late, 1)], 1)
    whole_rows = jax.ShapeDtypeStruct(rows_one.shape, BF16)
    own_rows = jax.ShapeDtypeStruct(layer_input.shape, F32)
    gain_sums = jax.ShapeDtypeStruct((1, layer_input.shape[1]), F32)
    rows_two, resid = line_call(
        middle_kernel, "middle", 2, True, (whole_rows, own_rows), (attn_partial, layer_input, gain_two)
    )
    d_hidden = dot_nt(grad_rows, down)
    both = dot(rows_two, gate_up)
    gate_val, up_val = both[:, :units], both[:, units:]
    gate_sig = jax.nn.sigmoid(gate_val)
    silu_gate = gate_val * gate_sig
    hidden = (silu_gate * up_val).astype(BF16)
    d_gate = (d_hidden * up_val * gate_sig * (1.0 + gate_val * (1.0 - gate_sig))).astype(BF16)
    d_up = (d_hidden * silu_gate).astype(BF16)
    ffn_partial = dot(hidden, down).astype(BF16)
    ffn_sums, result, d_partial = ffn_grads(rows_two, grad_rows, (d_gate, d_up, hidden), ffn_partial, resid, gate_up)
    ffn_shard = group_scatter(ffn_sums)
    d_attn, d_resid, grad_second = line_call(
        turn_kernel, "turn", 3, True, (whole_rows, own_rows, gain_sums), (d_partial, resid, output_grad, gain_two)
    )
    d_gated = dot_nt(d_attn, project_full)
    d_raw, d_conv, d_head = delta_backward(
        doc_starts, seq_lengths, raw, conv_q, conv_k, conv_v, gain_head, mixed, solve, update, state, d_gated
    )
    mix_sums, ffn_shard = lax.optimization_barrier(
        (mix_grads(rows_one, d_attn, (d_raw, gated)), ffn_shard)
    )
    mix_shard = group_scatter(mix_sums)
    beta_start = 4 * width
    project_start = beta_start + head_width
    grad_gating, grad_query, grad_key, grad_value, grad_beta, grad_project = widen(
        mix_shard,
        [(index * width, (index + 1) * width, False) for index in range(4)]
        + [(beta_start, beta_start + heads, False), (project_start, project_start + width, True)],
        "widen_mix",
    )
    grad_gate, grad_up, grad_down = widen(
        ffn_shard, [(0, units, False), (units, 2 * units, False), (2 * units, 3 * units, True)], "widen_ffn"
    )
    mix_partial = dot_nt(d_raw, mix_full).astype(BF16)
    input_grad, grad_first = line_call(
        last_kernel, "last", 4, False, (own_rows, gain_sums),
        (mix_partial, layer_input, d_resid, gain_one),
    )
    gain_total, head_total, conv_totals = reduce_small(
        jnp.concatenate([grad_first, grad_second], axis=0), d_head, d_conv
    )
    return (
        result,
        input_grad,
        gain_total[0],
        grad_query,
        grad_key,
        grad_value,
        grad_gating,
        grad_beta,
        conv_totals[:, :width],
        conv_totals[:, width : 2 * width],
        conv_totals[:, 2 * width :],
        head_total[0],
        grad_project,
        gain_total[1],
        grad_gate,
        grad_up,
        grad_down,
    )


def solution(mesh):
    replicas, shards, count = (mesh.shape[name] for name in ("dp", "fsdp", "tensor"))
    mesh = jax.sharding.Mesh(
        mesh.devices.reshape(replicas // 2, 2, shards, count), ("pair", "core", "fsdp", "tensor")
    )
    placed = (
        P(("pair", "core", "fsdp", "tensor"), None),
        P("fsdp"),
        P("fsdp", "tensor"),
        P("fsdp", "tensor"),
        P("fsdp", "tensor"),
        P("fsdp", "tensor"),
        P("fsdp", "tensor"),
        P(None, "tensor"),
        P(None, "tensor"),
        P(None, "tensor"),
        P(),
        P("tensor", "fsdp"),
        P("fsdp"),
        P("fsdp", "tensor"),
        P("fsdp", "tensor"),
        P("tensor", "fsdp"),
        P(("pair", "core", "fsdp"), None),
        P(("pair", "core", "fsdp")),
        P(("pair", "core", "fsdp", "tensor"), None),
    )
    return jax.shard_map(
        body,
        mesh=mesh,
        in_specs=placed,
        out_specs=(
            P(("pair", "core", "fsdp", "tensor"), None),
            P(("pair", "core", "fsdp", "tensor"), None),
            P(("pair", "core", "fsdp")),
            P(("pair", "core", "fsdp"), "tensor"),
            P(("pair", "core", "fsdp"), "tensor"),
            P(("pair", "core", "fsdp"), "tensor"),
            P(("pair", "core", "fsdp"), "tensor"),
            P(("pair", "core", "fsdp"), "tensor"),
            P(None, "tensor"),
            P(None, "tensor"),
            P(None, "tensor"),
            P(),
            P("tensor", ("pair", "core", "fsdp")),
            P(("pair", "core", "fsdp")),
            P(("pair", "core", "fsdp"), "tensor"),
            P(("pair", "core", "fsdp"), "tensor"),
            P("tensor", ("pair", "core", "fsdp")),
        ),
        check_vma=False,
    )
```

```python
import functools
import jax, jax.numpy as jnp
from jax import lax
from jax.experimental import pallas as pl
from jax.experimental.pallas import tpu as pltpu
from jax.sharding import PartitionSpec as P

KERNEL = 4
CHUNK = 256
G, Q, K, V = range(4)
MESH = pl.DeviceIdType.MESH
F32 = jnp.float32
BF16 = jnp.bfloat16


def coordinates():
    replica = lax.axis_index("pair") * 2 + lax.axis_index("core")
    return replica, lax.axis_index("fsdp"), lax.axis_index("tensor")


def extents():
    return lax.axis_size("pair") * 2, lax.axis_size("fsdp"), lax.axis_size("tensor")


def device(replica, shard, place):
    return (lax.div(replica, 2), lax.rem(replica, 2), shard, place)


def dot(left, right):
    return jnp.dot(left, right, preferred_element_type=F32)


def dot_nt(left, right):
    return lax.dot_general(left, right, (((1,), (1,)), ((), ())), preferred_element_type=F32)


def dot_tn(left, right):
    return lax.dot_general(left, right, (((0,), (0,)), ((), ())), preferred_element_type=F32)


def lane_sum(values):
    return jnp.sum(values, axis=-1, keepdims=True)


def document_of(starts_ref, positions):
    total = jnp.zeros_like(positions)
    for entry in range(starts_ref.shape[1]):
        total = total + (positions >= starts_ref[0, entry]).astype(jnp.int32)
    return total


def fill_masks(starts_ref, length_ref, keep_ref, live_ref, carry_ref):
    rows, lanes = live_ref.shape
    place = lax.broadcasted_iota(jnp.int32, (rows, lanes), 0)
    docs = document_of(starts_ref, place)
    for delay in range(1, KERNEL):
        prior = document_of(starts_ref, place - delay)
        keep_ref[delay - 1] = jnp.where((prior == docs) & (place >= delay), 1.0, 0.0)
    live_ref[...] = jnp.where(place < length_ref[0], 1.0, 0.0)
    for edge in range(rows // CHUNK - 1):
        seam = jnp.int32((edge + 1) * CHUNK - 1)
        carry_ref[edge] = jnp.where(docs == document_of(starts_ref, seam), 1.0, 0.0)


def pair_mask(starts_ref, chunk):
    row = lax.broadcasted_iota(jnp.int32, (CHUNK, CHUNK), 0)
    col = lax.broadcasted_iota(jnp.int32, (CHUNK, CHUNK), 1)
    first = chunk * CHUNK
    same = document_of(starts_ref, row + first) == document_of(starts_ref, col + first)
    return same & (row > col), same & (row >= col)


def convolve(raw, taps, keep_ref):
    parts = [raw]
    for delay in range(1, KERNEL):
        parts.append(pltpu.roll(raw, delay, 0) * keep_ref[delay - 1])
    total = parts[0] * taps[KERNEL - 1 : KERNEL]
    for delay in range(1, KERNEL):
        total = total + parts[delay] * taps[KERNEL - 1 - delay : KERNEL - delay]
    return total, parts


def sigmoid(values):
    return 0.5 * jnp.tanh(0.5 * values) + 0.5


def column(values, index):
    lane = lax.broadcasted_iota(jnp.int32, values.shape, 1)
    return lane_sum(jnp.where(lane == index, values, 0.0))


def invert(system):
    size = system[0].shape[0]
    row = lax.broadcasted_iota(jnp.int32, (size, size), 0)
    col = lax.broadcasted_iota(jnp.int32, (size, size), 1)
    apart = row ^ col
    eye = jnp.where(row == col, 1.0, 0.0)
    low = [matrix.astype(BF16) for matrix in system]
    solved = [eye - jnp.where(apart == 1, matrix, 0.0) for matrix in system]
    step = 2
    while step < size:
        level = (apart >= step) & (apart < 2 * step)
        for index, matrix in enumerate(low):
            part = jnp.where(level, matrix, 0.0)
            held = solved[index].astype(BF16)
            solved[index] = solved[index] - dot(dot(held, part).astype(BF16), held)
        step *= 2
    refined = []
    for matrix, high, inverse in zip(system, low, solved):
        rest = (matrix - high.astype(F32)).astype(BF16)
        head = inverse.astype(BF16)
        tail = (inverse - head.astype(F32)).astype(BF16)
        product = dot(high, head) + dot(rest, head) + dot(high, tail)
        residue = eye - inverse - product
        refined.append(inverse + dot(head, residue.astype(BF16)))
    return refined


def unit_rows(conv):
    gate = sigmoid(conv)
    act = conv * gate
    scale = lax.rsqrt(lane_sum(act * act) + 1e-06)
    return gate, act, scale


TILE = 256
PROJECT_TILE = 512
ATTEND_TIMES = (1.2, 1.5, 0.9)


def backward_kernel(
    starts_ref, length_ref, raw_ref, conv_q_ref, conv_k_ref, conv_v_ref, gain_ref,
    mixed_ref, solve_ref, update_ref, state_ref, grad_ref,
    d_raw_ref, d_conv_ref, d_gain_ref,
    keep_ref, live_ref, carry_ref, strict_ref, incl_ref, d_query_ref, d_key_ref, d_value_ref, d_rate_ref,
):
    rows, head_width = live_ref.shape
    width = mixed_ref.shape[1]
    chunks = rows // CHUNK
    fill_masks(starts_ref, length_ref, keep_ref, live_ref, carry_ref)
    for chunk in range(chunks):
        strict, incl = pair_mask(starts_ref, chunk)
        strict_ref[chunk] = jnp.where(strict, 1.0, 0.0)
        incl_ref[chunk] = jnp.where(incl, 1.0, 0.0)
    d_gain_ref[...] = jnp.zeros_like(d_gain_ref)
    d_raw_ref[:, 4 * width :] = jnp.zeros((rows, head_width), BF16)

    @pl.loop(0, width // head_width)
    def _(head):
        start = pl.multiple_of(head * head_width, head_width)

        def place(index):
            return pl.ds(pl.multiple_of(index * width + start, head_width), head_width)

        cols = pl.ds(start, head_width)
        live = live_ref[...]
        mixed = mixed_ref[:, cols]
        norm = lax.rsqrt(lane_sum(mixed * mixed) * (1.0 / head_width) + 1e-05)
        gating = raw_ref[:, place(G)]
        gate = sigmoid(gating)
        normal = mixed * norm
        grad = grad_ref[:, cols].astype(F32) * live
        grad_gain = grad * gain_ref[...]
        swish = gating * gate
        d_raw_ref[:, place(G)] = (grad_gain * normal * gate * (1.0 + gating - swish)).astype(BF16)
        d_gain_ref[...] += jnp.sum(grad * normal * swish, axis=0, keepdims=True)
        d_normal = grad_gain * swish
        d_mixed = norm * (d_normal - normal * (lane_sum(d_normal * normal) * (1.0 / head_width)))
        d_mixed_low = d_mixed.astype(BF16)

        conv_q, parts_q = convolve(raw_ref[:, place(Q)], conv_q_ref[:, cols].astype(F32), keep_ref)
        gate_q, act_q, scale_q = unit_rows(conv_q)
        unit_q = act_q * scale_q
        query = unit_q.astype(BF16)
        conv_k, parts_k = convolve(raw_ref[:, place(K)], conv_k_ref[:, cols].astype(F32), keep_ref)
        gate_k, act_k, scale_k = unit_rows(conv_k)
        keyed = act_k * scale_k
        key_low = keyed.astype(BF16)
        conv_v, parts_v = convolve(raw_ref[:, place(V)], conv_v_ref[:, cols].astype(F32), keep_ref)
        gate_v = sigmoid(conv_v)
        valued = conv_v * gate_v
        sig = sigmoid(column(raw_ref[:, 4 * width :], head))
        rate = sig * live
        scaled_value = (valued * rate).astype(BF16)
        scaled_key = keyed * rate

        d_memory = None
        for chunk in range(chunks - 1, -1, -1):
            span = slice(chunk * CHUNK, (chunk + 1) * CHUNK)
            key_c, query_c, d_mixed_c = key_low[span], query[span], d_mixed_low[span]
            solve = solve_ref[head * chunks + chunk]
            update = update_ref[span, cols]
            incl, strict = incl_ref[chunk], strict_ref[chunk]
            score = (dot_nt(query_c, key_c) * incl).astype(BF16)
            d_update = dot_tn(score, d_mixed_c)
            d_key = None
            if d_memory is not None:
                last = carry_ref[chunk][span]
                d_memory_low = d_memory.astype(BF16)
                d_update = d_update + dot((keyed[span] * last).astype(BF16), d_memory_low)
                d_key = last * dot_nt(update, d_memory_low)
            d_update_low = d_update.astype(BF16)
            d_score = (dot_nt(d_mixed_c, update) * incl).astype(BF16)
            d_query = dot(d_score, key_c)
            d_key_score = dot_tn(d_score, query_c)
            d_key = d_key_score if d_key is None else d_key + d_key_score
            if chunk == 0:
                right = scaled_value[span]
                solved = dot(solve, right)
                d_right = dot_tn(solve, d_update_low)
                d_value_in = d_right
                d_rate = lane_sum(d_value_in * valued[span])
            else:
                carry = carry_ref[chunk - 1][span]
                state = state_ref[head * (chunks - 1) + chunk - 1]
                right = jnp.concatenate([scaled_value[span], (scaled_key[span] * carry).astype(BF16)], axis=1)
                solved = dot(solve, right)
                d_solved_key = -dot_nt(d_update_low, state)
                d_right = dot_tn(solve, jnp.concatenate([d_update_low, d_solved_key.astype(BF16)], axis=1))
                d_value_in = d_right[:, :head_width]
                d_key_in = d_right[:, head_width:] * carry
                carried = (carry * d_mixed[span]).astype(BF16)
                d_query = d_query + dot_nt(carried, state)
                d_key = d_key + rate[span] * d_key_in
                d_rate = lane_sum(d_value_in * valued[span] + d_key_in * keyed[span])
                fresh = dot_tn(query_c, carried) - dot_tn(solved[:, head_width:].astype(BF16), d_update_low)
                if d_memory is None:
                    d_memory = fresh
                else:
                    d_memory = d_memory * carry[CHUNK - 1 :] + fresh
            d_system = dot_nt(d_right.astype(BF16), solved.astype(BF16)) * -strict
            pair = dot_nt(key_c, key_c)
            d_rate = d_rate + lane_sum(d_system * pair)
            wide = jnp.concatenate([rate[span]] * (CHUNK // head_width), axis=1)
            d_pair = (d_system * wide).astype(BF16)
            d_key = d_key + dot(d_pair, key_c) + dot_tn(d_pair, key_c)
            d_query_ref[span] = d_query
            d_key_ref[span] = d_key
            d_value_ref[span] = rate[span] * d_value_in
            d_rate_ref[span] = jnp.broadcast_to(d_rate, (CHUNK, head_width))

        lane = lax.broadcasted_iota(jnp.int32, (rows, head_width), 1)
        d_beta = d_rate_ref[...] * rate * (1.0 - sig)
        tail = d_raw_ref[:, 4 * width :]
        d_raw_ref[:, 4 * width :] = jnp.where(lane == head, d_beta.astype(BF16), tail)

        def conv_back(index, d_conv, parts, taps):
            sums = [jnp.sum(d_conv * part, axis=0, keepdims=True) for part in parts]
            for delay in range(KERNEL):
                tap = KERNEL - 1 - delay
                d_conv_ref[tap : tap + 1, place(index - 1)] = sums[delay]
            total = d_conv * taps[KERNEL - 1 : KERNEL]
            for delay in range(1, KERNEL):
                tap = KERNEL - 1 - delay
                back = pltpu.roll(d_conv * keep_ref[delay - 1], rows - delay, 0)
                total = total + back * taps[tap : tap + 1]
            d_raw_ref[:, place(index)] = total.astype(BF16)

        def unit_back(d_unit, unit, scale, conv, act, gate):
            d_act = scale * (d_unit - unit * lane_sum(d_unit * unit))
            return d_act * gate * (1.0 + conv - act)

        conv_back(Q, unit_back(d_query_ref[...], unit_q, scale_q, conv_q, act_q, gate_q), parts_q, conv_q_ref[:, cols].astype(F32))
        conv_back(K, unit_back(d_key_ref[...], keyed, scale_k, conv_k, act_k, gate_k), parts_k, conv_k_ref[:, cols].astype(F32))
        d_conv_v = d_value_ref[...] * gate_v * (1.0 + conv_v - valued)
        conv_back(V, d_conv_v, parts_v, conv_v_ref[:, cols].astype(F32))


def delta_backward(starts, length, raw, conv_q, conv_k, conv_v, gain, mixed, solve, update, state, grad):
    rows = raw.shape[0]
    head_width = gain.shape[-1]
    width = conv_q.shape[1]
    heads, chunks = width // head_width, rows // CHUNK
    vmem = pl.BlockSpec(memory_space=pltpu.VMEM)
    smem = pl.BlockSpec(memory_space=pltpu.SMEM)
    return pl.pallas_call(
        backward_kernel,
        out_shape=(
            jax.ShapeDtypeStruct((rows, 4 * width + head_width), BF16),
            jax.ShapeDtypeStruct((KERNEL, 3 * width), F32),
            jax.ShapeDtypeStruct((1, head_width), F32),
        ),
        in_specs=[smem, smem] + [vmem] * 10,
        out_specs=[vmem] * 3,
        scratch_shapes=[
            pltpu.VMEM((KERNEL - 1, rows, head_width), F32),
            pltpu.VMEM((rows, head_width), F32),
            pltpu.VMEM((chunks - 1, rows, head_width), F32),
            pltpu.VMEM((chunks, CHUNK, CHUNK), F32),
            pltpu.VMEM((chunks, CHUNK, CHUNK), F32),
        ]
        + [pltpu.VMEM((rows, head_width), F32)] * 4,
        compiler_params=pltpu.CompilerParams(vmem_limit_bytes=18 * 2**20),
        cost_estimate=pl.CostEstimate(
            flops=2 * 12 * heads * chunks * CHUNK**3, bytes_accessed=16 * 2**20, transcendentals=0
        ),
        name="delta_backward",
    )(starts, length, raw, conv_q, conv_k, conv_v, gain, mixed, solve, update, state, grad)


def reduce_kernel(
    group_size, line_size, fsdp_size, gain_ref, head_ref, conv_ref, gain_out, head_out, conv_out,
    line_gain, line_head, stage, group_gain, group_conv,
    line_send, line_recv, group_send, group_recv,
):
    dp, fsdp, tensor = coordinates()
    group = dp * fsdp_size + fsdp
    size = gain_out.shape[1]

    def line_peer(shift):
        return device(dp, fsdp, lax.rem(tensor + shift, line_size))

    def group_peer(shift):
        peer = lax.rem(group + shift, group_size)
        return peer, device(lax.div(peer, fsdp_size), lax.rem(peer, fsdp_size), tensor)

    barrier = pltpu.get_barrier_semaphore()
    for shift in range(1, line_size):
        pl.semaphore_signal(barrier, inc=1, device_id=line_peer(shift), device_id_type=MESH)
    for shift in range(1, group_size):
        pl.semaphore_signal(barrier, inc=1, device_id=group_peer(shift)[1], device_id_type=MESH)
    pl.semaphore_wait(barrier, line_size + group_size - 2)

    copies = []
    for shift in range(1, line_size):
        for part, (source, target) in enumerate(((gain_ref, line_gain), (head_ref, line_head))):
            copy = pltpu.make_async_remote_copy(
                src_ref=source, dst_ref=target.at[shift - 1],
                send_sem=line_send.at[shift - 1, part], recv_sem=line_recv.at[shift - 1, part],
                device_id=line_peer(shift), device_id_type=MESH,
            )
            copy.start()
            copies.append(copy)
    conv_copies = []
    for shift in range(1, group_size):
        copy = pltpu.make_async_remote_copy(
            src_ref=conv_ref, dst_ref=group_conv.at[shift - 1],
            send_sem=group_send.at[shift - 1, 1], recv_sem=group_recv.at[shift - 1, 1],
            device_id=group_peer(shift)[1], device_id_type=MESH,
        )
        copy.start()
        conv_copies.append(copy)
    for copy in copies:
        copy.wait()
    gain = gain_ref[...]
    head = head_ref[...]
    for shift in range(1, line_size):
        gain = gain + line_gain[shift - 1]
        head = head + line_head[shift - 1]
    for peer in range(group_size):
        stage[peer] = jnp.zeros(stage.shape[1:], F32)
        stage[peer, :2, :size] = gain[:, peer * size : (peer + 1) * size]
        stage[peer, 2:3, : head.shape[1]] = head
    for copy in conv_copies:
        copy.wait()
    conv = conv_ref[...]
    for shift in range(1, group_size):
        conv = conv + group_conv[shift - 1]
    conv_out[...] = conv
    copies = []
    for shift in range(1, group_size):
        peer, where = group_peer(shift)
        copy = pltpu.make_async_remote_copy(
            src_ref=stage.at[peer], dst_ref=group_gain.at[shift - 1],
            send_sem=group_send.at[shift - 1, 0], recv_sem=group_recv.at[shift - 1, 0],
            device_id=where, device_id_type=MESH,
        )
        copy.start()
        copies.append(copy)
    for copy in copies:
        copy.wait()
    total = stage[group]
    for shift in range(1, group_size):
        total = total + group_gain[shift - 1]
    gain_out[...] = total[:2, :size]
    head_out[...] = total[2:3, : head.shape[1]]


def reduce_small(gain, head, conv):
    replicas, fsdp_size, line_size = extents()
    group_size = replicas * fsdp_size
    size = gain.shape[1] // group_size
    pad = max(size, head.shape[1])
    vmem = pl.BlockSpec(memory_space=pltpu.VMEM)
    dma = pltpu.SemaphoreType.DMA
    return pl.pallas_call(
        functools.partial(reduce_kernel, group_size, line_size, fsdp_size),
        out_shape=(
            jax.ShapeDtypeStruct((2, size), F32),
            jax.ShapeDtypeStruct(head.shape, F32),
            jax.ShapeDtypeStruct(conv.shape, F32),
        ),
        in_specs=[vmem] * 3,
        out_specs=[vmem] * 3,
        scratch_shapes=[
            pltpu.VMEM((line_size - 1,) + gain.shape, F32),
            pltpu.VMEM((line_size - 1,) + head.shape, F32),
            pltpu.VMEM((group_size, 8, pad), F32),
            pltpu.VMEM((group_size - 1, 8, pad), F32),
            pltpu.VMEM((group_size - 1,) + conv.shape, F32),
            dma((line_size - 1, 2)),
            dma((line_size - 1, 2)),
            dma((group_size - 1, 2)),
            dma((group_size - 1, 2)),
        ],
        compiler_params=pltpu.CompilerParams(collective_id=1, has_side_effects=True, vmem_limit_bytes=8 * 2**20),
        name="reduce_small",
    )(gain, head, conv)


def plan(count, parts, sums, rows, shared, unit, latency=1.5):
    backlog, add, end = 1.5, 0.15 + 0.8 / parts, 0.5 + 3.0 / parts
    rank = {"spread": 0, "relay": 0, "finish": 1, "forward": 2, "inject": 3}
    clock = [0.0] * count
    free, come = {}, [{} for _ in range(count)]
    todo = [set() for _ in range(count)]
    done = [0] * count
    at = [0] * count
    tasks = [[[] for _ in range(len(shared) + 1)] for _ in range(count)]
    own_finish = sums and not any(isinstance(step, tuple) for step in shared)
    for place in range(count):
        for part in range(parts):
            for step in (1, -1):
                behind = 0 <= place - step < count
                for slot in range(count - 1) if sums else ():
                    owner = count - 1 - slot if step > 0 else slot
                    if (owner - place) * step > 0:
                        todo[place].add(("forward" if behind else "inject", step, slot, part))
                for distance in range(1, count) if rows else ():
                    if 0 <= place - step * distance < count:
                        todo[place].add(("relay", step, distance, part))
            if rows and not sums:
                todo[place].add(("spread", 0, 0, part))
            if own_finish:
                todo[place].add(("finish", 0, 0, part))

    def ready(place, task):
        kind, step, slot, part = task
        if kind == "inject":
            return max(0.0, free.get((place, step), 0.0) - backlog * unit)
        if kind == "spread":
            return max([0.0] + [free.get((place, way), 0.0) - backlog * unit for way in (1, -1)])
        if kind == "forward":
            return come[place].get(("sum", step, slot, part))
        if kind == "relay":
            return come[place].get(("row", step, slot, part))
        if part != done[place]:
            return None
        times = [0.0]
        for way in (1, -1):
            if 0 <= place - way < count:
                times.append(come[place].get(("sum", way, count - 1 - place if way > 0 else place, part)))
        return None if None in times else max(times)

    def send(place, step, key):
        if 0 <= place + step < count:
            free[place, step] = max(clock[place], free.get((place, step), 0.0)) + unit
            come[place + step][key] = free[place, step] + latency

    def choices(place):
        found = [(ready(place, task), rank[task[0]], task[3], task[2], task[1], task) for task in todo[place]]
        found = [(max(clock[place], entry[0]),) + entry[1:] for entry in found if entry[0] is not None]
        if at[place] < len(shared):
            step = shared[at[place]]
            when = ready(place, ("finish", 0, 0, step[1])) if isinstance(step, tuple) else clock[place]
            if when is not None:
                found.append((max(when, clock[place]), 1 if isinstance(step, tuple) else 9, 0, 0, 0, step))
        return min(found, key=lambda entry: entry[:5]) if found else None

    while True:
        best = None
        for place in range(count):
            choice = choices(place)
            if choice is not None and (best is None or choice[0] < best[0][0]):
                best = (choice, place)
        if best is None:
            return max(clock), tasks
        choice, place = best
        clock[place] = choice[0]
        task = choice[5]
        if isinstance(task, float):
            clock[place] += task
            at[place] += 1
            continue
        if len(task) == 2:
            at[place] += 1
        else:
            todo[place].discard(task)
            tasks[place][at[place]].append(task)
        kind, step, slot, part = task if len(task) == 4 else ("finish", 0, 0, task[1])
        if kind in ("inject", "forward"):
            clock[place] += add if kind == "forward" else 0.02
            send(place, step, ("sum", step, slot, part))
        elif kind == "relay":
            clock[place] += 0.05
            if slot < count - 1:
                send(place, step, ("row", step, slot + 1, part))
        else:
            if kind == "finish":
                done[place] += 1
                clock[place] += end
            if rows:
                for way in (1, -1):
                    send(place, way, ("row", way, 1, part))


PARTS = 4
LANES = 512
FFN_MEMORY = 50 * 2**20
TURN_PARTS = 4
ATTEND_PARTS = 4
ATTEND_LATENCY, FFN_LATENCY = 1.5, 1.5
UNIT = 11.3


def rms_scale(values):
    return lax.rsqrt(jnp.mean(values * values, axis=-1, keepdims=True) + 1e-05)


def rms_back(values, scale_rows, gain, grad):
    scaled_grad = grad * gain
    inner = jnp.mean(scaled_grad * values, axis=-1, keepdims=True)
    return scale_rows * (scaled_grad - values * scale_rows * scale_rows * inner)


class Line:

    def __init__(self, count, rows, scratch, shared, sums, spreads, parts=PARTS, latency=1.5):
        self.count, self.rows, self.parts = count, rows, parts
        self.part = rows // parts
        scratch = list(scratch)
        self.sums, self.sends = {}, {}
        if sums:
            for step in (1, -1):
                self.sums[step] = [scratch.pop(0) for _ in range(4)]
            self.total_ref = scratch.pop(0)
        if spreads:
            for step in (1, -1):
                self.sends[step] = [scratch.pop(0) for _ in range(2)]
        self.replica, self.shard, self.place = coordinates()
        self.tasks = plan(count, parts, sums, spreads, shared, UNIT / parts, latency)[1]
        self.started = [[] for _ in range(count)]
        self.partial_ref = self.rows_ref = self.source_ref = self.finish = None

    def greet(self, others=()):
        barrier = pltpu.get_barrier_semaphore()
        for step in (1, -1):
            @pl.when(self.place < self.count - 1 if step > 0 else self.place > 0)
            def _():
                pl.semaphore_signal(
                    barrier, inc=1, device_id=device(self.replica, self.shard, self.place + step), device_id_type=MESH
                )
        for other in others:
            pl.semaphore_signal(barrier, inc=1, device_id=other, device_id_type=MESH)
        ends = (self.place == 0).astype(jnp.int32) + (self.place == self.count - 1).astype(jnp.int32)
        pl.semaphore_wait(barrier, 2 - ends + len(others))

    def span(self, owner, part):
        return pl.ds(pl.multiple_of(owner * self.rows + part * self.part, self.part), self.part)

    def sum_copy(self, source, step, slot, part):
        recv, _, send_sem, recv_sem = self.sums[step]
        return pltpu.make_async_remote_copy(
            src_ref=source, dst_ref=recv.at[slot, part],
            send_sem=send_sem.at[slot, part], recv_sem=recv_sem.at[slot, part],
            device_id=device(self.replica, self.shard, self.place + step), device_id_type=MESH,
        )

    def row_copy(self, step, owner, distance, part, source=None):
        send_sem, recv_sem = self.sends[step]
        where = self.rows_ref.at[self.span(owner, part)]
        return pltpu.make_async_remote_copy(
            src_ref=where if source is None else source, dst_ref=where,
            send_sem=send_sem.at[distance, part], recv_sem=recv_sem.at[distance, part],
            device_id=device(self.replica, self.shard, self.place + step), device_id_type=MESH,
        )

    def emit(self, place, task):
        kind, step, slot, part = task
        if kind in ("inject", "forward"):
            recv, send, _, _ = self.sums[step]
            owner = self.count - 1 - slot if step > 0 else slot
            source = self.partial_ref.at[self.span(owner, part)]
            if kind == "forward":
                self.sum_copy(source, step, slot, part).wait_recv()

                @pl.loop(0, self.partial_ref.shape[1] // LANES)
                def _(step_index):
                    cols = pl.ds(pl.multiple_of(step_index * LANES, LANES), LANES)
                    mine = self.partial_ref[self.span(owner, part), cols].astype(F32)
                    send[slot, part, :, cols] = (mine + recv[slot, part, :, cols].astype(F32)).astype(BF16)

                source = send.at[slot, part]
            copy = self.sum_copy(source, step, slot, part)
            copy.start()
        elif kind == "relay":
            owner = place - step * slot
            self.row_copy(step, owner, slot - 1, part).wait_recv()
            if slot < self.count - 1 and 0 <= place + step < self.count:
                self.row_copy(step, owner, slot, part).start()
        elif kind == "spread":
            self.spread_from(place, part)
        else:
            self.collect(part)
            self.finish(part, pl.ds(part * self.part, self.part), None)

    def spread_from(self, place, part):
        for step in (1, -1):
            if 0 <= place + step < self.count:
                source = None if self.source_ref is None else self.source_ref.at[pl.ds(part * self.part, self.part)]
                self.row_copy(step, place, 0, part, source).start()

    def run(self, index):
        for place in range(self.count):
            tasks = self.tasks[place][index]
            if tasks:
                @pl.when(self.place == place)
                def _():
                    for task in tasks:
                        self.emit(place, task)

    def run_at(self, base, step, count, stride=1):
        for index in range(count):
            if any(tasks[base + stride * index] for tasks in self.tasks):
                @pl.when(step == index)
                def _():
                    self.run(base + stride * index)

    def collect(self, part):
        places = []
        for step in (1, -1):
            recv, send, _, _ = self.sums[step]
            slot = self.count - 1 - self.place if step > 0 else self.place
            has = self.place > 0 if step > 0 else self.place < self.count - 1

            @pl.when(has)
            def _():
                self.sum_copy(send.at[0, part], step, slot, part).wait_recv()

            places.append((recv, slot, has))

        @pl.loop(0, self.partial_ref.shape[1] // LANES)
        def _(index):
            cols = pl.ds(pl.multiple_of(index * LANES, LANES), LANES)
            self.total_ref[:, cols] = self.partial_ref[self.span(self.place, part), cols].astype(F32)
            for recv, slot, has in places:
                @pl.when(has)
                def _():
                    self.total_ref[:, cols] += recv[slot, part, :, cols].astype(F32)

    def finish_all(self):
        @pl.loop(0, self.parts)
        def _(part):
            self.run_at(0, part, self.parts)
            self.collect(part)
            local = pl.ds(pl.multiple_of(part * self.part, self.part), self.part)
            self.finish(part, local, self.span(self.place, part))
            if self.sends:
                for place in range(self.count):
                    @pl.when(self.place == place)
                    def _():
                        self.spread_from(place, part)

        self.run(self.parts)
        self.drain()

    def drain(self):
        for place in range(self.count):
            @pl.when(self.place == place)
            def _():
                for part in range(self.parts):
                    for step in (1, -1):
                        if self.sums:
                            send = self.sums[step][1]
                            for slot in range(self.count - 1):
                                owner = self.count - 1 - slot if step > 0 else slot
                                if (owner - place) * step > 0:
                                    self.sum_copy(send.at[slot, part], step, slot, part).wait_send()
                        if self.sends and 0 <= place + step < self.count:
                            for distance in range(self.count - 1):
                                owner = place - step * distance
                                if 0 <= owner < self.count:
                                    self.row_copy(step, owner, distance, part).wait_send()


def line_scratch(count, rows, features, sums, spreads, parts=PARTS):
    dma = pltpu.SemaphoreType.DMA
    slots = (count - 1, parts)
    scratch = []
    if sums:
        for _ in range(2):
            scratch += [pltpu.VMEM(slots + (rows // parts, features), BF16)] * 2 + [dma(slots)] * 2
        scratch.append(pltpu.VMEM((rows // parts, features), F32))
    if spreads:
        scratch += [dma(slots)] * 4
    return scratch


def finishes(parts):
    return [("finish", part) for part in range(parts)]


def middle_kernel(count, partial_ref, input_ref, gain_ref, rows_ref, resid_ref, *scratch):
    line = Line(count, input_ref.shape[0], scratch, finishes(TURN_PARTS), True, True, TURN_PARTS)

    def finish(part, local, place):
        resid = input_ref[local, :].astype(F32) + line.total_ref[...]
        resid_ref[local, :] = resid
        rows_ref[place, :] = (resid * rms_scale(resid) * gain_ref[...]).astype(BF16)

    line.partial_ref, line.rows_ref, line.finish = partial_ref, rows_ref, finish
    line.greet()
    line.finish_all()


def turn_kernel(count, partial_ref, resid_ref, grad_ref, gain_ref, rows_ref, d_resid_ref, d_gain_ref, *scratch):
    line = Line(count, resid_ref.shape[0], scratch, finishes(TURN_PARTS), True, True, TURN_PARTS)

    def finish(part, local, place):
        resid, total = resid_ref[local, :], line.total_ref[...]
        scale = rms_scale(resid)
        sums = jnp.sum(total * resid * scale, axis=0, keepdims=True)
        d_gain_ref[...] += sums
        d_resid = grad_ref[local, :].astype(F32) + rms_back(resid, scale, gain_ref[...], total)
        d_resid_ref[local, :] = d_resid
        rows_ref[place, :] = d_resid.astype(BF16)

    d_gain_ref[...] = jnp.zeros_like(d_gain_ref)
    line.partial_ref, line.rows_ref, line.finish = partial_ref, rows_ref, finish
    line.greet()
    line.finish_all()


def last_kernel(count, partial_ref, input_ref, d_resid_ref, gain_ref, d_input_ref, d_gain_ref, *scratch):
    line = Line(count, input_ref.shape[0], scratch, finishes(PARTS), True, False)

    def finish(part, local, place):
        values, total = input_ref[local, :].astype(F32), line.total_ref[...]
        scale = rms_scale(values)
        sums = jnp.sum(total * values * scale, axis=0, keepdims=True)
        d_gain_ref[...] += sums
        d_input_ref[local, :] = d_resid_ref[local, :] + rms_back(values, scale, gain_ref[...], total)

    d_gain_ref[...] = jnp.zeros_like(d_gain_ref)
    line.partial_ref, line.finish = partial_ref, finish
    line.greet()
    line.finish_all()


def line_call(kernel, name, ident, spreads, out_shape, operands):
    count = lax.axis_size("tensor")
    partial_rows, features = operands[0].shape
    vmem = pl.BlockSpec(memory_space=pltpu.VMEM)
    return pl.pallas_call(
        functools.partial(kernel, count),
        out_shape=out_shape,
        in_specs=[vmem] * len(operands),
        out_specs=[vmem] * len(out_shape),
        scratch_shapes=line_scratch(
            count, partial_rows // count, features, True, spreads, TURN_PARTS if spreads else PARTS
        ),
        compiler_params=pltpu.CompilerParams(
            collective_id=ident, has_side_effects=True, vmem_limit_bytes=16 * 2**20
        ),
        cost_estimate=pl.CostEstimate(flops=10**9, bytes_accessed=60 * 2**20, transcendentals=0),
        name=name,
    )(*operands)


def begin_kernel(
    sizes, starts_ref, length_ref, input_ref, own_gains_ref, beta_ref, own_grad_ref,
    conv_q_ref, conv_k_ref, conv_v_ref, gain_ref,
    gating_ref, query_ref, key_ref, value_ref, project_ref, gate_ref, up_ref,
    gains_ref, partial_ref, grad_rows_ref, rows_ref, mix_ref, whole_project_ref, gate_up_ref,
    raw_ref, gated_ref, mixed_ref, solve_ref, update_ref, state_ref,
    all_rows, normed, mix_all, project_all, ffn_all, raw_all, gated_all, mixed_all, solve_all, update_all, state_all,
    keep_ref, live_ref, carry_ref, strict_ref, incl_ref,
    all_gains, all_beta, local_sem, store_sem, small_send, small_recv,
    first_send, first_recv, second_send, second_recv, third_send, third_recv, *row_sems,
):
    replicas, shards, count = sizes
    rows = input_ref.shape[0]
    width = query_ref.shape[1]
    heads = beta_ref.shape[0]
    share = query_ref.shape[0]
    units = gate_ref.shape[1]
    half = share // 2
    streams = [(ref, mix_all, False, 0, share, index * width) for index, ref in enumerate((gating_ref, query_ref, key_ref, value_ref))]
    streams.append((project_ref, project_all, True, 0, width, 0))
    for first_row in (0, half):
        for index, ref in enumerate((gate_ref, up_ref)):
            streams.append((ref, ffn_all, False, first_row, half, index * units))
    count_streams = len(streams)
    pairs = replicas // 2
    line = Line(count, rows, row_sems[:4], [], False, True, parts=2)
    line.rows_ref, line.source_ref = all_rows, input_ref
    replica, shard, place = line.replica, line.shard, line.place
    partner = replica + 1 - 2 * lax.rem(replica, 2)

    def across(step):
        return lax.rem(replica + 2 * step, replicas)

    def shard_at(shift):
        return lax.rem(shard + shift, shards)

    def held(stream, owner, part):
        ref, whole, spread_cols, first_row, height, col = streams[stream]
        size = height // replicas
        if spread_cols:
            return whole.at[
                pl.ds(pl.multiple_of(part * size, size), size), pl.ds(pl.multiple_of(owner * share, 128), share)
            ]
        start = owner * share + first_row + part * size
        return whole.at[pl.ds(pl.multiple_of(start, size), size), pl.ds(col, ref.shape[1])]

    def own(stream, part):
        ref, _, spread_cols, first_row, height, _ = streams[stream]
        size = height // replicas
        return ref.at[pl.ds(pl.multiple_of(first_row + part * size, size), size), :]

    def remote(source, target, send, recv, where):
        return pltpu.make_async_remote_copy(
            src_ref=source, dst_ref=target, send_sem=send, recv_sem=recv, device_id=where, device_id_type=MESH
        )

    def first(shift, stream, owner):
        return remote(
            own(stream, replica), held(stream, owner, replica),
            first_send.at[shift - 1, stream], first_recv.at[shift - 1, stream],
            device(replica, shard_at(shift), place),
        )

    def second(shift, step, stream, part):
        where = held(stream, shard_at(shards - shift), part)
        return remote(
            where, where, second_send.at[shift - 1, step - 1, stream], second_recv.at[shift - 1, step - 1, stream],
            device(across(step), shard, place),
        )

    def third(shift, step, stream, part):
        where = held(stream, shard_at(shards - shift), part)
        return remote(
            where, where, third_send.at[shift - 1, step, stream], third_recv.at[shift - 1, step, stream],
            device(partner, shard, place),
        )

    def spread(part):
        for there in range(count):
            @pl.when(place == there)
            def _():
                line.spread_from(there, part)

    def relay(distance, part):
        for there in range(count):
            @pl.when(place == there)
            def _():
                for step in (1, -1):
                    if 0 <= there - step * distance < count:
                        line.emit(there, ("relay", step, distance, part))

    features = share * shards
    cols = pl.ds(pl.multiple_of(shard * share, 128), share)
    smalls = ((own_gains_ref, all_gains.at[:, cols]), (beta_ref, all_beta.at[:, cols]))

    def small(shift, index):
        source, target = smalls[index]
        return remote(
            source, target, small_send.at[shift - 1, index], small_recv.at[shift - 1, index],
            device(replica, shard_at(shift), place),
        )

    others = [device(replica, shard_at(shift), place) for shift in range(1, shards)]
    others += [device(across(step), shard, place) for step in range(1, pairs)] + [device(partner, shard, place)]
    line.greet(others)
    for shift in range(1, shards):
        for index in range(len(smalls)):
            small(shift, index).start()
    for part in range(2):
        spread(part)
    for stream in range(count_streams):
        for shift in range(1, shards):
            first(shift, stream, shard).start()
    locals_ = [pltpu.make_async_copy(source, target, local_sem.at[index]) for index, (source, target) in enumerate(smalls)]
    own_rows = pl.ds(pl.multiple_of(shard * share, share), share)
    for index, ref in enumerate((gating_ref, query_ref, key_ref, value_ref)):
        locals_.append(pltpu.make_async_copy(
            ref, mix_all.at[own_rows, pl.ds(index * width, width)], local_sem.at[2 + index],
        ))
    locals_.append(pltpu.make_async_copy(project_ref, project_all.at[:, cols], local_sem.at[6]))
    for index, ref in enumerate((gate_ref, up_ref)):
        locals_.append(pltpu.make_async_copy(
            ref, ffn_all.at[own_rows, pl.ds(index * units, units)], local_sem.at[7 + index],
        ))
    for copy in locals_:
        copy.start()
    for copy in locals_[:2]:
        copy.wait()
    for shift in range(1, shards):
        for index in range(len(smalls)):
            small(shift, index).wait()
    gains_ref[...] = all_gains[...].astype(F32)
    lanes = mix_all.shape[1] - 4 * width
    beta = jnp.concatenate([all_beta[...].astype(F32), jnp.zeros((lanes - heads, features), F32)], axis=0)
    mix_all[:, 4 * width :] = beta.T.astype(BF16)

    def normalize(source, start, size):
        values = source[pl.ds(start, size), :].astype(F32)
        return (values * rms_scale(values) * gains_ref[0:1, :]).astype(BF16)

    normed[line.span(place, 0), :] = normalize(input_ref, 0, line.part)
    normed[line.span(place, 1), :] = normalize(input_ref, line.part, line.part)

    def serve(turn):
        if turn < count_streams:
            for shift in range(1, shards):
                first(shift, turn, shard_at(shards - shift)).wait_recv()
                for step in range(1, pairs):
                    second(shift, step, turn, replica).start()
                third(shift, 0, turn, replica).start()
        distance, part = turn // 2 + 1, turn % 2
        if distance < count:
            relay(distance, part)
        if 0 <= turn - 1 < count_streams:
            for shift in range(1, shards):
                for step in range(1, pairs):
                    came = across(pairs - step)
                    second(shift, step, turn - 1, came).wait_recv()
                    third(shift, step, turn - 1, came).start()
        if distance < count:
            for step in (1, -1):
                owner = place - step * distance
                inside = owner >= 0 if step > 0 else owner < count

                @pl.when(inside)
                def _():
                    start = pl.multiple_of(owner * rows + part * line.part, line.part)
                    normed[line.span(owner, part), :] = normalize(all_rows, start, line.part)
        if 0 <= turn - 2 < count_streams:
            for shift in range(1, shards):
                for step in range(pairs):
                    third(shift, step, turn - 2, replica).wait_recv()
    ready = max(6, 2 * (count - 1))
    for turn in range(ready):
        serve(turn)
    for copy in locals_[2:]:
        copy.wait()

    rows, head_width = live_ref.shape
    chunks = rows // CHUNK
    heads = width // head_width
    tiles, ends = 4 * width // TILE, features // PROJECT_TILE
    shared = [ATTEND_TIMES[0]] * tiles + [ATTEND_TIMES[1]] * (3 * heads) + [ATTEND_TIMES[2]] * ends
    first_line, line = line, Line(count, rows // count, row_sems[4:], shared, False, True, ATTEND_PARTS, ATTEND_LATENCY)
    line.rows_ref, line.source_ref = grad_rows_ref, own_grad_ref
    grad_rows_ref[pl.ds(pl.multiple_of(place * line.rows, line.rows), line.rows), :] = own_grad_ref[...]
    stores = [(normed, rows_ref), (mix_all, mix_ref), (ffn_all.at[own_rows], gate_up_ref.at[own_rows])]

    def store(index):
        return pltpu.make_async_copy(*stores[index], store_sem.at[index])

    for index in range(len(stores)):
        store(index).start()

    @pl.loop(0, tiles)
    def _(tile):
        line.run_at(0, tile, tiles)

        @pl.when(tile == tiles // 2)
        def _():
            serve(ready)

        cols = pl.ds(pl.multiple_of(tile * TILE, TILE), TILE)
        raw_all[:, cols] = dot(normed[...], mix_all[:, cols])

    raw_all[:, 4 * width :] = dot(normed[...], mix_all[:, 4 * width :])
    stores.append((raw_all, raw_ref))
    store(len(stores) - 1).start()
    serve(ready + 1)
    fill_masks(starts_ref, length_ref, keep_ref, live_ref, carry_ref)
    for chunk in range(chunks):
        strict, incl = pair_mask(starts_ref, chunk)
        strict_ref[chunk] = jnp.where(strict, 1.0, 0.0)
        incl_ref[chunk] = jnp.where(incl, 1.0, 0.0)

    @pl.loop(0, heads)
    def _(head):
        line.run_at(tiles, head, heads, 3)
        start = pl.multiple_of(head * head_width, head_width)

        def stream(index):
            return raw_all[:, pl.ds(pl.multiple_of(index * width + start, head_width), head_width)]

        cols = pl.ds(start, head_width)
        conv, _ = convolve(stream(Q), conv_q_ref[:, cols].astype(F32), keep_ref)
        _, act, scale = unit_rows(conv)
        query = (act * scale).astype(BF16)
        conv, _ = convolve(stream(K), conv_k_ref[:, cols].astype(F32), keep_ref)
        _, act, scale = unit_rows(conv)
        keyed = act * scale
        key_low = keyed.astype(BF16)
        conv, _ = convolve(stream(V), conv_v_ref[:, cols].astype(F32), keep_ref)
        valued = conv * sigmoid(conv)
        rate = sigmoid(column(raw_all[:, 4 * width :], head)) * live_ref[...]
        scaled_value = (valued * rate).astype(BF16)
        scaled_key = keyed * rate
        system = []
        for chunk in range(chunks):
            span = slice(chunk * CHUNK, (chunk + 1) * CHUNK)
            pair = dot_nt(key_low[span], key_low[span])
            wide = jnp.concatenate([rate[span]] * (CHUNK // head_width), axis=1)
            system.append(pair * wide * strict_ref[chunk])
        line.run_at(tiles + 1, head, heads, 3)
        memory = None
        inverses = invert(system)
        line.run_at(tiles + 2, head, heads, 3)
        for chunk, solved in enumerate(inverses):
            span = slice(chunk * CHUNK, (chunk + 1) * CHUNK)
            solve_low = solved.astype(BF16)
            solve_all[head * chunks + chunk] = solve_low
            score = dot_nt(query[span], key_low[span]) * incl_ref[chunk]
            if chunk == 0:
                update = dot(solve_low, scaled_value[span])
                update_low = update.astype(BF16)
                mixed = dot(score.astype(BF16), update_low)
            else:
                carry = carry_ref[chunk - 1][span]
                right = jnp.concatenate(
                    [scaled_value[span], (scaled_key[span] * carry).astype(BF16)], axis=1
                )
                both = dot(solve_low, right)
                memory_low = memory.astype(BF16)
                state_all[head * (chunks - 1) + chunk - 1] = memory_low
                update = both[:, :head_width] - dot(both[:, head_width:].astype(BF16), memory_low)
                update_low = update.astype(BF16)
                mixed = carry * dot(query[span], memory_low) + dot(score.astype(BF16), update_low)
            update_all[span, cols] = update_low
            mixed_all[span, cols] = mixed
            if chunk + 1 < chunks:
                last = (keyed[span] * carry_ref[chunk][span]).astype(BF16)
                fresh = dot_tn(last, update_low)
                if memory is None:
                    memory = fresh
                else:
                    memory = memory * carry_ref[chunk - 1][span][CHUNK - 1 :] + fresh
        mixed = mixed_all[:, cols]
        norm = lax.rsqrt(lane_sum(mixed * mixed) * (1.0 / head_width) + 1e-05)
        gating = stream(G)
        gated = mixed * norm * gain_ref[...] * (gating * sigmoid(gating)) * live_ref[...]
        gated_all[:, cols] = gated.astype(BF16)
        for index in range(1, heads, 2):
            @pl.when(head == index)
            def _():
                serve(ready + 2 + index // 2)

    stores += [
        (project_all, whole_project_ref), (gated_all, gated_ref), (mixed_all, mixed_ref), (solve_all, solve_ref),
        (update_all, update_ref), (state_all, state_ref),
    ]
    for shift in range(1, shards):
        there = pl.ds(pl.multiple_of(shard_at(shift) * share, half), half)
        stores.append((ffn_all.at[there], gate_up_ref.at[there]))
    for index in range(3 + 1, len(stores)):
        store(index).start()

    @pl.loop(0, ends)
    def _(tile):
        line.run_at(tiles + 3 * heads, tile, ends)
        cols = pl.ds(pl.multiple_of(tile * PROJECT_TILE, PROJECT_TILE), PROJECT_TILE)
        partial_ref[:, cols] = dot(gated_all[...], project_all[:, cols]).astype(BF16)

    line.run(tiles + 3 * heads + ends)
    line.drain()
    for turn in range(ready + 2 + heads // 2, count_streams + 2):
        serve(turn)
    for shift in range(1, shards):
        there = pl.ds(pl.multiple_of(shard_at(shift) * share + half, half), half)
        stores.append((ffn_all.at[there], gate_up_ref.at[there]))
        store(len(stores) - 1).start()
    for index in range(len(stores)):
        store(index).wait()

    for stream in range(count_streams):
        for shift in range(1, shards):
            first(shift, stream, shard).wait_send()
            for step in range(1, pairs):
                second(shift, step, stream, replica).wait_send()
            for step in range(pairs):
                third(shift, step, stream, replica).wait_send()
    first_line.drain()


def begin(starts, length, layer_input, first_gain, second_gain, w_beta, output_grad, convs, gain, mixers, w_project, ffn):
    replicas, shards, count = extents()
    rows, features = layer_input.shape
    share, width = mixers[0].shape
    heads_here = w_beta.shape[1]
    head_width = gain.shape[-1]
    seq_rows = count * rows
    heads, chunks = width // head_width, seq_rows // CHUNK
    pairs, far = replicas // 2, max(shards - 1, 1)
    streams = 9
    wide = 4 * width + head_width
    hbm_out = [
        ((seq_rows, features), BF16),
        ((features, wide), BF16),
        ((width, features), BF16),
        ((features, 2 * ffn[0].shape[1]), BF16),
        ((seq_rows, wide), F32),
        ((seq_rows, width), BF16),
        ((seq_rows, width), F32),
        ((heads * chunks, CHUNK, CHUNK), BF16),
        ((seq_rows, width), BF16),
        ((heads * (chunks - 1), head_width, head_width), BF16),
    ]
    vmem_out = [((2, features), F32), ((seq_rows, features), BF16), ((seq_rows, features), BF16)]
    vmem = pl.BlockSpec(memory_space=pltpu.VMEM)
    hbm = pl.BlockSpec(memory_space=pltpu.HBM)
    smem = pl.BlockSpec(memory_space=pltpu.SMEM)
    dma = pltpu.SemaphoreType.DMA
    weights = [pltpu.with_memory_space_constraint(weight, pltpu.HBM) for weight in (*mixers, w_project, *ffn)]
    return pl.pallas_call(
        functools.partial(begin_kernel, (replicas, shards, count)),
        out_shape=[jax.ShapeDtypeStruct(*entry) for entry in vmem_out] + [pltpu.HBM(*entry) for entry in hbm_out],
        in_specs=[smem] * 2 + [vmem] * 8 + [hbm] * 7,
        out_specs=[vmem] * 3 + [hbm] * len(hbm_out),
        scratch_shapes=[pltpu.VMEM((seq_rows, features), BF16)]
        + [pltpu.VMEM(*entry) for entry in hbm_out]
        + [
            pltpu.VMEM((KERNEL - 1, seq_rows, head_width), F32),
            pltpu.VMEM((seq_rows, head_width), F32),
            pltpu.VMEM((chunks - 1, seq_rows, head_width), F32),
            pltpu.VMEM((chunks, CHUNK, CHUNK), F32),
            pltpu.VMEM((chunks, CHUNK, CHUNK), F32),
            pltpu.VMEM((2, features), BF16),
            pltpu.VMEM((heads_here, features), BF16),
            dma((9,)),
            dma((10 + 2 * far,)),
            dma((far, 2)),
            dma((far, 2)),
            dma((far, streams)),
            dma((far, streams)),
            dma((far, max(pairs - 1, 1), streams)),
            dma((far, max(pairs - 1, 1), streams)),
            dma((far, pairs, streams)),
            dma((far, pairs, streams)),
        ]
        + line_scratch(count, rows, features, False, True, 2)
        + line_scratch(count, rows, features, False, True, ATTEND_PARTS),
        compiler_params=pltpu.CompilerParams(collective_id=5, has_side_effects=True, vmem_limit_bytes=56 * 2**20),
        cost_estimate=pl.CostEstimate(
            flops=2 * 36 * heads * chunks * CHUNK**3, bytes_accessed=60 * 2**20, transcendentals=0
        ),
        name="begin",
    )(
        starts, length, layer_input, jnp.stack([first_gain, second_gain]), w_beta.T, output_grad, *convs, gain, *weights
    )


def fetched(far_refs, scratch):
    count = len(far_refs)
    near, sems, rest = scratch[:count], scratch[count], scratch[count + 1 :]
    loads = [pltpu.make_async_copy(far, ref, sems.at[index]) for index, (far, ref) in enumerate(zip(far_refs, near))]
    for load in loads:
        load.start()
    return near, rest, loads


class Pair:

    def __init__(self, features, owners, left_ref, right_ref, grad_refs, out_ref, scratch):
        self.owners, self.left_ref, self.right_ref, self.grad_refs = owners, left_ref, right_ref, grad_refs
        self.out_ref = out_ref
        self.tiles, self.came, self.send_sem, self.recv_sem, self.out_sem = scratch
        self.core = lax.axis_index("core")
        replica, shard, place = coordinates()
        self.partner = device(replica + 1 - 2 * self.core, shard, place)
        self.blocks, self.size = out_ref.shape[:2]
        self.share = features // (2 * lax.axis_size("pair"))

    def copy(self, block):
        return pltpu.make_async_remote_copy(
            src_ref=self.tiles.at[block], dst_ref=self.came.at[block], send_sem=self.send_sem.at[block],
            recv_sem=self.recv_sem.at[block], device_id=self.partner, device_id_type=MESH,
        )

    def product(self, block, core):
        steps = self.share // self.size
        start = (lax.div(block, steps) * 2 + core) * self.share + lax.rem(block, steps) * self.size
        cols = pl.ds(pl.multiple_of(start, self.size), self.size)
        start = 0
        for owner, grad_ref in zip(self.owners, self.grad_refs):
            wide = grad_ref.shape[1]
            values = dot_tn((self.left_ref if owner == 0 else self.right_ref)[:, cols], grad_ref[...])
            yield slice(start, start + wide), values
            start += wide

    def theirs(self, block):
        for span, values in self.product(block, 1 - self.core):
            self.tiles[block, :, span] = values.astype(BF16)
        self.copy(block).start()

    def store(self, block):
        return pltpu.make_async_copy(self.tiles.at[block], self.out_ref.at[block], self.out_sem.at[block])

    def ours(self, block):
        self.copy(block).wait()
        for span, values in self.product(block, self.core):
            self.tiles[block, :, span] = (values + self.came[block, :, span].astype(F32)).astype(BF16)
        self.store(block).start()

    def drain(self):
        for block in range(self.blocks):
            self.store(block).wait()


def pair_shape(left, grads):
    features = left.shape[1]
    return features // (2 * CHUNK), CHUNK, sum(grad.shape[1] for grad in grads)


def pair_scratch(shape):
    dma = pltpu.SemaphoreType.DMA
    return [pltpu.VMEM(shape, BF16), pltpu.VMEM(shape, BF16)] + [dma(shape[:1])] * 3


def mix_grads_kernel(features, left_ref, right_ref, first_ref, second_ref, out_ref, *scratch):
    pair = Pair(features, (0, 1), left_ref, right_ref, (first_ref, second_ref), out_ref, scratch)
    barrier = pltpu.get_barrier_semaphore()
    pl.semaphore_signal(barrier, inc=1, device_id=pair.partner, device_id_type=MESH)
    pl.semaphore_wait(barrier, 1)
    pl.loop(0, pair.blocks)(pair.theirs)
    pl.loop(0, pair.blocks)(pair.ours)
    pair.drain()


def mix_grads(left, right, grads):
    shape = pair_shape(left, grads)
    vmem = pl.BlockSpec(memory_space=pltpu.VMEM)
    out = pl.pallas_call(
        functools.partial(mix_grads_kernel, left.shape[1]),
        out_shape=pltpu.HBM(shape, BF16),
        in_specs=[vmem] * 4,
        out_specs=pl.BlockSpec(memory_space=pltpu.HBM),
        scratch_shapes=pair_scratch(shape),
        compiler_params=pltpu.CompilerParams(collective_id=7, has_side_effects=True, vmem_limit_bytes=24 * 2**20),
        cost_estimate=pl.CostEstimate(
            flops=2 * left.shape[0] * left.shape[1] * shape[2], bytes_accessed=30 * 2**20, transcendentals=0
        ),
        name="mix_grads",
    )(left, right, *grads)
    return out.reshape(shape[0] * shape[1], shape[2])


BLOCK_TIME, TILE_TIME = 2.8, 1.3


def ffn_grads_kernel(
    count, features, partial_ref, gate_up_ref, left_far, right_far, d_gate_far, d_up_far, hidden_far, resid_far,
    out_ref, result_ref, d_partial_ref, *scratch,
):
    *scratch, weights, weights_sem = scratch
    near, scratch, loads = fetched((left_far, right_far, d_gate_far, d_up_far, hidden_far, resid_far), scratch)
    left_ref, right_ref, d_gate_ref, d_up_ref, hidden_ref, resid_ref = near
    weights_load = pltpu.make_async_copy(gate_up_ref, weights, weights_sem)
    pair = Pair(features, (0, 0, 1), left_ref, right_ref, (d_gate_ref, d_up_ref, hidden_ref), out_ref, scratch[:5])
    tiles = features // TILE
    units = d_gate_ref.shape[1]
    shared = [BLOCK_TIME] * (2 * pair.blocks) + [TILE_TIME] * tiles
    line = Line(count, resid_ref.shape[0], scratch[5:], shared, True, False, latency=FFN_LATENCY)

    def finish(part, local, place):
        result_ref[local, :] = (resid_ref[local, :] + line.total_ref[...]).astype(BF16)

    line.partial_ref, line.finish = partial_ref, finish
    line.greet([pair.partner])

    @pl.loop(0, pair.blocks)
    def _(block):
        line.run_at(0, block, pair.blocks)

        @pl.when(block == 0)
        def _():
            for load in loads:
                load.wait()
            weights_load.start()

        pair.theirs(block)

    @pl.loop(0, pair.blocks)
    def _(block):
        line.run_at(pair.blocks, block, pair.blocks)
        pair.ours(block)

    weights_load.wait()

    @pl.loop(0, tiles)
    def _(tile):
        line.run_at(2 * pair.blocks, tile, tiles)
        cols = pl.ds(pl.multiple_of(tile * TILE, TILE), TILE)
        values = dot_nt(d_gate_ref[...], weights[cols, :units]) + dot_nt(d_up_ref[...], weights[cols, units:])
        d_partial_ref[:, cols] = values.astype(BF16)

    line.run(2 * pair.blocks + tiles)
    line.drain()
    pair.drain()


def ffn_grads(left, right, grads, ffn_partial, resid, gate_up):
    count = lax.axis_size("tensor")
    far = (left, right, *grads, resid)
    shape = pair_shape(left, grads)
    vmem = pl.BlockSpec(memory_space=pltpu.VMEM)
    sums, result, d_partial = pl.pallas_call(
        functools.partial(ffn_grads_kernel, count, left.shape[1]),
        out_shape=(jax.ShapeDtypeStruct(shape, BF16), jax.ShapeDtypeStruct(resid.shape, BF16), jax.ShapeDtypeStruct(left.shape, BF16)),
        in_specs=[vmem] + [pl.BlockSpec(memory_space=pltpu.HBM)] * (1 + len(far)),
        out_specs=[pl.BlockSpec(memory_space=pltpu.HBM), vmem, vmem],
        scratch_shapes=[pltpu.VMEM(operand.shape, operand.dtype) for operand in far]
        + [pltpu.SemaphoreType.DMA((len(far),))]
        + pair_scratch(shape)
        + line_scratch(count, resid.shape[0], resid.shape[1], True, False)
        + [pltpu.VMEM(gate_up.shape, BF16), pltpu.SemaphoreType.DMA],
        compiler_params=pltpu.CompilerParams(collective_id=6, has_side_effects=True, vmem_limit_bytes=FFN_MEMORY),
        cost_estimate=pl.CostEstimate(
            flops=2 * left.shape[0] * left.shape[1] * shape[2], bytes_accessed=50 * 2**20, transcendentals=0
        ),
        name="ffn_grads",
    )(ffn_partial, *[pltpu.with_memory_space_constraint(operand, pltpu.HBM) for operand in (gate_up, *far)])
    return sums.reshape(shape[0] * shape[1], shape[2]), result, d_partial


def group_scatter(sums):
    return lax.psum_scatter(sums, ("pair", "fsdp"), scatter_dimension=0, tiled=True)


def widen_kernel(parts, shard_ref, *out_refs):
    for (start, stop, flip), out_ref in zip(parts, out_refs):
        values = shard_ref[:, start:stop].astype(F32)
        out_ref[...] = values.T if flip else values


def widen(shard, parts, name):
    rows = shard.shape[0]
    shapes = [(stop - start, rows) if flip else (rows, stop - start) for start, stop, flip in parts]
    vmem = pl.BlockSpec(memory_space=pltpu.VMEM)
    return pl.pallas_call(
        functools.partial(widen_kernel, parts),
        out_shape=[jax.ShapeDtypeStruct(shape, F32) for shape in shapes],
        in_specs=[vmem],
        out_specs=[vmem] * len(parts),
        compiler_params=pltpu.CompilerParams(vmem_limit_bytes=16 * 2**20),
        cost_estimate=pl.CostEstimate(flops=10**6, bytes_accessed=8 * 2**20, transcendentals=0),
        name=name,
    )(shard)


def gather_weights(pieces, axis):
    return lax.all_gather(jnp.concatenate(pieces, axis=1), ("fsdp", "pair", "core"), axis=axis, tiled=True)


def scatter_grads(grads, axis=0):
    return lax.psum_scatter(grads, ("pair", "core", "fsdp"), scatter_dimension=axis, tiled=True).astype(F32)


def body(
    layer_input,
    first_gain,
    w_query,
    w_key,
    w_value,
    w_gating,
    w_beta,
    conv_query,
    conv_key,
    conv_value,
    head_gain,
    w_project,
    second_gain,
    w_gate,
    w_up,
    w_down,
    doc_starts,
    seq_lengths,
    output_grad,
):
    replicas, replica = extents()[0], coordinates()[0]
    width = w_query.shape[1]
    units = w_gate.shape[1]
    heads = w_beta.shape[1]
    head_width = head_gain.shape[0]

    def piece(weight, axis):
        size = weight.shape[axis] // replicas
        return lax.dynamic_slice_in_dim(weight, replica * size, size, axis)

    input_float = layer_input.astype(F32)
    conv_q, conv_k, conv_v = conv_query, conv_key, conv_value
    gain_head = head_gain.astype(F32)[None, :]
    (
        gains, attn_partial, grad_rows, rows_one, mix_full, project_full, gate_up,
        raw, gated, mixed, solve, update, state,
    ) = begin(
        doc_starts, seq_lengths, layer_input, first_gain, second_gain, w_beta, output_grad, (conv_q, conv_k, conv_v),
        gain_head, (w_gating, w_query, w_key, w_value), w_project, (w_gate, w_up),
    )
    gain_one, gain_two = gains[:1], gains[1:]
    late, attn_partial = lax.optimization_barrier((w_down, attn_partial))
    down = gather_weights([piece(late, 1)], 1)
    whole_rows = jax.ShapeDtypeStruct(rows_one.shape, BF16)
    own_rows = jax.ShapeDtypeStruct(layer_input.shape, F32)
    gain_sums = jax.ShapeDtypeStruct((1, layer_input.shape[1]), F32)
    rows_two, resid = line_call(
        middle_kernel, "middle", 2, True, (whole_rows, own_rows), (attn_partial, layer_input, gain_two)
    )
    d_hidden = dot_nt(grad_rows, down)
    both = dot(rows_two, gate_up)
    gate_val, up_val = both[:, :units], both[:, units:]
    gate_sig = jax.nn.sigmoid(gate_val)
    silu_gate = gate_val * gate_sig
    hidden = (silu_gate * up_val).astype(BF16)
    d_gate = (d_hidden * up_val * gate_sig * (1.0 + gate_val * (1.0 - gate_sig))).astype(BF16)
    d_up = (d_hidden * silu_gate).astype(BF16)
    ffn_partial = dot(hidden, down).astype(BF16)
    ffn_sums, result, d_partial = ffn_grads(rows_two, grad_rows, (d_gate, d_up, hidden), ffn_partial, resid, gate_up)
    ffn_shard = group_scatter(ffn_sums)
    d_attn, d_resid, grad_second = line_call(
        turn_kernel, "turn", 3, True, (whole_rows, own_rows, gain_sums), (d_partial, resid, output_grad, gain_two)
    )
    d_gated = dot_nt(d_attn, project_full)
    d_raw, d_conv, d_head = delta_backward(
        doc_starts, seq_lengths, raw, conv_q, conv_k, conv_v, gain_head, mixed, solve, update, state, d_gated
    )
    mix_sums, ffn_shard = lax.optimization_barrier(
        (mix_grads(rows_one, d_attn, (d_raw, gated)), ffn_shard)
    )
    mix_shard = group_scatter(mix_sums)
    beta_start = 4 * width
    project_start = beta_start + head_width
    grad_gating, grad_query, grad_key, grad_value, grad_beta, grad_project = widen(
        mix_shard,
        [(index * width, (index + 1) * width, False) for index in range(4)]
        + [(beta_start, beta_start + heads, False), (project_start, project_start + width, True)],
        "widen_mix",
    )
    grad_gate, grad_up, grad_down = widen(
        ffn_shard, [(0, units, False), (units, 2 * units, False), (2 * units, 3 * units, True)], "widen_ffn"
    )
    mix_partial = dot_nt(d_raw, mix_full).astype(BF16)
    input_grad, grad_first = line_call(
        last_kernel, "last", 4, False, (own_rows, gain_sums),
        (mix_partial, layer_input, d_resid, gain_one),
    )
    gain_total, head_total, conv_totals = reduce_small(
        jnp.concatenate([grad_first, grad_second], axis=0), d_head, d_conv
    )
    return (
        result,
        input_grad,
        gain_total[0],
        grad_query,
        grad_key,
        grad_value,
        grad_gating,
        grad_beta,
        conv_totals[:, :width],
        conv_totals[:, width : 2 * width],
        conv_totals[:, 2 * width :],
        head_total[0],
        grad_project,
        gain_total[1],
        grad_gate,
        grad_up,
        grad_down,
    )


def solution(mesh):
    replicas, shards, count = (mesh.shape[name] for name in ("dp", "fsdp", "tensor"))
    mesh = jax.sharding.Mesh(
        mesh.devices.reshape(replicas // 2, 2, shards, count), ("pair", "core", "fsdp", "tensor")
    )
    placed = (
        P(("pair", "core", "fsdp", "tensor"), None),
        P("fsdp"),
        P("fsdp", "tensor"),
        P("fsdp", "tensor"),
        P("fsdp", "tensor"),
        P("fsdp", "tensor"),
        P("fsdp", "tensor"),
        P(None, "tensor"),
        P(None, "tensor"),
        P(None, "tensor"),
        P(),
        P("tensor", "fsdp"),
        P("fsdp"),
        P("fsdp", "tensor"),
        P("fsdp", "tensor"),
        P("tensor", "fsdp"),
        P(("pair", "core", "fsdp"), None),
        P(("pair", "core", "fsdp")),
        P(("pair", "core", "fsdp", "tensor"), None),
    )
    return jax.shard_map(
        body,
        mesh=mesh,
        in_specs=placed,
        out_specs=(
            P(("pair", "core", "fsdp", "tensor"), None),
            P(("pair", "core", "fsdp", "tensor"), None),
            P(("pair", "core", "fsdp")),
            P(("pair", "core", "fsdp"), "tensor"),
            P(("pair", "core", "fsdp"), "tensor"),
            P(("pair", "core", "fsdp"), "tensor"),
            P(("pair", "core", "fsdp"), "tensor"),
            P(("pair", "core", "fsdp"), "tensor"),
            P(None, "tensor"),
            P(None, "tensor"),
            P(None, "tensor"),
            P(),
            P("tensor", ("pair", "core", "fsdp")),
            P(("pair", "core", "fsdp")),
            P(("pair", "core", "fsdp"), "tensor"),
            P(("pair", "core", "fsdp"), "tensor"),
            P("tensor", ("pair", "core", "fsdp")),
        ),
        check_vma=False,
    )
```
